32 devices in a mesh: wide: 8 (over z, core), narrow: 4 (over y, x).
Axes of the slice: x: 2, y: 2, z: 4, core: 2. Of those that a mesh axis runs over, the one named last changes fastest.
Arguments:
- layer_input: bfloat16 [8192, 2048], P(('wide', 'narrow')), may hold values from -6 to 6
- w_query: bfloat16 [2048, 2048], P('wide', 'narrow'), may hold values from -0.125 to 0.125
- w_key: bfloat16 [2048, 1024], P('wide', 'narrow'), may hold values from -0.125 to 0.125
- w_value: bfloat16 [2048, 1024], P('wide', 'narrow'), may hold values from -0.125 to 0.125
- w_output: bfloat16 [2048, 2048], P('narrow', 'wide'), may hold values from -3 to 3
- w_gate: bfloat16 [2048, 6144], P('wide', 'narrow'), may hold values from -0.125 to 0.125
- w_up: bfloat16 [2048, 6144], P('wide', 'narrow'), may hold values from -0.125 to 0.125
- w_down: bfloat16 [6144, 2048], P('narrow', 'wide'), may hold values from -0.078125 to 0.078125
- attn_gain: float32 [2048], replicated, may hold values from 0.25 to 1.75
- mlp_gain: float32 [2048], replicated, may hold values from 0.25 to 1.75
- query_gain: float32 [128], replicated, may hold values from 0.25 to 1.75
- key_gain: float32 [128], replicated, may hold values from 0.25 to 1.75
- out_grad: bfloat16 [8192, 2048], P(('wide', 'narrow')), may hold values from -6 to 6
Outputs:
- layer_output: bfloat16 [8192, 2048], P(('wide', 'narrow'))
- input_grad: float32 [8192, 2048], P(('wide', 'narrow'))
- grad_query: float32 [2048, 2048], P('wide', 'narrow')
- grad_key: float32 [2048, 1024], P('wide', 'narrow')
- grad_value: float32 [2048, 1024], P('wide', 'narrow')
- grad_output: float32 [2048, 2048], P('narrow', 'wide')
- grad_gate: float32 [2048, 6144], P('wide', 'narrow')
- grad_up: float32 [2048, 6144], P('wide', 'narrow')
- grad_down: float32 [6144, 2048], P('narrow', 'wide')
- grad_attn_gain: float32 [2048], replicated
- grad_mlp_gain: float32 [2048], replicated
- grad_query_gain: float32 [128], replicated
- grad_key_gain: float32 [128], replicated
The draws below stay inside these ranges and needn't reach their ends.
All inputs are finite; a program needn't handle non-finite values.
Results may differ from the reference program's by a relative error of at most 0.024.
Values may be sent and summed in bfloat16 or wider, within the bound.
A program may use at most 192 MiB of HBM per device.

```python
import math
import jax
import jax.numpy as jnp
from jax import lax

D = 2048
H = 16
KV = 8
HD = 128
FF = 6144
SEQ = 8192


def shard_levels(own_key, extent, split, smallest, high):
    loudness = 1.0
    for axis_at, parts in split:
        steps = jax.random.uniform(jax.random.fold_in(jax.random.fold_in(own_key, 6), axis_at), (parts,), jnp.float32, smallest / len(split), high / len(split))
        loudness = loudness * jnp.repeat(jnp.exp(steps), extent[axis_at] // parts).reshape((-1,) + (1,) * (len(extent) - 1 - axis_at))
    return loudness


def gaussian(rng, shape, spread, limit, shards=(), kind=jnp.bfloat16):
    factor_of = shard_levels(rng, shape, shards, -0.22, 0.18) if shards else 1.0
    drawn = jax.random.normal(rng, shape, jnp.float32) * spread * factor_of
    return jnp.minimum(jnp.maximum(drawn, -limit), limit).astype(kind)


def setup_inputs(seed: int = 0) -> dict:
    key_list = jax.random.split(jax.random.key(seed), 14)
    layer_input = gaussian(key_list[0], (SEQ, D), 1.0, 6.0, ((0, 32),))
    w_query = gaussian(key_list[1], (D, H * HD), D ** -0.5, 0.125, ((0, 8), (1, 4)))
    w_key = gaussian(key_list[2], (D, KV * HD), D ** -0.5, 0.125, ((0, 8), (1, 4)))
    w_value = gaussian(key_list[3], (D, KV * HD), D ** -0.5, 0.125, ((0, 8), (1, 4)))
    w_output = gaussian(key_list[4], (H * HD, D), (H * HD * 16 * SEQ ** -1) ** -0.5, 3.0, ((0, 4), (1, 8)))
    w_gate = gaussian(key_list[5], (D, FF), D ** -0.5, 0.125, ((0, 8), (1, 4)))
    w_up = gaussian(key_list[6], (D, FF), D ** -0.5, 0.125, ((0, 8), (1, 4)))
    w_down = gaussian(key_list[7], (FF, D), FF ** -0.5, 0.078125, ((0, 4), (1, 8)))
    attn_gain = jnp.clip(1.0 + 0.15 * jax.random.normal(key_list[8], (D,), jnp.float32), 0.25, 1.75)
    mlp_gain = jnp.clip(1.0 + 0.15 * jax.random.normal(key_list[9], (D,), jnp.float32), 0.25, 1.75)
    query_gain = jnp.clip(1.0 + 0.15 * jax.random.normal(key_list[10], (HD,), jnp.float32), 0.25, 1.75)
    key_gain = jnp.clip(1.0 + 0.15 * jax.random.normal(key_list[11], (HD,), jnp.float32), 0.25, 1.75)
    out_grad = gaussian(key_list[12], (SEQ, D), 1.0, 6.0, ((0, 32),))
    return dict(layer_input=layer_input, w_query=w_query, w_key=w_key, w_value=w_value, w_output=w_output, w_gate=w_gate, w_up=w_up, w_down=w_down, attn_gain=attn_gain, mlp_gain=mlp_gain, query_gain=query_gain, key_gain=key_gain, out_grad=out_grad)


@jax.custom_vjp
def low(v):
    return lax.optimization_barrier(v.astype(jnp.bfloat16)).astype(jnp.float32)

@jax.custom_vjp
def low_back(v):
    return v

def low_keep(v):
    return (low(v), None)

def low_pass(kept, grad):
    return (grad,)

def back_keep(v):
    return (v, None)

def back_low(kept, grad):
    return (low(grad),)
low.defvjp(low_keep, low_pass)
low_back.defvjp(back_keep, back_low)
EPSILON = 1e-06
PRECISE = lax.Precision.HIGHEST
MASKED = -1e+30

def product(multiplier, multiplicand):
    return jnp.dot(multiplier, multiplicand, preferred_element_type=jnp.float32, precision=PRECISE)

def rms_norm(values, scaling):
    return values * lax.rsqrt(lax.optimization_barrier(jnp.mean(values * values, axis=-1, keepdims=True)) + EPSILON) * scaling

def rotation(positions, head_dim):
    steps_half = jnp.arange(head_dim // 2).astype(jnp.float32)
    inverse = jnp.exp(steps_half * (-2.0 * math.log(1000000.0) / head_dim))
    angles = positions.astype(jnp.float32)[:, None] * inverse[None, :]
    angles = jnp.concatenate([angles, angles], axis=1)
    return (jnp.cos(angles)[:, None, :], jnp.sin(angles)[:, None, :])

def rotary(values, cos_table, sin_table):
    half_dim = values.shape[-1] // 2
    turned = jnp.concatenate([-values[..., half_dim:], values[..., :half_dim]], axis=-1)
    return values * cos_table + turned * sin_table

def attend(queries, key_rows, value_rows):
    seq_len = queries.shape[0]
    block_rows = math.gcd(seq_len, 512)
    groups = H // KV
    grouped = queries.reshape(seq_len // block_rows, block_rows, KV, groups, HD)
    starts = jnp.arange(seq_len // block_rows).astype(jnp.int32) * block_rows
    key_pos = jnp.arange(seq_len).astype(jnp.int32)
    score_scale = HD ** (-0.5)

    def one_block(pieces):
        query_block, first_row = pieces
        scores = jnp.einsum('qkgd,skd->kgqs', query_block, key_rows, precision=PRECISE) * score_scale
        scores = low_back(scores)
        query_pos = first_row + jnp.arange(block_rows).astype(jnp.int32)
        allowed = key_pos[None, :] <= query_pos[:, None]
        scores = jnp.where(allowed, scores, MASKED)
        largest = lax.optimization_barrier(jnp.max(scores, axis=-1, keepdims=True))
        weights = jnp.exp(scores - largest)
        weights = weights / lax.optimization_barrier(jnp.sum(weights, axis=-1, keepdims=True))
        return jnp.einsum('kgqs,skd->qkgd', low(weights), value_rows, precision=PRECISE)
    mixed_heads = lax.map(jax.checkpoint(one_block), (grouped, starts))
    return mixed_heads.reshape(seq_len, H * HD)

def layer(layer_input, w_query, w_key, w_value, w_output, w_gate, w_up, w_down, attn_gain, mlp_gain, query_gain, key_gain):
    seq_len = layer_input.shape[0]
    normed = low(rms_norm(layer_input, attn_gain))
    query_proj = low_back(product(normed, w_query)).reshape(seq_len, H, HD)
    key_proj = low_back(product(normed, w_key)).reshape(seq_len, KV, HD)
    value_rows = low(low_back(product(normed, w_value))).reshape(seq_len, KV, HD)
    cos_table, sin_table = rotation(jnp.arange(seq_len).astype(jnp.int32), HD)
    queries = low(rotary(rms_norm(query_proj, query_gain), cos_table, sin_table))
    key_rows = low(rotary(rms_norm(key_proj, key_gain), cos_table, sin_table))
    attended = low(low_back(attend(queries, key_rows, value_rows)))
    middle = layer_input + low_back(product(attended, w_output))
    normed_mlp = low(rms_norm(middle, mlp_gain))
    gate_proj = low_back(product(normed_mlp, w_gate))
    up_proj = low_back(product(normed_mlp, w_up))
    hidden = low(gate_proj * jax.nn.sigmoid(gate_proj) * up_proj)
    return middle + low_back(product(hidden, w_down))

def reference(layer_input, w_query, w_key, w_value, w_output, w_gate, w_up, w_down, attn_gain, mlp_gain, query_gain, key_gain, out_grad):
    operands = (layer_input, w_query, w_key, w_value, w_output, w_gate, w_up, w_down, attn_gain, mlp_gain, query_gain, key_gain)
    floats = [operand.astype(jnp.float32) for operand in operands]
    result, backward = jax.vjp(layer, *floats)
    grads_all = backward(out_grad.astype(jnp.float32))
    return (result.astype(jnp.bfloat16), grads_all[0], grads_all[1], grads_all[2], grads_all[3], grads_all[4], grads_all[5], grads_all[6], grads_all[7], grads_all[8], grads_all[9], grads_all[10], grads_all[11])
```

```python
import functools
import math

import jax
import jax.numpy as jnp
from jax import lax
from jax.experimental import pallas as pl
from jax.experimental.pallas import tpu as pltpu
from jax.sharding import PartitionSpec as P

EPSILON = 1e-06
MASKED = -1e30
F32 = jnp.float32
BF = jnp.bfloat16
MESH = pl.DeviceIdType.MESH
NT = (((1,), (1,)), ((), ()))
NN = (((1,), (0,)), ((), ()))
TN = (((0,), (0,)), ((), ()))


def dg(a, b, dims):
    return lax.dot_general(a, b, dims, preferred_element_type=F32)


class Place:
    def __init__(self, wide, narrow):
        self.W, self.N = wide, narrow
        self.C, self.half = wide // 2, narrow // 2
        self.w, self.n = lax.axis_index("wide"), lax.axis_index("narrow")
        self.k, self.c = self.w // 2, lax.rem(self.w, 2)
        self.far = 2 * (self.C - 1 - self.k) + 1
        late = (self.n >= self.half).astype(jnp.int32)
        self.group = lax.rem(self.c + late, 2)
        self.slot = jnp.where(self.group == 0, self.n, lax.rem(self.n + self.half, self.N))

    def owner(self, j):
        core = 1 if j >= self.half else 0
        n = jnp.where(self.c == 0, j, (j + self.half) % self.N)
        return core, n

    def owner_is_me(self, j):
        core, n = self.owner(j)
        return (self.c == core) & (self.n == n)


def enter(p, far=False, ring=False):
    barrier = pltpu.get_barrier_semaphore()

    def greet(device):
        pl.semaphore_signal(barrier, inc=1, device_id=device, device_id_type=MESH)

    for core in range(2):
        for n in range(p.N):

            @pl.when((p.c != core) | (p.n != n))
            def _():
                greet((2 * p.k + core, n))

    peers = 2 * p.N - 1
    if ring:
        for k in range(p.C):

            @pl.when(p.k != k)
            def _():
                greet((2 * k, p.n))
                greet((2 * k + 1, p.n))

        peers += 2 * (p.C - 1)
    elif far:
        greet((2 * (p.C - 1 - p.k) + p.c, p.n))
        peers += 1
    pl.semaphore_wait(barrier, peers)


def swap_rows(p, src, dst, send_sem, recv_sem):
    return pltpu.make_async_remote_copy(
        src_ref=src, dst_ref=dst, send_sem=send_sem, recv_sem=recv_sem, device_id=(p.far, p.n), device_id_type=MESH
    )


def spread_start(p, src, gathered, rows, send_sems, recv_sems, local_sem):
    view = gathered.at[pl.ds(pl.multiple_of(p.slot * rows, rows), rows)]
    for t in range(p.N):
        mine = (p.group == p.c) & (p.n == t)

        @pl.when(mine)
        def _():
            pltpu.make_async_copy(src, view, local_sem).start()

        @pl.when(jnp.logical_not(mine))
        def _():
            pltpu.make_async_remote_copy(
                src_ref=src,
                dst_ref=view,
                send_sem=send_sems.at[t],
                recv_sem=recv_sems.at[p.slot],
                device_id=(2 * p.k + p.group, t),
                device_id_type=MESH,
            ).start()


def spread_wait(p, src, gathered, rows, send_sems, recv_sems, local_sem):
    for t in range(p.N):
        mine = (p.group == p.c) & (p.n == t)

        @pl.when(mine)
        def _():
            pltpu.make_async_copy(src, gathered.at[pl.ds(0, rows)], local_sem).wait()

        @pl.when(jnp.logical_not(mine))
        def _():
            pltpu.make_async_copy(src, gathered.at[pl.ds(0, rows)], send_sems.at[t]).wait()

    for j in range(p.N):

        @pl.when(jnp.logical_not(p.owner_is_me(j)))
        def _():
            pltpu.make_async_copy(src, gathered.at[pl.ds(j * rows, rows)], recv_sems.at[j]).wait()


def sum_start(p, part, recv, rows, send_sems, recv_sems, local_sem):
    for j in range(p.N):
        core, n = p.owner(j)
        mine = p.owner_is_me(j)

        @pl.when(mine)
        def _():
            pltpu.make_async_copy(part.at[pl.ds(j * rows, rows)], recv.at[p.n], local_sem).start()

        @pl.when(jnp.logical_not(mine))
        def _():
            pltpu.make_async_remote_copy(
                src_ref=part.at[pl.ds(j * rows, rows)],
                dst_ref=recv.at[p.n],
                send_sem=send_sems.at[j],
                recv_sem=recv_sems.at[p.n],
                device_id=(2 * p.k + core, n),
                device_id_type=MESH,
            ).start()


def sum_wait(p, part, recv, rows, send_sems, recv_sems, local_sem):
    for t in range(p.N):
        mine = (p.group == p.c) & (p.n == t)

        @pl.when(mine)
        def _():
            pltpu.make_async_copy(part.at[pl.ds(0, rows)], recv.at[t], local_sem).wait()

        @pl.when(jnp.logical_not(mine))
        def _():
            pltpu.make_async_copy(part.at[pl.ds(0, rows)], recv.at[t], recv_sems.at[t]).wait()

    for j in range(p.N):

        @pl.when(jnp.logical_not(p.owner_is_me(j)))
        def _():
            pltpu.make_async_copy(part.at[pl.ds(j * rows, rows)], recv.at[0], send_sems.at[j]).wait()


def row_loop(rows, step, body):
    def one(i, carry):
        body(pl.ds(pl.multiple_of(i * step, step), step))
        return carry

    lax.fori_loop(0, rows // step, one, 0)


STEP = 64


def inv_rms(u):
    return lax.rsqrt(jnp.mean(u * u, axis=-1, keepdims=True) + EPSILON)


def total(recv, at, count):
    out = recv[0, at, :].astype(F32)
    for t in range(1, count):
        out = out + recv[t, at, :].astype(F32)
    return out


def swap_in(p, x_ref, own_ref, sems):
    @pl.when(p.c == 1)
    def _():
        copy = swap_rows(p, x_ref, own_ref, sems.at[0], sems.at[1])
        copy.start()
        copy.wait()

    @pl.when(p.c == 0)
    def _():
        own_ref[...] = x_ref[...]


def swap_out(p, buf, out_ref, sems):
    @pl.when(p.c == 1)
    def _():
        copy = swap_rows(p, buf, out_ref, sems.at[0], sems.at[1])
        copy.start()
        copy.wait()

    @pl.when(p.c == 0)
    def _():
        out_ref[...] = buf[...]


def input_kernel(wide, narrow, norm, x_ref, gain_ref, own_ref, gathered, buf, send, recv, local, swap):
    p = Place(wide, narrow)
    rows = x_ref.shape[0]
    enter(p, far=True)
    swap_in(p, x_ref, own_ref, swap)
    if norm:

        def body(at):
            u = own_ref[at, :].astype(F32)
            buf[at, :] = (u * inv_rms(u) * gain_ref[...]).astype(BF)

        row_loop(rows, STEP, body)
    src = buf if norm else own_ref
    spread_start(p, src, gathered, rows, send, recv, local)
    spread_wait(p, src, gathered, rows, send, recv, local)


def middle_kernel(wide, narrow, part, own_ref, gain_ref, mid_ref, gathered, got, buf, send, recv, local, send2, recv2, local2):
    p = Place(wide, narrow)
    rows = own_ref.shape[0]
    enter(p)
    sum_start(p, part, got, rows, send, recv, local)
    sum_wait(p, part, got, rows, send, recv, local)

    def body(at):
        u = own_ref[at, :].astype(F32) + total(got, at, p.N)
        mid_ref[at, :] = u
        buf[at, :] = (u * inv_rms(u) * gain_ref[...]).astype(BF)

    row_loop(rows, STEP, body)
    spread_start(p, buf, gathered, rows, send2, recv2, local2)
    spread_wait(p, buf, gathered, rows, send2, recv2, local2)


def output_kernel(wide, narrow, part, mid_ref, out_ref, got, buf, send, recv, local, swap):
    p = Place(wide, narrow)
    rows = mid_ref.shape[0]
    enter(p, far=True)
    sum_start(p, part, got, rows, send, recv, local)
    sum_wait(p, part, got, rows, send, recv, local)

    def body(at):
        buf[at, :] = (mid_ref[at, :] + total(got, at, p.N)).astype(BF)

    row_loop(rows, STEP, body)
    swap_out(p, buf, out_ref, swap)


def norm_back(u, gain, cot):
    r = inv_rms(u)
    a = cot * gain
    du = r * a - u * (r * r * r) * jnp.mean(a * u, axis=-1, keepdims=True)
    return du, jnp.sum(cot * u * r, axis=0, keepdims=True)


def middle_back_kernel(
    wide, narrow, part, mid_ref, gain_ref, grad_ref, back_ref, dgain_ref, gathered,
    got, buf, send, recv, local, send2, recv2, local2,
):
    p = Place(wide, narrow)
    rows = mid_ref.shape[0]
    enter(p)
    sum_start(p, part, got, rows, send, recv, local)
    dgain_ref[...] = jnp.zeros_like(dgain_ref)
    sum_wait(p, part, got, rows, send, recv, local)

    def body(at):
        du, dgain = norm_back(mid_ref[at, :], gain_ref[...], total(got, at, p.N))
        back = grad_ref[at, :].astype(F32) + du
        back_ref[at, :] = back
        buf[at, :] = back.astype(BF)
        dgain_ref[...] += dgain

    row_loop(rows, STEP, body)
    spread_start(p, buf, gathered, rows, send2, recv2, local2)
    spread_wait(p, buf, gathered, rows, send2, recv2, local2)


def input_back_kernel(
    wide, narrow, part, own_ref, gain_ref, back_ref, gains_ref, out_ref, gsum_ref,
    got, buf, far_buf, gbuf, gbuf2, send, recv, local, swap, gsend, grecv, gsend2, grecv2,
):
    p = Place(wide, narrow)
    rows, dim = own_ref.shape
    enter(p, ring=True)
    sum_start(p, part, got, rows, send, recv, local)
    gsum_ref[...] = gains_ref[...]
    sum_wait(p, part, got, rows, send, recv, local)

    def body(at):
        du, dgain = norm_back(own_ref[at, :].astype(F32), gain_ref[...], total(got, at, p.N))
        grad = back_ref[at, :] + du
        out_ref[at, :] = grad
        buf[at, :] = grad.astype(BF)
        gsum_ref[:, :dim] += dgain

    row_loop(rows, STEP, body)

    @pl.when(p.c == 1)
    def _():
        swap_rows(p, buf, far_buf, swap.at[0], swap.at[1]).start()

    def share(me, count, here, slots, sends, recvs, device):
        slots[me] = here[...]
        for t in range(count):

            @pl.when(me != t)
            def _():
                pltpu.make_async_remote_copy(
                    src_ref=here, dst_ref=slots.at[me], send_sem=sends.at[t], recv_sem=recvs.at[me],
                    device_id=device(t), device_id_type=MESH,
                ).start()

        for t in range(count):

            @pl.when(me != t)
            def _():
                pltpu.make_async_copy(here, slots.at[t], sends.at[t]).wait()
                pltpu.make_async_copy(here, slots.at[t], recvs.at[t]).wait()

        out = slots[0]
        for t in range(1, count):
            out = out + slots[t]
        here[...] = out

    share(p.n, narrow, gsum_ref, gbuf, gsend, grecv, lambda t: (p.w, t))
    share(p.w, wide, gsum_ref, gbuf2, gsend2, grecv2, lambda t: (t, p.n))

    @pl.when(p.c == 1)
    def _():
        swap_rows(p, buf, far_buf, swap.at[0], swap.at[1]).wait()
        row_loop(rows, STEP, lambda at: out_ref.__setitem__((at, slice(None)), far_buf[at, :].astype(F32)))


DMA = pltpu.SemaphoreType.DMA
VM = pl.BlockSpec(memory_space=pltpu.VMEM)
HB = pl.BlockSpec(memory_space=pl.ANY)


def comm_call(kernel, name, cid, out_shape, in_specs, out_specs, scratch, *args):
    return pl.pallas_call(
        kernel,
        out_shape=out_shape,
        in_specs=in_specs,
        out_specs=out_specs,
        scratch_shapes=scratch,
        compiler_params=pltpu.CompilerParams(collective_id=cid, has_side_effects=True, vmem_limit_bytes=40 << 20),
        cost_estimate=pl.CostEstimate(flops=0, bytes_accessed=160_000_000, transcendentals=0),
        name=name,
    )(*args)


def sds(shape, kind):
    return jax.ShapeDtypeStruct(shape, kind)


def fwd_kernel(sub, tab, q_ref, kv_ref, o_ref, l_ref, acc, lsum):
    s=pl.program_id(0)
    B=q_ref.shape[0]; HD=kv_ref.shape[1]//2; G=q_ref.shape[1]//HD
    diag=tab[2,s]; first=tab[3,s]; last=tab[4,s]
    @pl.when(first==1)
    def _():
        acc[...]=jnp.zeros_like(acc); lsum[...]=jnp.zeros_like(lsum)
    def work(masked):
        k=kv_ref[:,:HD]; v=kv_ref[:,HD:]
        for g in range(G):
            for i in range(B//sub):
                rows=pl.ds(i*sub,sub)
                q=q_ref[rows,g*HD:(g+1)*HD]
                kn=(i+1)*sub if masked else B
                sc=dg(q,k[:kn],NT)
                if masked:
                    r=lax.broadcasted_iota(jnp.int32,sc.shape,0)+i*sub
                    cc=lax.broadcasted_iota(jnp.int32,sc.shape,1)
                    sc=jnp.where(cc<=r,sc,MASKED)
                p=jnp.exp2(sc)
                t=p[:,:128]
                for j in range(1,kn//128): t=t+p[:,j*128:(j+1)*128]
                lsum[g,rows,:]+=t
                acc[rows,g*HD:(g+1)*HD]+=dg(p.astype(BF),v[:kn],NN)
    @pl.when(diag==0)
    def _(): work(False)
    @pl.when(diag==1)
    def _(): work(True)
    @pl.when(last==1)
    def _():
        lane=lax.broadcasted_iota(jnp.int32,(B,128),1)
        lo=jnp.zeros((B,128),F32)
        for g in range(G):
            l=jnp.sum(lsum[g],axis=1,keepdims=True)
            o_ref[:,g*HD:(g+1)*HD]=acc[:,g*HD:(g+1)*HD]/l
            lo=jnp.where(lane==g,jnp.log2(l),lo)
        l_ref[...]=lo

def attn_fwd(tab, q, kv, B, sub=512):
    R,W=q.shape; HD=kv.shape[1]//2; G=W//HD; steps=tab.shape[1]
    return pl.pallas_call(functools.partial(fwd_kernel,sub),
        out_shape=(jax.ShapeDtypeStruct((R,W),F32),jax.ShapeDtypeStruct((R,128),F32)),
        grid_spec=pltpu.PrefetchScalarGridSpec(num_scalar_prefetch=1,grid=(steps,),
            in_specs=[pl.BlockSpec((B,W),lambda s,t:(t[0,s],0)),pl.BlockSpec((B,2*HD),lambda s,t:(t[1,s],0))],
            out_specs=[pl.BlockSpec((B,W),lambda s,t:(t[0,s],0)),pl.BlockSpec((B,128),lambda s,t:(t[0,s],0))],
            scratch_shapes=[pltpu.VMEM((B,W),F32),pltpu.VMEM((G,B,128),F32)]),
        compiler_params=pltpu.CompilerParams(vmem_limit_bytes=48<<20),
        cost_estimate=pl.CostEstimate(flops=steps*B*B*HD*G*4,bytes_accessed=steps*B*HD*8,transcendentals=steps*B*B*G),
        name="attn_fwd")(tab,q,kv)

def bwd_kernel(sub, scale, tab, q_ref, do_ref, kv_ref, st_ref, z_ref, dq_ref, dkv_ref, dqa, dkva):
    s=pl.program_id(0); steps=pl.num_programs(0)
    B=q_ref.shape[0]; HD=kv_ref.shape[1]//2; G=q_ref.shape[1]//HD
    qi=tab[0,s]; diag=tab[2,s]; first=tab[3,s]; last=tab[4,s]
    @pl.when(s==0)
    def _(): dqa[...]=jnp.zeros_like(dqa)
    @pl.when(first==1)
    def _(): dkva[...]=jnp.zeros_like(dkva)
    def work(masked):
        for g in range(G):
            hs=slice(g*HD,(g+1)*HD)
            for i in range(B//sub):
                rows=slice(i*sub,(i+1)*sub)
                kn=(i+1)*sub if masked else B
                k=kv_ref[:kn,:HD]; v=kv_ref[:kn,HD:]
                q=q_ref[rows,hs]; do=do_ref[rows,hs]
                lse=st_ref[g:g+1,rows]; dl=st_ref[G+g:G+g+1,rows]
                sc=dg(k,q,NT)-lse
                if masked:
                    kk=lax.broadcasted_iota(jnp.int32,sc.shape,0)
                    r=lax.broadcasted_iota(jnp.int32,sc.shape,1)+i*sub
                    sc=jnp.where(kk<=r,sc,MASKED)
                p=jnp.exp2(sc)
                dp=dg(v,do,NT)
                dkva[:kn,HD:]+=dg(p.astype(BF),do,NN)
                ds=(p*(dp-dl)).astype(BF)
                dkva[:kn,:HD]+=dg(ds,q,NN)
                dqa[qi,rows,hs]+=dg(ds,k,TN)
    @pl.when(diag==0)
    def _(): work(False)
    @pl.when(diag==1)
    def _(): work(True)
    @pl.when(last==1)
    def _():
        dkv_ref[:,:HD]=(dkva[:,:HD]*math.log(2.0)).astype(BF)
        dkv_ref[:,HD:]=dkva[:,HD:].astype(BF)
    @pl.when(s==steps-1)
    def _():
        for i in range(dqa.shape[0]):
            dq_ref[i*B:(i+1)*B,:]=dqa[i]*scale

def attn_bwd(tab, q, do, kv, stats, B, sub=512):
    R,W=q.shape; HD=kv.shape[1]//2; G=W//HD; steps=tab.shape[1]; NB=R//B
    zeros=jnp.zeros(kv.shape,BF)
    return pl.pallas_call(functools.partial(bwd_kernel,sub,HD**-0.5),
        out_shape=(jax.ShapeDtypeStruct((R,W),F32),jax.ShapeDtypeStruct(kv.shape,BF)),
        grid_spec=pltpu.PrefetchScalarGridSpec(num_scalar_prefetch=1,grid=(steps,),
            in_specs=[pl.BlockSpec((B,W),lambda s,t:(t[0,s],0)),pl.BlockSpec((B,W),lambda s,t:(t[0,s],0)),
                      pl.BlockSpec((B,2*HD),lambda s,t:(t[1,s],0)),pl.BlockSpec((stats.shape[0],B),lambda s,t:(0,t[0,s])),
                      pl.BlockSpec(memory_space=pl.ANY)],
            out_specs=[pl.BlockSpec((R,W),lambda s,t:(0,0)),pl.BlockSpec((B,2*HD),lambda s,t:(t[1,s],0))],
            scratch_shapes=[pltpu.VMEM((NB,B,W),F32),pltpu.VMEM((B,2*HD),F32)]),
        input_output_aliases={5:1},
        compiler_params=pltpu.CompilerParams(vmem_limit_bytes=48<<20),
        cost_estimate=pl.CostEstimate(flops=steps*B*B*HD*G*10,bytes_accessed=steps*B*HD*16,transcendentals=steps*B*B*G),
        name="attn_bwd")(tab,q,do,kv,stats,zeros)

def place(w, C):
    k=w//2; t=w%2
    return 4*k+t, 4*C-1-4*k-t
def block_row(b, C):
    m=b%4
    k=jnp.where(m<2,b//4,(4*C-1-b)//4)
    t=jnp.where((m==1)|(m==2),1,0)
    return 2*(2*k+t)+jnp.where(m<2,0,1)
def tables(w, C):
    A,Bb=place(w,C)
    n=4*C+1
    s=jnp.arange(n,dtype=jnp.int32)
    inA=s<=A
    qi=jnp.where(inA,0,1); b=jnp.where(inA,s,s-A-1)
    diag=jnp.where(inA,s==A,s==n-1); first=(b==0)
    fw=jnp.stack([qi,block_row(b,C),diag.astype(jnp.int32),first.astype(jnp.int32),diag.astype(jnp.int32)]).astype(jnp.int32)
    sm=jnp.minimum(A,Bb); qs=jnp.where(A<Bb,0,1)
    both=s<2*(sm+1)
    b2=jnp.where(both,s//2,s-(sm+1))
    qi2=jnp.where(both,jnp.where(s%2==0,qs,1-qs),1-qs)
    own=jnp.where(qi2==0,A,Bb)
    diag2=(b2==own)
    first2=jnp.where(both,s%2==0,True); last2=jnp.where(both,s%2==1,True)
    bw=jnp.stack([qi2,block_row(b2,C),diag2.astype(jnp.int32),first2.astype(jnp.int32),last2.astype(jnp.int32)]).astype(jnp.int32)
    return fw,bw


def rotation(positions, head_dim):
    steps_half = jnp.arange(head_dim // 2).astype(F32)
    inverse = jnp.exp(steps_half * (-2.0 * math.log(1000000.0) / head_dim))
    angles = positions.astype(F32)[:, None] * inverse[None, :]
    angles = jnp.concatenate([angles, angles], axis=1)
    return (jnp.cos(angles)[:, None, :], jnp.sin(angles)[:, None, :])


def rms_norm(values, scaling):
    return values * lax.rsqrt(jnp.mean(values * values, axis=-1, keepdims=True) + EPSILON) * scaling


def rotary(values, cos_table, sin_table):
    half_dim = values.shape[-1] // 2
    turned = jnp.concatenate([-values[..., half_dim:], values[..., :half_dim]], axis=-1)
    return values * cos_table + turned * sin_table


def swiglu(gate_proj, up_proj):
    return gate_proj * jax.nn.sigmoid(gate_proj) * up_proj


def per_device(
    wide, narrow,
    layer_input, w_query, w_key, w_value, w_output, w_gate, w_up, w_down,
    attn_gain, mlp_gain, query_gain, key_gain, out_grad,
):
    hd = query_gain.shape[0]
    rows, dim = layer_input.shape
    all_rows = narrow * rows
    chips = wide // 2
    block = all_rows // 2
    qw, kw = w_query.shape[1], w_key.shape[1]
    ff = w_gate.shape[1]
    groups = qw // kw
    kv_heads = kw // hd
    w = lax.axis_index("wide")
    fwd_tab, bwd_tab = tables(w, chips)
    first, second = place(w, chips)
    at = jnp.arange(block, dtype=jnp.int32)
    positions = jnp.concatenate([first * block + at, second * block + at])
    cos_table, sin_table = rotation(positions, hd)

    def gather(shard):
        return lax.all_gather(shard, "wide", axis=0, tiled=True)

    def scatter(grad):
        return lax.psum_scatter(grad.astype(BF), "wide", scatter_dimension=0, tiled=True).astype(F32)

    n_sems = [DMA((narrow,)), DMA((narrow,)), DMA]
    recv_buf = pltpu.VMEM((narrow, rows, dim), BF)
    row_buf = pltpu.VMEM((rows, dim), BF)
    low_rows, full_rows, all_low = sds((rows, dim), BF), sds((rows, dim), F32), sds((all_rows, dim), BF)
    ring = functools.partial

    w_qkv = gather(jnp.concatenate([w_query, w_key, w_value], axis=1))
    own, normed_all = comm_call(
        ring(input_kernel, wide, narrow, True), "input_rows", 0, (low_rows, all_low), [VM, VM], (VM, HB),
        [row_buf, *n_sems, DMA((2,))], layer_input, attn_gain[None],
    )
    w_o = gather(w_output.T)
    qkv = dg(normed_all, w_qkv, NN)
    query_proj, key_proj = qkv[:, :qw], qkv[:, qw : qw + kw]
    value_low = qkv[:, qw + kw :].astype(BF)

    def heads_of(projected, scaling):
        return rotary(rms_norm(projected.reshape(all_rows, -1, hd), scaling), cos_table, sin_table)

    fold = hd**-0.5 * math.log2(math.e)
    queries = (heads_of(query_proj, query_gain) * fold).astype(BF).reshape(all_rows, qw)
    keys = heads_of(key_proj, key_gain).astype(BF).reshape(all_rows, kw)
    gw = groups * hd
    kvs = [
        gather(jnp.concatenate([keys[:, h * hd : (h + 1) * hd], value_low[:, h * hd : (h + 1) * hd]], axis=1))
        for h in range(kv_heads)
    ]
    grad_own, grad_all = comm_call(
        ring(input_kernel, wide, narrow, False), "grad_rows", 1, (low_rows, all_low), [VM, VM], (VM, HB),
        [row_buf, *n_sems, DMA((2,))], out_grad, attn_gain[None],
    )
    w_g, w_u, w_d = gather(w_gate), gather(w_up), gather(w_down.T)
    q_heads = [queries[:, h * gw : (h + 1) * gw] for h in range(kv_heads)]
    mixed = [attn_fwd(fwd_tab, q_heads[h], kvs[h], block) for h in range(kv_heads)]
    attended = jnp.concatenate([o for o, _ in mixed], axis=1)
    attended_low = attended.astype(BF)
    middle, normed_mlp = comm_call(
        ring(middle_kernel, wide, narrow), "middle_rows", 2, (full_rows, all_low), [HB, VM, VM], (VM, HB),
        [recv_buf, row_buf, *n_sems, *n_sems], dg(attended_low, w_o, NT).astype(BF), own, mlp_gain[None],
    )
    gate_proj = dg(normed_mlp, w_g, NN)
    up_proj = dg(normed_mlp, w_u, NN)
    hidden_low = swiglu(gate_proj, up_proj).astype(BF)
    hidden_back = dg(grad_all, w_d, NN)
    _, swiglu_back = jax.vjp(swiglu, gate_proj, up_proj)
    gate_back, up_back = swiglu_back(hidden_back)
    gate_low, up_low = gate_back.astype(BF), up_back.astype(BF)
    mlp_back = (dg(gate_low, w_g, NT) + dg(up_low, w_u, NT)).astype(BF)
    middle_back, mlp_gain_part, middle_all = comm_call(
        ring(middle_back_kernel, wide, narrow), "middle_back", 3, (full_rows, sds((1, dim), F32), all_low),
        [HB, VM, VM, VM], (VM, VM, HB), [recv_buf, row_buf, *n_sems, *n_sems],
        mlp_back, middle, mlp_gain[None], grad_own,
    )
    grad_down = scatter(dg(grad_all, hidden_low, TN)).T
    grad_gate = scatter(dg(normed_mlp, gate_low, TN))
    grad_up = scatter(dg(normed_mlp, up_low, TN))
    attn_back = dg(middle_all, w_o, NN).astype(BF)
    grad_output = scatter(dg(middle_all, attended_low, TN)).T
    row_delta = jnp.sum((attn_back.astype(F32) * attended).reshape(all_rows, -1, hd), axis=-1)
    pad = jnp.zeros((8 - 2 * groups, all_rows), F32)
    backs = []
    for h in range(kv_heads):
        stats = jnp.concatenate(
            [mixed[h][1][:, :groups].T, row_delta[:, h * groups : (h + 1) * groups].T, pad], axis=0
        )
        backs.append(attn_bwd(bwd_tab, q_heads[h], attn_back[:, h * gw : (h + 1) * gw], kvs[h], stats, block))
    (layer_output,) = comm_call(
        ring(output_kernel, wide, narrow), "output_rows", 4, (low_rows,), [HB, VM], (VM,),
        [recv_buf, row_buf, *n_sems, DMA((2,))], dg(hidden_low, w_d, NT).astype(BF), middle,
    )
    query_back = jnp.concatenate([b[0] for b in backs], axis=1)
    kv_back = [scatter(b[1]) for b in backs]
    key_back = jnp.concatenate([b[:, :hd] for b in kv_back], axis=1)
    value_grad_low = jnp.concatenate([b[:, hd:] for b in kv_back], axis=1).astype(BF)
    _, query_vjp = jax.vjp(heads_of, query_proj, query_gain)
    query_proj_back, query_gain_part = query_vjp(query_back.reshape(all_rows, -1, hd))
    _, key_vjp = jax.vjp(heads_of, key_proj, key_gain)
    key_proj_back, key_gain_part = key_vjp(key_back.reshape(all_rows, -1, hd))
    qkv_low = jnp.concatenate([query_proj_back.astype(BF), key_proj_back.astype(BF), value_grad_low], axis=1)
    normed_back = dg(qkv_low, w_qkv, NT).astype(BF)
    gains = jnp.concatenate([jnp.zeros((dim,), F32), mlp_gain_part[0], query_gain_part, key_gain_part])[None]
    grad_qkv = scatter(dg(normed_all, qkv_low, TN))
    gvec = sds(gains.shape, F32)
    input_grad, gain_sums = comm_call(
        ring(input_back_kernel, wide, narrow), "input_back", 5, (full_rows, gvec), [HB, VM, VM, VM, VM], (VM, VM),
        [recv_buf, row_buf, row_buf, pltpu.VMEM((narrow, *gains.shape), F32), pltpu.VMEM((wide, *gains.shape), F32),
         *n_sems, DMA((2,)), DMA((narrow,)), DMA((narrow,)), DMA((wide,)), DMA((wide,))],
        normed_back, own, attn_gain[None], middle_back, gains,
    )
    g = gain_sums[0]
    return (
        layer_output, input_grad,
        grad_qkv[:, :qw], grad_qkv[:, qw : qw + kw], grad_qkv[:, qw + kw :],
        grad_output, grad_gate, grad_up, grad_down,
        g[:dim], g[dim : 2 * dim], g[2 * dim : 2 * dim + hd], g[2 * dim + hd :],
    )


def solution(mesh):
    rows = P(("wide", "narrow"), None)
    weight, turned = P("wide", "narrow"), P("narrow", "wide")
    return jax.shard_map(
        functools.partial(per_device, mesh.shape["wide"], mesh.shape["narrow"]),
        mesh=mesh,
        in_specs=(rows, weight, weight, weight, turned, weight, weight, turned, P(), P(), P(), P(), rows),
        out_specs=(rows, rows, weight, weight, weight, turned, weight, weight, turned, P(), P(), P(), P()),
        check_vma=False,
    )
```

```python
import functools
import math

import jax
import jax.numpy as jnp
from jax import lax
from jax.experimental import pallas as pl
from jax.experimental.pallas import tpu as pltpu
from jax.sharding import PartitionSpec as P

EPSILON = 1e-06
MASKED = -1e30
F32 = jnp.float32
BF = jnp.bfloat16
MESH = pl.DeviceIdType.MESH
NT = (((1,), (1,)), ((), ()))
NN = (((1,), (0,)), ((), ()))
TN = (((0,), (0,)), ((), ()))


def dg(a, b, dims):
    return lax.dot_general(a, b, dims, preferred_element_type=F32)
DMA = pltpu.SemaphoreType.DMA


class Place:
    def __init__(self, wide, narrow):
        self.W, self.N = wide, narrow
        self.C, self.half = wide // 2, narrow // 2
        self.w, self.n = lax.axis_index("wide"), lax.axis_index("narrow")
        self.k, self.c = self.w // 2, lax.rem(self.w, 2)
        self.far = 2 * (self.C - 1 - self.k) + 1
        late = (self.n >= self.half).astype(jnp.int32)
        self.group = lax.rem(self.c + late, 2)
        self.slot = jnp.where(self.group == 0, self.n, lax.rem(self.n + self.half, self.N))

    def owner(self, j):
        core = 1 if j >= self.half else 0
        n = jnp.where(self.c == 0, j, (j + self.half) % self.N)
        return core, n

    def owner_is_me(self, j):
        core, n = self.owner(j)
        return (self.c == core) & (self.n == n)


def enter(p, line=False, ring=False):
    barrier = pltpu.get_barrier_semaphore()

    def greet(device):
        pl.semaphore_signal(barrier, inc=1, device_id=device, device_id_type=MESH)

    for core in range(2):
        for n in range(p.N):

            @pl.when((p.c != core) | (p.n != n))
            def _():
                greet((2 * p.k + core, n))

    peers = 2 * p.N - 1
    if line or ring:
        for k in range(p.C):

            @pl.when(p.k != k)
            def _():
                greet((2 * k + p.c, p.n))
                if ring:
                    greet((2 * k + 1 - p.c, p.n))

        peers += (2 if ring else 1) * (p.C - 1)
    pl.semaphore_wait(barrier, peers)


def swap_rows(p, src, dst, send_sem, recv_sem):
    return pltpu.make_async_remote_copy(
        src_ref=src, dst_ref=dst, send_sem=send_sem, recv_sem=recv_sem, device_id=(p.far, p.n), device_id_type=MESH
    )


def spread_start(p, src, gathered, rows, send_sems, recv_sems, local_sem):
    view = gathered.at[pl.ds(pl.multiple_of(p.slot * rows, rows), rows)]
    for t in range(p.N):
        mine = (p.group == p.c) & (p.n == t)

        @pl.when(mine)
        def _():
            pltpu.make_async_copy(src, view, local_sem).start()

        @pl.when(jnp.logical_not(mine))
        def _():
            pltpu.make_async_remote_copy(
                src_ref=src,
                dst_ref=view,
                send_sem=send_sems.at[t],
                recv_sem=recv_sems.at[p.slot],
                device_id=(2 * p.k + p.group, t),
                device_id_type=MESH,
            ).start()


def spread_wait(p, src, gathered, rows, send_sems, recv_sems, local_sem):
    for t in range(p.N):
        mine = (p.group == p.c) & (p.n == t)

        @pl.when(mine)
        def _():
            pltpu.make_async_copy(src, gathered.at[pl.ds(0, rows)], local_sem).wait()

        @pl.when(jnp.logical_not(mine))
        def _():
            pltpu.make_async_copy(src, gathered.at[pl.ds(0, rows)], send_sems.at[t]).wait()

    for j in range(p.N):

        @pl.when(jnp.logical_not(p.owner_is_me(j)))
        def _():
            pltpu.make_async_copy(src, gathered.at[pl.ds(j * rows, rows)], recv_sems.at[j]).wait()


def sum_start(p, part, recv, rows, send_sems, recv_sems, local_sem):
    for j in range(p.N):
        core, n = p.owner(j)
        mine = p.owner_is_me(j)

        @pl.when(mine)
        def _():
            pltpu.make_async_copy(part.at[pl.ds(j * rows, rows)], recv.at[p.n], local_sem).start()

        @pl.when(jnp.logical_not(mine))
        def _():
            pltpu.make_async_remote_copy(
                src_ref=part.at[pl.ds(j * rows, rows)],
                dst_ref=recv.at[p.n],
                send_sem=send_sems.at[j],
                recv_sem=recv_sems.at[p.n],
                device_id=(2 * p.k + core, n),
                device_id_type=MESH,
            ).start()


def sum_wait(p, part, recv, rows, send_sems, recv_sems, local_sem):
    for t in range(p.N):
        mine = (p.group == p.c) & (p.n == t)

        @pl.when(mine)
        def _():
            pltpu.make_async_copy(part.at[pl.ds(0, rows)], recv.at[t], local_sem).wait()

        @pl.when(jnp.logical_not(mine))
        def _():
            pltpu.make_async_copy(part.at[pl.ds(0, rows)], recv.at[t], recv_sems.at[t]).wait()

    for j in range(p.N):

        @pl.when(jnp.logical_not(p.owner_is_me(j)))
        def _():
            pltpu.make_async_copy(part.at[pl.ds(j * rows, rows)], recv.at[0], send_sems.at[j]).wait()


def line_sems(p_chips):
    return [DMA((2, p_chips + 1)), DMA((p_chips,)), DMA((p_chips,)), DMA((p_chips,)), DMA]


def line_parts(p, full, rows):
    return lambda s, core: full.at[pl.ds(pl.multiple_of((2 * s + core) * rows, rows), rows)]


def line_copy(p, src, dst, send, recv, k, core):
    return pltpu.make_async_remote_copy(
        src_ref=src, dst_ref=dst, send_sem=send, recv_sem=recv, device_id=(2 * k + core, p.n), device_id_type=MESH
    )


def inside(p, k):
    return (k >= 0) & (k < p.C)


def line_start(p, src, full, rows, zsend, zrecv, csend, crecv, local):
    at = line_parts(p, full, rows)
    for i, sign in enumerate((1, -1)):
        for d in (1, 2):
            t = p.k + sign * d

            @pl.when(inside(p, t))
            def _():
                line_copy(p, src, at(p.k, p.c), zsend.at[i, d], zrecv.at[p.k], t, p.c).start()

    pltpu.make_async_copy(src, at(p.k, p.c), local).start()
    line_copy(p, src, at(p.k, p.c), csend.at[p.k], crecv.at[p.k], p.k, 1 - p.c).start()


def line_finish(p, src, full, rows, zsend, zrecv, csend, crecv, local):
    at = line_parts(p, full, rows)
    for d in range(1, p.C):
        for i, sign in enumerate((1, -1)):
            s, t = p.k - sign * d, p.k + sign

            @pl.when(inside(p, s))
            def _():
                pltpu.make_async_copy(src, at(s, p.c), zrecv.at[s]).wait()
                if d >= 2:

                    @pl.when(inside(p, t))
                    def _():
                        line_copy(p, at(s, p.c), at(s, p.c), zsend.at[i, d + 1], zrecv.at[s], t, p.c).start()

                line_copy(p, at(s, p.c), at(s, p.c), csend.at[s], crecv.at[s], p.k, 1 - p.c).start()

    pltpu.make_async_copy(src, at(p.k, p.c), local).wait()
    for s in range(p.C):
        pltpu.make_async_copy(src, at(s, p.c), csend.at[s]).wait()
        pltpu.make_async_copy(src, at(s, 1 - p.c), crecv.at[s]).wait()
    for i, sign in enumerate((1, -1)):
        for d in (1, 2):

            @pl.when(inside(p, p.k + sign * d))
            def _():
                pltpu.make_async_copy(src, at(p.k, p.c), zsend.at[i, d]).wait()

        for d in range(2, p.C):

            @pl.when(inside(p, p.k - sign * d) & inside(p, p.k + sign))
            def _():
                pltpu.make_async_copy(src, at(p.k, p.c), zsend.at[i, d + 1]).wait()


def line_sum_bufs(chips, rows, width):
    return [pltpu.VMEM((chips, rows, width), BF)] * 3 + [pltpu.VMEM((2, 2, rows, width), BF), pltpu.VMEM((rows, width), F32)]


def line_sum_sems(chips):
    return [DMA((chips,)), DMA((chips,)), DMA((chips,)), DMA((2, chips)), DMA((chips,)), DMA((2, 2))]


def line_sum_start(p, part, rows, bufs, sems):
    own, inbox, _, _, _ = bufs
    load, csend, crecv, _, _, _ = sems
    at = line_parts(p, part, rows)
    for s in range(p.C):
        line_copy(p, at(s, 1 - p.c), inbox.at[s], csend.at[s], crecv.at[s], p.k, 1 - p.c).start()
        pltpu.make_async_copy(at(s, p.c), own.at[s], load.at[s]).start()


def line_sum_run(p, part, rows, bufs, sems):
    own, inbox, relay, box, acc = bufs
    load, csend, crecv, zsend, rrecv, zrecv = sems
    at = line_parts(p, part, rows)

    def pair(t):
        pltpu.make_async_copy(at(0, 0), own.at[t], load.at[t]).wait()
        pltpu.make_async_copy(at(0, 0), inbox.at[t], crecv.at[t]).wait()

    for d in range(p.C - 1, 0, -1):
        for i, sign in enumerate((1, -1)):
            t = p.k + sign * d

            @pl.when(inside(p, t))
            def _():
                pair(t)

                def add(rows_at):
                    both = own[t, rows_at, :].astype(F32) + inbox[t, rows_at, :].astype(F32)
                    own[t, rows_at, :] = both.astype(BF)

                row_loop(rows, 128, add)
                if d >= 2:

                    @pl.when(inside(p, p.k - sign))
                    def _():
                        pltpu.make_async_copy(at(0, 0), relay.at[t], rrecv.at[t]).wait()

                        def add_relay(rows_at):
                            both = own[t, rows_at, :].astype(F32) + relay[t, rows_at, :].astype(F32)
                            own[t, rows_at, :] = both.astype(BF)

                        row_loop(rows, 128, add_relay)

                if d >= 3:
                    line_copy(p, own.at[t], relay.at[t], zsend.at[i, d], rrecv.at[t], p.k + sign, p.c).start()
                else:
                    line_copy(p, own.at[t], box.at[i, d - 1], zsend.at[i, d], zrecv.at[i, d - 1], t, p.c).start()

    pair(p.k)

    def first(rows_at):
        acc[rows_at, :] = own[p.k, rows_at, :].astype(F32) + inbox[p.k, rows_at, :].astype(F32)

    row_loop(rows, 128, first)
    for i, sign in enumerate((1, -1)):
        for d in (1, 2):

            @pl.when(inside(p, p.k - sign * d))
            def _():
                pltpu.make_async_copy(at(0, 0), box.at[i, d - 1], zrecv.at[i, d - 1]).wait()

                def more(rows_at):
                    acc[rows_at, :] += box[i, d - 1, rows_at, :].astype(F32)

                row_loop(rows, 128, more)

        for d in range(1, p.C):

            @pl.when(inside(p, p.k + sign * d))
            def _():
                pltpu.make_async_copy(at(0, 0), own.at[0], zsend.at[i, d]).wait()

    for s in range(p.C):
        pltpu.make_async_copy(at(0, 0), inbox.at[s], csend.at[s]).wait()


def row_loop(rows, step, body):
    def one(i, carry):
        body(pl.ds(pl.multiple_of(i * step, step), step))
        return carry

    lax.fori_loop(0, rows // step, one, 0)


STEP = 64


def inv_rms(u):
    return lax.rsqrt(jnp.mean(u * u, axis=-1, keepdims=True) + EPSILON)


def total(recv, at, count):
    out = recv[0, at, :].astype(F32)
    for t in range(1, count):
        out = out + recv[t, at, :].astype(F32)
    return out


def swap_out(p, buf, out_ref, sems):
    @pl.when(p.c == 1)
    def _():
        copy = swap_rows(p, buf, out_ref, sems.at[0], sems.at[1])
        copy.start()
        copy.wait()

    @pl.when(p.c == 0)
    def _():
        out_ref[...] = buf[...]


def input_kernel(
    wide, narrow, norm, x_ref, gain_ref, shard, own_ref, gathered, full, buf, send, recv, local, swap, *line
):
    p = Place(wide, narrow)
    rows = x_ref.shape[0]
    enter(p, line=True)

    @pl.when(p.c == 1)
    def _():
        swap_rows(p, x_ref, own_ref, swap.at[0], swap.at[1]).start()

    line_start(p, shard, full, shard.shape[0], *line)

    @pl.when(p.c == 1)
    def _():
        swap_rows(p, x_ref, own_ref, swap.at[0], swap.at[1]).wait()

    @pl.when(p.c == 0)
    def _():
        own_ref[...] = x_ref[...]

    if norm:

        def body(at):
            u = own_ref[at, :].astype(F32)
            buf[at, :] = (u * inv_rms(u) * gain_ref[...]).astype(BF)

        row_loop(rows, STEP, body)
    src = buf if norm else own_ref
    spread_start(p, src, gathered, rows, send, recv, local)
    line_finish(p, shard, full, shard.shape[0], *line)
    spread_wait(p, src, gathered, rows, send, recv, local)


def middle_kernel(wide, narrow, part, own_ref, gain_ref, mid_ref, gathered, got, buf, send, recv, local, send2, recv2, local2):
    p = Place(wide, narrow)
    rows = own_ref.shape[0]
    enter(p)
    sum_start(p, part, got, rows, send, recv, local)
    sum_wait(p, part, got, rows, send, recv, local)

    def body(at):
        u = own_ref[at, :].astype(F32) + total(got, at, p.N)
        mid_ref[at, :] = u
        buf[at, :] = (u * inv_rms(u) * gain_ref[...]).astype(BF)

    row_loop(rows, STEP, body)
    spread_start(p, buf, gathered, rows, send2, recv2, local2)
    spread_wait(p, buf, gathered, rows, send2, recv2, local2)


def output_kernel(wide, narrow, part, mid_ref, dkv, out_ref, kv_ref, got, buf, send, recv, local, swap, *line):
    p = Place(wide, narrow)
    rows = mid_ref.shape[0]
    kv_rows = kv_ref.shape[0]
    bufs, sems = line[:5], line[5:]
    enter(p, line=True)
    line_sum_start(p, dkv, kv_rows, bufs, sems)
    sum_start(p, part, got, rows, send, recv, local)
    line_sum_run(p, dkv, kv_rows, bufs, sems)
    row_loop(kv_rows, 128, lambda at: kv_ref.__setitem__((at, slice(None)), bufs[4][at, :].astype(BF)))
    sum_wait(p, part, got, rows, send, recv, local)

    def body(at):
        buf[at, :] = (mid_ref[at, :] + total(got, at, p.N)).astype(BF)

    row_loop(rows, STEP, body)
    swap_out(p, buf, out_ref, swap)


def norm_back(u, gain, cot):
    r = inv_rms(u)
    a = cot * gain
    du = r * a - u * (r * r * r) * jnp.mean(a * u, axis=-1, keepdims=True)
    return du, jnp.sum(cot * u * r, axis=0, keepdims=True)


def middle_back_kernel(
    wide, narrow, part, mid_ref, gain_ref, grad_ref, back_ref, dgain_ref, gathered,
    got, buf, send, recv, local, send2, recv2, local2,
):
    p = Place(wide, narrow)
    rows = mid_ref.shape[0]
    enter(p)
    sum_start(p, part, got, rows, send, recv, local)
    dgain_ref[...] = jnp.zeros_like(dgain_ref)
    sum_wait(p, part, got, rows, send, recv, local)

    def body(at):
        du, dgain = norm_back(mid_ref[at, :], gain_ref[...], total(got, at, p.N))
        back = grad_ref[at, :].astype(F32) + du
        back_ref[at, :] = back
        buf[at, :] = back.astype(BF)
        dgain_ref[...] += dgain

    row_loop(rows, STEP, body)
    spread_start(p, buf, gathered, rows, send2, recv2, local2)
    spread_wait(p, buf, gathered, rows, send2, recv2, local2)


def input_back_kernel(
    wide, narrow, part, own_ref, gain_ref, back_ref, gains_ref, out_ref, gsum_ref,
    got, buf, far_buf, gbuf, gbuf2, send, recv, local, swap, gsend, grecv, gsend2, grecv2,
):
    p = Place(wide, narrow)
    rows, dim = own_ref.shape
    enter(p, ring=True)
    sum_start(p, part, got, rows, send, recv, local)
    gsum_ref[...] = gains_ref[...]
    sum_wait(p, part, got, rows, send, recv, local)

    def body(at):
        du, dgain = norm_back(own_ref[at, :].astype(F32), gain_ref[...], total(got, at, p.N))
        grad = back_ref[at, :] + du
        out_ref[at, :] = grad
        buf[at, :] = grad.astype(BF)
        gsum_ref[:, :dim] += dgain

    row_loop(rows, STEP, body)

    @pl.when(p.c == 1)
    def _():
        swap_rows(p, buf, far_buf, swap.at[0], swap.at[1]).start()

    def share(me, count, here, slots, sends, recvs, device):
        slots[me] = here[...]
        for t in range(count):

            @pl.when(me != t)
            def _():
                pltpu.make_async_remote_copy(
                    src_ref=here, dst_ref=slots.at[me], send_sem=sends.at[t], recv_sem=recvs.at[me],
                    device_id=device(t), device_id_type=MESH,
                ).start()

        for t in range(count):

            @pl.when(me != t)
            def _():
                pltpu.make_async_copy(here, slots.at[t], sends.at[t]).wait()
                pltpu.make_async_copy(here, slots.at[t], recvs.at[t]).wait()

        out = slots[0]
        for t in range(1, count):
            out = out + slots[t]
        here[...] = out

    share(p.n, narrow, gsum_ref, gbuf, gsend, grecv, lambda t: (p.w, t))
    share(p.w, wide, gsum_ref, gbuf2, gsend2, grecv2, lambda t: (t, p.n))

    @pl.when(p.c == 1)
    def _():
        swap_rows(p, buf, far_buf, swap.at[0], swap.at[1]).wait()
        row_loop(rows, STEP, lambda at: out_ref.__setitem__((at, slice(None)), far_buf[at, :].astype(F32)))


VM = pl.BlockSpec(memory_space=pltpu.VMEM)
HB = pl.BlockSpec(memory_space=pl.ANY)


def comm_call(kernel, name, cid, out_shape, in_specs, out_specs, scratch, *args):
    return pl.pallas_call(
        kernel,
        out_shape=out_shape,
        in_specs=in_specs,
        out_specs=out_specs,
        scratch_shapes=scratch,
        compiler_params=pltpu.CompilerParams(collective_id=cid, has_side_effects=True, vmem_limit_bytes=52 << 20),
        cost_estimate=pl.CostEstimate(flops=0, bytes_accessed=160_000_000, transcendentals=0),
        name=name,
    )(*args)


def sds(shape, kind):
    return jax.ShapeDtypeStruct(shape, kind)


def plain(kernel, name, grid, in_specs, out_specs, out_shape, flops, nbytes, *args, scratch=(), aliases=None):
    return pl.pallas_call(
        kernel,
        out_shape=out_shape,
        grid=grid,
        in_specs=in_specs,
        out_specs=out_specs,
        scratch_shapes=scratch,
        input_output_aliases=aliases or {},
        compiler_params=pltpu.CompilerParams(vmem_limit_bytes=52 << 20),
        cost_estimate=pl.CostEstimate(flops=flops, bytes_accessed=nbytes, transcendentals=0),
        name=name,
    )(*args)


def whole(shape):
    return pl.BlockSpec(shape, lambda *i: (0,) * len(shape), pipeline_mode=pl.Buffered(1))


def by_rows(tm, width):
    return pl.BlockSpec((tm, width), lambda i: (i, 0))


def mlp_fwd_kernel(x_ref, w_ref, gu_ref, h_ref):
    t = h_ref.shape[1]
    y = dg(x_ref[...], w_ref[...], NN)
    gate, up = y[:, :t], y[:, t:]
    gu_ref[...] = y
    h_ref[...] = (gate * jax.nn.sigmoid(gate) * up).astype(BF)


def mlp_fwd(x, w, t):
    rows, dim = x.shape
    ff2 = w.shape[1]
    return plain(
        mlp_fwd_kernel, "mlp_fwd", (ff2 // (2 * t),),
        [whole((rows, dim)), pl.BlockSpec((dim, 2 * t), lambda i: (0, i))],
        [pl.BlockSpec((rows, 2 * t), lambda i: (0, i)), pl.BlockSpec((rows, t), lambda i: (0, i))],
        (sds((rows, ff2), F32), sds((rows, ff2 // 2), BF)),
        2 * rows * dim * ff2, rows * dim * 2 + dim * ff2 * 2 + rows * ff2 * 5, x, w,
    )


def mlp_bwd_kernel(g_ref, w_ref, gu_ref, out_ref):
    t = w_ref.shape[1]
    hb = dg(g_ref[...], w_ref[...], NN)
    gate, up = gu_ref[:, :t], gu_ref[:, t:]
    s = jax.nn.sigmoid(gate)
    gs = hb * s
    out_ref[:, :t] = (gs * up * (1.0 + gate * (1.0 - s))).astype(BF)
    out_ref[:, t:] = (gs * gate).astype(BF)


def mlp_bwd(g, w, gu, t):
    rows, dim = g.shape
    ff = w.shape[1]
    return plain(
        mlp_bwd_kernel, "mlp_bwd", (ff // t,),
        [whole((rows, dim)), pl.BlockSpec((dim, t), lambda i: (0, i)), pl.BlockSpec((rows, 2 * t), lambda i: (0, i))],
        pl.BlockSpec((rows, 2 * t), lambda i: (0, i)), sds((rows, 2 * ff), BF),
        2 * rows * dim * ff, rows * dim * 2 + dim * ff * 2 + rows * ff * 12, g, w, gu,
    )


def nt_kernel(a_ref, b_ref, o_ref):
    o_ref[...] = dg(a_ref[...], b_ref[...], NT).astype(BF)


def mm_nt(a, b, name, tn=256):
    rows, depth = a.shape
    cols = b.shape[0]
    return plain(
        nt_kernel, name, (cols // tn,), [whole((rows, depth)), by_rows(tn, depth)],
        pl.BlockSpec((rows, tn), lambda i: (0, i)), sds((rows, cols), BF),
        2 * rows * cols * depth, 2 * (rows * depth + cols * depth + rows * cols), a, b,
    )


def turn(u):
    return pltpu.roll(u, u.shape[-1] // 2, 1)


def qkv_kernel(qw, kw, hd, fold, x_ref, w_ref, cos_ref, sin_ref, qg_ref, kg_ref, proj_ref, q_ref, kv_ref):
    y = dg(x_ref[...], w_ref[...], NN)
    cos, sin = cos_ref[...], sin_ref[...]
    proj_ref[...] = y[:, : qw + kw]

    def head(lo, gain):
        u = y[:, lo : lo + hd]
        v = u * inv_rms(u) * gain
        return v * cos + turn(v) * sin

    for h in range(qw // hd):
        q_ref[:, h * hd : (h + 1) * hd] = (head(h * hd, qg_ref[...]) * fold).astype(BF)
    for h in range(kw // hd):
        kv_ref[:, 2 * h * hd : (2 * h + 1) * hd] = head(qw + h * hd, kg_ref[...]).astype(BF)
        kv_ref[:, (2 * h + 1) * hd : (2 * h + 2) * hd] = y[:, qw + kw + h * hd : qw + kw + (h + 1) * hd].astype(BF)


def qkv_fwd(x, w, cos, sin, qg, kg, qw, kw, fold):
    rows, dim = x.shape
    hd = cos.shape[1]
    width = qw + 2 * kw
    tm = 256
    return plain(
        functools.partial(qkv_kernel, qw, kw, hd, fold), "qkv_fwd", (rows // tm,),
        [by_rows(tm, dim), whole((dim, width)), by_rows(tm, hd), by_rows(tm, hd), whole((1, hd)), whole((1, hd))],
        [by_rows(tm, qw + kw), by_rows(tm, qw), by_rows(tm, 2 * kw)],
        [sds((rows, qw + kw), F32), sds((rows, qw), BF), sds((rows, 2 * kw), BF)],
        2 * rows * dim * width, 2 * (rows * dim + dim * width) + rows * width * 6, x, w, cos, sin, qg, kg,
    )


def head_back(cot, u, gain, cos, sin):
    cot = cot * cos - turn(cot) * sin
    return norm_back(u, gain, cot)


def q_back_kernel(hd, dq_ref, u_ref, cos_ref, sin_ref, g_ref, low_ref, dgain_ref):
    @pl.when(pl.program_id(0) == 0)
    def _():
        dgain_ref[...] = jnp.zeros_like(dgain_ref)

    for h in range(dq_ref.shape[1] // hd):
        at = slice(h * hd, (h + 1) * hd)
        du, dgain = head_back(dq_ref[:, at], u_ref[:, at], g_ref[...], cos_ref[...], sin_ref[...])
        low_ref[:, at] = du.astype(BF)
        dgain_ref[...] += dgain


def q_back(dq, proj, cos, sin, gain):
    rows, qw = dq.shape
    hd = cos.shape[1]
    tm = 256
    return plain(
        functools.partial(q_back_kernel, hd), "q_back", (rows // tm,),
        [by_rows(tm, qw), by_rows(tm, qw), by_rows(tm, hd), by_rows(tm, hd), whole((1, hd))],
        [by_rows(tm, qw), pl.BlockSpec((1, hd), lambda i: (0, 0))], [sds((rows, qw), BF), sds((1, hd), F32)],
        rows * qw * 20, rows * qw * 10, dq, proj, cos, sin, gain,
    )


def kv_back_kernel(qw, kw, hd, q_ref, u_ref, cos_ref, sin_ref, g_ref, w_ref, *refs):
    s_ref, low_ref, back_ref, dgain_ref = refs

    @pl.when(pl.program_id(0) == 0)
    def _():
        dgain_ref[...] = jnp.zeros_like(dgain_ref)

    low_ref[:, :qw] = q_ref[...]
    for h in range(kw // hd):
        key = slice(2 * h * hd, (2 * h + 1) * hd)
        value = slice((2 * h + 1) * hd, (2 * h + 2) * hd)
        at = slice(qw + h * hd, qw + (h + 1) * hd)
        du, dgain = head_back(s_ref[:, key].astype(F32), u_ref[:, at], g_ref[...], cos_ref[...], sin_ref[...])
        low_ref[:, at] = du.astype(BF)
        low_ref[:, qw + kw + h * hd : qw + kw + (h + 1) * hd] = s_ref[:, value]
        dgain_ref[...] += dgain
    back_ref[...] = dg(low_ref[...], w_ref[...], NT).astype(BF)


def kv_back(q_low, proj, cos, sin, gain, w, sums, kw):
    rows, qw = q_low.shape
    hd = cos.shape[1]
    dim = w.shape[0]
    width = qw + 2 * kw
    tm = 256
    return plain(
        functools.partial(kv_back_kernel, qw, kw, hd), "kv_back", (rows // tm,),
        [by_rows(tm, qw), by_rows(tm, qw + kw), by_rows(tm, hd), by_rows(tm, hd), whole((1, hd)), whole((dim, width))]
        + [by_rows(tm, 2 * kw)],
        [by_rows(tm, width), by_rows(tm, dim), pl.BlockSpec((1, hd), lambda i: (0, 0))],
        [sds((rows, width), BF), sds((rows, dim), BF), sds((1, hd), F32)],
        2 * rows * dim * width, 2 * (rows * dim + dim * width) + rows * width * 6,
        q_low, proj, cos, sin, gain, w, sums,
    )


def attn_back_kernel(hd, x_ref, w_ref, o_ref, back_ref, delta_ref):
    back = dg(x_ref[...], w_ref[...], NN).astype(BF)
    back_ref[...] = back
    rows, width = back.shape
    lane = lax.broadcasted_iota(jnp.int32, (rows, hd), 1)
    out = jnp.zeros((rows, hd), F32)
    for h in range(width // hd):
        at = slice(h * hd, (h + 1) * hd)
        out = jnp.where(lane == h, jnp.sum(back[:, at].astype(F32) * o_ref[:, at], axis=1, keepdims=True), out)
    delta_ref[...] = jnp.transpose(out)[: delta_ref.shape[0]]


def attn_back(x, w, o, at):
    rows, dim = x.shape
    width = o.shape[1]
    tm = 256
    return plain(
        functools.partial(attn_back_kernel, 128), "attn_back", (rows // tm,),
        [by_rows(tm, dim), pl.BlockSpec((dim, width), lambda i: (0, at), pipeline_mode=pl.Buffered(1)), by_rows(tm, width)],
        [by_rows(tm, width), pl.BlockSpec((8, tm), lambda i: (0, i))], [sds((rows, width), BF), sds((8, rows), F32)],
        2 * rows * dim * width, 2 * (rows * dim + dim * width) + rows * width * 6, x, w, o,
    )


def fwd_kernel(groups, hd, tab, q_ref, kv_ref, *refs):
    o_ref, low_ref, lse_ref, acc, lsum = refs[-5:]
    s = pl.program_id(0)
    block = q_ref.shape[0]
    diag, first, last = tab[2, s], tab[3, s], tab[4, s]

    @pl.when(first == 1)
    def _():
        acc[...] = jnp.zeros_like(acc)
        lsum[...] = jnp.zeros_like(lsum)

    def work(masked):
        k, v = kv_ref[:, :hd], kv_ref[:, hd:]
        for g in range(groups):
            at = slice(g * hd, (g + 1) * hd)
            scores = dg(q_ref[:, at], k, NT)
            if masked:
                row = lax.broadcasted_iota(jnp.int32, scores.shape, 0)
                col = lax.broadcasted_iota(jnp.int32, scores.shape, 1)
                scores = jnp.where(col <= row, scores, MASKED)
            probs = jnp.exp2(scores)
            part = probs[:, :128]
            for j in range(1, block // 128):
                part = part + probs[:, j * 128 : (j + 1) * 128]
            lsum[g] += part
            acc[:, at] += dg(probs.astype(BF), v, NN)

    @pl.when(diag == 0)
    def _():
        work(False)

    @pl.when(diag == 1)
    def _():
        work(True)

    @pl.when(last == 1)
    def _():
        lane = lax.broadcasted_iota(jnp.int32, (block, 128), 1)
        lse = jnp.zeros((block, 128), F32)
        for g in range(groups):
            at = slice(g * hd, (g + 1) * hd)
            l = jnp.sum(lsum[g], axis=1, keepdims=True)
            out = acc[:, at] / l
            o_ref[:, at] = out
            low_ref[:, at] = out.astype(BF)
            lse = jnp.where(lane == g, jnp.log2(l), lse)
        lse_ref[...] = jnp.transpose(lse)[: lse_ref.shape[0]]


def attn_fwd(tab, q, kv, head, groups, hd, before, block):
    rows, width = q.shape
    gw = groups * hd
    steps = tab.shape[1]
    mine = pl.BlockSpec((block, gw), lambda s, t: (t[0, s], head))
    return pl.pallas_call(
        functools.partial(fwd_kernel, groups, hd),
        out_shape=(sds((rows, width), F32), sds((rows, width), BF), sds((8, rows), F32)),
        grid_spec=pltpu.PrefetchScalarGridSpec(
            num_scalar_prefetch=1,
            grid=(steps,),
            in_specs=[mine, pl.BlockSpec((block, 2 * hd), lambda s, t: (t[1, s], head))] + [HB] * len(before),
            out_specs=[mine, mine, pl.BlockSpec((8, block), lambda s, t: (0, t[0, s]))],
            scratch_shapes=[pltpu.VMEM((block, gw), F32), pltpu.VMEM((groups, block, 128), F32)],
        ),
        input_output_aliases={3: 0, 4: 1} if before else {},
        compiler_params=pltpu.CompilerParams(vmem_limit_bytes=48 << 20),
        cost_estimate=pl.CostEstimate(
            flops=steps * block * block * gw * 4,
            bytes_accessed=steps * block * hd * 8,
            transcendentals=steps * block * block * groups,
        ),
        name="attn_fwd",
    )(tab, q, kv, *before)


def bwd_kernel(groups, hd, first_head, tab, q_ref, do_ref, kv_ref, lse_ref, delta_ref, *refs):
    dq_ref, dkv_ref, dq_sum, dkv_sum = refs[-4:]
    s = pl.program_id(0)
    block = q_ref.shape[0]
    qi, diag, first, last = tab[0, s], tab[2, s], tab[3, s], tab[4, s]

    @pl.when(s == 0)
    def _():
        dq_sum[...] = jnp.zeros_like(dq_sum)

    @pl.when(first == 1)
    def _():
        dkv_sum[...] = jnp.zeros_like(dkv_sum)

    def work(masked):
        k, v = kv_ref[:, :hd], kv_ref[:, hd:]
        for g in range(groups):
            at = slice(g * hd, (g + 1) * hd)
            q, do = q_ref[:, at], do_ref[:, at]
            scores = dg(k, q, NT) - lse_ref[g : g + 1, :]
            if masked:
                row = lax.broadcasted_iota(jnp.int32, scores.shape, 0)
                col = lax.broadcasted_iota(jnp.int32, scores.shape, 1)
                scores = jnp.where(row <= col, scores, MASKED)
            probs = jnp.exp2(scores)
            dots = dg(v, do, NT)
            dkv_sum[:, hd:] += dg(probs.astype(BF), do, NN)
            h = first_head + g
            back = (probs * (dots - delta_ref[h : h + 1, :])).astype(BF)
            dkv_sum[:, :hd] += dg(back, q, NN)
            dq_sum[qi, :, at] += dg(back, k, TN)

    @pl.when(diag == 0)
    def _():
        work(False)

    @pl.when(diag == 1)
    def _():
        work(True)

    @pl.when(last == 1)
    def _():
        dkv_ref[:, :hd] = (dkv_sum[:, :hd] * math.log(2.0)).astype(BF)
        dkv_ref[:, hd:] = dkv_sum[:, hd:].astype(BF)

    @pl.when(s == pl.num_programs(0) - 1)
    def _():
        for i in range(dq_sum.shape[0]):
            dq_ref[i * block : (i + 1) * block, :] = dq_sum[i] * hd**-0.5


def attn_bwd(tab, q, do, kv, lse, delta, head, groups, hd, before, block):
    rows, width = q.shape
    gw = groups * hd
    steps = tab.shape[1]
    before = before or [jnp.zeros(kv.shape, BF)]
    mine = pl.BlockSpec((block, gw), lambda s, t: (t[0, s], head))
    keys = pl.BlockSpec((block, 2 * hd), lambda s, t: (t[1, s], head))
    stat = pl.BlockSpec((8, block), lambda s, t: (0, t[0, s]))
    return pl.pallas_call(
        functools.partial(bwd_kernel, groups, hd, head * groups),
        out_shape=(sds((rows, width), F32), sds(kv.shape, BF)),
        grid_spec=pltpu.PrefetchScalarGridSpec(
            num_scalar_prefetch=1,
            grid=(steps,),
            in_specs=[mine, mine, keys, stat, stat] + [HB] * len(before),
            out_specs=[pl.BlockSpec((rows, gw), lambda s, t: (0, head)), keys],
            scratch_shapes=[pltpu.VMEM((rows // block, block, gw), F32), pltpu.VMEM((block, 2 * hd), F32)],
        ),
        input_output_aliases={6: 0, 7: 1} if len(before) == 2 else {6: 1},
        compiler_params=pltpu.CompilerParams(vmem_limit_bytes=48 << 20),
        cost_estimate=pl.CostEstimate(
            flops=steps * block * block * gw * 10,
            bytes_accessed=steps * block * hd * 16,
            transcendentals=steps * block * block * groups,
        ),
        name="attn_bwd",
    )(tab, q, do, kv, lse, delta, *before)


def place(w, chips):
    k, core = w // 2, w % 2
    return 4 * k + core, 4 * chips - 1 - 4 * k - core


def block_row(b, chips):
    m = b % 4
    early = m < 2
    k = jnp.where(early, b // 4, (4 * chips - 1 - b) // 4)
    core = jnp.where((m == 1) | (m == 2), 1, 0)
    return 2 * (2 * k + core) + jnp.where(early, 0, 1)


def tables(w, chips):
    a, b = place(w, chips)
    count = 4 * chips + 1
    s = jnp.arange(count, dtype=jnp.int32)
    in_a = s <= a
    key = jnp.where(in_a, s, s - a - 1)
    diag = jnp.where(in_a, s == a, s == count - 1)
    fwd = [jnp.where(in_a, 0, 1), block_row(key, chips), diag, key == 0, diag]
    less, low = jnp.minimum(a, b), jnp.where(a < b, 0, 1)
    both = s < 2 * (less + 1)
    even = s % 2 == 0
    key = jnp.where(both, s // 2, s - (less + 1))
    query = jnp.where(both & even, low, 1 - low)
    diag = key == jnp.where(query == 0, a, b)
    bwd = [query, block_row(key, chips), diag, ~both | even, ~both | ~even]
    return tuple(jnp.stack([row.astype(jnp.int32) for row in rows]) for rows in (fwd, bwd))


def rotation(positions, head_dim):
    steps_half = jnp.arange(head_dim // 2).astype(F32)
    inverse = jnp.exp(steps_half * (-2.0 * math.log(1000000.0) / head_dim))
    angles = positions.astype(F32)[:, None] * inverse[None, :]
    cos, sin = jnp.cos(angles), jnp.sin(angles)
    return jnp.concatenate([cos, cos], axis=1), jnp.concatenate([-sin, sin], axis=1)


def per_device(
    wide, narrow,
    layer_input, w_query, w_key, w_value, w_output, w_gate, w_up, w_down,
    attn_gain, mlp_gain, query_gain, key_gain, out_grad,
):
    hd = query_gain.shape[0]
    rows, dim = layer_input.shape
    all_rows = narrow * rows
    chips = wide // 2
    block = all_rows // 2
    qw, kw = w_query.shape[1], w_key.shape[1]
    ff = w_gate.shape[1]
    groups = qw // kw
    kv_heads = kw // hd
    w = lax.axis_index("wide")
    fwd_tab, bwd_tab = tables(w, chips)
    first, second = place(w, chips)
    at = jnp.arange(block, dtype=jnp.int32)
    positions = jnp.concatenate([first * block + at, second * block + at])
    cos_table, sin_table = rotation(positions, hd)

    def gather(shard):
        return lax.all_gather(shard, "wide", axis=0, tiled=True)

    def scatter(grad):
        return lax.psum_scatter(grad, "wide", scatter_dimension=0, tiled=True)

    t = math.gcd(ff, 256)

    def weave(gate, up):
        return jnp.stack([gate.reshape(-1, ff // t, t), up.reshape(-1, ff // t, t)], axis=2).reshape(-1, 2 * ff)

    n_sems = [DMA((narrow,)), DMA((narrow,)), DMA]
    recv_buf = pltpu.VMEM((narrow, rows, dim), BF)
    row_buf = pltpu.VMEM((rows, dim), BF)
    low_rows, full_rows, all_low = sds((rows, dim), BF), sds((rows, dim), F32), sds((all_rows, dim), BF)
    ring = functools.partial
    qg, kg = query_gain[None], key_gain[None]
    after = lax.optimization_barrier

    w_gu, w_d = gather(weave(w_gate, w_up)), gather(w_down.T)
    in_specs, in_outs = [VM, VM, HB], (VM, HB, HB)
    in_scratch = [row_buf, *n_sems, DMA((2,)), *line_sems(chips)]
    shard = jnp.concatenate([w_query, w_key, w_value, w_output.T], axis=1)
    own, normed_all, w_attn = comm_call(
        ring(input_kernel, wide, narrow, True), "input_rows", 0,
        (low_rows, all_low, sds((dim, shard.shape[1]), BF)), in_specs, in_outs, in_scratch,
        layer_input, attn_gain[None], shard,
    )
    proj, queries, kv_own = qkv_fwd(
        normed_all, w_attn, cos_table, sin_table, qg, kg, qw, kw, hd**-0.5 * math.log2(math.e)
    )
    grad_own, grad_all, kv = comm_call(
        ring(input_kernel, wide, narrow, False), "grad_rows", 1,
        (low_rows, all_low, sds((wide * all_rows, 2 * kw), BF)), in_specs, in_outs, in_scratch,
        out_grad, attn_gain[None], kv_own,
    )
    mixed, lses = (), []
    for h in range(kv_heads):
        *mixed, lse = attn_fwd(fwd_tab, queries, kv, h, groups, hd, mixed, block)
        lses.append(lse)
    attended, attended_low = mixed
    w_o = w_attn[:, qw + 2 * kw :]
    middle, normed_mlp = comm_call(
        ring(middle_kernel, wide, narrow), "middle_rows", 2, (full_rows, all_low), [HB, VM, VM], (VM, HB),
        [recv_buf, row_buf, *n_sems, *n_sems], dg(attended_low, w_o, NT).astype(BF), own, mlp_gain[None],
    )
    gate_up, hidden_low = mlp_fwd(normed_mlp, w_gu, t)
    grad_down = dg(grad_all, hidden_low, TN).astype(BF)
    w_d, _ = after((w_d, grad_down))
    gu_low = mlp_bwd(grad_all, w_d, gate_up, t)
    grad_gu = dg(normed_mlp, gu_low, TN).astype(BF)
    mlp_back = mm_nt(gu_low, w_gu, "mlp_back")
    mlp_back, _ = after((mlp_back, grad_gu))
    grad_down, grad_gu = scatter(grad_down), scatter(grad_gu)
    middle_back, mlp_gain_part, middle_all = comm_call(
        ring(middle_back_kernel, wide, narrow), "middle_back", 3, (full_rows, sds((1, dim), F32), all_low),
        [HB, VM, VM, VM], (VM, VM, HB), [recv_buf, row_buf, *n_sems, *n_sems],
        mlp_back, middle, mlp_gain[None], grad_own,
    )
    back, delta = attn_back(middle_all, w_attn, attended, (qw + 2 * kw) // qw)
    backs = ()
    for h in range(kv_heads):
        backs = attn_bwd(bwd_tab, queries, back, kv, lses[h], delta, h, groups, hd, backs, block)
    query_back, dkv = backs
    hidden_late, middle_late, _ = after((hidden_low, middle_all, dkv))
    grad_output = dg(middle_late, attended_low, TN).astype(BF)
    dkv, grad_down = after((dkv, grad_down))
    layer_output, kv_sum = comm_call(
        ring(output_kernel, wide, narrow), "output_rows", 4, (low_rows, sds((all_rows, 2 * kw), BF)),
        [HB, VM, HB], (VM, VM),
        [recv_buf, row_buf, *n_sems, DMA((2,)), *line_sum_bufs(chips, all_rows, 2 * kw), *line_sum_sems(chips)],
        dg(hidden_late, w_d, NT).astype(BF), middle, dkv,
    )
    q_low, query_gain_part = q_back(query_back, proj, cos_table, sin_table, qg)
    qkv_low, normed_back, key_gain_part = kv_back(q_low, proj, cos_table, sin_table, kg, w_attn, kv_sum, kw)
    grad_qkv = jnp.concatenate([dg(normed_all, qkv_low, TN).astype(BF), grad_output], axis=1)
    normed_back, grad_qkv, grad_gu = after((normed_back, grad_qkv, grad_gu))
    grad_qkv = scatter(grad_qkv)
    gains = jnp.concatenate([jnp.zeros((1, dim), F32), mlp_gain_part, query_gain_part, key_gain_part], axis=1)
    gvec = sds(gains.shape, F32)
    input_grad, gain_sums = comm_call(
        ring(input_back_kernel, wide, narrow), "input_back", 5, (full_rows, gvec), [HB, VM, VM, VM, VM], (VM, VM),
        [recv_buf, row_buf, row_buf, pltpu.VMEM((narrow, *gains.shape), F32), pltpu.VMEM((wide, *gains.shape), F32),
         *n_sems, DMA((2,)), DMA((narrow,)), DMA((narrow,)), DMA((wide,)), DMA((wide,))],
        normed_back, own, attn_gain[None], middle_back, gains,
    )
    g = gain_sums[0]
    grad_gu = grad_gu.reshape(-1, ff // t, 2, t).astype(F32)
    grad_qkv = grad_qkv.astype(F32)
    return (
        layer_output, input_grad,
        grad_qkv[:, :qw], grad_qkv[:, qw : qw + kw], grad_qkv[:, qw + kw : qw + 2 * kw],
        grad_qkv[:, qw + 2 * kw :].T, grad_gu[:, :, 0].reshape(-1, ff), grad_gu[:, :, 1].reshape(-1, ff),
        grad_down.T.astype(F32),
        g[:dim], g[dim : 2 * dim], g[2 * dim : 2 * dim + hd], g[2 * dim + hd :],
    )


def solution(mesh):
    rows = P(("wide", "narrow"), None)
    weight, turned = P("wide", "narrow"), P("narrow", "wide")
    return jax.shard_map(
        functools.partial(per_device, mesh.shape["wide"], mesh.shape["narrow"]),
        mesh=mesh,
        in_specs=(rows, weight, weight, weight, turned, weight, weight, turned, P(), P(), P(), P(), rows),
        out_specs=(rows, rows, weight, weight, weight, turned, weight, weight, turned, P(), P(), P(), P()),
        check_vma=False,
    )
```

```python
import functools
import math

import jax
import jax.numpy as jnp
from jax import lax
from jax.experimental import pallas as pl
from jax.experimental.pallas import tpu as pltpu
from jax.sharding import PartitionSpec as P

EPSILON = 1e-06
MASKED = -1e30
F32 = jnp.float32
BF = jnp.bfloat16
MESH = pl.DeviceIdType.MESH
NT = (((1,), (1,)), ((), ()))
NN = (((1,), (0,)), ((), ()))
TN = (((0,), (0,)), ((), ()))


def dg(a, b, dims):
    return lax.dot_general(a, b, dims, preferred_element_type=F32)
DMA = pltpu.SemaphoreType.DMA


class Place:
    def __init__(self, wide, narrow):
        self.W, self.N = wide, narrow
        self.C, self.half = wide // 2, narrow // 2
        self.w, self.n = lax.axis_index("wide"), lax.axis_index("narrow")
        self.k, self.c = self.w // 2, lax.rem(self.w, 2)
        self.far = 2 * (self.C - 1 - self.k) + 1
        late = (self.n >= self.half).astype(jnp.int32)
        self.group = lax.rem(self.c + late, 2)
        self.slot = jnp.where(self.group == 0, self.n, lax.rem(self.n + self.half, self.N))

    def owner(self, j):
        core = 1 if j >= self.half else 0
        n = jnp.where(self.c == 0, j, (j + self.half) % self.N)
        return core, n

    def owner_is_me(self, j):
        core, n = self.owner(j)
        return (self.c == core) & (self.n == n)


def enter(p, line=False, ring=False):
    barrier = pltpu.get_barrier_semaphore()

    def greet(device):
        pl.semaphore_signal(barrier, inc=1, device_id=device, device_id_type=MESH)

    for core in range(2):
        for n in range(p.N):

            @pl.when((p.c != core) | (p.n != n))
            def _():
                greet((2 * p.k + core, n))

    peers = 2 * p.N - 1
    if line or ring:
        for k in range(p.C):

            @pl.when(p.k != k)
            def _():
                greet((2 * k + p.c, p.n))
                if ring:
                    greet((2 * k + 1 - p.c, p.n))

        peers += (2 if ring else 1) * (p.C - 1)
    pl.semaphore_wait(barrier, peers)


def swap_rows(p, src, dst, send_sem, recv_sem):
    return pltpu.make_async_remote_copy(
        src_ref=src, dst_ref=dst, send_sem=send_sem, recv_sem=recv_sem, device_id=(p.far, p.n), device_id_type=MESH
    )


def slot_of(p, n, group):
    return jnp.where(group == 0, n, lax.rem(n + p.half, p.N))


def neighbours(p):
    return p.n + 1 - 2 * lax.rem(p.n, 2), lax.rem(p.n + 2, 4), 3 - p.n


def to(src, dst, send, recv, wide, narrow):
    return pltpu.make_async_remote_copy(
        src_ref=src, dst_ref=dst, send_sem=send, recv_sem=recv, device_id=(wide, narrow), device_id_type=MESH
    )


def spread_sems(narrow):
    return [DMA((narrow, 2)), DMA((narrow, 2)), DMA((2,)), DMA((2,))]


def spread_start(p, src, gathered, rows, send, recv, local, onward):
    half = rows // 2
    view = lambda i: gathered.at[pl.ds(pl.multiple_of(p.slot * rows + i * half, half), half)]
    part = lambda i: src.at[pl.ds(i * half, half)]
    mine = p.group == p.c
    square = p.N == 4
    if square:
        nx, ny, _ = neighbours(p)
        targets = [(nx, (0, 1)), (ny, (1, 0))]
        order = [(t, q, i) for q in range(2) for t, halves in targets for i in (halves[q],)]
        for t, q, i in order:
            at = 0 if t is nx else 1
            to(part(i), view(i), send.at[at, i], recv.at[p.slot, i], 2 * p.k + p.group, t).start()
    else:
        for t in range(p.N):

            @pl.when(p.n != t)
            def _():
                for i in range(2):
                    to(part(i), view(i), send.at[t, i], recv.at[p.slot, i], 2 * p.k + p.group, t).start()

    @pl.when(mine)
    def _():
        for i in range(2):
            pltpu.make_async_copy(part(i), view(i), local.at[i]).start()

    @pl.when(jnp.logical_not(mine))
    def _():
        for i in range(2):
            to(part(i), view(i), local.at[i], recv.at[p.slot, i], 2 * p.k + p.group, p.n).start()


def spread_wait(p, src, gathered, rows, send, recv, local, onward):
    half = rows // 2
    piece = src.at[pl.ds(0, half)]
    mine = p.group == p.c
    at = lambda j, i: gathered.at[pl.ds(pl.multiple_of(j * rows + i * half, half), half)]

    def arrive(j, i):
        pltpu.make_async_copy(piece, at(j, i), recv.at[j, i]).wait()

    if p.N == 4:
        nx, ny, nd = neighbours(p)
        jx, jy, jd = (slot_of(p, n, p.c) for n in (nx, ny, nd))
        arrive(jx, 0)
        to(at(jx, 0), at(jx, 0), onward.at[0], recv.at[jx, 0], p.w, ny).start()
        arrive(jy, 1)
        to(at(jy, 1), at(jy, 1), onward.at[1], recv.at[jy, 1], p.w, nx).start()
        arrive(jx, 1)
        arrive(jy, 0)
        arrive(jd, 0)
        arrive(jd, 1)
        for i in range(2):
            pltpu.make_async_copy(piece, at(0, 0), onward.at[i]).wait()
            for t in range(2):
                pltpu.make_async_copy(piece, at(0, 0), send.at[t, i]).wait()
    else:
        for t in range(p.N):

            @pl.when(p.n != t)
            def _():
                for i in range(2):
                    pltpu.make_async_copy(piece, at(0, 0), send.at[t, i]).wait()
                    arrive(slot_of(p, t, p.c), i)

    for i in range(2):
        pltpu.make_async_copy(piece, at(0, 0), local.at[i]).wait()

    @pl.when(jnp.logical_not(mine))
    def _():
        arrive(slot_of(p, p.n, p.c), 0)
        arrive(slot_of(p, p.n, p.c), 1)


def sum_bufs(narrow, rows, dim):
    if narrow == 4:
        half = pltpu.VMEM((2, 2, rows, dim // 2), BF)
        return [half, half, pltpu.VMEM((2, rows, dim), BF)]
    return [pltpu.VMEM((narrow, rows, dim), BF)]


def sum_sems(narrow):
    if narrow == 4:
        return [DMA((2, 2)), DMA((2, 2)), DMA((2, 2)), DMA((4,)), DMA((4,))]
    return [DMA((narrow,)), DMA((narrow,)), DMA]


def pieces(p, part, rows, dim):
    half = dim // 2
    return lambda j, i: part.at[pl.ds(pl.multiple_of(j * rows, rows), rows), pl.ds(i * half, half)]


def sum_start(p, part, rows, dim, bufs, sems):
    if p.N != 4:
        (got,), (send, recv, local) = bufs, sems
        for j in range(p.N):
            core, n = p.owner(j)
            mine = p.owner_is_me(j)
            src = part.at[pl.ds(j * rows, rows)]

            @pl.when(mine)
            def _():
                pltpu.make_async_copy(src, got.at[p.n], local).start()

            @pl.when(jnp.logical_not(mine))
            def _():
                to(src, got.at[p.n], send.at[j], recv.at[p.n], 2 * p.k + core, n).start()

        return
    own, inbox, _ = bufs
    load, send, recv, _, _ = sems
    piece = pieces(p, part, rows, dim)
    nx, ny, nd = neighbours(p)
    across, here = slot_of(p, nd, p.c), slot_of(p, p.n, p.c)
    for i, n in enumerate((nx, ny)):
        to(piece(across, i), inbox.at[i, 0], send.at[i, 0], recv.at[i, 0], p.w, n).start()
    for i, n in enumerate((ny, nx)):
        pltpu.make_async_copy(piece(slot_of(p, n, p.c), i), own.at[i, 0], load.at[i, 0]).start()
    for i, n in enumerate((nx, ny)):
        to(piece(slot_of(p, n, p.c), i), inbox.at[i, 1], send.at[i, 1], recv.at[i, 1], p.w, n).start()
        pltpu.make_async_copy(piece(here, i), own.at[i, 1], load.at[i, 1]).start()


def core_of(p, j):
    return (j >= p.half).astype(jnp.int32)


def sum_wait(p, part, rows, dim, bufs, sems):
    if p.N != 4:
        (got,), (send, recv, local) = bufs, sems
        for t in range(p.N):
            mine = (p.group == p.c) & (p.n == t)

            @pl.when(mine)
            def _():
                pltpu.make_async_copy(part.at[pl.ds(0, rows)], got.at[t], local).wait()

            @pl.when(jnp.logical_not(mine))
            def _():
                pltpu.make_async_copy(part.at[pl.ds(0, rows)], got.at[t], recv.at[t]).wait()

        for j in range(p.N):

            @pl.when(jnp.logical_not(p.owner_is_me(j)))
            def _():
                pltpu.make_async_copy(part.at[pl.ds(j * rows, rows)], got.at[0], send.at[j]).wait()

        return
    own, inbox, box = bufs
    load, send, recv, send2, recv2 = sems
    piece = pieces(p, part, rows, dim)
    half = dim // 2
    nx, ny, _ = neighbours(p)
    cols = lambda i: pl.ds(i * half, half)

    def add(i, q):
        pltpu.make_async_copy(piece(0, 0), own.at[i, q], load.at[i, q]).wait()
        pltpu.make_async_copy(piece(0, 0), inbox.at[i, q], recv.at[i, q]).wait()

        def body(at):
            own[i, q, at, :] = (own[i, q, at, :].astype(F32) + inbox[i, q, at, :].astype(F32)).astype(BF)

        row_loop(rows, 64, body)

    for i, n in enumerate((ny, nx)):
        add(i, 0)
        j = slot_of(p, n, p.c)
        to(own.at[i, 0], box.at[1, :, cols(i)], send2.at[i], recv2.at[i], 2 * p.k + core_of(p, j), n).start()
    j = slot_of(p, p.n, p.c)
    keep = core_of(p, j) == p.c
    for i in range(2):
        add(i, 1)

        @pl.when(keep)
        def _():
            pltpu.make_async_copy(own.at[i, 1], box.at[0, :, cols(i)], send2.at[2 + i]).start()

        @pl.when(jnp.logical_not(keep))
        def _():
            to(own.at[i, 1], box.at[0, :, cols(i)], send2.at[2 + i], recv2.at[2 + i], 2 * p.k + core_of(p, j), p.n).start()

    for i in range(2):
        for q in range(2):
            pltpu.make_async_copy(piece(0, 0), inbox.at[i, q], send.at[i, q]).wait()
        pltpu.make_async_copy(own.at[i, 0], box.at[1, :, cols(i)], send2.at[i]).wait()
        pltpu.make_async_copy(own.at[i, 0], box.at[1, :, cols(i)], recv2.at[i]).wait()
        pltpu.make_async_copy(own.at[i, 1], box.at[0, :, cols(i)], send2.at[2 + i]).wait()

        @pl.when(p.group != p.c)
        def _():
            pltpu.make_async_copy(own.at[i, 1], box.at[0, :, cols(i)], recv2.at[2 + i]).wait()


def total(p, bufs, at):
    if p.N == 4:
        box = bufs[2]
        return box[0, at, :].astype(F32) + box[1, at, :].astype(F32)
    got = bufs[0]
    out = got[0, at, :].astype(F32)
    for t in range(1, p.N):
        out = out + got[t, at, :].astype(F32)
    return out


def line_sems(p_chips):
    return [DMA((2, p_chips + 1)), DMA((p_chips,)), DMA((p_chips,)), DMA((p_chips,)), DMA]


def line_parts(p, full, rows):
    return lambda s, core: full.at[pl.ds(pl.multiple_of((2 * s + core) * rows, rows), rows)]


def line_copy(p, src, dst, send, recv, k, core):
    return pltpu.make_async_remote_copy(
        src_ref=src, dst_ref=dst, send_sem=send, recv_sem=recv, device_id=(2 * k + core, p.n), device_id_type=MESH
    )


def inside(p, k):
    return (k >= 0) & (k < p.C)


def line_start(p, src, full, rows, zsend, zrecv, csend, crecv, local):
    at = line_parts(p, full, rows)
    for i, sign in enumerate((1, -1)):
        for d in (1, 2):
            t = p.k + sign * d

            @pl.when(inside(p, t))
            def _():
                line_copy(p, src, at(p.k, p.c), zsend.at[i, d], zrecv.at[p.k], t, p.c).start()

    pltpu.make_async_copy(src, at(p.k, p.c), local).start()
    line_copy(p, src, at(p.k, p.c), csend.at[p.k], crecv.at[p.k], p.k, 1 - p.c).start()


def line_finish(p, src, full, rows, zsend, zrecv, csend, crecv, local):
    at = line_parts(p, full, rows)
    for d in range(1, p.C):
        for i, sign in enumerate((1, -1)):
            s, t = p.k - sign * d, p.k + sign

            @pl.when(inside(p, s))
            def _():
                pltpu.make_async_copy(src, at(s, p.c), zrecv.at[s]).wait()
                if d >= 2:

                    @pl.when(inside(p, t))
                    def _():
                        line_copy(p, at(s, p.c), at(s, p.c), zsend.at[i, d + 1], zrecv.at[s], t, p.c).start()

                line_copy(p, at(s, p.c), at(s, p.c), csend.at[s], crecv.at[s], p.k, 1 - p.c).start()

    pltpu.make_async_copy(src, at(p.k, p.c), local).wait()
    for s in range(p.C):
        pltpu.make_async_copy(src, at(s, p.c), csend.at[s]).wait()
        pltpu.make_async_copy(src, at(s, 1 - p.c), crecv.at[s]).wait()
    for i, sign in enumerate((1, -1)):
        for d in (1, 2):

            @pl.when(inside(p, p.k + sign * d))
            def _():
                pltpu.make_async_copy(src, at(p.k, p.c), zsend.at[i, d]).wait()

        for d in range(2, p.C):

            @pl.when(inside(p, p.k - sign * d) & inside(p, p.k + sign))
            def _():
                pltpu.make_async_copy(src, at(p.k, p.c), zsend.at[i, d + 1]).wait()


def line_sum_bufs(chips, rows, width):
    return [pltpu.VMEM((chips, rows, width), BF)] * 3 + [pltpu.VMEM((2, 2, rows, width), BF), pltpu.VMEM((rows, width), F32)]


def line_sum_sems(chips):
    return [DMA((chips,)), DMA((chips,)), DMA((chips,)), DMA((2, chips)), DMA((chips,)), DMA((2, 2))]


def line_sum_start(p, part, rows, bufs, sems):
    own, inbox, _, _, _ = bufs
    load, csend, crecv, _, _, _ = sems
    at = line_parts(p, part, rows)
    for s in range(p.C):
        line_copy(p, at(s, 1 - p.c), inbox.at[s], csend.at[s], crecv.at[s], p.k, 1 - p.c).start()
        pltpu.make_async_copy(at(s, p.c), own.at[s], load.at[s]).start()


def line_sum_run(p, part, rows, bufs, sems):
    own, inbox, relay, box, acc = bufs
    load, csend, crecv, zsend, rrecv, zrecv = sems
    at = line_parts(p, part, rows)

    def pair(t):
        pltpu.make_async_copy(at(0, 0), own.at[t], load.at[t]).wait()
        pltpu.make_async_copy(at(0, 0), inbox.at[t], crecv.at[t]).wait()

    for d in range(p.C - 1, 0, -1):
        for i, sign in enumerate((1, -1)):
            t = p.k + sign * d

            @pl.when(inside(p, t))
            def _():
                pair(t)

                def add(rows_at):
                    both = own[t, rows_at, :].astype(F32) + inbox[t, rows_at, :].astype(F32)
                    own[t, rows_at, :] = both.astype(BF)

                row_loop(rows, 128, add)
                if d >= 2:

                    @pl.when(inside(p, p.k - sign))
                    def _():
                        pltpu.make_async_copy(at(0, 0), relay.at[t], rrecv.at[t]).wait()

                        def add_relay(rows_at):
                            both = own[t, rows_at, :].astype(F32) + relay[t, rows_at, :].astype(F32)
                            own[t, rows_at, :] = both.astype(BF)

                        row_loop(rows, 128, add_relay)

                if d >= 3:
                    line_copy(p, own.at[t], relay.at[t], zsend.at[i, d], rrecv.at[t], p.k + sign, p.c).start()
                else:
                    line_copy(p, own.at[t], box.at[i, d - 1], zsend.at[i, d], zrecv.at[i, d - 1], t, p.c).start()

    pair(p.k)

    def first(rows_at):
        acc[rows_at, :] = own[p.k, rows_at, :].astype(F32) + inbox[p.k, rows_at, :].astype(F32)

    row_loop(rows, 128, first)
    for i, sign in enumerate((1, -1)):
        for d in (1, 2):

            @pl.when(inside(p, p.k - sign * d))
            def _():
                pltpu.make_async_copy(at(0, 0), box.at[i, d - 1], zrecv.at[i, d - 1]).wait()

                def more(rows_at):
                    acc[rows_at, :] += box[i, d - 1, rows_at, :].astype(F32)

                row_loop(rows, 128, more)

        for d in range(1, p.C):

            @pl.when(inside(p, p.k + sign * d))
            def _():
                pltpu.make_async_copy(at(0, 0), own.at[0], zsend.at[i, d]).wait()

    for s in range(p.C):
        pltpu.make_async_copy(at(0, 0), inbox.at[s], csend.at[s]).wait()


def row_loop(rows, step, body):
    def one(i, carry):
        body(pl.ds(pl.multiple_of(i * step, step), step))
        return carry

    lax.fori_loop(0, rows // step, one, 0)


STEP = 64


def inv_rms(u):
    return lax.rsqrt(jnp.mean(u * u, axis=-1, keepdims=True) + EPSILON)


def swap_out(p, buf, out_ref, sems):
    @pl.when(p.c == 1)
    def _():
        copy = swap_rows(p, buf, out_ref, sems.at[0], sems.at[1])
        copy.start()
        copy.wait()

    @pl.when(p.c == 0)
    def _():
        out_ref[...] = buf[...]


def input_kernel(wide, narrow, first, x_ref, gain_ref, shard, own_ref, gathered, full, buf, swap, go, *sems):
    p = Place(wide, narrow)
    rows = x_ref.shape[0]
    spread, line = sems[:4], sems[4:]
    enter(p, line=True)

    def start_line():
        line_start(p, shard, full, shard.shape[0], *line)

    @pl.when(p.c == 1)
    def _():
        swap_rows(p, x_ref, own_ref, swap.at[0], swap.at[1]).start()

    if not first:
        start_line()

    @pl.when(p.c == 1)
    def _():
        swap_rows(p, x_ref, own_ref, swap.at[0], swap.at[1]).wait()
        if first:
            pl.semaphore_signal(go, inc=1, device_id=(2 * p.k, p.n), device_id_type=MESH)
            start_line()

    @pl.when(p.c == 0)
    def _():
        own_ref[...] = x_ref[...]

    if first:

        def body(at):
            u = own_ref[at, :].astype(F32)
            buf[at, :] = (u * inv_rms(u) * gain_ref[...]).astype(BF)

        row_loop(rows, STEP, body)
    src = buf if first else own_ref
    spread_start(p, src, gathered, rows, *spread)
    if first:

        @pl.when(p.c == 0)
        def _():
            pl.semaphore_wait(go, 1)
            start_line()

        spread_wait(p, src, gathered, rows, *spread)
        line_finish(p, shard, full, shard.shape[0], *line)
    else:
        line_finish(p, shard, full, shard.shape[0], *line)
        spread_wait(p, src, gathered, rows, *spread)


def middle_kernel(wide, narrow, part, own_ref, gain_ref, mid_ref, gathered, buf, *refs):
    p = Place(wide, narrow)
    rows, dim = own_ref.shape
    bufs, sems, spread = split_refs(narrow, refs)
    enter(p)
    sum_start(p, part, rows, dim, bufs, sems)
    sum_wait(p, part, rows, dim, bufs, sems)

    def body(at):
        u = own_ref[at, :].astype(F32) + total(p, bufs, at)
        mid_ref[at, :] = u
        buf[at, :] = (u * inv_rms(u) * gain_ref[...]).astype(BF)

    row_loop(rows, STEP, body)
    spread_start(p, buf, gathered, rows, *spread)
    spread_wait(p, buf, gathered, rows, *spread)


def split_refs(narrow, refs):
    bufs, sems = (3, 5) if narrow == 4 else (1, 3)
    return refs[:bufs], refs[bufs : bufs + sems], refs[bufs + sems :]


def output_kernel(wide, narrow, part, mid_ref, dkv, out_ref, kv_ref, buf, swap, *refs):
    p = Place(wide, narrow)
    rows, dim = mid_ref.shape
    kv_rows = kv_ref.shape[0]
    bufs, sems, line = split_refs(narrow, refs)
    line_bufs, line_sem = line[:5], line[5:]
    enter(p, line=True)
    line_sum_start(p, dkv, kv_rows, line_bufs, line_sem)
    sum_start(p, part, rows, dim, bufs, sems)
    line_sum_run(p, dkv, kv_rows, line_bufs, line_sem)
    row_loop(kv_rows, 128, lambda at: kv_ref.__setitem__((at, slice(None)), line_bufs[4][at, :].astype(BF)))
    sum_wait(p, part, rows, dim, bufs, sems)

    def body(at):
        buf[at, :] = (mid_ref[at, :] + total(p, bufs, at)).astype(BF)

    row_loop(rows, STEP, body)
    swap_out(p, buf, out_ref, swap)


def norm_back(u, gain, cot):
    r = inv_rms(u)
    a = cot * gain
    du = r * a - u * (r * r * r) * jnp.mean(a * u, axis=-1, keepdims=True)
    return du, jnp.sum(cot * u * r, axis=0, keepdims=True)


def middle_back_kernel(wide, narrow, part, mid_ref, gain_ref, grad_ref, back_ref, dgain_ref, gathered, buf, *refs):
    p = Place(wide, narrow)
    rows, dim = mid_ref.shape
    bufs, sems, spread = split_refs(narrow, refs)
    enter(p)
    sum_start(p, part, rows, dim, bufs, sems)
    dgain_ref[...] = jnp.zeros_like(dgain_ref)
    sum_wait(p, part, rows, dim, bufs, sems)

    def body(at):
        du, dgain = norm_back(mid_ref[at, :], gain_ref[...], total(p, bufs, at))
        back = grad_ref[at, :].astype(F32) + du
        back_ref[at, :] = back
        buf[at, :] = back.astype(BF)
        dgain_ref[...] += dgain

    row_loop(rows, STEP, body)
    spread_start(p, buf, gathered, rows, *spread)
    spread_wait(p, buf, gathered, rows, *spread)


def input_back_kernel(
    wide, narrow, part, own_ref, gain_ref, back_ref, gains_ref, wgrad, out_ref, gsum_ref, wsum_ref,
    buf, far_buf, gbuf, gbuf2, swap, gsend, grecv, gsend2, grecv2, *refs,
):
    p = Place(wide, narrow)
    rows, dim = own_ref.shape
    w_rows = wsum_ref.shape[0]
    bufs, sems, line = split_refs(narrow, refs)
    line_bufs, line_sem = (*line[:4], wsum_ref), line[4:]
    enter(p, ring=True)
    line_sum_start(p, wgrad, w_rows, line_bufs, line_sem)
    sum_start(p, part, rows, dim, bufs, sems)
    gsum_ref[...] = gains_ref[...]
    sum_wait(p, part, rows, dim, bufs, sems)

    def body(at):
        du, dgain = norm_back(own_ref[at, :].astype(F32), gain_ref[...], total(p, bufs, at))
        grad = back_ref[at, :] + du
        out_ref[at, :] = grad
        buf[at, :] = grad.astype(BF)
        gsum_ref[:, :dim] += dgain

    row_loop(rows, STEP, body)

    @pl.when(p.c == 1)
    def _():
        swap_rows(p, buf, far_buf, swap.at[0], swap.at[1]).start()

    def share(me, count, here, slots, sends, recvs, device):
        slots[me] = here[...]
        for t in range(count):

            @pl.when(me != t)
            def _():
                wide_at, narrow_at = device(t)
                to(here, slots.at[me], sends.at[t], recvs.at[me], wide_at, narrow_at).start()

        for t in range(count):

            @pl.when(me != t)
            def _():
                pltpu.make_async_copy(here, slots.at[t], sends.at[t]).wait()
                pltpu.make_async_copy(here, slots.at[t], recvs.at[t]).wait()

        out = slots[0]
        for t in range(1, count):
            out = out + slots[t]
        here[...] = out

    share(p.n, narrow, gsum_ref, gbuf, gsend, grecv, lambda t: (p.w, t))
    line_sum_run(p, wgrad, w_rows, line_bufs, line_sem)
    share(p.w, wide, gsum_ref, gbuf2, gsend2, grecv2, lambda t: (t, p.n))

    @pl.when(p.c == 1)
    def _():
        swap_rows(p, buf, far_buf, swap.at[0], swap.at[1]).wait()
        row_loop(rows, STEP, lambda at: out_ref.__setitem__((at, slice(None)), far_buf[at, :].astype(F32)))


VM = pl.BlockSpec(memory_space=pltpu.VMEM)
HB = pl.BlockSpec(memory_space=pl.ANY)


def comm_call(kernel, name, cid, out_shape, in_specs, out_specs, scratch, *args):
    return pl.pallas_call(
        kernel,
        out_shape=out_shape,
        in_specs=in_specs,
        out_specs=out_specs,
        scratch_shapes=scratch,
        compiler_params=pltpu.CompilerParams(collective_id=cid, has_side_effects=True, vmem_limit_bytes=52 << 20),
        cost_estimate=pl.CostEstimate(flops=0, bytes_accessed=160_000_000, transcendentals=0),
        name=name,
    )(*args)


def sds(shape, kind):
    return jax.ShapeDtypeStruct(shape, kind)


def plain(kernel, name, grid, in_specs, out_specs, out_shape, flops, nbytes, *args, scratch=(), aliases=None):
    return pl.pallas_call(
        kernel,
        out_shape=out_shape,
        grid=grid,
        in_specs=in_specs,
        out_specs=out_specs,
        scratch_shapes=scratch,
        input_output_aliases=aliases or {},
        compiler_params=pltpu.CompilerParams(vmem_limit_bytes=52 << 20),
        cost_estimate=pl.CostEstimate(flops=flops, bytes_accessed=nbytes, transcendentals=0),
        name=name,
    )(*args)


def whole(shape):
    return pl.BlockSpec(shape, lambda *i: (0,) * len(shape), pipeline_mode=pl.Buffered(1))


def by_rows(tm, width):
    return pl.BlockSpec((tm, width), lambda i: (i, 0))


def mlp_fwd_kernel(x_ref, w_ref, gu_ref, h_ref):
    t = h_ref.shape[1]
    y = dg(x_ref[...], w_ref[...], NN)
    gate, up = y[:, :t], y[:, t:]
    gu_ref[...] = y
    h_ref[...] = (gate * jax.nn.sigmoid(gate) * up).astype(BF)


def mlp_fwd(x, w, t):
    rows, dim = x.shape
    ff2 = w.shape[1]
    return plain(
        mlp_fwd_kernel, "mlp_fwd", (ff2 // (2 * t),),
        [whole((rows, dim)), pl.BlockSpec((dim, 2 * t), lambda i: (0, i))],
        [pl.BlockSpec((rows, 2 * t), lambda i: (0, i)), pl.BlockSpec((rows, t), lambda i: (0, i))],
        (sds((rows, ff2), F32), sds((rows, ff2 // 2), BF)),
        2 * rows * dim * ff2, rows * dim * 2 + dim * ff2 * 2 + rows * ff2 * 5, x, w,
    )


def mlp_bwd_kernel(g_ref, w_ref, gu_ref, out_ref):
    t = w_ref.shape[1]
    hb = dg(g_ref[...], w_ref[...], NN)
    gate, up = gu_ref[:, :t], gu_ref[:, t:]
    s = jax.nn.sigmoid(gate)
    gs = hb * s
    out_ref[:, :t] = (gs * up * (1.0 + gate * (1.0 - s))).astype(BF)
    out_ref[:, t:] = (gs * gate).astype(BF)


def mlp_bwd(g, w, gu, t):
    rows, dim = g.shape
    ff = w.shape[1]
    return plain(
        mlp_bwd_kernel, "mlp_bwd", (ff // t,),
        [whole((rows, dim)), pl.BlockSpec((dim, t), lambda i: (0, i)), pl.BlockSpec((rows, 2 * t), lambda i: (0, i))],
        pl.BlockSpec((rows, 2 * t), lambda i: (0, i)), sds((rows, 2 * ff), BF),
        2 * rows * dim * ff, rows * dim * 2 + dim * ff * 2 + rows * ff * 12, g, w, gu,
    )


def nt_kernel(a_ref, b_ref, o_ref):
    o_ref[...] = dg(a_ref[...], b_ref[...], NT).astype(BF)


def mm_nt(a, b, name, tn=256):
    rows, depth = a.shape
    cols = b.shape[0]
    return plain(
        nt_kernel, name, (cols // tn,), [whole((rows, depth)), by_rows(tn, depth)],
        pl.BlockSpec((rows, tn), lambda i: (0, i)), sds((rows, cols), BF),
        2 * rows * cols * depth, 2 * (rows * depth + cols * depth + rows * cols), a, b,
    )


def turn(u):
    return pltpu.roll(u, u.shape[-1] // 2, 1)


def qkv_kernel(qw, kw, hd, fold, x_ref, w_ref, cos_ref, sin_ref, qg_ref, kg_ref, proj_ref, q_ref, kv_ref):
    y = dg(x_ref[...], w_ref[...], NN)
    cos, sin = cos_ref[...], sin_ref[...]
    proj_ref[...] = y[:, : qw + kw]

    def head(lo, gain):
        u = y[:, lo : lo + hd]
        v = u * inv_rms(u) * gain
        return v * cos + turn(v) * sin

    for h in range(qw // hd):
        q_ref[:, h * hd : (h + 1) * hd] = (head(h * hd, qg_ref[...]) * fold).astype(BF)
    for h in range(kw // hd):
        kv_ref[:, 2 * h * hd : (2 * h + 1) * hd] = head(qw + h * hd, kg_ref[...]).astype(BF)
        kv_ref[:, (2 * h + 1) * hd : (2 * h + 2) * hd] = y[:, qw + kw + h * hd : qw + kw + (h + 1) * hd].astype(BF)


def qkv_fwd(x, w, cos, sin, qg, kg, qw, kw, fold):
    rows, dim = x.shape
    hd = cos.shape[1]
    width = qw + 2 * kw
    tm = 256
    return plain(
        functools.partial(qkv_kernel, qw, kw, hd, fold), "qkv_fwd", (rows // tm,),
        [by_rows(tm, dim), whole((dim, width)), by_rows(tm, hd), by_rows(tm, hd), whole((1, hd)), whole((1, hd))],
        [by_rows(tm, qw + kw), by_rows(tm, qw), by_rows(tm, 2 * kw)],
        [sds((rows, qw + kw), F32), sds((rows, qw), BF), sds((rows, 2 * kw), BF)],
        2 * rows * dim * width, 2 * (rows * dim + dim * width) + rows * width * 6, x, w, cos, sin, qg, kg,
    )


def head_back(cot, u, gain, cos, sin):
    cot = cot * cos - turn(cot) * sin
    return norm_back(u, gain, cot)


def q_back_kernel(hd, dq_ref, u_ref, cos_ref, sin_ref, g_ref, low_ref, dgain_ref):
    @pl.when(pl.program_id(0) == 0)
    def _():
        dgain_ref[...] = jnp.zeros_like(dgain_ref)

    for h in range(dq_ref.shape[1] // hd):
        at = slice(h * hd, (h + 1) * hd)
        du, dgain = head_back(dq_ref[:, at], u_ref[:, at], g_ref[...], cos_ref[...], sin_ref[...])
        low_ref[:, at] = du.astype(BF)
        dgain_ref[...] += dgain


def q_back(dq, proj, cos, sin, gain):
    rows, qw = dq.shape
    hd = cos.shape[1]
    tm = 256
    return plain(
        functools.partial(q_back_kernel, hd), "q_back", (rows // tm,),
        [by_rows(tm, qw), by_rows(tm, qw), by_rows(tm, hd), by_rows(tm, hd), whole((1, hd))],
        [by_rows(tm, qw), pl.BlockSpec((1, hd), lambda i: (0, 0))], [sds((rows, qw), BF), sds((1, hd), F32)],
        rows * qw * 20, rows * qw * 10, dq, proj, cos, sin, gain,
    )


def kv_back_kernel(qw, kw, hd, q_ref, u_ref, cos_ref, sin_ref, g_ref, w_ref, *refs):
    s_ref, low_ref, back_ref, dgain_ref = refs

    @pl.when(pl.program_id(0) == 0)
    def _():
        dgain_ref[...] = jnp.zeros_like(dgain_ref)

    low_ref[:, :qw] = q_ref[...]
    for h in range(kw // hd):
        key = slice(2 * h * hd, (2 * h + 1) * hd)
        value = slice((2 * h + 1) * hd, (2 * h + 2) * hd)
        at = slice(qw + h * hd, qw + (h + 1) * hd)
        du, dgain = head_back(s_ref[:, key].astype(F32), u_ref[:, at], g_ref[...], cos_ref[...], sin_ref[...])
        low_ref[:, at] = du.astype(BF)
        low_ref[:, qw + kw + h * hd : qw + kw + (h + 1) * hd] = s_ref[:, value]
        dgain_ref[...] += dgain
    back_ref[...] = dg(low_ref[...], w_ref[...], NT).astype(BF)


def kv_back(q_low, proj, cos, sin, gain, w, sums, kw):
    rows, qw = q_low.shape
    hd = cos.shape[1]
    dim = w.shape[0]
    width = qw + 2 * kw
    tm = 256
    return plain(
        functools.partial(kv_back_kernel, qw, kw, hd), "kv_back", (rows // tm,),
        [by_rows(tm, qw), by_rows(tm, qw + kw), by_rows(tm, hd), by_rows(tm, hd), whole((1, hd)), whole((dim, width))]
        + [by_rows(tm, 2 * kw)],
        [by_rows(tm, width), by_rows(tm, dim), pl.BlockSpec((1, hd), lambda i: (0, 0))],
        [sds((rows, width), BF), sds((rows, dim), BF), sds((1, hd), F32)],
        2 * rows * dim * width, 2 * (rows * dim + dim * width) + rows * width * 6,
        q_low, proj, cos, sin, gain, w, sums,
    )


def attn_back_kernel(hd, x_ref, w_ref, o_ref, back_ref, delta_ref):
    back = dg(x_ref[...], w_ref[...], NN).astype(BF)
    back_ref[...] = back
    rows, width = back.shape
    lane = lax.broadcasted_iota(jnp.int32, (rows, hd), 1)
    out = jnp.zeros((rows, hd), F32)
    for h in range(width // hd):
        at = slice(h * hd, (h + 1) * hd)
        out = jnp.where(lane == h, jnp.sum(back[:, at].astype(F32) * o_ref[:, at], axis=1, keepdims=True), out)
    delta_ref[...] = jnp.transpose(out)[: delta_ref.shape[0]]


def attn_back(x, w, o, at):
    rows, dim = x.shape
    width = o.shape[1]
    tm = 256
    return plain(
        functools.partial(attn_back_kernel, 128), "attn_back", (rows // tm,),
        [by_rows(tm, dim), pl.BlockSpec((dim, width), lambda i: (0, at), pipeline_mode=pl.Buffered(1)), by_rows(tm, width)],
        [by_rows(tm, width), pl.BlockSpec((8, tm), lambda i: (0, i))], [sds((rows, width), BF), sds((8, rows), F32)],
        2 * rows * dim * width, 2 * (rows * dim + dim * width) + rows * width * 6, x, w, o,
    )


def fwd_kernel(groups, hd, tab, q_ref, kv_ref, *refs):
    o_ref, low_ref, lse_ref, acc, lsum = refs[-5:]
    s = pl.program_id(0)
    block = q_ref.shape[0]
    diag, first, last = tab[2, s], tab[3, s], tab[4, s]

    @pl.when(first == 1)
    def _():
        acc[...] = jnp.zeros_like(acc)
        lsum[...] = jnp.zeros_like(lsum)

    def work(masked):
        k, v = kv_ref[:, :hd], kv_ref[:, hd:]
        for g in range(groups):
            at = slice(g * hd, (g + 1) * hd)
            scores = dg(q_ref[:, at], k, NT)
            if masked:
                row = lax.broadcasted_iota(jnp.int32, scores.shape, 0)
                col = lax.broadcasted_iota(jnp.int32, scores.shape, 1)
                scores = jnp.where(col <= row, scores, MASKED)
            probs = jnp.exp2(scores)
            part = probs[:, :128]
            for j in range(1, block // 128):
                part = part + probs[:, j * 128 : (j + 1) * 128]
            lsum[g] += part
            acc[:, at] += dg(probs.astype(BF), v, NN)

    @pl.when(diag == 0)
    def _():
        work(False)

    @pl.when(diag == 1)
    def _():
        work(True)

    @pl.when(last == 1)
    def _():
        lane = lax.broadcasted_iota(jnp.int32, (block, 128), 1)
        lse = jnp.zeros((block, 128), F32)
        for g in range(groups):
            at = slice(g * hd, (g + 1) * hd)
            l = jnp.sum(lsum[g], axis=1, keepdims=True)
            out = acc[:, at] / l
            o_ref[:, at] = out
            low_ref[:, at] = out.astype(BF)
            lse = jnp.where(lane == g, jnp.log2(l), lse)
        lse_ref[...] = jnp.transpose(lse)[: lse_ref.shape[0]]


def attn_fwd(tab, q, kv, head, groups, hd, before, block):
    rows, width = q.shape
    gw = groups * hd
    steps = tab.shape[1]
    mine = pl.BlockSpec((block, gw), lambda s, t: (t[0, s], head))
    return pl.pallas_call(
        functools.partial(fwd_kernel, groups, hd),
        out_shape=(sds((rows, width), F32), sds((rows, width), BF), sds((8, rows), F32)),
        grid_spec=pltpu.PrefetchScalarGridSpec(
            num_scalar_prefetch=1,
            grid=(steps,),
            in_specs=[mine, pl.BlockSpec((block, 2 * hd), lambda s, t: (t[1, s], head))] + [HB] * len(before),
            out_specs=[mine, mine, pl.BlockSpec((8, block), lambda s, t: (0, t[0, s]))],
            scratch_shapes=[pltpu.VMEM((block, gw), F32), pltpu.VMEM((groups, block, 128), F32)],
        ),
        input_output_aliases={3: 0, 4: 1} if before else {},
        compiler_params=pltpu.CompilerParams(vmem_limit_bytes=48 << 20),
        cost_estimate=pl.CostEstimate(
            flops=steps * block * block * gw * 4,
            bytes_accessed=steps * block * hd * 8,
            transcendentals=steps * block * block * groups,
        ),
        name="attn_fwd",
    )(tab, q, kv, *before)


def bwd_kernel(groups, hd, first_head, tab, q_ref, do_ref, kv_ref, lse_ref, delta_ref, *refs):
    dq_ref, dkv_ref, dq_sum, dkv_sum = refs[-4:]
    s = pl.program_id(0)
    block = q_ref.shape[0]
    qi, diag, first, last = tab[0, s], tab[2, s], tab[3, s], tab[4, s]

    @pl.when(s == 0)
    def _():
        dq_sum[...] = jnp.zeros_like(dq_sum)

    @pl.when(first == 1)
    def _():
        dkv_sum[...] = jnp.zeros_like(dkv_sum)

    def work(masked):
        k, v = kv_ref[:, :hd], kv_ref[:, hd:]
        for g in range(groups):
            at = slice(g * hd, (g + 1) * hd)
            q, do = q_ref[:, at], do_ref[:, at]
            scores = dg(k, q, NT) - lse_ref[g : g + 1, :]
            if masked:
                row = lax.broadcasted_iota(jnp.int32, scores.shape, 0)
                col = lax.broadcasted_iota(jnp.int32, scores.shape, 1)
                scores = jnp.where(row <= col, scores, MASKED)
            probs = jnp.exp2(scores)
            dots = dg(v, do, NT)
            dkv_sum[:, hd:] += dg(probs.astype(BF), do, NN)
            h = first_head + g
            back = (probs * (dots - delta_ref[h : h + 1, :])).astype(BF)
            dkv_sum[:, :hd] += dg(back, q, NN)
            dq_sum[qi, :, at] += dg(back, k, TN)

    @pl.when(diag == 0)
    def _():
        work(False)

    @pl.when(diag == 1)
    def _():
        work(True)

    @pl.when(last == 1)
    def _():
        dkv_ref[:, :hd] = (dkv_sum[:, :hd] * math.log(2.0)).astype(BF)
        dkv_ref[:, hd:] = dkv_sum[:, hd:].astype(BF)

    @pl.when(s == pl.num_programs(0) - 1)
    def _():
        for i in range(dq_sum.shape[0]):
            dq_ref[i * block : (i + 1) * block, :] = dq_sum[i] * hd**-0.5


def attn_bwd(tab, q, do, kv, lse, delta, head, groups, hd, before, block):
    rows, width = q.shape
    gw = groups * hd
    steps = tab.shape[1]
    before = before or [jnp.zeros(kv.shape, BF)]
    mine = pl.BlockSpec((block, gw), lambda s, t: (t[0, s], head))
    keys = pl.BlockSpec((block, 2 * hd), lambda s, t: (t[1, s], head))
    stat = pl.BlockSpec((8, block), lambda s, t: (0, t[0, s]))
    return pl.pallas_call(
        functools.partial(bwd_kernel, groups, hd, head * groups),
        out_shape=(sds((rows, width), F32), sds(kv.shape, BF)),
        grid_spec=pltpu.PrefetchScalarGridSpec(
            num_scalar_prefetch=1,
            grid=(steps,),
            in_specs=[mine, mine, keys, stat, stat] + [HB] * len(before),
            out_specs=[pl.BlockSpec((rows, gw), lambda s, t: (0, head)), keys],
            scratch_shapes=[pltpu.VMEM((rows // block, block, gw), F32), pltpu.VMEM((block, 2 * hd), F32)],
        ),
        input_output_aliases={6: 0, 7: 1} if len(before) == 2 else {6: 1},
        compiler_params=pltpu.CompilerParams(vmem_limit_bytes=48 << 20),
        cost_estimate=pl.CostEstimate(
            flops=steps * block * block * gw * 10,
            bytes_accessed=steps * block * hd * 16,
            transcendentals=steps * block * block * groups,
        ),
        name="attn_bwd",
    )(tab, q, do, kv, lse, delta, *before)


def place(w, chips):
    k, core = w // 2, w % 2
    return 4 * k + core, 4 * chips - 1 - 4 * k - core


def block_row(b, chips):
    m = b % 4
    early = m < 2
    k = jnp.where(early, b // 4, (4 * chips - 1 - b) // 4)
    core = jnp.where((m == 1) | (m == 2), 1, 0)
    return 2 * (2 * k + core) + jnp.where(early, 0, 1)


def tables(w, chips):
    a, b = place(w, chips)
    count = 4 * chips + 1
    s = jnp.arange(count, dtype=jnp.int32)
    in_a = s <= a
    key = jnp.where(in_a, s, s - a - 1)
    diag = jnp.where(in_a, s == a, s == count - 1)
    fwd = [jnp.where(in_a, 0, 1), block_row(key, chips), diag, key == 0, diag]
    less, low = jnp.minimum(a, b), jnp.where(a < b, 0, 1)
    both = s < 2 * (less + 1)
    even = s % 2 == 0
    key = jnp.where(both, s // 2, s - (less + 1))
    query = jnp.where(both & even, low, 1 - low)
    diag = key == jnp.where(query == 0, a, b)
    bwd = [query, block_row(key, chips), diag, ~both | even, ~both | ~even]
    return tuple(jnp.stack([row.astype(jnp.int32) for row in rows]) for rows in (fwd, bwd))


def rotation(positions, head_dim):
    steps_half = jnp.arange(head_dim // 2).astype(F32)
    inverse = jnp.exp(steps_half * (-2.0 * math.log(1000000.0) / head_dim))
    angles = positions.astype(F32)[:, None] * inverse[None, :]
    cos, sin = jnp.cos(angles), jnp.sin(angles)
    return jnp.concatenate([cos, cos], axis=1), jnp.concatenate([-sin, sin], axis=1)


def per_device(
    wide, narrow,
    layer_input, w_query, w_key, w_value, w_output, w_gate, w_up, w_down,
    attn_gain, mlp_gain, query_gain, key_gain, out_grad,
):
    hd = query_gain.shape[0]
    rows, dim = layer_input.shape
    all_rows = narrow * rows
    chips = wide // 2
    block = all_rows // 2
    qw, kw = w_query.shape[1], w_key.shape[1]
    ff = w_gate.shape[1]
    groups = qw // kw
    kv_heads = kw // hd
    w = lax.axis_index("wide")
    fwd_tab, bwd_tab = tables(w, chips)
    first, second = place(w, chips)
    at = jnp.arange(block, dtype=jnp.int32)
    positions = jnp.concatenate([first * block + at, second * block + at])
    cos_table, sin_table = rotation(positions, hd)

    def gather(shard):
        return lax.all_gather(shard, "wide", axis=0, tiled=True)

    def scatter(grad):
        return lax.psum_scatter(grad, "wide", scatter_dimension=0, tiled=True)

    t = math.gcd(ff, 256)

    def weave(gate, up):
        return jnp.stack([gate.reshape(-1, ff // t, t), up.reshape(-1, ff // t, t)], axis=2).reshape(-1, 2 * ff)

    spread_s = spread_sems(narrow)
    sum_s = [*sum_bufs(narrow, rows, dim), *sum_sems(narrow)]
    row_buf = pltpu.VMEM((rows, dim), BF)
    low_rows, full_rows, all_low = sds((rows, dim), BF), sds((rows, dim), F32), sds((all_rows, dim), BF)
    ring = functools.partial
    qg, kg = query_gain[None], key_gain[None]
    after = lax.optimization_barrier

    in_specs, in_outs = [VM, VM, HB], (VM, HB, HB)
    in_scratch = [row_buf, DMA((2,)), pltpu.SemaphoreType.REGULAR, *spread_s, *line_sems(chips)]
    shard = jnp.concatenate([w_query, w_key, w_value, w_output.T], axis=1)
    own, normed_all, w_attn = comm_call(
        ring(input_kernel, wide, narrow, True), "input_rows", 0,
        (low_rows, all_low, sds((dim, shard.shape[1]), BF)), in_specs, in_outs, in_scratch,
        layer_input, attn_gain[None], shard,
    )
    proj, queries, kv_own = qkv_fwd(
        normed_all, w_attn, cos_table, sin_table, qg, kg, qw, kw, hd**-0.5 * math.log2(math.e)
    )
    grad_own, grad_all, kv = comm_call(
        ring(input_kernel, wide, narrow, False), "grad_rows", 1,
        (low_rows, all_low, sds((wide * all_rows, 2 * kw), BF)), in_specs, in_outs, in_scratch,
        out_grad, attn_gain[None], kv_own,
    )
    gu_shard, kv = after((weave(w_gate, w_up), kv))
    w_gu = gather(gu_shard)
    w_d = gather(after((w_down.T, kv))[0])
    mixed, lses = (), []
    for h in range(kv_heads):
        *mixed, lse = attn_fwd(fwd_tab, queries, kv, h, groups, hd, mixed, block)
        lses.append(lse)
    attended, attended_low = mixed
    w_o = w_attn[:, qw + 2 * kw :]
    middle, normed_mlp = comm_call(
        ring(middle_kernel, wide, narrow), "middle_rows", 2, (full_rows, all_low), [HB, VM, VM], (VM, HB),
        [row_buf, *sum_s, *spread_s], dg(attended_low, w_o, NT).astype(BF), own, mlp_gain[None],
    )
    gate_up, hidden_low = mlp_fwd(normed_mlp, w_gu, t)
    grad_down = dg(grad_all, hidden_low, TN).astype(BF)
    w_d, _ = after((w_d, grad_down))
    gu_low = mlp_bwd(grad_all, w_d, gate_up, t)
    grad_gu = dg(normed_mlp, gu_low, TN).astype(BF)
    mlp_back = mm_nt(gu_low, w_gu, "mlp_back")
    mlp_back, _ = after((mlp_back, grad_gu))
    grad_down, grad_gu = scatter(grad_down), scatter(grad_gu)
    middle_back, mlp_gain_part, middle_all = comm_call(
        ring(middle_back_kernel, wide, narrow), "middle_back", 3, (full_rows, sds((1, dim), F32), all_low),
        [HB, VM, VM, VM], (VM, VM, HB), [row_buf, *sum_s, *spread_s],
        mlp_back, middle, mlp_gain[None], grad_own,
    )
    back, delta = attn_back(middle_all, w_attn, attended, (qw + 2 * kw) // qw)
    grad_output = dg(middle_all, attended_low, TN).astype(BF)
    back, grad_output = after((back, grad_output))
    grad_output, _ = after((grad_output, grad_down))
    grad_output = scatter(grad_output)
    backs = ()
    for h in range(kv_heads):
        backs = attn_bwd(bwd_tab, queries, back, kv, lses[h], delta, h, groups, hd, backs, block)
    query_back, dkv = backs
    hidden_late, dkv, grad_down = after((hidden_low, dkv, grad_down))
    layer_output, kv_sum = comm_call(
        ring(output_kernel, wide, narrow), "output_rows", 4, (low_rows, sds((all_rows, 2 * kw), BF)),
        [HB, VM, HB], (VM, VM),
        [row_buf, DMA((2,)), *sum_s, *line_sum_bufs(chips, all_rows, 2 * kw), *line_sum_sems(chips)],
        dg(hidden_late, w_d, NT).astype(BF), middle, dkv,
    )
    q_low, query_gain_part = q_back(query_back, proj, cos_table, sin_table, qg)
    qkv_low, normed_back, key_gain_part = kv_back(q_low, proj, cos_table, sin_table, kg, w_attn, kv_sum, kw)
    grad_qkv = dg(normed_all, qkv_low, TN).astype(BF)
    normed_back, grad_gu, grad_output = after((normed_back, grad_gu, grad_output))
    gains = jnp.concatenate([jnp.zeros((1, dim), F32), mlp_gain_part, query_gain_part, key_gain_part], axis=1)
    gvec = sds(gains.shape, F32)
    input_grad, gain_sums, grad_qkv = comm_call(
        ring(input_back_kernel, wide, narrow), "input_back", 5, (full_rows, gvec, sds((dim // wide, qw + 2 * kw), F32)),
        [HB, VM, VM, VM, VM, HB], (VM, VM, VM),
        [row_buf, row_buf, pltpu.VMEM((narrow, *gains.shape), F32), pltpu.VMEM((wide, *gains.shape), F32),
         DMA((2,)), DMA((narrow,)), DMA((narrow,)), DMA((wide,)), DMA((wide,)),
         *sum_s, *line_sum_bufs(chips, dim // wide, qw + 2 * kw)[:4], *line_sum_sems(chips)],
        normed_back, own, attn_gain[None], middle_back, gains, grad_qkv,
    )
    g = gain_sums[0]
    grad_gu = grad_gu.reshape(-1, ff // t, 2, t).astype(F32)
    return (
        layer_output, input_grad,
        grad_qkv[:, :qw], grad_qkv[:, qw : qw + kw], grad_qkv[:, qw + kw :],
        grad_output.T.astype(F32), grad_gu[:, :, 0].reshape(-1, ff), grad_gu[:, :, 1].reshape(-1, ff),
        grad_down.T.astype(F32),
        g[:dim], g[dim : 2 * dim], g[2 * dim : 2 * dim + hd], g[2 * dim + hd :],
    )


def solution(mesh):
    rows = P(("wide", "narrow"), None)
    weight, turned = P("wide", "narrow"), P("narrow", "wide")
    return jax.shard_map(
        functools.partial(per_device, mesh.shape["wide"], mesh.shape["narrow"]),
        mesh=mesh,
        in_specs=(rows, weight, weight, weight, turned, weight, weight, turned, P(), P(), P(), P(), rows),
        out_specs=(rows, rows, weight, weight, weight, turned, weight, weight, turned, P(), P(), P(), P()),
        check_vma=False,
    )
```

```python
import functools
import math

import jax
import jax.numpy as jnp
from jax import lax
from jax.experimental import pallas as pl
from jax.experimental.pallas import tpu as pltpu
from jax.sharding import PartitionSpec as P

EPSILON = 1e-06
MASKED = -1e30
F32 = jnp.float32
BF = jnp.bfloat16
MESH = pl.DeviceIdType.MESH
NT = (((1,), (1,)), ((), ()))
NN = (((1,), (0,)), ((), ()))
TN = (((0,), (0,)), ((), ()))


def dg(a, b, dims):
    return lax.dot_general(a, b, dims, preferred_element_type=F32)
DMA = pltpu.SemaphoreType.DMA


class Place:
    def __init__(self, wide, narrow):
        self.W, self.N = wide, narrow
        self.C, self.half = wide // 2, narrow // 2
        self.w, self.n = lax.axis_index("wide"), lax.axis_index("narrow")
        self.k, self.c = self.w // 2, lax.rem(self.w, 2)
        self.far = 2 * (self.C - 1 - self.k) + 1
        late = (self.n >= self.half).astype(jnp.int32)
        self.group = lax.rem(self.c + late, 2)
        self.slot = jnp.where(self.group == 0, self.n, lax.rem(self.n + self.half, self.N))

    def owner(self, j):
        core = 1 if j >= self.half else 0
        n = jnp.where(self.c == 0, j, (j + self.half) % self.N)
        return core, n

    def owner_is_me(self, j):
        core, n = self.owner(j)
        return (self.c == core) & (self.n == n)


def enter(p, line=False, ring=False):
    barrier = pltpu.get_barrier_semaphore()

    def greet(device):
        pl.semaphore_signal(barrier, inc=1, device_id=device, device_id_type=MESH)

    for core in range(2):
        for n in range(p.N):

            @pl.when((p.c != core) | (p.n != n))
            def _():
                greet((2 * p.k + core, n))

    peers = 2 * p.N - 1
    if line or ring:
        for k in range(p.C):

            @pl.when(p.k != k)
            def _():
                greet((2 * k + p.c, p.n))
                if ring:
                    greet((2 * k + 1 - p.c, p.n))

        peers += (2 if ring else 1) * (p.C - 1)
    pl.semaphore_wait(barrier, peers)


def swap_rows(p, src, dst, send_sem, recv_sem):
    return pltpu.make_async_remote_copy(
        src_ref=src, dst_ref=dst, send_sem=send_sem, recv_sem=recv_sem, device_id=(p.far, p.n), device_id_type=MESH
    )


def slot_of(p, n, group):
    return jnp.where(group == 0, n, lax.rem(n + p.half, p.N))


def neighbours(p):
    return p.n + 1 - 2 * lax.rem(p.n, 2), lax.rem(p.n + 2, 4), 3 - p.n


def to(src, dst, send, recv, wide, narrow):
    return pltpu.make_async_remote_copy(
        src_ref=src, dst_ref=dst, send_sem=send, recv_sem=recv, device_id=(wide, narrow), device_id_type=MESH
    )


def spread_sems(narrow):
    return [DMA((narrow, 2)), DMA((narrow, 2)), DMA((2,)), DMA((2,))]


def spread_start(p, src, gathered, rows, send, recv, local, onward):
    half = rows // 2
    view = lambda i: gathered.at[pl.ds(pl.multiple_of(p.slot * rows + i * half, half), half)]
    part = lambda i: src.at[pl.ds(i * half, half)]
    mine = p.group == p.c
    square = p.N == 4
    if square:
        nx, ny, _ = neighbours(p)
        targets = [(nx, (0, 1)), (ny, (1, 0))]
        order = [(t, q, i) for q in range(2) for t, halves in targets for i in (halves[q],)]
        for t, q, i in order:
            at = 0 if t is nx else 1
            to(part(i), view(i), send.at[at, i], recv.at[p.slot, i], 2 * p.k + p.group, t).start()
    else:
        for t in range(p.N):

            @pl.when(p.n != t)
            def _():
                for i in range(2):
                    to(part(i), view(i), send.at[t, i], recv.at[p.slot, i], 2 * p.k + p.group, t).start()

    @pl.when(mine)
    def _():
        for i in range(2):
            pltpu.make_async_copy(part(i), view(i), local.at[i]).start()

    @pl.when(jnp.logical_not(mine))
    def _():
        for i in range(2):
            to(part(i), view(i), local.at[i], recv.at[p.slot, i], 2 * p.k + p.group, p.n).start()


def spread_wait(p, src, gathered, rows, send, recv, local, onward):
    half = rows // 2
    piece = src.at[pl.ds(0, half)]
    mine = p.group == p.c
    at = lambda j, i: gathered.at[pl.ds(pl.multiple_of(j * rows + i * half, half), half)]

    def arrive(j, i):
        pltpu.make_async_copy(piece, at(j, i), recv.at[j, i]).wait()

    if p.N == 4:
        nx, ny, nd = neighbours(p)
        jx, jy, jd = (slot_of(p, n, p.c) for n in (nx, ny, nd))
        arrive(jx, 0)
        to(at(jx, 0), at(jx, 0), onward.at[0], recv.at[jx, 0], p.w, ny).start()
        arrive(jy, 1)
        to(at(jy, 1), at(jy, 1), onward.at[1], recv.at[jy, 1], p.w, nx).start()
        arrive(jx, 1)
        arrive(jy, 0)
        arrive(jd, 0)
        arrive(jd, 1)
        for i in range(2):
            pltpu.make_async_copy(piece, at(0, 0), onward.at[i]).wait()
            for t in range(2):
                pltpu.make_async_copy(piece, at(0, 0), send.at[t, i]).wait()
    else:
        for t in range(p.N):

            @pl.when(p.n != t)
            def _():
                for i in range(2):
                    pltpu.make_async_copy(piece, at(0, 0), send.at[t, i]).wait()
                    arrive(slot_of(p, t, p.c), i)

    for i in range(2):
        pltpu.make_async_copy(piece, at(0, 0), local.at[i]).wait()

    @pl.when(jnp.logical_not(mine))
    def _():
        arrive(slot_of(p, p.n, p.c), 0)
        arrive(slot_of(p, p.n, p.c), 1)


def sum_bufs(narrow, rows, dim):
    if narrow == 4:
        half = pltpu.VMEM((2, 2, rows, dim // 2), BF)
        return [half, half, pltpu.VMEM((2, rows, dim), BF)]
    return [pltpu.VMEM((narrow, rows, dim), BF)]


def sum_sems(narrow):
    if narrow == 4:
        return [DMA((2, 2)), DMA((2, 2)), DMA((2, 2)), DMA((4,)), DMA((4,))]
    return [DMA((narrow,)), DMA((narrow,)), DMA]


def pieces(p, part, rows, dim):
    half = dim // 2
    return lambda j, i: part.at[pl.ds(pl.multiple_of(j * rows, rows), rows), pl.ds(i * half, half)]


def sum_start(p, part, rows, dim, bufs, sems):
    if p.N != 4:
        (got,), (send, recv, local) = bufs, sems
        for j in range(p.N):
            core, n = p.owner(j)
            mine = p.owner_is_me(j)
            src = part.at[pl.ds(j * rows, rows)]

            @pl.when(mine)
            def _():
                pltpu.make_async_copy(src, got.at[p.n], local).start()

            @pl.when(jnp.logical_not(mine))
            def _():
                to(src, got.at[p.n], send.at[j], recv.at[p.n], 2 * p.k + core, n).start()

        return
    own, inbox, _ = bufs
    load, send, recv, _, _ = sems
    piece = pieces(p, part, rows, dim)
    nx, ny, nd = neighbours(p)
    across, here = slot_of(p, nd, p.c), slot_of(p, p.n, p.c)
    for i, n in enumerate((nx, ny)):
        to(piece(across, i), inbox.at[i, 0], send.at[i, 0], recv.at[i, 0], p.w, n).start()
    for i, n in enumerate((ny, nx)):
        pltpu.make_async_copy(piece(slot_of(p, n, p.c), i), own.at[i, 0], load.at[i, 0]).start()
    for i, n in enumerate((nx, ny)):
        to(piece(slot_of(p, n, p.c), i), inbox.at[i, 1], send.at[i, 1], recv.at[i, 1], p.w, n).start()
        pltpu.make_async_copy(piece(here, i), own.at[i, 1], load.at[i, 1]).start()


def core_of(p, j):
    return (j >= p.half).astype(jnp.int32)


def sum_wait(p, part, rows, dim, bufs, sems):
    if p.N != 4:
        (got,), (send, recv, local) = bufs, sems
        for t in range(p.N):
            mine = (p.group == p.c) & (p.n == t)

            @pl.when(mine)
            def _():
                pltpu.make_async_copy(part.at[pl.ds(0, rows)], got.at[t], local).wait()

            @pl.when(jnp.logical_not(mine))
            def _():
                pltpu.make_async_copy(part.at[pl.ds(0, rows)], got.at[t], recv.at[t]).wait()

        for j in range(p.N):

            @pl.when(jnp.logical_not(p.owner_is_me(j)))
            def _():
                pltpu.make_async_copy(part.at[pl.ds(j * rows, rows)], got.at[0], send.at[j]).wait()

        return
    own, inbox, box = bufs
    load, send, recv, send2, recv2 = sems
    piece = pieces(p, part, rows, dim)
    half = dim // 2
    nx, ny, _ = neighbours(p)
    cols = lambda i: pl.ds(i * half, half)

    def add(i, q):
        pltpu.make_async_copy(piece(0, 0), own.at[i, q], load.at[i, q]).wait()
        pltpu.make_async_copy(piece(0, 0), inbox.at[i, q], recv.at[i, q]).wait()

        def body(at):
            own[i, q, at, :] = (own[i, q, at, :].astype(F32) + inbox[i, q, at, :].astype(F32)).astype(BF)

        row_loop(rows, 64, body)

    for i, n in enumerate((ny, nx)):
        add(i, 0)
        j = slot_of(p, n, p.c)
        to(own.at[i, 0], box.at[1, :, cols(i)], send2.at[i], recv2.at[i], 2 * p.k + core_of(p, j), n).start()
    j = slot_of(p, p.n, p.c)
    keep = core_of(p, j) == p.c
    for i in range(2):
        add(i, 1)

        @pl.when(keep)
        def _():
            pltpu.make_async_copy(own.at[i, 1], box.at[0, :, cols(i)], send2.at[2 + i]).start()

        @pl.when(jnp.logical_not(keep))
        def _():
            to(own.at[i, 1], box.at[0, :, cols(i)], send2.at[2 + i], recv2.at[2 + i], 2 * p.k + core_of(p, j), p.n).start()

    for i in range(2):
        for q in range(2):
            pltpu.make_async_copy(piece(0, 0), inbox.at[i, q], send.at[i, q]).wait()
        pltpu.make_async_copy(own.at[i, 0], box.at[1, :, cols(i)], send2.at[i]).wait()
        pltpu.make_async_copy(own.at[i, 0], box.at[1, :, cols(i)], recv2.at[i]).wait()
        pltpu.make_async_copy(own.at[i, 1], box.at[0, :, cols(i)], send2.at[2 + i]).wait()

        @pl.when(p.group != p.c)
        def _():
            pltpu.make_async_copy(own.at[i, 1], box.at[0, :, cols(i)], recv2.at[2 + i]).wait()


def total(p, bufs, at):
    if p.N == 4:
        box = bufs[2]
        return box[0, at, :].astype(F32) + box[1, at, :].astype(F32)
    got = bufs[0]
    out = got[0, at, :].astype(F32)
    for t in range(1, p.N):
        out = out + got[t, at, :].astype(F32)
    return out


def line_sems(chips):
    return [DMA((2, chips)), DMA((chips,)), DMA((chips,)), DMA((chips,)), DMA]


def line_parts(p, full, rows):
    return lambda s, core: full.at[pl.ds(pl.multiple_of((2 * s + core) * rows, rows), rows)]


def line_copy(p, src, dst, send, recv, k, core):
    return pltpu.make_async_remote_copy(
        src_ref=src, dst_ref=dst, send_sem=send, recv_sem=recv, device_id=(2 * k + core, p.n), device_id_type=MESH
    )


def inside(p, k):
    return (k >= 0) & (k < p.C)


def line_start(p, src, full, rows, zsend, zrecv, csend, crecv, local):
    at = line_parts(p, full, rows)
    for i, sign in enumerate((1, -1)):

        @pl.when(inside(p, p.k + sign))
        def _():
            line_copy(p, src, at(p.k, p.c), zsend.at[i, 0], zrecv.at[p.k], p.k + sign, p.c).start()

    pltpu.make_async_copy(src, at(p.k, p.c), local).start()
    line_copy(p, src, at(p.k, p.c), csend.at[p.k], crecv.at[p.k], p.k, 1 - p.c).start()


def line_finish(p, src, full, rows, zsend, zrecv, csend, crecv, local):
    at = line_parts(p, full, rows)
    for d in range(1, p.C):
        for i, sign in enumerate((1, -1)):
            s, t = p.k - sign * d, p.k + sign

            @pl.when(inside(p, s))
            def _():
                pltpu.make_async_copy(src, at(s, p.c), zrecv.at[s]).wait()

                @pl.when(inside(p, t))
                def _():
                    line_copy(p, at(s, p.c), at(s, p.c), zsend.at[i, d], zrecv.at[s], t, p.c).start()

                line_copy(p, at(s, p.c), at(s, p.c), csend.at[s], crecv.at[s], p.k, 1 - p.c).start()

    pltpu.make_async_copy(src, at(p.k, p.c), local).wait()
    for s in range(p.C):
        pltpu.make_async_copy(src, at(s, p.c), csend.at[s]).wait()
        pltpu.make_async_copy(src, at(s, 1 - p.c), crecv.at[s]).wait()
    for i, sign in enumerate((1, -1)):
        for d in range(p.C):

            @pl.when(inside(p, p.k - sign * d) & inside(p, p.k + sign))
            def _():
                pltpu.make_async_copy(src, at(p.k, p.c), zsend.at[i, d]).wait()


def line_sum_bufs(chips, rows, width):
    return [pltpu.VMEM((chips, rows, width), BF)] * 3 + [pltpu.VMEM((2, rows, width), BF), pltpu.VMEM((rows, width), F32)]


def line_sum_sems(chips):
    return [DMA((chips,)), DMA((chips,)), DMA((chips,)), DMA((2, chips)), DMA((chips,)), DMA((2,))]


def line_sum_start(p, part, rows, bufs, sems):
    own, inbox, _, _, _ = bufs
    load, csend, crecv, _, _, _ = sems
    at = line_parts(p, part, rows)

    def share(s):
        line_copy(p, at(s, 1 - p.c), inbox.at[s], csend.at[s], crecv.at[s], p.k, 1 - p.c).start()
        pltpu.make_async_copy(at(s, p.c), own.at[s], load.at[s]).start()

    for d in range(p.C - 1, 0, -1):
        for sign in (1, -1):
            s = p.k + sign * d

            @pl.when(inside(p, s))
            def _():
                share(s)

    share(p.k)


def line_sum_run(p, part, rows, bufs, sems):
    own, inbox, relay, box, acc = bufs
    load, csend, crecv, zsend, rrecv, zrecv = sems
    at = line_parts(p, part, rows)
    step = math.gcd(rows, 128)

    def pair(t):
        pltpu.make_async_copy(at(0, 0), own.at[t], load.at[t]).wait()
        pltpu.make_async_copy(at(0, 0), inbox.at[t], crecv.at[t]).wait()

    for d in range(p.C - 1, 0, -1):
        for i, sign in enumerate((1, -1)):
            t = p.k + sign * d
            behind = inside(p, p.k - sign)

            @pl.when(inside(p, t))
            def _():
                pair(t)

                @pl.when(jnp.logical_not(behind))
                def _():
                    def add(rows_at):
                        both = own[t, rows_at, :].astype(F32) + inbox[t, rows_at, :].astype(F32)
                        own[t, rows_at, :] = both.astype(BF)

                    row_loop(rows, step, add)

                @pl.when(behind)
                def _():
                    pltpu.make_async_copy(at(0, 0), relay.at[t], rrecv.at[t]).wait()

                    def add(rows_at):
                        both = own[t, rows_at, :].astype(F32) + inbox[t, rows_at, :].astype(F32)
                        own[t, rows_at, :] = (both + relay[t, rows_at, :].astype(F32)).astype(BF)

                    row_loop(rows, step, add)

                if d >= 2:
                    line_copy(p, own.at[t], relay.at[t], zsend.at[i, d], rrecv.at[t], p.k + sign, p.c).start()
                else:
                    line_copy(p, own.at[t], box.at[i], zsend.at[i, d], zrecv.at[i], t, p.c).start()

    pair(p.k)

    def first(rows_at):
        acc[rows_at, :] = own[p.k, rows_at, :].astype(F32) + inbox[p.k, rows_at, :].astype(F32)

    row_loop(rows, step, first)
    for i, sign in enumerate((1, -1)):

        @pl.when(inside(p, p.k - sign))
        def _():
            pltpu.make_async_copy(at(0, 0), box.at[i], zrecv.at[i]).wait()

            def more(rows_at):
                acc[rows_at, :] += box[i, rows_at, :].astype(F32)

            row_loop(rows, step, more)

        for d in range(1, p.C):

            @pl.when(inside(p, p.k + sign * d))
            def _():
                pltpu.make_async_copy(at(0, 0), own.at[0], zsend.at[i, d]).wait()

    for s in range(p.C):
        pltpu.make_async_copy(at(0, 0), inbox.at[s], csend.at[s]).wait()


def row_loop(rows, step, body):
    def one(i, carry):
        body(pl.ds(pl.multiple_of(i * step, step), step))
        return carry

    lax.fori_loop(0, rows // step, one, 0)


STEP = 64


def inv_rms(u):
    return lax.rsqrt(jnp.mean(u * u, axis=-1, keepdims=True) + EPSILON)


def swap_out(p, buf, out_ref, sems):
    @pl.when(p.c == 1)
    def _():
        copy = swap_rows(p, buf, out_ref, sems.at[0], sems.at[1])
        copy.start()
        copy.wait()

    @pl.when(p.c == 0)
    def _():
        out_ref[...] = buf[...]


def weave(gate_ref, up_ref, both_ref):
    ff = gate_ref.shape[1]
    t = math.gcd(ff, 256)
    for i in range(0, ff, t):
        both_ref[:, 2 * i : 2 * i + t] = gate_ref[:, i : i + t]
        both_ref[:, 2 * i + t : 2 * i + 2 * t] = up_ref[:, i : i + t]


def unweave_kernel(both_ref, gate_ref, up_ref):
    ff = gate_ref.shape[1]
    t = math.gcd(ff, 256)
    for i in range(0, ff, t):
        gate_ref[:, i : i + t] = both_ref[:, 2 * i : 2 * i + t].astype(F32)
        up_ref[:, i : i + t] = both_ref[:, 2 * i + t : 2 * i + 2 * t].astype(F32)


def input_kernel(wide, narrow, norm, *refs):
    if norm:
        x_ref, gain_ref, shard, gate_ref, up_ref, own_ref, gathered, full, gu_ref, buf, swap, *sems = refs
    else:
        x_ref, shard, own_ref, gathered, full, swap, *sems = refs
    p = Place(wide, narrow)
    rows = x_ref.shape[0]
    spread, line = sems[:4], sems[4:]
    enter(p, line=True)

    @pl.when(p.c == 1)
    def _():
        swap_rows(p, x_ref, own_ref, swap.at[0], swap.at[1]).start()

    line_start(p, shard, full, shard.shape[0], *line)
    if norm:
        weave(gate_ref, up_ref, gu_ref)

    @pl.when(p.c == 1)
    def _():
        swap_rows(p, x_ref, own_ref, swap.at[0], swap.at[1]).wait()

    @pl.when(p.c == 0)
    def _():
        own_ref[...] = x_ref[...]

    if norm:

        def body(at):
            u = own_ref[at, :].astype(F32)
            buf[at, :] = (u * inv_rms(u) * gain_ref[...]).astype(BF)

        row_loop(rows, STEP, body)
    src = buf if norm else own_ref
    spread_start(p, src, gathered, rows, *spread)
    line_finish(p, shard, full, shard.shape[0], *line)
    spread_wait(p, src, gathered, rows, *spread)


def middle_kernel(wide, narrow, part, own_ref, gain_ref, mid_ref, gathered, buf, *refs):
    p = Place(wide, narrow)
    rows, dim = own_ref.shape
    bufs, sems, spread = split_refs(narrow, refs)
    enter(p)
    sum_start(p, part, rows, dim, bufs, sems)
    sum_wait(p, part, rows, dim, bufs, sems)

    def body(at):
        u = own_ref[at, :].astype(F32) + total(p, bufs, at)
        mid_ref[at, :] = u
        buf[at, :] = (u * inv_rms(u) * gain_ref[...]).astype(BF)

    row_loop(rows, STEP, body)
    spread_start(p, buf, gathered, rows, *spread)
    spread_wait(p, buf, gathered, rows, *spread)


def split_refs(narrow, refs):
    bufs, sems = (3, 5) if narrow == 4 else (1, 3)
    return refs[:bufs], refs[bufs : bufs + sems], refs[bufs + sems :]


def output_kernel(wide, narrow, part, mid_ref, dkv, out_ref, kv_ref, buf, swap, *refs):
    p = Place(wide, narrow)
    rows, dim = mid_ref.shape
    kv_rows = kv_ref.shape[0]
    bufs, sems, line = split_refs(narrow, refs)
    line_bufs, line_sem = line[:5], line[5:]
    enter(p, line=True)
    line_sum_start(p, dkv, kv_rows, line_bufs, line_sem)
    sum_start(p, part, rows, dim, bufs, sems)
    line_sum_run(p, dkv, kv_rows, line_bufs, line_sem)
    row_loop(kv_rows, 128, lambda at: kv_ref.__setitem__((at, slice(None)), line_bufs[4][at, :].astype(BF)))
    sum_wait(p, part, rows, dim, bufs, sems)

    def body(at):
        buf[at, :] = (mid_ref[at, :] + total(p, bufs, at)).astype(BF)

    row_loop(rows, STEP, body)
    swap_out(p, buf, out_ref, swap)


def norm_back(u, gain, cot):
    r = inv_rms(u)
    a = cot * gain
    du = r * a - u * (r * r * r) * jnp.mean(a * u, axis=-1, keepdims=True)
    return du, jnp.sum(cot * u * r, axis=0, keepdims=True)


def middle_back_kernel(wide, narrow, part, mid_ref, gain_ref, grad_ref, back_ref, dgain_ref, gathered, buf, *refs):
    p = Place(wide, narrow)
    rows, dim = mid_ref.shape
    bufs, sems, spread = split_refs(narrow, refs)
    enter(p)
    sum_start(p, part, rows, dim, bufs, sems)
    dgain_ref[...] = jnp.zeros_like(dgain_ref)
    sum_wait(p, part, rows, dim, bufs, sems)

    def body(at):
        du, dgain = norm_back(mid_ref[at, :], gain_ref[...], total(p, bufs, at))
        back = grad_ref[at, :].astype(F32) + du
        back_ref[at, :] = back
        buf[at, :] = back.astype(BF)
        dgain_ref[...] += dgain

    row_loop(rows, STEP, body)
    spread_start(p, buf, gathered, rows, *spread)
    spread_wait(p, buf, gathered, rows, *spread)


def input_back_kernel(
    wide, narrow, part, own_ref, gain_ref, back_ref, gains_ref, wgrad, out_ref, gsum_ref, wsum_ref,
    buf, far_buf, gbuf, gbuf2, swap, gsend, grecv, gsend2, grecv2, *refs,
):
    p = Place(wide, narrow)
    rows, dim = own_ref.shape
    w_rows = wsum_ref.shape[0]
    bufs, sems, line = split_refs(narrow, refs)
    line_bufs, line_sem = (*line[:4], wsum_ref), line[4:]
    enter(p, ring=True)
    line_sum_start(p, wgrad, w_rows, line_bufs, line_sem)
    sum_start(p, part, rows, dim, bufs, sems)
    gsum_ref[...] = gains_ref[...]
    sum_wait(p, part, rows, dim, bufs, sems)

    def body(at):
        du, dgain = norm_back(own_ref[at, :].astype(F32), gain_ref[...], total(p, bufs, at))
        grad = back_ref[at, :] + du
        out_ref[at, :] = grad
        buf[at, :] = grad.astype(BF)
        gsum_ref[:, :dim] += dgain

    row_loop(rows, STEP, body)

    @pl.when(p.c == 1)
    def _():
        swap_rows(p, buf, far_buf, swap.at[0], swap.at[1]).start()

    def share(me, count, here, slots, sends, recvs, device):
        slots[me] = here[...]
        for t in range(count):

            @pl.when(me != t)
            def _():
                wide_at, narrow_at = device(t)
                to(here, slots.at[me], sends.at[t], recvs.at[me], wide_at, narrow_at).start()

        for t in range(count):

            @pl.when(me != t)
            def _():
                pltpu.make_async_copy(here, slots.at[t], sends.at[t]).wait()
                pltpu.make_async_copy(here, slots.at[t], recvs.at[t]).wait()

        out = slots[0]
        for t in range(1, count):
            out = out + slots[t]
        here[...] = out

    share(p.n, narrow, gsum_ref, gbuf, gsend, grecv, lambda t: (p.w, t))
    line_sum_run(p, wgrad, w_rows, line_bufs, line_sem)
    share(p.w, wide, gsum_ref, gbuf2, gsend2, grecv2, lambda t: (t, p.n))

    @pl.when(p.c == 1)
    def _():
        swap_rows(p, buf, far_buf, swap.at[0], swap.at[1]).wait()
        row_loop(rows, STEP, lambda at: out_ref.__setitem__((at, slice(None)), far_buf[at, :].astype(F32)))


VM = pl.BlockSpec(memory_space=pltpu.VMEM)
HB = pl.BlockSpec(memory_space=pl.ANY)


def comm_call(kernel, name, cid, out_shape, in_specs, out_specs, scratch, *args):
    return pl.pallas_call(
        kernel,
        out_shape=out_shape,
        in_specs=in_specs,
        out_specs=out_specs,
        scratch_shapes=scratch,
        compiler_params=pltpu.CompilerParams(collective_id=cid, has_side_effects=True, vmem_limit_bytes=52 << 20),
        cost_estimate=pl.CostEstimate(flops=0, bytes_accessed=160_000_000, transcendentals=0),
        name=name,
    )(*args)


def sds(shape, kind):
    return jax.ShapeDtypeStruct(shape, kind)


def plain(kernel, name, grid, in_specs, out_specs, out_shape, flops, nbytes, *args, scratch=(), aliases=None):
    return pl.pallas_call(
        kernel,
        out_shape=out_shape,
        grid=grid,
        in_specs=in_specs,
        out_specs=out_specs,
        scratch_shapes=scratch,
        input_output_aliases=aliases or {},
        compiler_params=pltpu.CompilerParams(vmem_limit_bytes=52 << 20),
        cost_estimate=pl.CostEstimate(flops=flops, bytes_accessed=nbytes, transcendentals=0),
        name=name,
    )(*args)


def whole(shape):
    return pl.BlockSpec(shape, lambda *i: (0,) * len(shape), pipeline_mode=pl.Buffered(1))


def by_rows(tm, width):
    return pl.BlockSpec((tm, width), lambda i: (i, 0))


def mlp_fwd_kernel(x_ref, w_ref, gu_ref, h_ref):
    t = h_ref.shape[1]
    y = dg(x_ref[...], w_ref[...], NN)
    gate, up = y[:, :t], y[:, t:]
    gu_ref[...] = y
    h_ref[...] = (gate * jax.nn.sigmoid(gate) * up).astype(BF)


def mlp_fwd(x, w, t):
    rows, dim = x.shape
    ff2 = w.shape[1]
    return plain(
        mlp_fwd_kernel, "mlp_fwd", (ff2 // (2 * t),),
        [whole((rows, dim)), pl.BlockSpec((dim, 2 * t), lambda i: (0, i))],
        [pl.BlockSpec((rows, 2 * t), lambda i: (0, i)), pl.BlockSpec((rows, t), lambda i: (0, i))],
        (sds((rows, ff2), F32), sds((rows, ff2 // 2), BF)),
        2 * rows * dim * ff2, rows * dim * 2 + dim * ff2 * 2 + rows * ff2 * 5, x, w,
    )


def mlp_bwd_kernel(g_ref, w_ref, gu_ref, out_ref):
    t = w_ref.shape[1]
    hb = dg(g_ref[...], w_ref[...], NN)
    gate, up = gu_ref[:, :t], gu_ref[:, t:]
    s = jax.nn.sigmoid(gate)
    gs = hb * s
    out_ref[:, :t] = (gs * up * (1.0 + gate * (1.0 - s))).astype(BF)
    out_ref[:, t:] = (gs * gate).astype(BF)


def mlp_bwd(g, w, gu, t):
    rows, dim = g.shape
    ff = w.shape[1]
    return plain(
        mlp_bwd_kernel, "mlp_bwd", (ff // t,),
        [whole((rows, dim)), pl.BlockSpec((dim, t), lambda i: (0, i)), pl.BlockSpec((rows, 2 * t), lambda i: (0, i))],
        pl.BlockSpec((rows, 2 * t), lambda i: (0, i)), sds((rows, 2 * ff), BF),
        2 * rows * dim * ff, rows * dim * 2 + dim * ff * 2 + rows * ff * 12, g, w, gu,
    )


def nt_kernel(a_ref, b_ref, o_ref):
    o_ref[...] = dg(a_ref[...], b_ref[...], NT).astype(BF)


def mm_nt(a, b, name, tn=256):
    rows, depth = a.shape
    cols = b.shape[0]
    return plain(
        nt_kernel, name, (cols // tn,), [whole((rows, depth)), by_rows(tn, depth)],
        pl.BlockSpec((rows, tn), lambda i: (0, i)), sds((rows, cols), BF),
        2 * rows * cols * depth, 2 * (rows * depth + cols * depth + rows * cols), a, b,
    )


def turn(u):
    return pltpu.roll(u, u.shape[-1] // 2, 1)


def qkv_kernel(qw, kw, hd, fold, x_ref, w_ref, cos_ref, sin_ref, qg_ref, kg_ref, proj_ref, q_ref, kv_ref):
    y = dg(x_ref[...], w_ref[...], NN)
    cos, sin = cos_ref[...], sin_ref[...]
    proj_ref[...] = y[:, : qw + kw]

    def head(lo, gain):
        u = y[:, lo : lo + hd]
        v = u * inv_rms(u) * gain
        return v * cos + turn(v) * sin

    for h in range(qw // hd):
        q_ref[:, h * hd : (h + 1) * hd] = (head(h * hd, qg_ref[...]) * fold).astype(BF)
    for h in range(kw // hd):
        kv_ref[:, 2 * h * hd : (2 * h + 1) * hd] = head(qw + h * hd, kg_ref[...]).astype(BF)
        kv_ref[:, (2 * h + 1) * hd : (2 * h + 2) * hd] = y[:, qw + kw + h * hd : qw + kw + (h + 1) * hd].astype(BF)


def qkv_fwd(x, w, cos, sin, qg, kg, qw, kw, fold):
    rows, dim = x.shape
    hd = cos.shape[1]
    width = qw + 2 * kw
    tm = 256
    return plain(
        functools.partial(qkv_kernel, qw, kw, hd, fold), "qkv_fwd", (rows // tm,),
        [by_rows(tm, dim), whole((dim, width)), by_rows(tm, hd), by_rows(tm, hd), whole((1, hd)), whole((1, hd))],
        [by_rows(tm, qw + kw), by_rows(tm, qw), by_rows(tm, 2 * kw)],
        [sds((rows, qw + kw), F32), sds((rows, qw), BF), sds((rows, 2 * kw), BF)],
        2 * rows * dim * width, 2 * (rows * dim + dim * width) + rows * width * 6, x, w, cos, sin, qg, kg,
    )


def head_back(cot, u, gain, cos, sin):
    cot = cot * cos - turn(cot) * sin
    return norm_back(u, gain, cot)


def q_back_kernel(hd, dq_ref, u_ref, cos_ref, sin_ref, g_ref, low_ref, dgain_ref):
    @pl.when(pl.program_id(0) == 0)
    def _():
        dgain_ref[...] = jnp.zeros_like(dgain_ref)

    for h in range(dq_ref.shape[1] // hd):
        at = slice(h * hd, (h + 1) * hd)
        du, dgain = head_back(dq_ref[:, at], u_ref[:, at], g_ref[...], cos_ref[...], sin_ref[...])
        low_ref[:, at] = du.astype(BF)
        dgain_ref[...] += dgain


def q_back(dq, proj, cos, sin, gain):
    rows, qw = dq.shape
    hd = cos.shape[1]
    tm = 256
    return plain(
        functools.partial(q_back_kernel, hd), "q_back", (rows // tm,),
        [by_rows(tm, qw), by_rows(tm, qw), by_rows(tm, hd), by_rows(tm, hd), whole((1, hd))],
        [by_rows(tm, qw), pl.BlockSpec((1, hd), lambda i: (0, 0))], [sds((rows, qw), BF), sds((1, hd), F32)],
        rows * qw * 20, rows * qw * 10, dq, proj, cos, sin, gain,
    )


def kv_back_kernel(qw, kw, hd, q_ref, u_ref, cos_ref, sin_ref, g_ref, w_ref, *refs):
    s_ref, low_ref, back_ref, dgain_ref = refs

    @pl.when(pl.program_id(0) == 0)
    def _():
        dgain_ref[...] = jnp.zeros_like(dgain_ref)

    low_ref[:, :qw] = q_ref[...]
    for h in range(kw // hd):
        key = slice(2 * h * hd, (2 * h + 1) * hd)
        value = slice((2 * h + 1) * hd, (2 * h + 2) * hd)
        at = slice(qw + h * hd, qw + (h + 1) * hd)
        du, dgain = head_back(s_ref[:, key].astype(F32), u_ref[:, at], g_ref[...], cos_ref[...], sin_ref[...])
        low_ref[:, at] = du.astype(BF)
        low_ref[:, qw + kw + h * hd : qw + kw + (h + 1) * hd] = s_ref[:, value]
        dgain_ref[...] += dgain
    back_ref[...] = dg(low_ref[...], w_ref[...], NT).astype(BF)


def kv_back(q_low, proj, cos, sin, gain, w, sums, kw):
    rows, qw = q_low.shape
    hd = cos.shape[1]
    dim = w.shape[0]
    width = qw + 2 * kw
    tm = 256
    return plain(
        functools.partial(kv_back_kernel, qw, kw, hd), "kv_back", (rows // tm,),
        [by_rows(tm, qw), by_rows(tm, qw + kw), by_rows(tm, hd), by_rows(tm, hd), whole((1, hd)), whole((dim, width))]
        + [by_rows(tm, 2 * kw)],
        [by_rows(tm, width), by_rows(tm, dim), pl.BlockSpec((1, hd), lambda i: (0, 0))],
        [sds((rows, width), BF), sds((rows, dim), BF), sds((1, hd), F32)],
        2 * rows * dim * width, 2 * (rows * dim + dim * width) + rows * width * 6,
        q_low, proj, cos, sin, gain, w, sums,
    )


def attn_back_kernel(hd, x_ref, w_ref, o_ref, back_ref, delta_ref):
    back = dg(x_ref[...], w_ref[...], NN).astype(BF)
    back_ref[...] = back
    rows, width = back.shape
    lane = lax.broadcasted_iota(jnp.int32, (rows, hd), 1)
    out = jnp.zeros((rows, hd), F32)
    for h in range(width // hd):
        at = slice(h * hd, (h + 1) * hd)
        out = jnp.where(lane == h, jnp.sum(back[:, at].astype(F32) * o_ref[:, at], axis=1, keepdims=True), out)
    delta_ref[...] = jnp.transpose(out)[: delta_ref.shape[0]]


def attn_back(x, w, o, at):
    rows, dim = x.shape
    width = o.shape[1]
    tm = 256
    return plain(
        functools.partial(attn_back_kernel, 128), "attn_back", (rows // tm,),
        [by_rows(tm, dim), pl.BlockSpec((dim, width), lambda i: (0, at), pipeline_mode=pl.Buffered(1)), by_rows(tm, width)],
        [by_rows(tm, width), pl.BlockSpec((8, tm), lambda i: (0, i))], [sds((rows, width), BF), sds((8, rows), F32)],
        2 * rows * dim * width, 2 * (rows * dim + dim * width) + rows * width * 6, x, w, o,
    )


def attn_grads_kernel(x_ref, low_ref, m_ref, a_ref, out_ref):
    width = low_ref.shape[1]
    out_ref[:, :width] = dg(x_ref[...], low_ref[...], TN).astype(BF)
    out_ref[:, width:] = dg(m_ref[...], a_ref[...], TN).astype(BF)


def attn_grads(x, low, m, a):
    rows, dim = x.shape
    width, qw = low.shape[1], a.shape[1]
    tm = 256
    cols = pl.BlockSpec((rows, tm), lambda i: (0, i))
    return plain(
        attn_grads_kernel, "attn_grads", (dim // tm,), [cols, whole((rows, width)), cols, whole((rows, qw))],
        by_rows(tm, width + qw), sds((dim, width + qw), BF),
        2 * rows * dim * (width + qw), 2 * rows * (2 * dim + width + qw) + 2 * dim * (width + qw), x, low, m, a,
    )


def fwd_kernel(groups, hd, tab, q_ref, kv_ref, *refs):
    o_ref, low_ref, lse_ref, acc, lsum = refs[-5:]
    s = pl.program_id(0)
    block = q_ref.shape[0]
    diag, first, last = tab[2, s], tab[3, s], tab[4, s]

    @pl.when(first == 1)
    def _():
        acc[...] = jnp.zeros_like(acc)
        lsum[...] = jnp.zeros_like(lsum)

    def work(masked):
        k, v = kv_ref[:, :hd], kv_ref[:, hd:]
        for g in range(groups):
            at = slice(g * hd, (g + 1) * hd)
            scores = dg(q_ref[:, at], k, NT)
            if masked:
                row = lax.broadcasted_iota(jnp.int32, scores.shape, 0)
                col = lax.broadcasted_iota(jnp.int32, scores.shape, 1)
                scores = jnp.where(col <= row, scores, MASKED)
            probs = jnp.exp2(scores)
            part = probs[:, :128]
            for j in range(1, block // 128):
                part = part + probs[:, j * 128 : (j + 1) * 128]
            lsum[g] += part
            acc[:, at] += dg(probs.astype(BF), v, NN)

    @pl.when(diag == 0)
    def _():
        work(False)

    @pl.when(diag == 1)
    def _():
        work(True)

    @pl.when(last == 1)
    def _():
        lane = lax.broadcasted_iota(jnp.int32, (block, 128), 1)
        lse = jnp.zeros((block, 128), F32)
        for g in range(groups):
            at = slice(g * hd, (g + 1) * hd)
            l = jnp.sum(lsum[g], axis=1, keepdims=True)
            out = acc[:, at] / l
            o_ref[:, at] = out
            low_ref[:, at] = out.astype(BF)
            lse = jnp.where(lane == g, jnp.log2(l), lse)
        lse_ref[...] = jnp.transpose(lse)[: lse_ref.shape[0]]


def attn_fwd(tab, q, kv, head, groups, hd, before, block):
    rows, width = q.shape
    gw = groups * hd
    steps = tab.shape[1]
    mine = pl.BlockSpec((block, gw), lambda s, t: (t[0, s], head))
    return pl.pallas_call(
        functools.partial(fwd_kernel, groups, hd),
        out_shape=(sds((rows, width), F32), sds((rows, width), BF), sds((8, rows), F32)),
        grid_spec=pltpu.PrefetchScalarGridSpec(
            num_scalar_prefetch=1,
            grid=(steps,),
            in_specs=[mine, pl.BlockSpec((block, 2 * hd), lambda s, t: (t[1, s], head))] + [HB] * len(before),
            out_specs=[mine, mine, pl.BlockSpec((8, block), lambda s, t: (0, t[0, s]))],
            scratch_shapes=[pltpu.VMEM((block, gw), F32), pltpu.VMEM((groups, block, 128), F32)],
        ),
        input_output_aliases={3: 0, 4: 1} if before else {},
        compiler_params=pltpu.CompilerParams(vmem_limit_bytes=48 << 20),
        cost_estimate=pl.CostEstimate(
            flops=steps * block * block * gw * 4,
            bytes_accessed=steps * block * hd * 8,
            transcendentals=steps * block * block * groups,
        ),
        name="attn_fwd",
    )(tab, q, kv, *before)


def bwd_kernel(groups, hd, first_head, tab, q_ref, do_ref, kv_ref, lse_ref, delta_ref, *refs):
    dq_ref, dkv_ref, dq_sum, dkv_sum = refs[-4:]
    s = pl.program_id(0)
    block = q_ref.shape[0]
    qi, diag, first, last = tab[0, s], tab[2, s], tab[3, s], tab[4, s]

    @pl.when(s == 0)
    def _():
        dq_sum[...] = jnp.zeros_like(dq_sum)

    @pl.when(first == 1)
    def _():
        dkv_sum[...] = jnp.zeros_like(dkv_sum)

    def work(masked):
        k, v = kv_ref[:, :hd], kv_ref[:, hd:]
        for g in range(groups):
            at = slice(g * hd, (g + 1) * hd)
            q, do = q_ref[:, at], do_ref[:, at]
            scores = dg(k, q, NT) - lse_ref[g : g + 1, :]
            if masked:
                row = lax.broadcasted_iota(jnp.int32, scores.shape, 0)
                col = lax.broadcasted_iota(jnp.int32, scores.shape, 1)
                scores = jnp.where(row <= col, scores, MASKED)
            probs = jnp.exp2(scores)
            dots = dg(v, do, NT)
            dkv_sum[:, hd:] += dg(probs.astype(BF), do, NN)
            h = first_head + g
            back = (probs * (dots - delta_ref[h : h + 1, :])).astype(BF)
            dkv_sum[:, :hd] += dg(back, q, NN)
            dq_sum[qi, :, at] += dg(back, k, TN)

    @pl.when(diag == 0)
    def _():
        work(False)

    @pl.when(diag == 1)
    def _():
        work(True)

    @pl.when(last == 1)
    def _():
        dkv_ref[:, :hd] = (dkv_sum[:, :hd] * math.log(2.0)).astype(BF)
        dkv_ref[:, hd:] = dkv_sum[:, hd:].astype(BF)

    @pl.when(s == pl.num_programs(0) - 1)
    def _():
        for i in range(dq_sum.shape[0]):
            dq_ref[i * block : (i + 1) * block, :] = dq_sum[i] * hd**-0.5


def attn_bwd(tab, q, do, kv, lse, delta, head, groups, hd, before, block):
    rows, width = q.shape
    gw = groups * hd
    steps = tab.shape[1]
    before = before or [jnp.zeros(kv.shape, BF)]
    mine = pl.BlockSpec((block, gw), lambda s, t: (t[0, s], head))
    keys = pl.BlockSpec((block, 2 * hd), lambda s, t: (t[1, s], head))
    stat = pl.BlockSpec((8, block), lambda s, t: (0, t[0, s]))
    return pl.pallas_call(
        functools.partial(bwd_kernel, groups, hd, head * groups),
        out_shape=(sds((rows, width), F32), sds(kv.shape, BF)),
        grid_spec=pltpu.PrefetchScalarGridSpec(
            num_scalar_prefetch=1,
            grid=(steps,),
            in_specs=[mine, mine, keys, stat, stat] + [HB] * len(before),
            out_specs=[pl.BlockSpec((rows, gw), lambda s, t: (0, head)), keys],
            scratch_shapes=[pltpu.VMEM((rows // block, block, gw), F32), pltpu.VMEM((block, 2 * hd), F32)],
        ),
        input_output_aliases={6: 0, 7: 1} if len(before) == 2 else {6: 1},
        compiler_params=pltpu.CompilerParams(vmem_limit_bytes=48 << 20),
        cost_estimate=pl.CostEstimate(
            flops=steps * block * block * gw * 10,
            bytes_accessed=steps * block * hd * 16,
            transcendentals=steps * block * block * groups,
        ),
        name="attn_bwd",
    )(tab, q, do, kv, lse, delta, *before)


def place(w, chips):
    k, core = w // 2, w % 2
    return 4 * k + core, 4 * chips - 1 - 4 * k - core


def block_row(b, chips):
    m = b % 4
    early = m < 2
    k = jnp.where(early, b // 4, (4 * chips - 1 - b) // 4)
    core = jnp.where((m == 1) | (m == 2), 1, 0)
    return 2 * (2 * k + core) + jnp.where(early, 0, 1)


def tables(w, chips):
    a, b = place(w, chips)
    count = 4 * chips + 1
    s = jnp.arange(count, dtype=jnp.int32)
    in_a = s <= a
    key = jnp.where(in_a, s, s - a - 1)
    diag = jnp.where(in_a, s == a, s == count - 1)
    fwd = [jnp.where(in_a, 0, 1), block_row(key, chips), diag, key == 0, diag]
    less, low = jnp.minimum(a, b), jnp.where(a < b, 0, 1)
    both = s < 2 * (less + 1)
    even = s % 2 == 0
    key = jnp.where(both, s // 2, s - (less + 1))
    query = jnp.where(both & even, low, 1 - low)
    diag = key == jnp.where(query == 0, a, b)
    bwd = [query, block_row(key, chips), diag, ~both | even, ~both | ~even]
    return tuple(jnp.stack([row.astype(jnp.int32) for row in rows]) for rows in (fwd, bwd))


def rotation(positions, head_dim):
    steps_half = jnp.arange(head_dim // 2).astype(F32)
    inverse = jnp.exp(steps_half * (-2.0 * math.log(1000000.0) / head_dim))
    angles = positions.astype(F32)[:, None] * inverse[None, :]
    cos, sin = jnp.cos(angles), jnp.sin(angles)
    return jnp.concatenate([cos, cos], axis=1), jnp.concatenate([-sin, sin], axis=1)


def per_device(
    wide, narrow,
    layer_input, w_query, w_key, w_value, w_output, w_gate, w_up, w_down,
    attn_gain, mlp_gain, query_gain, key_gain, out_grad,
):
    hd = query_gain.shape[0]
    rows, dim = layer_input.shape
    all_rows = narrow * rows
    chips = wide // 2
    block = all_rows // 2
    qw, kw = w_query.shape[1], w_key.shape[1]
    ff = w_gate.shape[1]
    groups = qw // kw
    kv_heads = kw // hd
    w = lax.axis_index("wide")
    fwd_tab, bwd_tab = tables(w, chips)
    first, second = place(w, chips)
    at = jnp.arange(block, dtype=jnp.int32)
    positions = jnp.concatenate([first * block + at, second * block + at])
    cos_table, sin_table = rotation(positions, hd)

    def gather(shard):
        return lax.all_gather(shard, "wide", axis=0, tiled=True)

    def scatter(grad):
        return lax.psum_scatter(grad, "wide", scatter_dimension=0, tiled=True)

    t = math.gcd(ff, 256)

    spread_s = spread_sems(narrow)
    sum_s = [*sum_bufs(narrow, rows, dim), *sum_sems(narrow)]
    row_buf = pltpu.VMEM((rows, dim), BF)
    low_rows, full_rows, all_low = sds((rows, dim), BF), sds((rows, dim), F32), sds((all_rows, dim), BF)
    ring = functools.partial
    qg, kg = query_gain[None], key_gain[None]
    after = lax.optimization_barrier

    in_scratch = [DMA((2,)), *spread_s, *line_sems(chips)]
    shard = jnp.concatenate([w_query, w_key, w_value, w_output.T], axis=1)
    own, normed_all, w_attn, gu_shard = comm_call(
        ring(input_kernel, wide, narrow, True), "input_rows", 0,
        (low_rows, all_low, sds((dim, shard.shape[1]), BF), sds((w_gate.shape[0], 2 * ff), BF)),
        [VM, VM, HB, VM, VM], (VM, HB, HB, VM), [row_buf, *in_scratch],
        layer_input, attn_gain[None], shard, w_gate, w_up,
    )
    proj, queries, kv_own = qkv_fwd(
        normed_all, w_attn, cos_table, sin_table, qg, kg, qw, kw, hd**-0.5 * math.log2(math.e)
    )
    grad_own, grad_all, kv = comm_call(
        ring(input_kernel, wide, narrow, False), "grad_rows", 1,
        (low_rows, all_low, sds((wide * all_rows, 2 * kw), BF)), [VM, HB], (VM, HB, HB), in_scratch,
        out_grad, kv_own,
    )
    gu_shard, w_down, kv = after((gu_shard, w_down, kv))
    w_gu, w_d = gather(gu_shard), gather(w_down.T)
    mixed, lses = (), []
    for h in range(kv_heads):
        *mixed, lse = attn_fwd(fwd_tab, queries, kv, h, groups, hd, mixed, block)
        lses.append(lse)
    attended, attended_low = mixed
    w_o = w_attn[:, qw + 2 * kw :]
    middle, normed_mlp = comm_call(
        ring(middle_kernel, wide, narrow), "middle_rows", 2, (full_rows, all_low), [HB, VM, VM], (VM, HB),
        [row_buf, *sum_s, *spread_s], dg(attended_low, w_o, NT).astype(BF), own, mlp_gain[None],
    )
    gate_up, hidden_low = mlp_fwd(normed_mlp, w_gu, t)
    grad_down = dg(grad_all, hidden_low, TN).astype(BF)
    w_d, _ = after((w_d, grad_down))
    gu_low = mlp_bwd(grad_all, w_d, gate_up, t)
    grad_gu = dg(normed_mlp, gu_low, TN).astype(BF)
    mlp_back = mm_nt(gu_low, w_gu, "mlp_back")
    mlp_back, _ = after((mlp_back, grad_gu))
    grad_down, grad_gu = scatter(grad_down), scatter(grad_gu)
    middle_back, mlp_gain_part, middle_all = comm_call(
        ring(middle_back_kernel, wide, narrow), "middle_back", 3, (full_rows, sds((1, dim), F32), all_low),
        [HB, VM, VM, VM], (VM, VM, HB), [row_buf, *sum_s, *spread_s],
        mlp_back, middle, mlp_gain[None], grad_own,
    )
    back, delta = attn_back(middle_all, w_attn, attended, (qw + 2 * kw) // qw)
    backs = ()
    for h in range(kv_heads):
        backs = attn_bwd(bwd_tab, queries, back, kv, lses[h], delta, h, groups, hd, backs, block)
    query_back, dkv = backs
    hidden_late, dkv, grad_down = after((hidden_low, dkv, grad_down))
    layer_output, kv_sum = comm_call(
        ring(output_kernel, wide, narrow), "output_rows", 4, (low_rows, sds((all_rows, 2 * kw), BF)),
        [HB, VM, HB], (VM, VM),
        [row_buf, DMA((2,)), *sum_s, *line_sum_bufs(chips, all_rows, 2 * kw), *line_sum_sems(chips)],
        dg(hidden_late, w_d, NT).astype(BF), middle, dkv,
    )
    q_low, query_gain_part = q_back(query_back, proj, cos_table, sin_table, qg)
    qkv_low, normed_back, key_gain_part = kv_back(q_low, proj, cos_table, sin_table, kg, w_attn, kv_sum, kw)
    grad_attn = attn_grads(normed_all, qkv_low, middle_all, attended_low)
    normed_back, grad_gu = after((normed_back, grad_gu))
    half = sds((dim // wide, ff), F32)
    grad_gate, grad_up = plain(
        unweave_kernel, "unweave", (1,), [whole(grad_gu.shape)], [whole(half.shape)] * 2, [half, half], 0, grad_gu.size * 6, grad_gu
    )
    gains = jnp.concatenate([jnp.zeros((1, dim), F32), mlp_gain_part, query_gain_part, key_gain_part], axis=1)
    gvec = sds(gains.shape, F32)
    input_grad, gain_sums, grad_qkv = comm_call(
        ring(input_back_kernel, wide, narrow), "input_back", 5, (full_rows, gvec, sds((dim // wide, 2 * qw + 2 * kw), F32)),
        [HB, VM, VM, VM, VM, HB], (VM, VM, VM),
        [row_buf, row_buf, pltpu.VMEM((narrow, *gains.shape), F32), pltpu.VMEM((wide, *gains.shape), F32),
         DMA((2,)), DMA((narrow,)), DMA((narrow,)), DMA((wide,)), DMA((wide,)),
         *sum_s, *line_sum_bufs(chips, dim // wide, 2 * qw + 2 * kw)[:4], *line_sum_sems(chips)],
        normed_back, own, attn_gain[None], middle_back, gains, grad_attn,
    )
    g = gain_sums[0]
    return (
        layer_output, input_grad,
        grad_qkv[:, :qw], grad_qkv[:, qw : qw + kw], grad_qkv[:, qw + kw : qw + 2 * kw],
        grad_qkv[:, qw + 2 * kw :].T, grad_gate, grad_up,
        grad_down.T.astype(F32),
        g[:dim], g[dim : 2 * dim], g[2 * dim : 2 * dim + hd], g[2 * dim + hd :],
    )


def solution(mesh):
    rows = P(("wide", "narrow"), None)
    weight, turned = P("wide", "narrow"), P("narrow", "wide")
    return jax.shard_map(
        functools.partial(per_device, mesh.shape["wide"], mesh.shape["narrow"]),
        mesh=mesh,
        in_specs=(rows, weight, weight, weight, turned, weight, weight, turned, P(), P(), P(), P(), rows),
        out_specs=(rows, rows, weight, weight, weight, turned, weight, weight, turned, P(), P(), P(), P()),
        check_vma=False,
    )
```

```python
import functools
import math

import jax
import jax.numpy as jnp
from jax import lax
from jax.experimental import pallas as pl
from jax.experimental.pallas import tpu as pltpu
from jax.sharding import PartitionSpec as P

EPSILON = 1e-06
MASKED = -1e30
F32 = jnp.float32
BF = jnp.bfloat16
MESH = pl.DeviceIdType.MESH
NT = (((1,), (1,)), ((), ()))
NN = (((1,), (0,)), ((), ()))
TN = (((0,), (0,)), ((), ()))


def dg(a, b, dims):
    return lax.dot_general(a, b, dims, preferred_element_type=F32)
DMA = pltpu.SemaphoreType.DMA


class Place:
    def __init__(self, wide, narrow):
        self.W, self.N = wide, narrow
        self.C, self.half = wide // 2, narrow // 2
        self.w, self.n = lax.axis_index("wide"), lax.axis_index("narrow")
        self.k, self.c = self.w // 2, lax.rem(self.w, 2)
        self.far = 2 * (self.C - 1 - self.k) + 1
        late = (self.n >= self.half).astype(jnp.int32)
        self.group = lax.rem(self.c + late, 2)
        self.slot = jnp.where(self.group == 0, self.n, lax.rem(self.n + self.half, self.N))

    def owner(self, j):
        core = 1 if j >= self.half else 0
        n = jnp.where(self.c == 0, j, (j + self.half) % self.N)
        return core, n

    def owner_is_me(self, j):
        core, n = self.owner(j)
        return (self.c == core) & (self.n == n)


def enter(p, line=False, ring=False):
    barrier = pltpu.get_barrier_semaphore()

    def greet(device):
        pl.semaphore_signal(barrier, inc=1, device_id=device, device_id_type=MESH)

    for core in range(2):
        for n in range(p.N):

            @pl.when((p.c != core) | (p.n != n))
            def _():
                greet((2 * p.k + core, n))

    peers = 2 * p.N - 1
    if line or ring:
        for k in range(p.C):

            @pl.when(p.k != k)
            def _():
                greet((2 * k + p.c, p.n))
                if ring:
                    greet((2 * k + 1 - p.c, p.n))

        peers += (2 if ring else 1) * (p.C - 1)
    pl.semaphore_wait(barrier, peers)


def swap_rows(p, src, dst, send_sem, recv_sem):
    return pltpu.make_async_remote_copy(
        src_ref=src, dst_ref=dst, send_sem=send_sem, recv_sem=recv_sem, device_id=(p.far, p.n), device_id_type=MESH
    )


def slot_of(p, n, group):
    return jnp.where(group == 0, n, lax.rem(n + p.half, p.N))


def neighbours(p):
    return p.n + 1 - 2 * lax.rem(p.n, 2), lax.rem(p.n + 2, 4), 3 - p.n


def to(src, dst, send, recv, wide, narrow):
    return pltpu.make_async_remote_copy(
        src_ref=src, dst_ref=dst, send_sem=send, recv_sem=recv, device_id=(wide, narrow), device_id_type=MESH
    )


def spread_sems(narrow):
    return [DMA((narrow, 2)), DMA((narrow, 2)), DMA((2,)), DMA((2,))]


def spread_start(p, src, gathered, rows, send, recv, local, onward):
    half = rows // 2
    view = lambda i: gathered.at[pl.ds(pl.multiple_of(p.slot * rows + i * half, half), half)]
    part = lambda i: src.at[pl.ds(i * half, half)]
    mine = p.group == p.c
    square = p.N == 4
    if square:
        nx, ny, _ = neighbours(p)
        targets = [(nx, (0, 1)), (ny, (1, 0))]
        order = [(t, q, i) for q in range(2) for t, halves in targets for i in (halves[q],)]
        for t, q, i in order:
            at = 0 if t is nx else 1
            to(part(i), view(i), send.at[at, i], recv.at[p.slot, i], 2 * p.k + p.group, t).start()
    else:
        for t in range(p.N):

            @pl.when(p.n != t)
            def _():
                for i in range(2):
                    to(part(i), view(i), send.at[t, i], recv.at[p.slot, i], 2 * p.k + p.group, t).start()

    @pl.when(mine)
    def _():
        for i in range(2):
            pltpu.make_async_copy(part(i), view(i), local.at[i]).start()

    @pl.when(jnp.logical_not(mine))
    def _():
        for i in range(2):
            to(part(i), view(i), local.at[i], recv.at[p.slot, i], 2 * p.k + p.group, p.n).start()


def spread_pass(p, src, gathered, rows, send, recv, local, onward):
    if p.N == 4:
        half = rows // 2
        piece = src.at[pl.ds(0, half)]
        nx, ny, _ = neighbours(p)
        for i, (n, other) in enumerate(((nx, ny), (ny, nx))):
            j = slot_of(p, n, p.c)
            here = gathered.at[pl.ds(pl.multiple_of(j * rows + i * half, half), half)]
            pltpu.make_async_copy(piece, here, recv.at[j, i]).wait()
            to(here, here, onward.at[i], recv.at[j, i], p.w, other).start()


def spread_end(p, src, gathered, rows, send, recv, local, onward):
    half = rows // 2
    piece = src.at[pl.ds(0, half)]
    mine = p.group == p.c
    at = lambda j, i: gathered.at[pl.ds(pl.multiple_of(j * rows + i * half, half), half)]

    def arrive(j, i):
        pltpu.make_async_copy(piece, at(j, i), recv.at[j, i]).wait()

    if p.N == 4:
        nx, ny, nd = neighbours(p)
        jx, jy, jd = (slot_of(p, n, p.c) for n in (nx, ny, nd))
        arrive(jx, 1)
        arrive(jy, 0)
        arrive(jd, 0)
        arrive(jd, 1)
        for i in range(2):
            pltpu.make_async_copy(piece, at(0, 0), onward.at[i]).wait()
            for t in range(2):
                pltpu.make_async_copy(piece, at(0, 0), send.at[t, i]).wait()
    else:
        for t in range(p.N):

            @pl.when(p.n != t)
            def _():
                for i in range(2):
                    pltpu.make_async_copy(piece, at(0, 0), send.at[t, i]).wait()
                    arrive(slot_of(p, t, p.c), i)

    for i in range(2):
        pltpu.make_async_copy(piece, at(0, 0), local.at[i]).wait()

    @pl.when(jnp.logical_not(mine))
    def _():
        arrive(slot_of(p, p.n, p.c), 0)
        arrive(slot_of(p, p.n, p.c), 1)


def sum_bufs(narrow, rows, dim):
    if narrow == 4:
        half = pltpu.VMEM((2, 2, rows, dim // 2), BF)
        return [half, half, pltpu.VMEM((2, rows, dim), BF)]
    return [pltpu.VMEM((narrow, rows, dim), BF)]


def sum_sems(narrow):
    if narrow == 4:
        return [DMA((2, 2)), DMA((2, 2)), DMA((2, 2)), DMA((4,)), DMA((4,))]
    return [DMA((narrow,)), DMA((narrow,)), DMA]


def pieces(p, part, rows, dim):
    half = dim // 2
    return lambda j, i: part.at[pl.ds(pl.multiple_of(j * rows, rows), rows), pl.ds(i * half, half)]


def sum_start(p, part, rows, dim, bufs, sems):
    if p.N != 4:
        (got,), (send, recv, local) = bufs, sems
        for j in range(p.N):
            core, n = p.owner(j)
            mine = p.owner_is_me(j)
            src = part.at[pl.ds(j * rows, rows)]

            @pl.when(mine)
            def _():
                pltpu.make_async_copy(src, got.at[p.n], local).start()

            @pl.when(jnp.logical_not(mine))
            def _():
                to(src, got.at[p.n], send.at[j], recv.at[p.n], 2 * p.k + core, n).start()

        return
    own, inbox, _ = bufs
    load, send, recv, _, _ = sems
    piece = pieces(p, part, rows, dim)
    nx, ny, nd = neighbours(p)
    across, here = slot_of(p, nd, p.c), slot_of(p, p.n, p.c)
    for i, n in enumerate((nx, ny)):
        to(piece(across, i), inbox.at[i, 0], send.at[i, 0], recv.at[i, 0], p.w, n).start()
    for i, n in enumerate((ny, nx)):
        pltpu.make_async_copy(piece(slot_of(p, n, p.c), i), own.at[i, 0], load.at[i, 0]).start()
    for i, n in enumerate((nx, ny)):
        to(piece(slot_of(p, n, p.c), i), inbox.at[i, 1], send.at[i, 1], recv.at[i, 1], p.w, n).start()
        pltpu.make_async_copy(piece(here, i), own.at[i, 1], load.at[i, 1]).start()


def core_of(p, j):
    return (j >= p.half).astype(jnp.int32)


def sum_pass(p, part, rows, dim, bufs, sems):
    if p.N != 4:
        return
    own, inbox, box = bufs
    load, send, recv, send2, recv2 = sems
    piece = pieces(p, part, rows, dim)
    half = dim // 2
    nx, ny, _ = neighbours(p)
    cols = lambda i: pl.ds(i * half, half)

    def add(i, q):
        pltpu.make_async_copy(piece(0, 0), own.at[i, q], load.at[i, q]).wait()
        pltpu.make_async_copy(piece(0, 0), inbox.at[i, q], recv.at[i, q]).wait()

        def body(at):
            own[i, q, at, :] = (own[i, q, at, :].astype(F32) + inbox[i, q, at, :].astype(F32)).astype(BF)

        row_loop(rows, 64, body)

    for i, n in enumerate((ny, nx)):
        add(i, 0)
        j = slot_of(p, n, p.c)
        to(own.at[i, 0], box.at[1, :, cols(i)], send2.at[i], recv2.at[i], 2 * p.k + core_of(p, j), n).start()
    j = slot_of(p, p.n, p.c)
    keep = core_of(p, j) == p.c
    for i in range(2):
        add(i, 1)

        @pl.when(keep)
        def _():
            pltpu.make_async_copy(own.at[i, 1], box.at[0, :, cols(i)], send2.at[2 + i]).start()

        @pl.when(jnp.logical_not(keep))
        def _():
            to(own.at[i, 1], box.at[0, :, cols(i)], send2.at[2 + i], recv2.at[2 + i], 2 * p.k + core_of(p, j), p.n).start()


def sum_end(p, part, rows, dim, bufs, sems):
    if p.N != 4:
        (got,), (send, recv, local) = bufs, sems
        for t in range(p.N):
            mine = (p.group == p.c) & (p.n == t)

            @pl.when(mine)
            def _():
                pltpu.make_async_copy(part.at[pl.ds(0, rows)], got.at[t], local).wait()

            @pl.when(jnp.logical_not(mine))
            def _():
                pltpu.make_async_copy(part.at[pl.ds(0, rows)], got.at[t], recv.at[t]).wait()

        for j in range(p.N):

            @pl.when(jnp.logical_not(p.owner_is_me(j)))
            def _():
                pltpu.make_async_copy(part.at[pl.ds(j * rows, rows)], got.at[0], send.at[j]).wait()

        return
    own, inbox, box = bufs
    load, send, recv, send2, recv2 = sems
    piece = pieces(p, part, rows, dim)
    half = dim // 2
    cols = lambda i: pl.ds(i * half, half)
    for i in range(2):
        for q in range(2):
            pltpu.make_async_copy(piece(0, 0), inbox.at[i, q], send.at[i, q]).wait()
        pltpu.make_async_copy(own.at[i, 0], box.at[1, :, cols(i)], send2.at[i]).wait()
        pltpu.make_async_copy(own.at[i, 0], box.at[1, :, cols(i)], recv2.at[i]).wait()
        pltpu.make_async_copy(own.at[i, 1], box.at[0, :, cols(i)], send2.at[2 + i]).wait()

        @pl.when(p.group != p.c)
        def _():
            pltpu.make_async_copy(own.at[i, 1], box.at[0, :, cols(i)], recv2.at[2 + i]).wait()


def total(p, bufs, at):
    if p.N == 4:
        box = bufs[2]
        return box[0, at, :].astype(F32) + box[1, at, :].astype(F32)
    got = bufs[0]
    out = got[0, at, :].astype(F32)
    for t in range(1, p.N):
        out = out + got[t, at, :].astype(F32)
    return out


PARTS = 4


def line_sems(chips):
    return [DMA((2, chips, PARTS)), DMA((chips, PARTS)), DMA((chips, PARTS)), DMA((chips, PARTS)), DMA]


def line_parts(p, full, rows):
    size = rows // PARTS

    def at(s, core, q=None):
        first = (2 * s + core) * rows
        if q is None:
            return full.at[pl.ds(pl.multiple_of(first, rows), rows)]
        return full.at[pl.ds(pl.multiple_of(first + q * size, size), size)]

    return at


def each_part(body):
    def one(q, carry):
        body(q)
        return carry

    lax.fori_loop(0, PARTS, one, 0)


def line_copy(p, src, dst, send, recv, k, core):
    return pltpu.make_async_remote_copy(
        src_ref=src, dst_ref=dst, send_sem=send, recv_sem=recv, device_id=(2 * k + core, p.n), device_id_type=MESH
    )


def inside(p, k):
    return (k >= 0) & (k < p.C)


def line_start(p, src, full, rows, zsend, zrecv, csend, crecv, local):
    at = line_parts(p, full, rows)
    size = rows // PARTS

    def push(q):
        part = src.at[pl.ds(pl.multiple_of(q * size, size), size)]
        for i, sign in enumerate((1, -1)):

            @pl.when(inside(p, p.k + sign))
            def _():
                line_copy(p, part, at(p.k, p.c, q), zsend.at[i, 0, q], zrecv.at[p.k, q], p.k + sign, p.c).start()

        line_copy(p, part, at(p.k, p.c, q), csend.at[p.k, q], crecv.at[p.k, q], p.k, 1 - p.c).start()

    each_part(push)
    pltpu.make_async_copy(src, at(p.k, p.c), local).start()


def line_steps(p, src, full, rows, zsend, zrecv, csend, crecv, local):
    at = line_parts(p, full, rows)
    piece = src.at[pl.ds(0, rows // PARTS)]

    def at_distance(d):
        def onward(q):
            for i, sign in enumerate((1, -1)):
                s, t = p.k - sign * d, p.k + sign

                @pl.when(inside(p, s))
                def _():
                    here = at(s, p.c, q)
                    pltpu.make_async_copy(piece, here, zrecv.at[s, q]).wait()

                    @pl.when(inside(p, t))
                    def _():
                        line_copy(p, here, here, zsend.at[i, d, q], zrecv.at[s, q], t, p.c).start()

                    line_copy(p, here, here, csend.at[s, q], crecv.at[s, q], p.k, 1 - p.c).start()

        each_part(onward)

    def settle(q):
        here = at(p.k, p.c, q)
        for s in range(p.C):
            pltpu.make_async_copy(piece, here, csend.at[s, q]).wait()
            pltpu.make_async_copy(piece, at(s, 1 - p.c, q), crecv.at[s, q]).wait()
        for i, sign in enumerate((1, -1)):
            for d in range(p.C):

                @pl.when(inside(p, p.k - sign * d) & inside(p, p.k + sign))
                def _():
                    pltpu.make_async_copy(piece, here, zsend.at[i, d, q]).wait()

    def end():
        pltpu.make_async_copy(src, at(p.k, p.c), local).wait()
        each_part(settle)

    return [functools.partial(at_distance, d) for d in range(1, p.C)] + [end]


def line_sum_bufs(chips, rows, width):
    return [pltpu.VMEM((chips, rows, width), BF)] * 3 + [pltpu.VMEM((2, rows, width), BF), pltpu.VMEM((rows, width), F32)]


def line_sum_sems(chips):
    return [
        DMA((chips, PARTS)), DMA((chips, PARTS)), DMA((chips, PARTS)), DMA((2, chips, PARTS)), DMA((chips, PARTS)),
        DMA((2, PARTS)),
    ]


def line_sum_start(p, part, rows, bufs, sems):
    own, inbox, _, _, _ = bufs
    load, csend, crecv, _, _, _ = sems
    at = line_parts(p, part, rows)
    size = rows // PARTS

    def share(s):
        def one(q):
            here = pl.ds(pl.multiple_of(q * size, size), size)
            line_copy(p, at(s, 1 - p.c, q), inbox.at[s, here], csend.at[s, q], crecv.at[s, q], p.k, 1 - p.c).start()
            pltpu.make_async_copy(at(s, p.c, q), own.at[s, here], load.at[s, q]).start()

        each_part(one)

    for d in range(p.C - 1, 0, -1):
        for sign in (1, -1):
            s = p.k + sign * d

            @pl.when(inside(p, s))
            def _():
                share(s)

    share(p.k)


def line_sum_steps(p, part, rows, bufs, sems):
    own, inbox, relay, box, acc = bufs
    load, csend, crecv, zsend, rrecv, zrecv = sems
    size = rows // PARTS
    step = math.gcd(size, 128)
    piece = line_parts(p, part, rows)(0, 0, 0)

    def rows_of(q):
        return pl.ds(pl.multiple_of(q * size, size), size)

    def add(q, body):
        def one(j, carry):
            body(pl.ds(pl.multiple_of(q * size + j * step, step), step))
            return carry

        lax.fori_loop(0, size // step, one, 0)

    def pair(t, q):
        pltpu.make_async_copy(piece, own.at[t, rows_of(q)], load.at[t, q]).wait()
        pltpu.make_async_copy(piece, inbox.at[t, rows_of(q)], crecv.at[t, q]).wait()

    def at_distance(d):
        def onward(q):
            here = rows_of(q)
            for i, sign in enumerate((1, -1)):
                t = p.k + sign * d
                behind = inside(p, p.k - sign)

                @pl.when(inside(p, t))
                def _():
                    pair(t, q)

                    @pl.when(jnp.logical_not(behind))
                    def _():
                        def two(at):
                            own[t, at, :] = (own[t, at, :].astype(F32) + inbox[t, at, :].astype(F32)).astype(BF)

                        add(q, two)

                    @pl.when(behind)
                    def _():
                        pltpu.make_async_copy(piece, relay.at[t, here], rrecv.at[t, q]).wait()

                        def three(at):
                            both = own[t, at, :].astype(F32) + inbox[t, at, :].astype(F32)
                            own[t, at, :] = (both + relay[t, at, :].astype(F32)).astype(BF)

                        add(q, three)

                    src = own.at[t, here]
                    if d >= 2:
                        line_copy(p, src, relay.at[t, here], zsend.at[i, d, q], rrecv.at[t, q], p.k + sign, p.c).start()
                    else:
                        line_copy(p, src, box.at[i, here], zsend.at[i, d, q], zrecv.at[i, q], t, p.c).start()

        each_part(onward)

    def last(q):
        here = rows_of(q)
        pair(p.k, q)

        def first(at):
            acc[at, :] = own[p.k, at, :].astype(F32) + inbox[p.k, at, :].astype(F32)

        add(q, first)
        for i, sign in enumerate((1, -1)):

            @pl.when(inside(p, p.k - sign))
            def _():
                pltpu.make_async_copy(piece, box.at[i, here], zrecv.at[i, q]).wait()

                def more(at):
                    acc[at, :] += box[i, at, :].astype(F32)

                add(q, more)

            for d in range(1, p.C):

                @pl.when(inside(p, p.k + sign * d))
                def _():
                    pltpu.make_async_copy(piece, own.at[0, here], zsend.at[i, d, q]).wait()

        for s in range(p.C):
            pltpu.make_async_copy(piece, inbox.at[s, here], csend.at[s, q]).wait()

    return [functools.partial(at_distance, d) for d in range(p.C - 1, 0, -1)] + [lambda: each_part(last)]


def row_loop(rows, step, body):
    def one(i, carry):
        body(pl.ds(pl.multiple_of(i * step, step), step))
        return carry

    lax.fori_loop(0, rows // step, one, 0)


STEP = 64


def inv_rms(u):
    return lax.rsqrt(jnp.mean(u * u, axis=-1, keepdims=True) + EPSILON)


def swap_start(p, buf, out_ref, sems):
    @pl.when(p.c == 1)
    def _():
        swap_rows(p, buf, out_ref, sems.at[0], sems.at[1]).start()

    @pl.when(p.c == 0)
    def _():
        out_ref[...] = buf[...]


def swap_end(p, buf, out_ref, sems):
    @pl.when(p.c == 1)
    def _():
        swap_rows(p, buf, out_ref, sems.at[0], sems.at[1]).wait()


def weave(gate_ref, up_ref, both_ref):
    ff = gate_ref.shape[1]
    t = math.gcd(ff, 256)
    for i in range(0, ff, t):
        both_ref[:, 2 * i : 2 * i + t] = gate_ref[:, i : i + t]
        both_ref[:, 2 * i + t : 2 * i + 2 * t] = up_ref[:, i : i + t]


def unweave_kernel(both_ref, gate_ref, up_ref):
    ff = gate_ref.shape[1]
    t = math.gcd(ff, 256)
    for i in range(0, ff, t):
        gate_ref[:, i : i + t] = both_ref[:, 2 * i : 2 * i + t].astype(F32)
        up_ref[:, i : i + t] = both_ref[:, 2 * i + t : 2 * i + 2 * t].astype(F32)


def input_kernel(wide, narrow, norm, *refs):
    if norm:
        x_ref, gain_ref, shard, gate_ref, up_ref, own_ref, gathered, full, gu_ref, buf, swap, *sems = refs
    else:
        x_ref, shard, own_ref, gathered, full, swap, *sems = refs
    p = Place(wide, narrow)
    rows = x_ref.shape[0]
    spread, line = sems[:4], sems[4:]
    src = buf if norm else own_ref
    enter(p, line=True)

    @pl.when(p.c == 1)
    def _():
        swap_rows(p, x_ref, own_ref, swap.at[0], swap.at[1]).start()

    line_start(p, shard, full, shard.shape[0], *line)
    *steps, end = line_steps(p, shard, full, shard.shape[0], *line)

    def share():
        if norm:

            def body(at):
                u = own_ref[at, :].astype(F32)
                buf[at, :] = (u * inv_rms(u) * gain_ref[...]).astype(BF)

            row_loop(rows, STEP, body)
        spread_start(p, src, gathered, rows, *spread)

    @pl.when(p.c == 0)
    def _():
        own_ref[...] = x_ref[...]
        share()

    if norm:
        weave(gate_ref, up_ref, gu_ref)
    steps[0]()

    @pl.when(p.c == 1)
    def _():
        swap_rows(p, x_ref, own_ref, swap.at[0], swap.at[1]).wait()
        share()

    for step in steps[1:-1]:
        step()
    spread_pass(p, src, gathered, rows, *spread)
    steps[-1]()
    spread_end(p, src, gathered, rows, *spread)
    end()


def middle_kernel(wide, narrow, part, own_ref, gain_ref, mid_ref, gathered, buf, *refs):
    p = Place(wide, narrow)
    rows, dim = own_ref.shape
    bufs, sems, spread = split_refs(narrow, refs)
    enter(p)
    sum_start(p, part, rows, dim, bufs, sems)
    sum_pass(p, part, rows, dim, bufs, sems)
    sum_end(p, part, rows, dim, bufs, sems)

    def body(at):
        u = own_ref[at, :].astype(F32) + total(p, bufs, at)
        mid_ref[at, :] = u
        buf[at, :] = (u * inv_rms(u) * gain_ref[...]).astype(BF)

    row_loop(rows, STEP, body)
    spread_start(p, buf, gathered, rows, *spread)
    spread_pass(p, buf, gathered, rows, *spread)
    spread_end(p, buf, gathered, rows, *spread)


def split_refs(narrow, refs):
    bufs, sems = (3, 5) if narrow == 4 else (1, 3)
    return refs[:bufs], refs[bufs : bufs + sems], refs[bufs + sems :]


def output_kernel(wide, narrow, part, mid_ref, dkv, out_ref, kv_ref, buf, swap, *refs):
    p = Place(wide, narrow)
    rows, dim = mid_ref.shape
    kv_rows = kv_ref.shape[0]
    bufs, sems, line = split_refs(narrow, refs)
    line_bufs, line_sem = line[:5], line[5:]
    enter(p, line=True)
    line_sum_start(p, dkv, kv_rows, line_bufs, line_sem)
    sum_start(p, part, rows, dim, bufs, sems)
    first, *steps, last = line_sum_steps(p, dkv, kv_rows, line_bufs, line_sem)
    first()
    sum_pass(p, part, rows, dim, bufs, sems)
    steps[0]()
    sum_end(p, part, rows, dim, bufs, sems)

    def body(at):
        buf[at, :] = (mid_ref[at, :] + total(p, bufs, at)).astype(BF)

    row_loop(rows, STEP, body)
    swap_start(p, buf, out_ref, swap)
    for step in steps[1:]:
        step()
    last()
    row_loop(kv_rows, 128, lambda at: kv_ref.__setitem__((at, slice(None)), line_bufs[4][at, :].astype(BF)))
    swap_end(p, buf, out_ref, swap)


def norm_back(u, gain, cot):
    r = inv_rms(u)
    a = cot * gain
    du = r * a - u * (r * r * r) * jnp.mean(a * u, axis=-1, keepdims=True)
    return du, jnp.sum(cot * u * r, axis=0, keepdims=True)


def middle_back_kernel(wide, narrow, part, mid_ref, gain_ref, grad_ref, back_ref, dgain_ref, gathered, buf, *refs):
    p = Place(wide, narrow)
    rows, dim = mid_ref.shape
    bufs, sems, spread = split_refs(narrow, refs)
    enter(p)
    sum_start(p, part, rows, dim, bufs, sems)
    dgain_ref[...] = jnp.zeros_like(dgain_ref)
    sum_pass(p, part, rows, dim, bufs, sems)
    sum_end(p, part, rows, dim, bufs, sems)

    def body(at):
        du, dgain = norm_back(mid_ref[at, :], gain_ref[...], total(p, bufs, at))
        back = grad_ref[at, :].astype(F32) + du
        back_ref[at, :] = back
        buf[at, :] = back.astype(BF)
        dgain_ref[...] += dgain

    row_loop(rows, STEP, body)
    spread_start(p, buf, gathered, rows, *spread)
    spread_pass(p, buf, gathered, rows, *spread)
    spread_end(p, buf, gathered, rows, *spread)


def share_start(me, count, here, slots, sends, recvs, device):
    slots[me] = here[...]
    for t in range(count):

        @pl.when(me != t)
        def _():
            wide_at, narrow_at = device(t)
            to(here, slots.at[me], sends.at[t], recvs.at[me], wide_at, narrow_at).start()


def share_end(me, count, here, slots, sends, recvs):
    for t in range(count):

        @pl.when(me != t)
        def _():
            pltpu.make_async_copy(here, slots.at[t], sends.at[t]).wait()
            pltpu.make_async_copy(here, slots.at[t], recvs.at[t]).wait()

    out = slots[0]
    for t in range(1, count):
        out = out + slots[t]
    here[...] = out


def input_back_kernel(
    wide, narrow, part, own_ref, gain_ref, back_ref, gains_ref, wgrad, out_ref, gsum_ref, wsum_ref,
    buf, far_buf, gbuf, gbuf2, swap, gsend, grecv, gsend2, grecv2, *refs,
):
    p = Place(wide, narrow)
    rows, dim = own_ref.shape
    w_rows = wsum_ref.shape[0]
    bufs, sems, line = split_refs(narrow, refs)
    line_bufs, line_sem = (*line[:4], wsum_ref), line[4:]
    enter(p, ring=True)
    line_sum_start(p, wgrad, w_rows, line_bufs, line_sem)
    sum_start(p, part, rows, dim, bufs, sems)
    first, *steps, last = line_sum_steps(p, wgrad, w_rows, line_bufs, line_sem)
    gsum_ref[...] = gains_ref[...]
    first()
    sum_pass(p, part, rows, dim, bufs, sems)
    steps[0]()
    sum_end(p, part, rows, dim, bufs, sems)

    def body(at):
        du, dgain = norm_back(own_ref[at, :].astype(F32), gain_ref[...], total(p, bufs, at))
        grad = back_ref[at, :] + du
        out_ref[at, :] = grad
        buf[at, :] = grad.astype(BF)
        gsum_ref[:, :dim] += dgain

    row_loop(rows, STEP, body)

    @pl.when(p.c == 1)
    def _():
        swap_rows(p, buf, far_buf, swap.at[0], swap.at[1]).start()

    share_start(p.n, narrow, gsum_ref, gbuf, gsend, grecv, lambda t: (p.w, t))
    for step in steps[1:]:
        step()
    share_end(p.n, narrow, gsum_ref, gbuf, gsend, grecv)
    share_start(p.w, wide, gsum_ref, gbuf2, gsend2, grecv2, lambda t: (t, p.n))
    last()
    share_end(p.w, wide, gsum_ref, gbuf2, gsend2, grecv2)

    @pl.when(p.c == 1)
    def _():
        swap_rows(p, buf, far_buf, swap.at[0], swap.at[1]).wait()
        row_loop(rows, STEP, lambda at: out_ref.__setitem__((at, slice(None)), far_buf[at, :].astype(F32)))


VM = pl.BlockSpec(memory_space=pltpu.VMEM)
HB = pl.BlockSpec(memory_space=pl.ANY)


def comm_call(kernel, name, cid, out_shape, in_specs, out_specs, scratch, *args):
    return pl.pallas_call(
        kernel,
        out_shape=out_shape,
        in_specs=in_specs,
        out_specs=out_specs,
        scratch_shapes=scratch,
        compiler_params=pltpu.CompilerParams(collective_id=cid, has_side_effects=True, vmem_limit_bytes=52 << 20),
        cost_estimate=pl.CostEstimate(flops=0, bytes_accessed=160_000_000, transcendentals=0),
        name=name,
    )(*args)


def sds(shape, kind):
    return jax.ShapeDtypeStruct(shape, kind)


def plain(kernel, name, grid, in_specs, out_specs, out_shape, flops, nbytes, *args, scratch=(), aliases=None):
    return pl.pallas_call(
        kernel,
        out_shape=out_shape,
        grid=grid,
        in_specs=in_specs,
        out_specs=out_specs,
        scratch_shapes=scratch,
        input_output_aliases=aliases or {},
        compiler_params=pltpu.CompilerParams(vmem_limit_bytes=52 << 20),
        cost_estimate=pl.CostEstimate(flops=flops, bytes_accessed=nbytes, transcendentals=0),
        name=name,
    )(*args)


def whole(shape):
    return pl.BlockSpec(shape, lambda *i: (0,) * len(shape), pipeline_mode=pl.Buffered(1))


def by_rows(tm, width):
    return pl.BlockSpec((tm, width), lambda i: (i, 0))


def mlp_fwd_kernel(x_ref, w_ref, gu_ref, h_ref):
    t = h_ref.shape[1]
    y = dg(x_ref[...], w_ref[...], NN)
    gate, up = y[:, :t], y[:, t:]
    gu_ref[...] = y
    h_ref[...] = (gate * jax.nn.sigmoid(gate) * up).astype(BF)


def mlp_fwd(x, w, t):
    rows, dim = x.shape
    ff2 = w.shape[1]
    return plain(
        mlp_fwd_kernel, "mlp_fwd", (ff2 // (2 * t),),
        [whole((rows, dim)), pl.BlockSpec((dim, 2 * t), lambda i: (0, i))],
        [pl.BlockSpec((rows, 2 * t), lambda i: (0, i)), pl.BlockSpec((rows, t), lambda i: (0, i))],
        (sds((rows, ff2), F32), sds((rows, ff2 // 2), BF)),
        2 * rows * dim * ff2, rows * dim * 2 + dim * ff2 * 2 + rows * ff2 * 5, x, w,
    )


def mlp_bwd_kernel(g_ref, w_ref, gu_ref, out_ref):
    t = w_ref.shape[1]
    hb = dg(g_ref[...], w_ref[...], NN)
    gate, up = gu_ref[:, :t], gu_ref[:, t:]
    s = jax.nn.sigmoid(gate)
    gs = hb * s
    out_ref[:, :t] = (gs * up * (1.0 + gate * (1.0 - s))).astype(BF)
    out_ref[:, t:] = (gs * gate).astype(BF)


def mlp_bwd(g, w, gu, t):
    rows, dim = g.shape
    ff = w.shape[1]
    return plain(
        mlp_bwd_kernel, "mlp_bwd", (ff // t,),
        [whole((rows, dim)), pl.BlockSpec((dim, t), lambda i: (0, i)), pl.BlockSpec((rows, 2 * t), lambda i: (0, i))],
        pl.BlockSpec((rows, 2 * t), lambda i: (0, i)), sds((rows, 2 * ff), BF),
        2 * rows * dim * ff, rows * dim * 2 + dim * ff * 2 + rows * ff * 12, g, w, gu,
    )


def nt_kernel(a_ref, b_ref, o_ref):
    o_ref[...] = dg(a_ref[...], b_ref[...], NT).astype(BF)


def mm_nt(a, b, name, tn=256):
    rows, depth = a.shape
    cols = b.shape[0]
    return plain(
        nt_kernel, name, (cols // tn,), [whole((rows, depth)), by_rows(tn, depth)],
        pl.BlockSpec((rows, tn), lambda i: (0, i)), sds((rows, cols), BF),
        2 * rows * cols * depth, 2 * (rows * depth + cols * depth + rows * cols), a, b,
    )


def turn(u):
    return pltpu.roll(u, u.shape[-1] // 2, 1)


def qkv_kernel(qw, kw, hd, fold, x_ref, w_ref, cos_ref, sin_ref, qg_ref, kg_ref, proj_ref, q_ref, kv_ref):
    y = dg(x_ref[...], w_ref[...], NN)
    cos, sin = cos_ref[...], sin_ref[...]
    proj_ref[...] = y[:, : qw + kw]

    def head(lo, gain):
        u = y[:, lo : lo + hd]
        v = u * inv_rms(u) * gain
        return v * cos + turn(v) * sin

    for h in range(qw // hd):
        q_ref[:, h * hd : (h + 1) * hd] = (head(h * hd, qg_ref[...]) * fold).astype(BF)
    for h in range(kw // hd):
        kv_ref[:, 2 * h * hd : (2 * h + 1) * hd] = head(qw + h * hd, kg_ref[...]).astype(BF)
        kv_ref[:, (2 * h + 1) * hd : (2 * h + 2) * hd] = y[:, qw + kw + h * hd : qw + kw + (h + 1) * hd].astype(BF)


def qkv_fwd(x, w, cos, sin, qg, kg, qw, kw, fold):
    rows, dim = x.shape
    hd = cos.shape[1]
    width = qw + 2 * kw
    tm = 256
    return plain(
        functools.partial(qkv_kernel, qw, kw, hd, fold), "qkv_fwd", (rows // tm,),
        [by_rows(tm, dim), whole((dim, width)), by_rows(tm, hd), by_rows(tm, hd), whole((1, hd)), whole((1, hd))],
        [by_rows(tm, qw + kw), by_rows(tm, qw), by_rows(tm, 2 * kw)],
        [sds((rows, qw + kw), F32), sds((rows, qw), BF), sds((rows, 2 * kw), BF)],
        2 * rows * dim * width, 2 * (rows * dim + dim * width) + rows * width * 6, x, w, cos, sin, qg, kg,
    )


def head_back(cot, u, gain, cos, sin):
    cot = cot * cos - turn(cot) * sin
    return norm_back(u, gain, cot)


def q_back_kernel(hd, dq_ref, u_ref, cos_ref, sin_ref, g_ref, low_ref, dgain_ref):
    @pl.when(pl.program_id(0) == 0)
    def _():
        dgain_ref[...] = jnp.zeros_like(dgain_ref)

    for h in range(dq_ref.shape[1] // hd):
        at = slice(h * hd, (h + 1) * hd)
        du, dgain = head_back(dq_ref[:, at], u_ref[:, at], g_ref[...], cos_ref[...], sin_ref[...])
        low_ref[:, at] = du.astype(BF)
        dgain_ref[...] += dgain


def q_back(dq, proj, cos, sin, gain):
    rows, qw = dq.shape
    hd = cos.shape[1]
    tm = 256
    return plain(
        functools.partial(q_back_kernel, hd), "q_back", (rows // tm,),
        [by_rows(tm, qw), by_rows(tm, qw), by_rows(tm, hd), by_rows(tm, hd), whole((1, hd))],
        [by_rows(tm, qw), pl.BlockSpec((1, hd), lambda i: (0, 0))], [sds((rows, qw), BF), sds((1, hd), F32)],
        rows * qw * 20, rows * qw * 10, dq, proj, cos, sin, gain,
    )


def kv_back_kernel(qw, kw, hd, q_ref, u_ref, cos_ref, sin_ref, g_ref, w_ref, *refs):
    s_ref, low_ref, back_ref, dgain_ref = refs

    @pl.when(pl.program_id(0) == 0)
    def _():
        dgain_ref[...] = jnp.zeros_like(dgain_ref)

    low_ref[:, :qw] = q_ref[...]
    for h in range(kw // hd):
        key = slice(2 * h * hd, (2 * h + 1) * hd)
        value = slice((2 * h + 1) * hd, (2 * h + 2) * hd)
        at = slice(qw + h * hd, qw + (h + 1) * hd)
        du, dgain = head_back(s_ref[:, key].astype(F32), u_ref[:, at], g_ref[...], cos_ref[...], sin_ref[...])
        low_ref[:, at] = du.astype(BF)
        low_ref[:, qw + kw + h * hd : qw + kw + (h + 1) * hd] = s_ref[:, value]
        dgain_ref[...] += dgain
    back_ref[...] = dg(low_ref[...], w_ref[...], NT).astype(BF)


def kv_back(q_low, proj, cos, sin, gain, w, sums, kw):
    rows, qw = q_low.shape
    hd = cos.shape[1]
    dim = w.shape[0]
    width = qw + 2 * kw
    tm = 256
    return plain(
        functools.partial(kv_back_kernel, qw, kw, hd), "kv_back", (rows // tm,),
        [by_rows(tm, qw), by_rows(tm, qw + kw), by_rows(tm, hd), by_rows(tm, hd), whole((1, hd)), whole((dim, width))]
        + [by_rows(tm, 2 * kw)],
        [by_rows(tm, width), by_rows(tm, dim), pl.BlockSpec((1, hd), lambda i: (0, 0))],
        [sds((rows, width), BF), sds((rows, dim), BF), sds((1, hd), F32)],
        2 * rows * dim * width, 2 * (rows * dim + dim * width) + rows * width * 6,
        q_low, proj, cos, sin, gain, w, sums,
    )


def attn_back_kernel(hd, groups, x_ref, w_ref, o_ref, back_ref, delta_ref):
    back = dg(x_ref[...], w_ref[...], NN).astype(BF)
    back_ref[...] = back
    rows, width = back.shape
    lane = lax.broadcasted_iota(jnp.int32, (rows, hd), 1)
    out = jnp.zeros((rows, hd), F32)
    for h in range(width // hd):
        at = slice(h * hd, (h + 1) * hd)
        row = 8 * (h // groups) + h % groups
        out = jnp.where(lane == row, jnp.sum(back[:, at].astype(F32) * o_ref[:, at], axis=1, keepdims=True), out)
    delta_ref[...] = jnp.transpose(out)[: delta_ref.shape[0]]


def attn_back(x, w, o, at, groups, hd):
    rows, dim = x.shape
    width = o.shape[1]
    tm = 256
    stats = 8 * width // (groups * hd)
    return plain(
        functools.partial(attn_back_kernel, hd, groups), "attn_back", (rows // tm,),
        [by_rows(tm, dim), pl.BlockSpec((dim, width), lambda i: (0, at), pipeline_mode=pl.Buffered(1)), by_rows(tm, width)],
        [by_rows(tm, width), pl.BlockSpec((stats, tm), lambda i: (0, i))], [sds((rows, width), BF), sds((stats, rows), F32)],
        2 * rows * dim * width, 2 * (rows * dim + dim * width) + rows * width * 6, x, w, o,
    )


def attn_grads_kernel(x_ref, low_ref, m_ref, a_ref, out_ref):
    width = low_ref.shape[1]
    out_ref[:, :width] = dg(x_ref[...], low_ref[...], TN).astype(BF)
    out_ref[:, width:] = dg(m_ref[...], a_ref[...], TN).astype(BF)


def attn_grads(x, low, m, a):
    rows, dim = x.shape
    width, qw = low.shape[1], a.shape[1]
    tm = 256
    cols = pl.BlockSpec((rows, tm), lambda i: (0, i))
    return plain(
        attn_grads_kernel, "attn_grads", (dim // tm,), [cols, whole((rows, width)), cols, whole((rows, qw))],
        by_rows(tm, width + qw), sds((dim, width + qw), BF),
        2 * rows * dim * (width + qw), 2 * rows * (2 * dim + width + qw) + 2 * dim * (width + qw), x, low, m, a,
    )


def fwd_kernel(groups, hd, tab, q_ref, kv_ref, o_ref, low_ref, lse_ref, acc, lsum):
    s = pl.program_id(1)
    block = q_ref.shape[0]
    diag, first, last = tab[2, s], tab[3, s], tab[4, s]

    @pl.when(first == 1)
    def _():
        acc[...] = jnp.zeros_like(acc)
        lsum[...] = jnp.zeros_like(lsum)

    def work(masked):
        k, v = kv_ref[:, :hd], kv_ref[:, hd:]
        for g in range(groups):
            at = slice(g * hd, (g + 1) * hd)
            scores = dg(q_ref[:, at], k, NT)
            if masked:
                row = lax.broadcasted_iota(jnp.int32, scores.shape, 0)
                col = lax.broadcasted_iota(jnp.int32, scores.shape, 1)
                scores = jnp.where(col <= row, scores, MASKED)
            probs = jnp.exp2(scores)
            part = probs[:, :128]
            for j in range(1, block // 128):
                part = part + probs[:, j * 128 : (j + 1) * 128]
            lsum[g] += part
            acc[:, at] += dg(probs.astype(BF), v, NN)

    @pl.when(diag == 0)
    def _():
        work(False)

    @pl.when(diag == 1)
    def _():
        work(True)

    @pl.when(last == 1)
    def _():
        lane = lax.broadcasted_iota(jnp.int32, (block, 128), 1)
        lse = jnp.zeros((block, 128), F32)
        for g in range(groups):
            at = slice(g * hd, (g + 1) * hd)
            l = jnp.sum(lsum[g], axis=1, keepdims=True)
            out = acc[:, at] / l
            o_ref[:, at] = out
            low_ref[:, at] = out.astype(BF)
            lse = jnp.where(lane == g, jnp.log2(l), lse)
        lse_ref[...] = jnp.transpose(lse)[: lse_ref.shape[0]]


def attn_fwd(tab, q, kv, groups, hd, block):
    rows, width = q.shape
    gw = groups * hd
    heads = width // gw
    steps = tab.shape[1]
    mine = pl.BlockSpec((block, gw), lambda h, s, t: (t[0, s], h))
    return pl.pallas_call(
        functools.partial(fwd_kernel, groups, hd),
        out_shape=(sds((rows, width), F32), sds((rows, width), BF), sds((8 * heads, rows), F32)),
        grid_spec=pltpu.PrefetchScalarGridSpec(
            num_scalar_prefetch=1,
            grid=(heads, steps),
            in_specs=[mine, pl.BlockSpec((block, 2 * hd), lambda h, s, t: (t[1, s], h))],
            out_specs=[mine, mine, pl.BlockSpec((8, block), lambda h, s, t: (h, t[0, s]))],
            scratch_shapes=[pltpu.VMEM((block, gw), F32), pltpu.VMEM((groups, block, 128), F32)],
        ),
        compiler_params=pltpu.CompilerParams(vmem_limit_bytes=48 << 20),
        cost_estimate=pl.CostEstimate(
            flops=heads * steps * block * block * gw * 4,
            bytes_accessed=heads * steps * block * hd * 8,
            transcendentals=heads * steps * block * block * groups,
        ),
        name="attn_fwd",
    )(tab, q, kv)


def bwd_kernel(groups, hd, tab, q_ref, do_ref, kv_ref, lse_ref, delta_ref, zeros, dq_ref, dkv_ref, dq_sum, dkv_sum):
    s = pl.program_id(1)
    block = q_ref.shape[0]
    qi, diag, first, last = tab[0, s], tab[2, s], tab[3, s], tab[4, s]

    @pl.when(s == 0)
    def _():
        dq_sum[...] = jnp.zeros_like(dq_sum)

    @pl.when(first == 1)
    def _():
        dkv_sum[...] = jnp.zeros_like(dkv_sum)

    def work(masked):
        k, v = kv_ref[:, :hd], kv_ref[:, hd:]
        for g in range(groups):
            at = slice(g * hd, (g + 1) * hd)
            q, do = q_ref[:, at], do_ref[:, at]
            scores = dg(k, q, NT) - lse_ref[g : g + 1, :]
            if masked:
                row = lax.broadcasted_iota(jnp.int32, scores.shape, 0)
                col = lax.broadcasted_iota(jnp.int32, scores.shape, 1)
                scores = jnp.where(row <= col, scores, MASKED)
            probs = jnp.exp2(scores)
            dots = dg(v, do, NT)
            dkv_sum[:, hd:] += dg(probs.astype(BF), do, NN)
            back = (probs * (dots - delta_ref[g : g + 1, :])).astype(BF)
            dkv_sum[:, :hd] += dg(back, q, NN)
            dq_sum[qi, :, at] += dg(back, k, TN)

    @pl.when(diag == 0)
    def _():
        work(False)

    @pl.when(diag == 1)
    def _():
        work(True)

    @pl.when(last == 1)
    def _():
        dkv_ref[:, :hd] = (dkv_sum[:, :hd] * math.log(2.0)).astype(BF)
        dkv_ref[:, hd:] = dkv_sum[:, hd:].astype(BF)

    @pl.when(s == pl.num_programs(1) - 1)
    def _():
        for i in range(dq_sum.shape[0]):
            dq_ref[i * block : (i + 1) * block, :] = dq_sum[i] * hd**-0.5


def attn_bwd(tab, q, do, kv, lse, delta, groups, hd, block):
    rows, width = q.shape
    gw = groups * hd
    heads = width // gw
    steps = tab.shape[1]
    mine = pl.BlockSpec((block, gw), lambda h, s, t: (t[0, s], h))
    keys = pl.BlockSpec((block, 2 * hd), lambda h, s, t: (t[1, s], h))
    stat = pl.BlockSpec((8, block), lambda h, s, t: (h, t[0, s]))
    return pl.pallas_call(
        functools.partial(bwd_kernel, groups, hd),
        out_shape=(sds((rows, width), F32), sds(kv.shape, BF)),
        grid_spec=pltpu.PrefetchScalarGridSpec(
            num_scalar_prefetch=1,
            grid=(heads, steps),
            in_specs=[mine, mine, keys, stat, stat, HB],
            out_specs=[pl.BlockSpec((rows, gw), lambda h, s, t: (0, h)), keys],
            scratch_shapes=[pltpu.VMEM((rows // block, block, gw), F32), pltpu.VMEM((block, 2 * hd), F32)],
        ),
        input_output_aliases={6: 1},
        compiler_params=pltpu.CompilerParams(vmem_limit_bytes=48 << 20),
        cost_estimate=pl.CostEstimate(
            flops=heads * steps * block * block * gw * 10,
            bytes_accessed=heads * steps * block * hd * 16,
            transcendentals=heads * steps * block * block * groups,
        ),
        name="attn_bwd",
    )(tab, q, do, kv, lse, delta, jnp.zeros(kv.shape, BF))


def place(w, chips):
    k, core = w // 2, w % 2
    return 4 * k + core, 4 * chips - 1 - 4 * k - core


def block_row(b, chips):
    m = b % 4
    early = m < 2
    k = jnp.where(early, b // 4, (4 * chips - 1 - b) // 4)
    core = jnp.where((m == 1) | (m == 2), 1, 0)
    return 2 * (2 * k + core) + jnp.where(early, 0, 1)


def tables(w, chips):
    a, b = place(w, chips)
    count = 4 * chips + 1
    s = jnp.arange(count, dtype=jnp.int32)
    in_a = s <= a
    key = jnp.where(in_a, s, s - a - 1)
    diag = jnp.where(in_a, s == a, s == count - 1)
    fwd = [jnp.where(in_a, 0, 1), block_row(key, chips), diag, key == 0, diag]
    less, low = jnp.minimum(a, b), jnp.where(a < b, 0, 1)
    both = s < 2 * (less + 1)
    even = s % 2 == 0
    key = jnp.where(both, s // 2, s - (less + 1))
    query = jnp.where(both & even, low, 1 - low)
    diag = key == jnp.where(query == 0, a, b)
    bwd = [query, block_row(key, chips), diag, ~both | even, ~both | ~even]
    return tuple(jnp.stack([row.astype(jnp.int32) for row in rows]) for rows in (fwd, bwd))


def rotation(positions, head_dim):
    steps_half = jnp.arange(head_dim // 2).astype(F32)
    inverse = jnp.exp(steps_half * (-2.0 * math.log(1000000.0) / head_dim))
    angles = positions.astype(F32)[:, None] * inverse[None, :]
    cos, sin = jnp.cos(angles), jnp.sin(angles)
    return jnp.concatenate([cos, cos], axis=1), jnp.concatenate([-sin, sin], axis=1)


def per_device(
    wide, narrow,
    layer_input, w_query, w_key, w_value, w_output, w_gate, w_up, w_down,
    attn_gain, mlp_gain, query_gain, key_gain, out_grad,
):
    hd = query_gain.shape[0]
    rows, dim = layer_input.shape
    all_rows = narrow * rows
    chips = wide // 2
    block = all_rows // 2
    qw, kw = w_query.shape[1], w_key.shape[1]
    ff = w_gate.shape[1]
    groups = qw // kw
    kv_heads = kw // hd
    w = lax.axis_index("wide")
    fwd_tab, bwd_tab = tables(w, chips)
    first, second = place(w, chips)
    at = jnp.arange(block, dtype=jnp.int32)
    positions = jnp.concatenate([first * block + at, second * block + at])
    cos_table, sin_table = rotation(positions, hd)

    def gather(shard):
        return lax.all_gather(shard, "wide", axis=0, tiled=True)

    def scatter(grad):
        return lax.psum_scatter(grad, "wide", scatter_dimension=0, tiled=True)

    t = math.gcd(ff, 256)

    spread_s = spread_sems(narrow)
    sum_s = [*sum_bufs(narrow, rows, dim), *sum_sems(narrow)]
    row_buf = pltpu.VMEM((rows, dim), BF)
    low_rows, full_rows, all_low = sds((rows, dim), BF), sds((rows, dim), F32), sds((all_rows, dim), BF)
    ring = functools.partial
    qg, kg = query_gain[None], key_gain[None]
    after = lax.optimization_barrier

    in_scratch = [DMA((2,)), *spread_s, *line_sems(chips)]
    shard = jnp.concatenate([w_query, w_key, w_value, w_output.T], axis=1)
    own, normed_all, w_attn, gu_shard = comm_call(
        ring(input_kernel, wide, narrow, True), "input_rows", 0,
        (low_rows, all_low, sds((dim, shard.shape[1]), BF), sds((w_gate.shape[0], 2 * ff), BF)),
        [VM, VM, HB, VM, VM], (VM, HB, HB, VM), [row_buf, *in_scratch],
        layer_input, attn_gain[None], shard, w_gate, w_up,
    )
    proj, queries, kv_own = qkv_fwd(
        normed_all, w_attn, cos_table, sin_table, qg, kg, qw, kw, hd**-0.5 * math.log2(math.e)
    )
    grad_own, grad_all, kv = comm_call(
        ring(input_kernel, wide, narrow, False), "grad_rows", 1,
        (low_rows, all_low, sds((wide * all_rows, 2 * kw), BF)), [VM, HB], (VM, HB, HB), in_scratch,
        out_grad, kv_own,
    )
    gu_shard, w_down, kv = after((gu_shard, w_down, kv))
    w_gu, w_d = gather(gu_shard), gather(w_down.T)
    attended, attended_low, lse = attn_fwd(fwd_tab, queries, kv, groups, hd, block)
    w_o = w_attn[:, qw + 2 * kw :]
    middle, normed_mlp = comm_call(
        ring(middle_kernel, wide, narrow), "middle_rows", 2, (full_rows, all_low), [HB, VM, VM], (VM, HB),
        [row_buf, *sum_s, *spread_s], dg(attended_low, w_o, NT).astype(BF), own, mlp_gain[None],
    )
    gate_up, hidden_low = mlp_fwd(normed_mlp, w_gu, t)
    grad_down = dg(grad_all, hidden_low, TN).astype(BF)
    w_d, _ = after((w_d, grad_down))
    gu_low = mlp_bwd(grad_all, w_d, gate_up, t)
    grad_gu = dg(normed_mlp, gu_low, TN).astype(BF)
    mlp_back = mm_nt(gu_low, w_gu, "mlp_back")
    mlp_back, _ = after((mlp_back, grad_gu))
    grad_down, grad_gu = scatter(grad_down), scatter(grad_gu)
    middle_back, mlp_gain_part, middle_all = comm_call(
        ring(middle_back_kernel, wide, narrow), "middle_back", 3, (full_rows, sds((1, dim), F32), all_low),
        [HB, VM, VM, VM], (VM, VM, HB), [row_buf, *sum_s, *spread_s],
        mlp_back, middle, mlp_gain[None], grad_own,
    )
    back, delta = attn_back(middle_all, w_attn, attended, (qw + 2 * kw) // qw, groups, hd)
    query_back, dkv = attn_bwd(bwd_tab, queries, back, kv, lse, delta, groups, hd, block)
    hidden_late, dkv, grad_down = after((hidden_low, dkv, grad_down))
    layer_output, kv_sum = comm_call(
        ring(output_kernel, wide, narrow), "output_rows", 4, (low_rows, sds((all_rows, 2 * kw), BF)),
        [HB, VM, HB], (VM, VM),
        [row_buf, DMA((2,)), *sum_s, *line_sum_bufs(chips, all_rows, 2 * kw), *line_sum_sems(chips)],
        dg(hidden_late, w_d, NT).astype(BF), middle, dkv,
    )
    q_low, query_gain_part = q_back(query_back, proj, cos_table, sin_table, qg)
    qkv_low, normed_back, key_gain_part = kv_back(q_low, proj, cos_table, sin_table, kg, w_attn, kv_sum, kw)
    grad_attn = attn_grads(normed_all, qkv_low, middle_all, attended_low)
    normed_back, grad_gu = after((normed_back, grad_gu))
    half = sds((dim // wide, ff), F32)
    grad_gate, grad_up = plain(
        unweave_kernel, "unweave", (1,), [whole(grad_gu.shape)], [whole(half.shape)] * 2, [half, half], 0, grad_gu.size * 6, grad_gu
    )
    gains = jnp.concatenate([jnp.zeros((1, dim), F32), mlp_gain_part, query_gain_part, key_gain_part], axis=1)
    gvec = sds(gains.shape, F32)
    input_grad, gain_sums, grad_qkv = comm_call(
        ring(input_back_kernel, wide, narrow), "input_back", 5, (full_rows, gvec, sds((dim // wide, 2 * qw + 2 * kw), F32)),
        [HB, VM, VM, VM, VM, HB], (VM, VM, VM),
        [row_buf, row_buf, pltpu.VMEM((narrow, *gains.shape), F32), pltpu.VMEM((wide, *gains.shape), F32),
         DMA((2,)), DMA((narrow,)), DMA((narrow,)), DMA((wide,)), DMA((wide,)),
         *sum_s, *line_sum_bufs(chips, dim // wide, 2 * qw + 2 * kw)[:4], *line_sum_sems(chips)],
        normed_back, own, attn_gain[None], middle_back, gains, grad_attn,
    )
    g = gain_sums[0]
    return (
        layer_output, input_grad,
        grad_qkv[:, :qw], grad_qkv[:, qw : qw + kw], grad_qkv[:, qw + kw : qw + 2 * kw],
        grad_qkv[:, qw + 2 * kw :].T, grad_gate, grad_up,
        grad_down.T.astype(F32),
        g[:dim], g[dim : 2 * dim], g[2 * dim : 2 * dim + hd], g[2 * dim + hd :],
    )


def solution(mesh):
    rows = P(("wide", "narrow"), None)
    weight, turned = P("wide", "narrow"), P("narrow", "wide")
    return jax.shard_map(
        functools.partial(per_device, mesh.shape["wide"], mesh.shape["narrow"]),
        mesh=mesh,
        in_specs=(rows, weight, weight, weight, turned, weight, weight, turned, P(), P(), P(), P(), rows),
        out_specs=(rows, rows, weight, weight, weight, turned, weight, weight, turned, P(), P(), P(), P()),
        check_vma=False,
    )
```

```python
import functools
import math

import jax
import jax.numpy as jnp
from jax import lax
from jax.experimental import pallas as pl
from jax.experimental.pallas import tpu as pltpu
from jax.sharding import PartitionSpec as P

EPSILON = 1e-06
MASKED = -1e30
F32 = jnp.float32
BF = jnp.bfloat16
MESH = pl.DeviceIdType.MESH
NT = (((1,), (1,)), ((), ()))
NN = (((1,), (0,)), ((), ()))
TN = (((0,), (0,)), ((), ()))


def dg(a, b, dims):
    return lax.dot_general(a, b, dims, preferred_element_type=F32)
DMA = pltpu.SemaphoreType.DMA


class Place:
    def __init__(self, wide, narrow):
        self.W, self.N = wide, narrow
        self.C, self.half = wide // 2, narrow // 2
        self.w, self.n = lax.axis_index("wide"), lax.axis_index("narrow")
        self.k, self.c = self.w // 2, lax.rem(self.w, 2)
        self.far = 2 * (self.C - 1 - self.k) + 1
        self.moves = (self.c == 1) & ((self.k < self.C // 2 - 1) | (self.k > self.C // 2))
        late = (self.n >= self.half).astype(jnp.int32)
        self.group = lax.rem(self.c + late, 2)
        self.slot = jnp.where(self.group == 0, self.n, lax.rem(self.n + self.half, self.N))

    def owner(self, j):
        core = 1 if j >= self.half else 0
        n = jnp.where(self.c == 0, j, (j + self.half) % self.N)
        return core, n

    def owner_is_me(self, j):
        core, n = self.owner(j)
        return (self.c == core) & (self.n == n)


def enter(p, line=False, ring=False):
    barrier = pltpu.get_barrier_semaphore()

    def greet(device):
        pl.semaphore_signal(barrier, inc=1, device_id=device, device_id_type=MESH)

    for core in range(2):
        for n in range(p.N):

            @pl.when((p.c != core) | (p.n != n))
            def _():
                greet((2 * p.k + core, n))

    peers = 2 * p.N - 1
    if line or ring:
        for k in range(p.C):

            @pl.when(p.k != k)
            def _():
                greet((2 * k + p.c, p.n))
                if ring:
                    greet((2 * k + 1 - p.c, p.n))

        peers += (2 if ring else 1) * (p.C - 1)
    pl.semaphore_wait(barrier, peers)


def swap_rows(p, src, dst, send_sem, recv_sem):
    return pltpu.make_async_remote_copy(
        src_ref=src, dst_ref=dst, send_sem=send_sem, recv_sem=recv_sem, device_id=(p.far, p.n), device_id_type=MESH
    )


def slot_of(p, n, group):
    return jnp.where(group == 0, n, lax.rem(n + p.half, p.N))


def neighbours(p):
    return p.n + 1 - 2 * lax.rem(p.n, 2), lax.rem(p.n + 2, 4), 3 - p.n


def to(src, dst, send, recv, wide, narrow):
    return pltpu.make_async_remote_copy(
        src_ref=src, dst_ref=dst, send_sem=send, recv_sem=recv, device_id=(wide, narrow), device_id_type=MESH
    )


def spread_sems(narrow):
    return [DMA((narrow, 2)), DMA((narrow, 2)), DMA((2,)), DMA((2,))]


def spread_start(p, src, gathered, rows, send, recv, local, onward):
    half = rows // 2
    view = lambda i: gathered.at[pl.ds(pl.multiple_of(p.slot * rows + i * half, half), half)]
    part = lambda i: src.at[pl.ds(i * half, half)]
    mine = p.group == p.c
    square = p.N == 4
    if square:
        nx, ny, _ = neighbours(p)
        targets = [(nx, (0, 1)), (ny, (1, 0))]
        order = [(t, q, i) for q in range(2) for t, halves in targets for i in (halves[q],)]
        for t, q, i in order:
            at = 0 if t is nx else 1
            to(part(i), view(i), send.at[at, i], recv.at[p.slot, i], 2 * p.k + p.group, t).start()
    else:
        for t in range(p.N):

            @pl.when(p.n != t)
            def _():
                for i in range(2):
                    to(part(i), view(i), send.at[t, i], recv.at[p.slot, i], 2 * p.k + p.group, t).start()

    @pl.when(mine)
    def _():
        for i in range(2):
            pltpu.make_async_copy(part(i), view(i), local.at[i]).start()

    @pl.when(jnp.logical_not(mine))
    def _():
        for i in range(2):
            to(part(i), view(i), local.at[i], recv.at[p.slot, i], 2 * p.k + p.group, p.n).start()


def spread_pass(p, src, gathered, rows, send, recv, local, onward):
    if p.N == 4:
        half = rows // 2
        piece = src.at[pl.ds(0, half)]
        nx, ny, _ = neighbours(p)
        for i, (n, other) in enumerate(((nx, ny), (ny, nx))):
            j = slot_of(p, n, p.c)
            here = gathered.at[pl.ds(pl.multiple_of(j * rows + i * half, half), half)]
            pltpu.make_async_copy(piece, here, recv.at[j, i]).wait()
            to(here, here, onward.at[i], recv.at[j, i], p.w, other).start()


def spread_end(p, src, gathered, rows, send, recv, local, onward):
    half = rows // 2
    piece = src.at[pl.ds(0, half)]
    mine = p.group == p.c
    at = lambda j, i: gathered.at[pl.ds(pl.multiple_of(j * rows + i * half, half), half)]

    def arrive(j, i):
        pltpu.make_async_copy(piece, at(j, i), recv.at[j, i]).wait()

    if p.N == 4:
        nx, ny, nd = neighbours(p)
        jx, jy, jd = (slot_of(p, n, p.c) for n in (nx, ny, nd))
        arrive(jx, 1)
        arrive(jy, 0)
        arrive(jd, 0)
        arrive(jd, 1)
        for i in range(2):
            pltpu.make_async_copy(piece, at(0, 0), onward.at[i]).wait()
            for t in range(2):
                pltpu.make_async_copy(piece, at(0, 0), send.at[t, i]).wait()
    else:
        for t in range(p.N):

            @pl.when(p.n != t)
            def _():
                for i in range(2):
                    pltpu.make_async_copy(piece, at(0, 0), send.at[t, i]).wait()
                    arrive(slot_of(p, t, p.c), i)

    for i in range(2):
        pltpu.make_async_copy(piece, at(0, 0), local.at[i]).wait()

    @pl.when(jnp.logical_not(mine))
    def _():
        arrive(slot_of(p, p.n, p.c), 0)
        arrive(slot_of(p, p.n, p.c), 1)


def sum_bufs(narrow, rows, dim):
    if narrow == 4:
        half = pltpu.VMEM((2, 2, rows, dim // 2), BF)
        return [half, half, pltpu.VMEM((2, rows, dim), BF)]
    return [pltpu.VMEM((narrow, rows, dim), BF)]


def sum_sems(narrow):
    if narrow == 4:
        return [DMA((2, 2)), DMA((2, 2)), DMA((2, 2)), DMA((4,)), DMA((4,))]
    return [DMA((narrow,)), DMA((narrow,)), DMA]


def pieces(p, part, rows, dim):
    half = dim // 2
    return lambda j, i: part.at[pl.ds(pl.multiple_of(j * rows, rows), rows), pl.ds(i * half, half)]


def sum_start(p, part, rows, dim, bufs, sems):
    if p.N != 4:
        (got,), (send, recv, local) = bufs, sems
        for j in range(p.N):
            core, n = p.owner(j)
            mine = p.owner_is_me(j)
            src = part.at[pl.ds(j * rows, rows)]

            @pl.when(mine)
            def _():
                pltpu.make_async_copy(src, got.at[p.n], local).start()

            @pl.when(jnp.logical_not(mine))
            def _():
                to(src, got.at[p.n], send.at[j], recv.at[p.n], 2 * p.k + core, n).start()

        return
    own, inbox, _ = bufs
    load, send, recv, _, _ = sems
    piece = pieces(p, part, rows, dim)
    nx, ny, nd = neighbours(p)
    across, here = slot_of(p, nd, p.c), slot_of(p, p.n, p.c)
    for i, n in enumerate((nx, ny)):
        to(piece(across, i), inbox.at[i, 0], send.at[i, 0], recv.at[i, 0], p.w, n).start()
    for i, n in enumerate((ny, nx)):
        pltpu.make_async_copy(piece(slot_of(p, n, p.c), i), own.at[i, 0], load.at[i, 0]).start()
    for i, n in enumerate((nx, ny)):
        to(piece(slot_of(p, n, p.c), i), inbox.at[i, 1], send.at[i, 1], recv.at[i, 1], p.w, n).start()
        pltpu.make_async_copy(piece(here, i), own.at[i, 1], load.at[i, 1]).start()


def core_of(p, j):
    return (j >= p.half).astype(jnp.int32)


def sum_pass(p, part, rows, dim, bufs, sems):
    if p.N != 4:
        return
    own, inbox, box = bufs
    load, send, recv, send2, recv2 = sems
    piece = pieces(p, part, rows, dim)
    half = dim // 2
    nx, ny, _ = neighbours(p)
    cols = lambda i: pl.ds(i * half, half)

    def add(i, q):
        pltpu.make_async_copy(piece(0, 0), own.at[i, q], load.at[i, q]).wait()
        pltpu.make_async_copy(piece(0, 0), inbox.at[i, q], recv.at[i, q]).wait()

        def body(at):
            own[i, q, at, :] = (own[i, q, at, :].astype(F32) + inbox[i, q, at, :].astype(F32)).astype(BF)

        row_loop(rows, 64, body)

    for i, n in enumerate((ny, nx)):
        add(i, 0)
        j = slot_of(p, n, p.c)
        to(own.at[i, 0], box.at[1, :, cols(i)], send2.at[i], recv2.at[i], 2 * p.k + core_of(p, j), n).start()
    j = slot_of(p, p.n, p.c)
    keep = core_of(p, j) == p.c
    for i in range(2):
        add(i, 1)

        @pl.when(keep)
        def _():
            pltpu.make_async_copy(own.at[i, 1], box.at[0, :, cols(i)], send2.at[2 + i]).start()

        @pl.when(jnp.logical_not(keep))
        def _():
            to(own.at[i, 1], box.at[0, :, cols(i)], send2.at[2 + i], recv2.at[2 + i], 2 * p.k + core_of(p, j), p.n).start()


def sum_end(p, part, rows, dim, bufs, sems):
    if p.N != 4:
        (got,), (send, recv, local) = bufs, sems
        for t in range(p.N):
            mine = (p.group == p.c) & (p.n == t)

            @pl.when(mine)
            def _():
                pltpu.make_async_copy(part.at[pl.ds(0, rows)], got.at[t], local).wait()

            @pl.when(jnp.logical_not(mine))
            def _():
                pltpu.make_async_copy(part.at[pl.ds(0, rows)], got.at[t], recv.at[t]).wait()

        for j in range(p.N):

            @pl.when(jnp.logical_not(p.owner_is_me(j)))
            def _():
                pltpu.make_async_copy(part.at[pl.ds(j * rows, rows)], got.at[0], send.at[j]).wait()

        return
    own, inbox, box = bufs
    load, send, recv, send2, recv2 = sems
    piece = pieces(p, part, rows, dim)
    half = dim // 2
    cols = lambda i: pl.ds(i * half, half)
    for i in range(2):
        for q in range(2):
            pltpu.make_async_copy(piece(0, 0), inbox.at[i, q], send.at[i, q]).wait()
        pltpu.make_async_copy(own.at[i, 0], box.at[1, :, cols(i)], send2.at[i]).wait()
        pltpu.make_async_copy(own.at[i, 0], box.at[1, :, cols(i)], recv2.at[i]).wait()
        pltpu.make_async_copy(own.at[i, 1], box.at[0, :, cols(i)], send2.at[2 + i]).wait()

        @pl.when(p.group != p.c)
        def _():
            pltpu.make_async_copy(own.at[i, 1], box.at[0, :, cols(i)], recv2.at[2 + i]).wait()


def total(p, bufs, at):
    if p.N == 4:
        box = bufs[2]
        return box[0, at, :].astype(F32) + box[1, at, :].astype(F32)
    got = bufs[0]
    out = got[0, at, :].astype(F32)
    for t in range(1, p.N):
        out = out + got[t, at, :].astype(F32)
    return out


PARTS = 4


def line_sems(chips):
    return [DMA((2, chips, PARTS)), DMA((chips, PARTS)), DMA((chips, PARTS)), DMA((chips, PARTS)), DMA((PARTS,))]


def line_parts(p, full, rows):
    size = rows // PARTS

    def at(s, core, q=None):
        first = (2 * s + core) * rows
        if q is None:
            return full.at[pl.ds(pl.multiple_of(first, rows), rows)]
        return full.at[pl.ds(pl.multiple_of(first + q * size, size), size)]

    return at


def each_part(body):
    def one(q, carry):
        body(q)
        return carry

    lax.fori_loop(0, PARTS, one, 0)


def line_copy(p, src, dst, send, recv, k, core):
    return pltpu.make_async_remote_copy(
        src_ref=src, dst_ref=dst, send_sem=send, recv_sem=recv, device_id=(2 * k + core, p.n), device_id_type=MESH
    )


def inside(p, k):
    return (k >= 0) & (k < p.C)


def line_push(p, src, full, rows, zsend, zrecv, csend, crecv, local, q):
    size = rows // PARTS
    part = src.at[pl.ds(pl.multiple_of(q * size, size), size)]
    there = line_parts(p, full, rows)(p.k, p.c, q)
    for i, sign in enumerate((1, -1)):

        @pl.when(inside(p, p.k + sign))
        def _():
            line_copy(p, part, there, zsend.at[i, 0, q], zrecv.at[p.k, q], p.k + sign, p.c).start()

    line_copy(p, part, there, csend.at[p.k, q], crecv.at[p.k, q], p.k, 1 - p.c).start()
    pltpu.make_async_copy(part, there, local.at[q]).start()


def line_steps(p, src, full, rows, zsend, zrecv, csend, crecv, local):
    at = line_parts(p, full, rows)
    piece = src.at[pl.ds(0, rows // PARTS)]

    def at_distance(d):
        def onward(q):
            for i, sign in enumerate((1, -1)):
                s, t = p.k - sign * d, p.k + sign

                @pl.when(inside(p, s))
                def _():
                    here = at(s, p.c, q)
                    pltpu.make_async_copy(piece, here, zrecv.at[s, q]).wait()

                    @pl.when(inside(p, t))
                    def _():
                        line_copy(p, here, here, zsend.at[i, d, q], zrecv.at[s, q], t, p.c).start()

                    line_copy(p, here, here, csend.at[s, q], crecv.at[s, q], p.k, 1 - p.c).start()

        each_part(onward)

    def settle(q):
        here = at(p.k, p.c, q)
        pltpu.make_async_copy(piece, here, local.at[q]).wait()
        for s in range(p.C):
            pltpu.make_async_copy(piece, here, csend.at[s, q]).wait()
            pltpu.make_async_copy(piece, at(s, 1 - p.c, q), crecv.at[s, q]).wait()
        for i, sign in enumerate((1, -1)):
            for d in range(p.C):

                @pl.when(inside(p, p.k - sign * d) & inside(p, p.k + sign))
                def _():
                    pltpu.make_async_copy(piece, here, zsend.at[i, d, q]).wait()

    return [functools.partial(at_distance, d) for d in range(1, p.C)] + [lambda: each_part(settle)]


def line_sum_bufs(chips, rows, width):
    return [pltpu.VMEM((chips, rows, width), BF)] * 3 + [pltpu.VMEM((2, rows, width), BF), pltpu.VMEM((rows, width), F32)]


def line_sum_sems(chips):
    return [
        DMA((chips, PARTS)), DMA((chips, PARTS)), DMA((chips, PARTS)), DMA((2, chips, PARTS)), DMA((chips, PARTS)),
        DMA((2, PARTS)),
    ]


def line_sum_start(p, part, rows, bufs, sems):
    own, inbox, _, _, _ = bufs
    load, csend, crecv, _, _, _ = sems
    at = line_parts(p, part, rows)
    size = rows // PARTS

    def share(s):
        def one(q):
            here = pl.ds(pl.multiple_of(q * size, size), size)
            line_copy(p, at(s, 1 - p.c, q), inbox.at[s, here], csend.at[s, q], crecv.at[s, q], p.k, 1 - p.c).start()
            pltpu.make_async_copy(at(s, p.c, q), own.at[s, here], load.at[s, q]).start()

        each_part(one)

    for d in range(p.C - 1, 0, -1):
        for sign in (1, -1):
            s = p.k + sign * d

            @pl.when(inside(p, s))
            def _():
                share(s)

    share(p.k)


def line_sum_steps(p, part, rows, bufs, sems):
    own, inbox, relay, box, acc = bufs
    load, csend, crecv, zsend, rrecv, zrecv = sems
    size = rows // PARTS
    step = math.gcd(size, 128)
    piece = line_parts(p, part, rows)(0, 0, 0)

    def rows_of(q):
        return pl.ds(pl.multiple_of(q * size, size), size)

    def add(q, body):
        def one(j, carry):
            body(pl.ds(pl.multiple_of(q * size + j * step, step), step))
            return carry

        lax.fori_loop(0, size // step, one, 0)

    def pair(t, q):
        pltpu.make_async_copy(piece, own.at[t, rows_of(q)], load.at[t, q]).wait()
        pltpu.make_async_copy(piece, inbox.at[t, rows_of(q)], crecv.at[t, q]).wait()

    def at_distance(d):
        def onward(q):
            here = rows_of(q)
            for i, sign in enumerate((1, -1)):
                t = p.k + sign * d
                behind = inside(p, p.k - sign)

                @pl.when(inside(p, t))
                def _():
                    pair(t, q)

                    @pl.when(jnp.logical_not(behind))
                    def _():
                        def two(at):
                            own[t, at, :] = (own[t, at, :].astype(F32) + inbox[t, at, :].astype(F32)).astype(BF)

                        add(q, two)

                    @pl.when(behind)
                    def _():
                        pltpu.make_async_copy(piece, relay.at[t, here], rrecv.at[t, q]).wait()

                        def three(at):
                            both = own[t, at, :].astype(F32) + inbox[t, at, :].astype(F32)
                            own[t, at, :] = (both + relay[t, at, :].astype(F32)).astype(BF)

                        add(q, three)

                    src = own.at[t, here]
                    if d >= 2:
                        line_copy(p, src, relay.at[t, here], zsend.at[i, d, q], rrecv.at[t, q], p.k + sign, p.c).start()
                    else:
                        line_copy(p, src, box.at[i, here], zsend.at[i, d, q], zrecv.at[i, q], t, p.c).start()

        each_part(onward)

    def last(q):
        here = rows_of(q)
        pair(p.k, q)

        def first(at):
            acc[at, :] = own[p.k, at, :].astype(F32) + inbox[p.k, at, :].astype(F32)

        add(q, first)
        for i, sign in enumerate((1, -1)):

            @pl.when(inside(p, p.k - sign))
            def _():
                pltpu.make_async_copy(piece, box.at[i, here], zrecv.at[i, q]).wait()

                def more(at):
                    acc[at, :] += box[i, at, :].astype(F32)

                add(q, more)

            for d in range(1, p.C):

                @pl.when(inside(p, p.k + sign * d))
                def _():
                    pltpu.make_async_copy(piece, own.at[0, here], zsend.at[i, d, q]).wait()

        for s in range(p.C):
            pltpu.make_async_copy(piece, inbox.at[s, here], csend.at[s, q]).wait()

    return [functools.partial(at_distance, d) for d in range(p.C - 1, 0, -1)] + [lambda: each_part(last)]


def row_loop(rows, step, body):
    def one(i, carry):
        body(pl.ds(pl.multiple_of(i * step, step), step))
        return carry

    lax.fori_loop(0, rows // step, one, 0)


STEP = 64


def inv_rms(u):
    return lax.rsqrt(jnp.mean(u * u, axis=-1, keepdims=True) + EPSILON)


def swap_start(p, buf, out_ref, sems):
    @pl.when(p.moves)
    def _():
        swap_rows(p, buf, out_ref, sems.at[0], sems.at[1]).start()

    @pl.when(jnp.logical_not(p.moves))
    def _():
        out_ref[...] = buf[...]


def swap_end(p, buf, out_ref, sems):
    @pl.when(p.moves)
    def _():
        swap_rows(p, buf, out_ref, sems.at[0], sems.at[1]).wait()


def weave(gate_ref, up_ref, both_ref):
    ff = gate_ref.shape[1]
    t = math.gcd(ff, 256)
    for i in range(0, ff, t):
        both_ref[:, 2 * i : 2 * i + t] = gate_ref[:, i : i + t]
        both_ref[:, 2 * i + t : 2 * i + 2 * t] = up_ref[:, i : i + t]


def unweave_kernel(both_ref, gate_ref, up_ref):
    ff = gate_ref.shape[1]
    t = math.gcd(ff, 256)
    for i in range(0, ff, t):
        gate_ref[:, i : i + t] = both_ref[:, 2 * i : 2 * i + t].astype(F32)
        up_ref[:, i : i + t] = both_ref[:, 2 * i + t : 2 * i + 2 * t].astype(F32)


def input_kernel(
    wide, narrow, x_ref, gain_ref, shard, gate_ref, up_ref, own_ref, gathered, full, gu_ref, buf, swap, *sems
):
    p = Place(wide, narrow)
    rows = x_ref.shape[0]
    spread, line = sems[:4], (shard, full, shard.shape[0], *sems[4:])
    enter(p, line=True)

    @pl.when(p.moves)
    def _():
        swap_rows(p, x_ref, own_ref, swap.at[0], swap.at[1]).start()

    each_part(lambda q: line_push(p, *line, q))
    *steps, end = line_steps(p, *line)

    def share():
        def body(at):
            u = own_ref[at, :].astype(F32)
            buf[at, :] = (u * inv_rms(u) * gain_ref[...]).astype(BF)

        row_loop(rows, STEP, body)
        spread_start(p, buf, gathered, rows, *spread)

    @pl.when(jnp.logical_not(p.moves))
    def _():
        own_ref[...] = x_ref[...]
        share()

    weave(gate_ref, up_ref, gu_ref)
    steps[0]()

    @pl.when(p.moves)
    def _():
        swap_rows(p, x_ref, own_ref, swap.at[0], swap.at[1]).wait()
        share()

    for step in steps[1:-1]:
        step()
    spread_pass(p, buf, gathered, rows, *spread)
    steps[-1]()
    spread_end(p, buf, gathered, rows, *spread)
    end()


def turn(u):
    return pltpu.roll(u, u.shape[-1] // 2, 1)


def qkv_kernel(
    wide, narrow, qw, kw, fold, g_ref, x_ref, w_ref, cos_ref, sin_ref, qg_ref, kg_ref,
    own_ref, gathered, full, qproj_ref, kproj_ref, q_ref, kv_ref, w_buf, load, swap, *sems,
):
    p = Place(wide, narrow)
    rows = g_ref.shape[0]
    hd = cos_ref.shape[1]
    all_rows = x_ref.shape[0]
    size = all_rows // PARTS
    spread, line = sems[:4], (kv_ref, full, all_rows, *sems[4:])
    weights = pltpu.make_async_copy(w_ref.at[:, pl.ds(0, w_buf.shape[1])], w_buf, load)
    weights.start()
    enter(p, line=True)

    @pl.when(p.moves)
    def _():
        swap_rows(p, g_ref, own_ref, swap.at[0], swap.at[1]).start()

    @pl.when(jnp.logical_not(p.moves))
    def _():
        own_ref[...] = g_ref[...]
        spread_start(p, own_ref, gathered, rows, *spread)

    def project(q):
        at = pl.ds(pl.multiple_of(q * size, size), size)
        y = dg(x_ref[at, :], w_buf[...], NN)
        cos, sin = cos_ref[at, :], sin_ref[at, :]
        qproj_ref[at, :] = y[:, :qw]
        kproj_ref[at, :] = y[:, qw : qw + kw]

        def head(lo, gain):
            u = y[:, lo : lo + hd]
            v = u * inv_rms(u) * gain
            return v * cos + turn(v) * sin

        for h in range(kw // hd):
            kv_ref[at, 2 * h * hd : (2 * h + 1) * hd] = head(qw + h * hd, kg_ref[...]).astype(BF)
            kv_ref[at, (2 * h + 1) * hd : (2 * h + 2) * hd] = y[:, qw + kw + h * hd : qw + kw + (h + 1) * hd].astype(BF)
        line_push(p, *line, q)
        for h in range(qw // hd):
            q_ref[at, h * hd : (h + 1) * hd] = (head(h * hd, qg_ref[...]) * fold).astype(BF)

    weights.wait()
    each_part(project)
    *steps, end = line_steps(p, *line)
    steps[0]()

    @pl.when(p.moves)
    def _():
        swap_rows(p, g_ref, own_ref, swap.at[0], swap.at[1]).wait()
        spread_start(p, own_ref, gathered, rows, *spread)

    for step in steps[1:-1]:
        step()
    spread_pass(p, own_ref, gathered, rows, *spread)
    steps[-1]()
    spread_end(p, own_ref, gathered, rows, *spread)
    end()


def middle_kernel(wide, narrow, part, own_ref, gain_ref, mid_ref, gathered, buf, *refs):
    p = Place(wide, narrow)
    rows, dim = own_ref.shape
    bufs, sems, spread = split_refs(narrow, refs)
    enter(p)
    sum_start(p, part, rows, dim, bufs, sems)
    sum_pass(p, part, rows, dim, bufs, sems)
    sum_end(p, part, rows, dim, bufs, sems)

    def body(at):
        u = own_ref[at, :].astype(F32) + total(p, bufs, at)
        mid_ref[at, :] = u
        buf[at, :] = (u * inv_rms(u) * gain_ref[...]).astype(BF)

    row_loop(rows, STEP, body)
    spread_start(p, buf, gathered, rows, *spread)
    spread_pass(p, buf, gathered, rows, *spread)
    spread_end(p, buf, gathered, rows, *spread)


def split_refs(narrow, refs):
    bufs, sems = (3, 5) if narrow == 4 else (1, 3)
    return refs[:bufs], refs[bufs : bufs + sems], refs[bufs + sems :]


def norm_back(u, gain, cot):
    r = inv_rms(u)
    a = cot * gain
    du = r * a - u * (r * r * r) * jnp.mean(a * u, axis=-1, keepdims=True)
    return du, jnp.sum(cot * u * r, axis=0, keepdims=True)


def middle_back_kernel(
    wide, narrow, part, mid_ref, gain_ref, grad_ref, hidden, w_ref, back_ref, dgain_ref, gathered, next_ref,
    buf, h_buf, w_buf, load, *refs
):
    p = Place(wide, narrow)
    rows, dim = mid_ref.shape
    bufs, sems, spread = split_refs(narrow, refs)
    loads = [pltpu.make_async_copy(hidden, h_buf, load.at[0]), pltpu.make_async_copy(w_ref, w_buf, load.at[1])]
    enter(p)
    sum_start(p, part, rows, dim, bufs, sems)
    for copy in loads:
        copy.start()
    dgain_ref[...] = jnp.zeros_like(dgain_ref)
    sum_pass(p, part, rows, dim, bufs, sems)
    sum_end(p, part, rows, dim, bufs, sems)

    def body(at):
        du, dgain = norm_back(mid_ref[at, :], gain_ref[...], total(p, bufs, at))
        back = grad_ref[at, :].astype(F32) + du
        back_ref[at, :] = back
        buf[at, :] = back.astype(BF)
        dgain_ref[...] += dgain

    row_loop(rows, STEP, body)
    spread_start(p, buf, gathered, rows, *spread)
    for copy in loads:
        copy.wait()

    def down(at):
        next_ref[at, :] = dg(h_buf[at, :], w_buf[...], NT).astype(BF)

    row_loop(next_ref.shape[0], 256, down)
    spread_pass(p, buf, gathered, rows, *spread)
    spread_end(p, buf, gathered, rows, *spread)


def share_start(me, count, here, slots, sends, recvs, device):
    slots[me] = here[...]
    for t in range(count):

        @pl.when(me != t)
        def _():
            wide_at, narrow_at = device(t)
            to(here, slots.at[me], sends.at[t], recvs.at[me], wide_at, narrow_at).start()


def share_end(me, count, here, slots, sends, recvs):
    for t in range(count):

        @pl.when(me != t)
        def _():
            pltpu.make_async_copy(here, slots.at[t], sends.at[t]).wait()
            pltpu.make_async_copy(here, slots.at[t], recvs.at[t]).wait()

    out = slots[0]
    for t in range(1, count):
        out = out + slots[t]
    here[...] = out


def head_back(cot, u, gain, cos, sin):
    cot = cot * cos - turn(cot) * sin
    return norm_back(u, gain, cot)


def output_kernel(
    wide, narrow, part, mid_ref, dkv, dq, qproj, cos_ref, sin_ref, g_ref, x_ref, m_ref, a_ref,
    out_ref, kv_ref, low_ref, dgain_ref, wgrad_ref, buf, dq_buf, u_buf, x_buf, m_buf, a_buf, load, swap, *refs
):
    p = Place(wide, narrow)
    rows, dim = mid_ref.shape
    kv_rows = kv_ref.shape[0]
    width = low_ref.shape[1]
    hd = cos_ref.shape[1]
    bufs, sems, line = split_refs(narrow, refs)
    sums = (part, rows, dim, bufs, sems)
    chain = (p, dkv, kv_rows, line[:5], line[5:])
    pairs = ((dq, dq_buf), (qproj, u_buf), (x_ref, x_buf), (m_ref, m_buf), (a_ref, a_buf))
    loads = [pltpu.make_async_copy(src, dst, load.at[i]) for i, (src, dst) in enumerate(pairs)]
    enter(p, line=True)
    line_sum_start(*chain)
    sum_start(p, *sums)
    for copy in loads:
        copy.start()
    first, *steps, last = line_sum_steps(*chain)
    first()
    dgain_ref[...] = jnp.zeros_like(dgain_ref)
    for copy in loads[:2]:
        copy.wait()

    def through_heads(at):
        for h in range(width // hd):
            mine = slice(h * hd, (h + 1) * hd)
            du, dgain = head_back(dq_buf[at, mine], u_buf[at, mine], g_ref[...], cos_ref[at, :], sin_ref[at, :])
            low_ref[at, mine] = du.astype(BF)
            dgain_ref[...] += dgain

    row_loop(low_ref.shape[0], 128, through_heads)
    for copy in loads[2:]:
        copy.wait()

    def grads(first_tile, last_tile):
        def one(i, carry):
            at = pl.ds(pl.multiple_of(i * 256, 256), 256)
            wgrad_ref[at, :width] = dg(x_buf[:, at], low_ref[...], TN).astype(BF)
            wgrad_ref[at, width:] = dg(m_buf[:, at], a_buf[...], TN).astype(BF)
            return carry

        lax.fori_loop(first_tile, last_tile, one, 0)

    tiles = dim // 256
    grads(0, tiles // 2)
    sum_pass(p, *sums)
    steps[0]()
    sum_end(p, *sums)

    def body(at):
        buf[at, :] = (mid_ref[at, :] + total(p, bufs, at)).astype(BF)

    row_loop(rows, STEP, body)
    swap_start(p, buf, out_ref, swap)
    grads(tiles // 2, tiles)
    for step in steps[1:]:
        step()
    last()
    row_loop(kv_rows, 128, lambda at: kv_ref.__setitem__((at, slice(None)), line[4][at, :].astype(BF)))
    swap_end(p, buf, out_ref, swap)


def input_back_kernel(
    wide, narrow, qw, kw, own_ref, gain_ref, back_ref, gains_ref, wgrad, q_ref, kv_ref, proj_ref, cos_ref, sin_ref, kg_ref,
    w_ref, x_ref, out_ref, gsum_ref, wsum_ref, kvsum_ref,
    buf, far_buf, gbuf, gbuf2, low, part, kvgrad, w_buf, load, swap, gsend, grecv, gsend2, grecv2, *refs,
):
    p = Place(wide, narrow)
    rows, dim = own_ref.shape
    hd = cos_ref.shape[1]
    all_rows = x_ref.shape[0]
    w_rows = wsum_ref.shape[0]
    bufs, sems, line = split_refs(narrow, refs)
    sums = (part, rows, dim, bufs, sems)
    first_line = (p, wgrad, w_rows, (*line[:4], wsum_ref), line[4:10])
    second_line = (p, kvgrad, w_rows, (*line[10:14], kvsum_ref), line[14:])
    weights = pltpu.make_async_copy(w_ref.at[:, pl.ds(0, w_buf.shape[1])], w_buf, load)
    weights.start()
    enter(p, ring=True)
    line_sum_start(*first_line)
    gsum_ref[...] = gains_ref[...]
    size = min(all_rows, 256)
    weights.wait()

    def through_heads(at):
        low[at, :qw] = q_ref[at, :]
        for h in range(kw // hd):
            key = slice(2 * h * hd, (2 * h + 1) * hd)
            value = slice((2 * h + 1) * hd, (2 * h + 2) * hd)
            mine = slice(qw + h * hd, qw + (h + 1) * hd)
            du, dgain = head_back(
                kv_ref[at, key].astype(F32), proj_ref[at, h * hd : (h + 1) * hd], kg_ref[...], cos_ref[at, :], sin_ref[at, :]
            )
            low[at, mine] = du.astype(BF)
            low[at, qw + kw + h * hd : qw + kw + (h + 1) * hd] = kv_ref[at, value]
            gsum_ref[:, 2 * dim + hd :] += dgain
        part[at, :] = dg(low[at, :], w_buf[...], NT).astype(BF)

    row_loop(all_rows, size, through_heads)
    sum_start(p, *sums)
    first = line_sum_steps(*first_line)
    first[0]()

    def key_grads(at):
        kvgrad[at, :] = dg(x_ref[:, at], low[:, qw:], TN).astype(BF)

    row_loop(dim, 256, key_grads)
    line_sum_start(*second_line)
    second = line_sum_steps(*second_line)
    first[1]()
    sum_pass(p, *sums)
    second[0]()
    for step in first[2:-1]:
        step()
    sum_end(p, *sums)

    def body(at):
        du, dgain = norm_back(own_ref[at, :].astype(F32), gain_ref[...], total(p, bufs, at))
        grad = back_ref[at, :] + du
        out_ref[at, :] = grad
        buf[at, :] = grad.astype(BF)
        gsum_ref[:, :dim] += dgain

    row_loop(rows, STEP, body)

    @pl.when(p.moves)
    def _():
        swap_rows(p, buf, far_buf, swap.at[0], swap.at[1]).start()

    share_start(p.n, narrow, gsum_ref, gbuf, gsend, grecv, lambda t: (p.w, t))
    second[1]()
    first[-1]()
    share_end(p.n, narrow, gsum_ref, gbuf, gsend, grecv)
    share_start(p.w, wide, gsum_ref, gbuf2, gsend2, grecv2, lambda t: (t, p.n))
    for step in second[2:]:
        step()
    share_end(p.w, wide, gsum_ref, gbuf2, gsend2, grecv2)

    @pl.when(p.moves)
    def _():
        swap_rows(p, buf, far_buf, swap.at[0], swap.at[1]).wait()
        row_loop(rows, STEP, lambda at: out_ref.__setitem__((at, slice(None)), far_buf[at, :].astype(F32)))


VM = pl.BlockSpec(memory_space=pltpu.VMEM)


HB = pl.BlockSpec(memory_space=pl.ANY)


def comm_call(kernel, name, cid, out_shape, in_specs, out_specs, scratch, *args):
    return pl.pallas_call(
        kernel,
        out_shape=out_shape,
        in_specs=in_specs,
        out_specs=out_specs,
        scratch_shapes=scratch,
        compiler_params=pltpu.CompilerParams(collective_id=cid, has_side_effects=True, vmem_limit_bytes=60 << 20),
        cost_estimate=pl.CostEstimate(flops=0, bytes_accessed=160_000_000, transcendentals=0),
        name=name,
    )(*args)


def sds(shape, kind):
    return jax.ShapeDtypeStruct(shape, kind)


def plain(kernel, name, grid, in_specs, out_specs, out_shape, flops, nbytes, *args, scratch=(), aliases=None):
    return pl.pallas_call(
        kernel,
        out_shape=out_shape,
        grid=grid,
        in_specs=in_specs,
        out_specs=out_specs,
        scratch_shapes=scratch,
        input_output_aliases=aliases or {},
        compiler_params=pltpu.CompilerParams(vmem_limit_bytes=52 << 20),
        cost_estimate=pl.CostEstimate(flops=flops, bytes_accessed=nbytes, transcendentals=0),
        name=name,
    )(*args)


def whole(shape):
    return pl.BlockSpec(shape, lambda *i: (0,) * len(shape), pipeline_mode=pl.Buffered(1))


def by_rows(tm, width):
    return pl.BlockSpec((tm, width), lambda i: (i, 0))


def mlp_fwd_kernel(x_ref, w_ref, gu_ref, h_ref):
    t = h_ref.shape[1]
    y = dg(x_ref[...], w_ref[...], NN)
    gate, up = y[:, :t], y[:, t:]
    gu_ref[...] = y
    h_ref[...] = (gate * jax.nn.sigmoid(gate) * up).astype(BF)


def mlp_fwd(x, w, t):
    rows, dim = x.shape
    ff2 = w.shape[1]
    return plain(
        mlp_fwd_kernel, "mlp_fwd", (ff2 // (2 * t),),
        [whole((rows, dim)), pl.BlockSpec((dim, 2 * t), lambda i: (0, i))],
        [pl.BlockSpec((rows, 2 * t), lambda i: (0, i)), pl.BlockSpec((rows, t), lambda i: (0, i))],
        (sds((rows, ff2), F32), sds((rows, ff2 // 2), BF)),
        2 * rows * dim * ff2, rows * dim * 2 + dim * ff2 * 2 + rows * ff2 * 5, x, w,
    )


def mlp_bwd_kernel(g_ref, w_ref, gu_ref, out_ref):
    t = w_ref.shape[1]
    hb = dg(g_ref[...], w_ref[...], NN)
    gate, up = gu_ref[:, :t], gu_ref[:, t:]
    s = jax.nn.sigmoid(gate)
    gs = hb * s
    out_ref[:, :t] = (gs * up * (1.0 + gate * (1.0 - s))).astype(BF)
    out_ref[:, t:] = (gs * gate).astype(BF)


def mlp_bwd(g, w, gu, t):
    rows, dim = g.shape
    ff = w.shape[1]
    return plain(
        mlp_bwd_kernel, "mlp_bwd", (ff // t,),
        [whole((rows, dim)), pl.BlockSpec((dim, t), lambda i: (0, i)), pl.BlockSpec((rows, 2 * t), lambda i: (0, i))],
        pl.BlockSpec((rows, 2 * t), lambda i: (0, i)), sds((rows, 2 * ff), BF),
        2 * rows * dim * ff, rows * dim * 2 + dim * ff * 2 + rows * ff * 12, g, w, gu,
    )


def nt_kernel(a_ref, b_ref, o_ref):
    o_ref[...] = dg(a_ref[...], b_ref[...], NT).astype(BF)


def mm_nt(a, b, name, tn=256):
    rows, depth = a.shape
    cols = b.shape[0]
    return plain(
        nt_kernel, name, (cols // tn,), [whole((rows, depth)), by_rows(tn, depth)],
        pl.BlockSpec((rows, tn), lambda i: (0, i)), sds((rows, cols), BF),
        2 * rows * cols * depth, 2 * (rows * depth + cols * depth + rows * cols), a, b,
    )


def attn_back_kernel(hd, groups, x_ref, w_ref, o_ref, back_ref, delta_ref):
    back = dg(x_ref[...], w_ref[...], NN).astype(BF)
    back_ref[...] = back
    rows, width = back.shape
    lane = lax.broadcasted_iota(jnp.int32, (rows, hd), 1)
    out = jnp.zeros((rows, hd), F32)
    for h in range(width // hd):
        at = slice(h * hd, (h + 1) * hd)
        row = 8 * (h // groups) + h % groups
        out = jnp.where(lane == row, jnp.sum(back[:, at].astype(F32) * o_ref[:, at], axis=1, keepdims=True), out)
    delta_ref[...] = jnp.transpose(out)[: delta_ref.shape[0]]


def attn_back(x, w, o, at, groups, hd):
    rows, dim = x.shape
    width = o.shape[1]
    tm = 256
    stats = 8 * width // (groups * hd)
    return plain(
        functools.partial(attn_back_kernel, hd, groups), "attn_back", (rows // tm,),
        [by_rows(tm, dim), pl.BlockSpec((dim, width), lambda i: (0, at), pipeline_mode=pl.Buffered(1)), by_rows(tm, width)],
        [by_rows(tm, width), pl.BlockSpec((stats, tm), lambda i: (0, i))], [sds((rows, width), BF), sds((stats, rows), F32)],
        2 * rows * dim * width, 2 * (rows * dim + dim * width) + rows * width * 6, x, w, o,
    )


def fwd_kernel(groups, hd, tab, q_ref, kv_ref, o_ref, low_ref, lse_ref, acc, lsum):
    s = pl.program_id(1)
    block = q_ref.shape[0]
    diag, first, last = tab[2, s], tab[3, s], tab[4, s]

    @pl.when(first == 1)
    def _():
        acc[...] = jnp.zeros_like(acc)
        lsum[...] = jnp.zeros_like(lsum)

    def work(masked):
        k, v = kv_ref[:, :hd], kv_ref[:, hd:]
        for g in range(groups):
            at = slice(g * hd, (g + 1) * hd)
            scores = dg(q_ref[:, at], k, NT)
            if masked:
                row = lax.broadcasted_iota(jnp.int32, scores.shape, 0)
                col = lax.broadcasted_iota(jnp.int32, scores.shape, 1)
                scores = jnp.where(col <= row, scores, MASKED)
            probs = jnp.exp2(scores)
            part = probs[:, :128]
            for j in range(1, block // 128):
                part = part + probs[:, j * 128 : (j + 1) * 128]
            lsum[g] += part
            acc[:, at] += dg(probs.astype(BF), v, NN)

    @pl.when(diag == 0)
    def _():
        work(False)

    @pl.when(diag == 1)
    def _():
        work(True)

    @pl.when(last == 1)
    def _():
        lane = lax.broadcasted_iota(jnp.int32, (block, 128), 1)
        lse = jnp.zeros((block, 128), F32)
        for g in range(groups):
            at = slice(g * hd, (g + 1) * hd)
            l = jnp.sum(lsum[g], axis=1, keepdims=True)
            out = acc[:, at] / l
            o_ref[:, at] = out
            low_ref[:, at] = out.astype(BF)
            lse = jnp.where(lane == g, jnp.log2(l), lse)
        lse_ref[...] = jnp.transpose(lse)[: lse_ref.shape[0]]


def attn_fwd(tab, q, kv, groups, hd, block):
    rows, width = q.shape
    gw = groups * hd
    heads = width // gw
    steps = tab.shape[1]
    mine = pl.BlockSpec((block, gw), lambda h, s, t: (t[0, s], h))
    return pl.pallas_call(
        functools.partial(fwd_kernel, groups, hd),
        out_shape=(sds((rows, width), F32), sds((rows, width), BF), sds((8 * heads, rows), F32)),
        grid_spec=pltpu.PrefetchScalarGridSpec(
            num_scalar_prefetch=1,
            grid=(heads, steps),
            in_specs=[mine, pl.BlockSpec((block, 2 * hd), lambda h, s, t: (t[1, s], h))],
            out_specs=[mine, mine, pl.BlockSpec((8, block), lambda h, s, t: (h, t[0, s]))],
            scratch_shapes=[pltpu.VMEM((block, gw), F32), pltpu.VMEM((groups, block, 128), F32)],
        ),
        compiler_params=pltpu.CompilerParams(vmem_limit_bytes=48 << 20),
        cost_estimate=pl.CostEstimate(
            flops=heads * steps * block * block * gw * 4,
            bytes_accessed=heads * steps * block * hd * 8,
            transcendentals=heads * steps * block * block * groups,
        ),
        name="attn_fwd",
    )(tab, q, kv)


def bwd_kernel(groups, hd, tab, q_ref, do_ref, kv_ref, lse_ref, delta_ref, zeros, dq_ref, dkv_ref, dq_sum, dkv_sum):
    s = pl.program_id(1)
    block = q_ref.shape[0]
    qi, diag, first, last = tab[0, s], tab[2, s], tab[3, s], tab[4, s]

    @pl.when(s == 0)
    def _():
        dq_sum[...] = jnp.zeros_like(dq_sum)

    @pl.when(first == 1)
    def _():
        dkv_sum[...] = jnp.zeros_like(dkv_sum)

    def work(masked):
        k, v = kv_ref[:, :hd], kv_ref[:, hd:]
        for g in range(groups):
            at = slice(g * hd, (g + 1) * hd)
            q, do = q_ref[:, at], do_ref[:, at]
            scores = dg(k, q, NT) - lse_ref[g : g + 1, :]
            if masked:
                row = lax.broadcasted_iota(jnp.int32, scores.shape, 0)
                col = lax.broadcasted_iota(jnp.int32, scores.shape, 1)
                scores = jnp.where(row <= col, scores, MASKED)
            probs = jnp.exp2(scores)
            dots = dg(v, do, NT)
            dkv_sum[:, hd:] += dg(probs.astype(BF), do, NN)
            back = (probs * (dots - delta_ref[g : g + 1, :])).astype(BF)
            dkv_sum[:, :hd] += dg(back, q, NN)
            dq_sum[qi, :, at] += dg(back, k, TN)

    @pl.when(diag == 0)
    def _():
        work(False)

    @pl.when(diag == 1)
    def _():
        work(True)

    @pl.when(last == 1)
    def _():
        dkv_ref[:, :hd] = (dkv_sum[:, :hd] * math.log(2.0)).astype(BF)
        dkv_ref[:, hd:] = dkv_sum[:, hd:].astype(BF)

    @pl.when(s == pl.num_programs(1) - 1)
    def _():
        for i in range(dq_sum.shape[0]):
            dq_ref[i * block : (i + 1) * block, :] = dq_sum[i] * hd**-0.5


def attn_bwd(tab, q, do, kv, lse, delta, zeros, groups, hd, block):
    rows, width = q.shape
    gw = groups * hd
    heads = width // gw
    steps = tab.shape[1]
    mine = pl.BlockSpec((block, gw), lambda h, s, t: (t[0, s], h))
    keys = pl.BlockSpec((block, 2 * hd), lambda h, s, t: (t[1, s], h))
    stat = pl.BlockSpec((8, block), lambda h, s, t: (h, t[0, s]))
    return pl.pallas_call(
        functools.partial(bwd_kernel, groups, hd),
        out_shape=(sds((rows, width), F32), sds(kv.shape, BF)),
        grid_spec=pltpu.PrefetchScalarGridSpec(
            num_scalar_prefetch=1,
            grid=(heads, steps),
            in_specs=[mine, mine, keys, stat, stat, HB],
            out_specs=[pl.BlockSpec((rows, gw), lambda h, s, t: (0, h)), keys],
            scratch_shapes=[pltpu.VMEM((rows // block, block, gw), F32), pltpu.VMEM((block, 2 * hd), F32)],
        ),
        input_output_aliases={6: 1},
        compiler_params=pltpu.CompilerParams(vmem_limit_bytes=48 << 20),
        cost_estimate=pl.CostEstimate(
            flops=heads * steps * block * block * gw * 10,
            bytes_accessed=heads * steps * block * hd * 16,
            transcendentals=heads * steps * block * block * groups,
        ),
        name="attn_bwd",
    )(tab, q, do, kv, lse, delta, zeros)


def middle_chip(k, chips):
    return (k == chips // 2 - 1) | (k == chips // 2)


def place(w, chips):
    k, core = w // 2, w % 2
    return 4 * k + core, jnp.where(middle_chip(k, chips), 4 * k + 3, 4 * chips - 1 - 4 * k) - core


def block_row(b, chips):
    m, k = b % 4, b // 4
    early = m < 2
    k = jnp.where(early | middle_chip(k, chips), k, chips - 1 - k)
    core = jnp.where((m == 1) | (m == 2), 1, 0)
    return 2 * (2 * k + core) + jnp.where(early, 0, 1)


def tables(w, chips):
    a, b = place(w, chips)
    count = a + b + 2
    every = jnp.arange(4 * chips + 5, dtype=jnp.int32)
    s, idle = jnp.minimum(every, count - 1), every >= count
    in_a = s <= a
    key = jnp.where(in_a, s, s - a - 1)
    diag = jnp.where(in_a, s == a, s == count - 1)
    fwd = [jnp.where(in_a, 0, 1), block_row(key, chips), jnp.where(idle, 2, diag), ~idle & (key == 0), ~idle & diag]
    less, low = jnp.minimum(a, b), jnp.where(a < b, 0, 1)
    both = s < 2 * (less + 1)
    even = s % 2 == 0
    key = jnp.where(both, s // 2, s - (less + 1))
    query = jnp.where(both & even, low, 1 - low)
    diag = key == jnp.where(query == 0, a, b)
    bwd = [query, block_row(key, chips), jnp.where(idle, 2, diag), ~idle & (~both | even), ~idle & (~both | ~even)]
    return tuple(jnp.stack([row.astype(jnp.int32) for row in rows]) for rows in (fwd, bwd))


def rotation(positions, head_dim):
    steps_half = jnp.arange(head_dim // 2).astype(F32)
    inverse = jnp.exp(steps_half * (-2.0 * math.log(1000000.0) / head_dim))
    angles = positions.astype(F32)[:, None] * inverse[None, :]
    cos, sin = jnp.cos(angles), jnp.sin(angles)
    return jnp.concatenate([cos, cos], axis=1), jnp.concatenate([-sin, sin], axis=1)


def per_device(
    wide, narrow,
    layer_input, w_query, w_key, w_value, w_output, w_gate, w_up, w_down,
    attn_gain, mlp_gain, query_gain, key_gain, out_grad,
):
    hd = query_gain.shape[0]
    rows, dim = layer_input.shape
    all_rows = narrow * rows
    chips = wide // 2
    block = all_rows // 2
    qw, kw = w_query.shape[1], w_key.shape[1]
    ff = w_gate.shape[1]
    groups = qw // kw
    kv_heads = kw // hd
    w = lax.axis_index("wide")
    fwd_tab, bwd_tab = tables(w, chips)
    first, second = place(w, chips)
    at = jnp.arange(block, dtype=jnp.int32)
    positions = jnp.concatenate([first * block + at, second * block + at])
    cos_table, sin_table = rotation(positions, hd)

    def gather(shard):
        return lax.all_gather(shard, "wide", axis=0, tiled=True)

    def scatter(grad):
        return lax.psum_scatter(grad, "wide", scatter_dimension=0, tiled=True)

    t = math.gcd(ff, 256)

    spread_s = spread_sems(narrow)
    sum_s = [*sum_bufs(narrow, rows, dim), *sum_sems(narrow)]
    row_buf = pltpu.VMEM((rows, dim), BF)
    low_rows, full_rows, all_low = sds((rows, dim), BF), sds((rows, dim), F32), sds((all_rows, dim), BF)
    ring = functools.partial
    qg, kg = query_gain[None], key_gain[None]
    after = lax.optimization_barrier

    in_scratch = [DMA((2,)), *spread_s, *line_sems(chips)]
    shard = jnp.concatenate([w_query, w_key, w_value, w_output.T], axis=1)
    own, normed_all, w_attn, gu_shard = comm_call(
        ring(input_kernel, wide, narrow), "input_rows", 0,
        (low_rows, all_low, sds((dim, shard.shape[1]), BF), sds((w_gate.shape[0], 2 * ff), BF)),
        [VM, VM, HB, VM, VM], (VM, HB, HB, VM), [row_buf, *in_scratch],
        layer_input, attn_gain[None], shard, w_gate, w_up,
    )
    width = qw + 2 * kw
    grad_own, grad_all, kv, query_proj, key_proj, queries = comm_call(
        ring(qkv_kernel, wide, narrow, qw, kw, hd**-0.5 * math.log2(math.e)), "qkv_rows", 1,
        (low_rows, all_low, sds((wide * all_rows, 2 * kw), BF), sds((all_rows, qw), F32),
         sds((all_rows, kw), F32), sds((all_rows, qw), BF)),
        [VM, VM, HB, VM, VM, VM, VM], (VM, HB, HB, VM, VM, VM),
        [pltpu.VMEM((all_rows, 2 * kw), BF), pltpu.VMEM((dim, width), BF), DMA, *in_scratch],
        out_grad, normed_all, w_attn, cos_table, sin_table, qg, kg,
    )
    gu_shard, w_down, kv = after((gu_shard, w_down, kv))
    w_gu, w_d = gather(gu_shard), gather(w_down.T)
    attended, attended_low, lse = attn_fwd(fwd_tab, queries, kv, groups, hd, block)
    w_o = w_attn[:, qw + 2 * kw :]
    middle, normed_mlp = comm_call(
        ring(middle_kernel, wide, narrow), "middle_rows", 2, (full_rows, all_low), [HB, VM, VM], (VM, HB),
        [row_buf, *sum_s, *spread_s], dg(attended_low, w_o, NT).astype(BF), own, mlp_gain[None],
    )
    gate_up, hidden_low = mlp_fwd(normed_mlp, w_gu, t)
    grad_down = dg(grad_all, hidden_low, TN).astype(BF)
    w_d, _, zeros = after((w_d, grad_down, jnp.zeros(kv.shape, BF)))
    gu_low = mlp_bwd(grad_all, w_d, gate_up, t)
    grad_gu = dg(normed_mlp, gu_low, TN).astype(BF)
    mlp_back = mm_nt(gu_low, w_gu, "mlp_back")
    mlp_back, _ = after((mlp_back, grad_gu))
    grad_down, grad_gu = scatter(grad_down), scatter(grad_gu)
    middle_back, mlp_gain_part, middle_all, down_part = comm_call(
        ring(middle_back_kernel, wide, narrow), "middle_back", 3, (full_rows, sds((1, dim), F32), all_low, all_low),
        [HB, VM, VM, VM, HB, HB], (VM, VM, HB, VM),
        [row_buf, pltpu.VMEM((all_rows, ff), BF), pltpu.VMEM((dim, ff), BF), DMA((2,)), *sum_s, *spread_s],
        mlp_back, middle, mlp_gain[None], grad_own, hidden_low, w_d,
    )
    back, delta = attn_back(middle_all, w_attn, attended, width // qw, groups, hd)
    query_back, dkv = attn_bwd(bwd_tab, queries, back, kv, lse, delta, zeros, groups, hd, block)
    dkv, grad_down = after((dkv, grad_down))
    layer_output, kv_sum, q_low, query_gain_part, grad_qo = comm_call(
        ring(output_kernel, wide, narrow), "output_rows", 4,
        (low_rows, sds((all_rows, 2 * kw), BF), sds((all_rows, qw), BF), sds((1, hd), F32), sds((dim, 2 * qw), BF)),
        [HB, VM, HB, HB, HB, VM, VM, VM, HB, HB, HB], (VM, VM, VM, VM, VM),
        [row_buf, pltpu.VMEM((all_rows, qw), F32), pltpu.VMEM((all_rows, qw), F32), pltpu.VMEM((all_rows, dim), BF),
         pltpu.VMEM((all_rows, dim), BF), pltpu.VMEM((all_rows, qw), BF), DMA((5,)), DMA((2,)), *sum_s,
         *line_sum_bufs(chips, all_rows, 2 * kw), *line_sum_sems(chips)],
        down_part, middle, dkv, query_back, query_proj, cos_table, sin_table, qg, normed_all, middle_all, attended_low,
    )
    kv_sum, grad_gu = after((kv_sum, grad_gu))
    half = sds((dim // wide, ff), F32)
    grad_gate, grad_up = plain(
        unweave_kernel, "unweave", (1,), [whole(grad_gu.shape)], [whole(half.shape)] * 2, [half, half], 0, grad_gu.size * 6, grad_gu
    )
    gains = jnp.concatenate([jnp.zeros((1, dim), F32), mlp_gain_part, query_gain_part, jnp.zeros((1, hd), F32)], axis=1)
    w_rows = dim // wide
    input_grad, gain_sums, grad_qo, grad_kv = comm_call(
        ring(input_back_kernel, wide, narrow, qw, kw), "input_back", 5,
        (full_rows, sds(gains.shape, F32), sds((w_rows, 2 * qw), F32), sds((w_rows, 2 * kw), F32)),
        [VM, VM, VM, VM, HB, VM, VM, VM, VM, VM, VM, HB, VM],
        (VM, VM, VM, VM),
        [row_buf, row_buf, pltpu.VMEM((narrow, *gains.shape), F32), pltpu.VMEM((wide, *gains.shape), F32),
         pltpu.VMEM((all_rows, width), BF), pltpu.VMEM((all_rows, dim), BF), pltpu.VMEM((dim, 2 * kw), BF),
         pltpu.VMEM((dim, width), BF), DMA, DMA((2,)), DMA((narrow,)), DMA((narrow,)), DMA((wide,)), DMA((wide,)), *sum_s,
         *line_sum_bufs(chips, w_rows, 2 * qw)[:4], *line_sum_sems(chips),
         *line_sum_bufs(chips, w_rows, 2 * kw)[:4], *line_sum_sems(chips)],
        own, attn_gain[None], middle_back, gains, grad_qo, q_low, kv_sum, key_proj, cos_table, sin_table, kg, w_attn, normed_all,
    )
    g = gain_sums[0]
    return (
        layer_output, input_grad,
        grad_qo[:, :qw], grad_kv[:, :kw], grad_kv[:, kw:],
        grad_qo[:, qw:].T, grad_gate, grad_up,
        grad_down.T.astype(F32),
        g[:dim], g[dim : 2 * dim], g[2 * dim : 2 * dim + hd], g[2 * dim + hd :],
    )


def solution(mesh):
    rows = P(("wide", "narrow"), None)
    weight, turned = P("wide", "narrow"), P("narrow", "wide")
    return jax.shard_map(
        functools.partial(per_device, mesh.shape["wide"], mesh.shape["narrow"]),
        mesh=mesh,
        in_specs=(rows, weight, weight, weight, turned, weight, weight, turned, P(), P(), P(), P(), rows),
        out_specs=(rows, rows, weight, weight, weight, turned, weight, weight, turned, P(), P(), P(), P()),
        check_vma=False,
    )
```

```python
import functools
import math

import jax
import jax.numpy as jnp
from jax import lax
from jax.experimental import pallas as pl
from jax.experimental.pallas import tpu as pltpu
from jax.sharding import PartitionSpec as P

EPSILON = 1e-06
MASKED = -1e30
F32 = jnp.float32
BF = jnp.bfloat16
MESH = pl.DeviceIdType.MESH
NT = (((1,), (1,)), ((), ()))
NN = (((1,), (0,)), ((), ()))
TN = (((0,), (0,)), ((), ()))


def dg(a, b, dims):
    return lax.dot_general(a, b, dims, preferred_element_type=F32)
DMA = pltpu.SemaphoreType.DMA


class Place:
    def __init__(self, wide, narrow):
        self.W, self.N = wide, narrow
        self.C, self.half = wide // 2, narrow // 2
        self.w, self.n = lax.axis_index("wide"), lax.axis_index("narrow")
        self.k, self.c = self.w // 2, lax.rem(self.w, 2)
        self.far = 2 * (self.C - 1 - self.k) + 1
        self.moves = (self.c == 1) & ((self.k < self.C // 2 - 1) | (self.k > self.C // 2))
        late = (self.n >= self.half).astype(jnp.int32)
        self.group = lax.rem(self.c + late, 2)
        self.slot = jnp.where(self.group == 0, self.n, lax.rem(self.n + self.half, self.N))

    def owner(self, j):
        core = 1 if j >= self.half else 0
        n = jnp.where(self.c == 0, j, (j + self.half) % self.N)
        return core, n

    def owner_is_me(self, j):
        core, n = self.owner(j)
        return (self.c == core) & (self.n == n)


def enter(p, line=False, ring=False):
    barrier = pltpu.get_barrier_semaphore()

    def greet(device):
        pl.semaphore_signal(barrier, inc=1, device_id=device, device_id_type=MESH)

    for core in range(2):
        for n in range(p.N):

            @pl.when((p.c != core) | (p.n != n))
            def _():
                greet((2 * p.k + core, n))

    peers = 2 * p.N - 1
    if line or ring:
        for k in range(p.C):

            @pl.when(p.k != k)
            def _():
                greet((2 * k + p.c, p.n))
                if ring:
                    greet((2 * k + 1 - p.c, p.n))

        peers += (2 if ring else 1) * (p.C - 1)
    pl.semaphore_wait(barrier, peers)


def swap_rows(p, src, dst, send_sem, recv_sem):
    return pltpu.make_async_remote_copy(
        src_ref=src, dst_ref=dst, send_sem=send_sem, recv_sem=recv_sem, device_id=(p.far, p.n), device_id_type=MESH
    )


def slot_of(p, n, group):
    return jnp.where(group == 0, n, lax.rem(n + p.half, p.N))


def neighbours(p):
    return p.n + 1 - 2 * lax.rem(p.n, 2), lax.rem(p.n + 2, 4), 3 - p.n


def to(src, dst, send, recv, wide, narrow):
    return pltpu.make_async_remote_copy(
        src_ref=src, dst_ref=dst, send_sem=send, recv_sem=recv, device_id=(wide, narrow), device_id_type=MESH
    )


def spread_sems(narrow):
    return [DMA((narrow, 2)), DMA((narrow, 2)), DMA((2,)), DMA((2,))]


def spread_start(p, src, gathered, rows, send, recv, local, onward):
    half = rows // 2
    view = lambda i: gathered.at[pl.ds(pl.multiple_of(p.slot * rows + i * half, half), half)]
    part = lambda i: src.at[pl.ds(i * half, half)]
    mine = p.group == p.c
    square = p.N == 4
    if square:
        nx, ny, _ = neighbours(p)
        targets = [(nx, (0, 1)), (ny, (1, 0))]
        order = [(t, q, i) for q in range(2) for t, halves in targets for i in (halves[q],)]
        for t, q, i in order:
            at = 0 if t is nx else 1
            to(part(i), view(i), send.at[at, i], recv.at[p.slot, i], 2 * p.k + p.group, t).start()
    else:
        for t in range(p.N):

            @pl.when(p.n != t)
            def _():
                for i in range(2):
                    to(part(i), view(i), send.at[t, i], recv.at[p.slot, i], 2 * p.k + p.group, t).start()

    @pl.when(mine)
    def _():
        for i in range(2):
            pltpu.make_async_copy(part(i), view(i), local.at[i]).start()

    @pl.when(jnp.logical_not(mine))
    def _():
        for i in range(2):
            to(part(i), view(i), local.at[i], recv.at[p.slot, i], 2 * p.k + p.group, p.n).start()


def spread_pass(p, src, gathered, rows, send, recv, local, onward):
    if p.N == 4:
        half = rows // 2
        piece = src.at[pl.ds(0, half)]
        nx, ny, _ = neighbours(p)
        for i, (n, other) in enumerate(((nx, ny), (ny, nx))):
            j = slot_of(p, n, p.c)
            here = gathered.at[pl.ds(pl.multiple_of(j * rows + i * half, half), half)]
            pltpu.make_async_copy(piece, here, recv.at[j, i]).wait()
            to(here, here, onward.at[i], recv.at[j, i], p.w, other).start()


def spread_end(p, src, gathered, rows, send, recv, local, onward, on_slot=lambda j: None):
    half = rows // 2
    piece = src.at[pl.ds(0, half)]
    mine = p.group == p.c
    at = lambda j, i: gathered.at[pl.ds(pl.multiple_of(j * rows + i * half, half), half)]

    def arrive(j, i):
        pltpu.make_async_copy(piece, at(j, i), recv.at[j, i]).wait()

    for i in range(2):
        pltpu.make_async_copy(piece, at(0, 0), local.at[i]).wait()
    here = slot_of(p, p.n, p.c)

    @pl.when(jnp.logical_not(mine))
    def _():
        arrive(here, 0)
        arrive(here, 1)

    on_slot(here)
    if p.N == 4:
        nx, ny, nd = neighbours(p)
        jx, jy, jd = (slot_of(p, n, p.c) for n in (nx, ny, nd))
        arrive(jx, 1)
        on_slot(jx)
        arrive(jy, 0)
        on_slot(jy)
        arrive(jd, 0)
        arrive(jd, 1)
        on_slot(jd)
        for i in range(2):
            pltpu.make_async_copy(piece, at(0, 0), onward.at[i]).wait()
            for t in range(2):
                pltpu.make_async_copy(piece, at(0, 0), send.at[t, i]).wait()
    else:
        for t in range(p.N):

            @pl.when(p.n != t)
            def _():
                for i in range(2):
                    pltpu.make_async_copy(piece, at(0, 0), send.at[t, i]).wait()
                    arrive(slot_of(p, t, p.c), i)
                on_slot(slot_of(p, t, p.c))


def sum_bufs(narrow, rows, dim):
    if narrow == 4:
        half = pltpu.VMEM((2, 2, rows, dim // 2), BF)
        return [half, half, pltpu.VMEM((2, rows, dim), BF)]
    return [pltpu.VMEM((narrow, rows, dim), BF)]


def sum_sems(narrow):
    if narrow == 4:
        return [DMA((2, 2)), DMA((2, 2)), DMA((2, 2)), DMA((4,)), DMA((4,))]
    return [DMA((narrow,)), DMA((narrow,)), DMA]


def pieces(p, part, rows, dim):
    half = dim // 2
    return lambda j, i: part.at[pl.ds(pl.multiple_of(j * rows, rows), rows), pl.ds(i * half, half)]


def sum_start(p, part, rows, dim, bufs, sems):
    if p.N != 4:
        (got,), (send, recv, local) = bufs, sems
        for j in range(p.N):
            core, n = p.owner(j)
            mine = p.owner_is_me(j)
            src = part.at[pl.ds(j * rows, rows)]

            @pl.when(mine)
            def _():
                pltpu.make_async_copy(src, got.at[p.n], local).start()

            @pl.when(jnp.logical_not(mine))
            def _():
                to(src, got.at[p.n], send.at[j], recv.at[p.n], 2 * p.k + core, n).start()

        return
    own, inbox, _ = bufs
    load, send, recv, _, _ = sems
    piece = pieces(p, part, rows, dim)
    nx, ny, nd = neighbours(p)
    across, here = slot_of(p, nd, p.c), slot_of(p, p.n, p.c)
    for i, n in enumerate((nx, ny)):
        to(piece(across, i), inbox.at[i, 0], send.at[i, 0], recv.at[i, 0], p.w, n).start()
    for i, n in enumerate((ny, nx)):
        pltpu.make_async_copy(piece(slot_of(p, n, p.c), i), own.at[i, 0], load.at[i, 0]).start()
    for i, n in enumerate((nx, ny)):
        to(piece(slot_of(p, n, p.c), i), inbox.at[i, 1], send.at[i, 1], recv.at[i, 1], p.w, n).start()
        pltpu.make_async_copy(piece(here, i), own.at[i, 1], load.at[i, 1]).start()


def product_bufs(narrow, rows, dim):
    shape = (4, rows, dim // 2) if narrow == 4 else (narrow * rows, dim)
    return pltpu.VMEM(shape, BF)


def sum_start_of(p, product, out, rows, dim, bufs, sems):
    half = dim // 2
    if p.N != 4:

        def one(j, carry):
            for i in range(2):
                out[pl.ds(pl.multiple_of(j * rows, rows), rows), i * half : (i + 1) * half] = product(j, i)
            return carry

        lax.fori_loop(0, p.N, one, 0)
        sum_start(p, out, rows, dim, bufs, sems)
        return
    own, inbox, _ = bufs
    _, send, recv, _, _ = sems
    nx, ny, nd = neighbours(p)
    across, jx, jy, here = (slot_of(p, n, p.c) for n in (nd, nx, ny, p.n))

    def one(t, carry):
        i = lax.rem(t, 2)
        q = lax.rem(t // 2, 2)
        beside = jnp.where(i == 0, jx, jy)
        other = jnp.where(i == 0, jy, jx)
        j = jnp.where(t < 4, jnp.where(q == 0, across, beside), jnp.where(q == 0, other, here))
        y = product(j, i)

        @pl.when(t < 4)
        def _():
            out[t] = y
            to(out.at[t], inbox.at[i, q], send.at[i, q], recv.at[i, q], p.w, jnp.where(i == 0, nx, ny)).start()

        @pl.when(t >= 4)
        def _():
            own[i, q] = y

        return carry

    lax.fori_loop(0, 8, one, 0)


def core_of(p, j):
    return (j >= p.half).astype(jnp.int32)


def sum_pass(p, part, rows, dim, bufs, sems, loaded=False):
    if p.N != 4:
        return
    own, inbox, box = bufs
    load, send, recv, send2, recv2 = sems
    piece = lambda j, i: own.at[0, 0]
    half = dim // 2
    nx, ny, _ = neighbours(p)
    cols = lambda i: pl.ds(i * half, half)

    def add(i, q):
        if not loaded:
            pltpu.make_async_copy(piece(0, 0), own.at[i, q], load.at[i, q]).wait()
        pltpu.make_async_copy(piece(0, 0), inbox.at[i, q], recv.at[i, q]).wait()

        def body(at):
            own[i, q, at, :] = (own[i, q, at, :].astype(F32) + inbox[i, q, at, :].astype(F32)).astype(BF)

        row_loop(rows, 64, body)

    for i, n in enumerate((ny, nx)):
        add(i, 0)
        j = slot_of(p, n, p.c)
        to(own.at[i, 0], box.at[1, :, cols(i)], send2.at[i], recv2.at[i], 2 * p.k + core_of(p, j), n).start()
    j = slot_of(p, p.n, p.c)
    keep = core_of(p, j) == p.c
    for i in range(2):
        add(i, 1)

        @pl.when(keep)
        def _():
            pltpu.make_async_copy(own.at[i, 1], box.at[0, :, cols(i)], send2.at[2 + i]).start()

        @pl.when(jnp.logical_not(keep))
        def _():
            to(own.at[i, 1], box.at[0, :, cols(i)], send2.at[2 + i], recv2.at[2 + i], 2 * p.k + core_of(p, j), p.n).start()


def sum_end(p, part, rows, dim, bufs, sems):
    if p.N != 4:
        (got,), (send, recv, local) = bufs, sems
        for t in range(p.N):
            mine = (p.group == p.c) & (p.n == t)

            @pl.when(mine)
            def _():
                pltpu.make_async_copy(part.at[pl.ds(0, rows)], got.at[t], local).wait()

            @pl.when(jnp.logical_not(mine))
            def _():
                pltpu.make_async_copy(part.at[pl.ds(0, rows)], got.at[t], recv.at[t]).wait()

        for j in range(p.N):

            @pl.when(jnp.logical_not(p.owner_is_me(j)))
            def _():
                pltpu.make_async_copy(part.at[pl.ds(j * rows, rows)], got.at[0], send.at[j]).wait()

        return
    own, inbox, box = bufs
    load, send, recv, send2, recv2 = sems
    piece = lambda j, i: own.at[0, 0]
    half = dim // 2
    cols = lambda i: pl.ds(i * half, half)
    for i in range(2):
        for q in range(2):
            pltpu.make_async_copy(piece(0, 0), inbox.at[i, q], send.at[i, q]).wait()
        pltpu.make_async_copy(own.at[i, 0], box.at[1, :, cols(i)], send2.at[i]).wait()
        pltpu.make_async_copy(own.at[i, 0], box.at[1, :, cols(i)], recv2.at[i]).wait()
        pltpu.make_async_copy(own.at[i, 1], box.at[0, :, cols(i)], send2.at[2 + i]).wait()

        @pl.when(p.group != p.c)
        def _():
            pltpu.make_async_copy(own.at[i, 1], box.at[0, :, cols(i)], recv2.at[2 + i]).wait()


def total(p, bufs, at):
    if p.N == 4:
        box = bufs[2]
        return box[0, at, :].astype(F32) + box[1, at, :].astype(F32)
    got = bufs[0]
    out = got[0, at, :].astype(F32)
    for t in range(1, p.N):
        out = out + got[t, at, :].astype(F32)
    return out


PARTS = 4


def line_sems(chips):
    return [DMA((2, chips, PARTS)), DMA((chips, PARTS)), DMA((chips, PARTS)), DMA((chips, PARTS)), DMA((PARTS,))]


def line_parts(p, full, rows):
    size = rows // PARTS

    def at(s, core, q=None):
        first = (2 * s + core) * rows
        if q is None:
            return full.at[pl.ds(pl.multiple_of(first, rows), rows)]
        return full.at[pl.ds(pl.multiple_of(first + q * size, size), size)]

    return at


def each_part(body):
    def one(q, carry):
        body(q)
        return carry

    lax.fori_loop(0, PARTS, one, 0)


def line_copy(p, src, dst, send, recv, k, core):
    return pltpu.make_async_remote_copy(
        src_ref=src, dst_ref=dst, send_sem=send, recv_sem=recv, device_id=(2 * k + core, p.n), device_id_type=MESH
    )


def inside(p, k):
    return (k >= 0) & (k < p.C)


def line_push(p, src, full, rows, zsend, zrecv, csend, crecv, local, q):
    size = rows // PARTS
    part = src.at[pl.ds(pl.multiple_of(q * size, size), size)]
    there = line_parts(p, full, rows)(p.k, p.c, q)
    for i, sign in enumerate((1, -1)):

        @pl.when(inside(p, p.k + sign))
        def _():
            line_copy(p, part, there, zsend.at[i, 0, q], zrecv.at[p.k, q], p.k + sign, p.c).start()

    line_copy(p, part, there, csend.at[p.k, q], crecv.at[p.k, q], p.k, 1 - p.c).start()
    pltpu.make_async_copy(part, there, local.at[q]).start()


def line_steps(p, src, full, rows, zsend, zrecv, csend, crecv, local):
    at = line_parts(p, full, rows)
    piece = src.at[pl.ds(0, rows // PARTS)]

    def at_distance(d):
        def onward(q):
            for i, sign in enumerate((1, -1)):
                s, t = p.k - sign * d, p.k + sign

                @pl.when(inside(p, s))
                def _():
                    here = at(s, p.c, q)
                    pltpu.make_async_copy(piece, here, zrecv.at[s, q]).wait()

                    @pl.when(inside(p, t))
                    def _():
                        line_copy(p, here, here, zsend.at[i, d, q], zrecv.at[s, q], t, p.c).start()

                    line_copy(p, here, here, csend.at[s, q], crecv.at[s, q], p.k, 1 - p.c).start()

        each_part(onward)

    def settle(q):
        here = at(p.k, p.c, q)
        pltpu.make_async_copy(piece, here, local.at[q]).wait()
        for s in range(p.C):
            pltpu.make_async_copy(piece, here, csend.at[s, q]).wait()
            pltpu.make_async_copy(piece, at(s, 1 - p.c, q), crecv.at[s, q]).wait()
        for i, sign in enumerate((1, -1)):
            for d in range(p.C):

                @pl.when(inside(p, p.k - sign * d) & inside(p, p.k + sign))
                def _():
                    pltpu.make_async_copy(piece, here, zsend.at[i, d, q]).wait()

    return [functools.partial(at_distance, d) for d in range(1, p.C)] + [lambda: each_part(settle)]


def line_sum_bufs(chips, rows, width):
    return [pltpu.VMEM((chips, rows, width), BF)] * 3 + [pltpu.VMEM((2, rows, width), BF), pltpu.VMEM((rows, width), F32)]


def line_sum_sems(chips):
    return [
        DMA((chips, PARTS)), DMA((chips, PARTS)), DMA((chips, PARTS)), DMA((2, chips, PARTS)), DMA((chips, PARTS)),
        DMA((2, PARTS)),
    ]


def line_sum_start(p, part, rows, bufs, sems):
    own, inbox, _, _, _ = bufs
    load, csend, crecv, _, _, _ = sems
    at = line_parts(p, part, rows)
    size = rows // PARTS

    def share(s):
        def one(q):
            here = pl.ds(pl.multiple_of(q * size, size), size)
            line_copy(p, at(s, 1 - p.c, q), inbox.at[s, here], csend.at[s, q], crecv.at[s, q], p.k, 1 - p.c).start()
            pltpu.make_async_copy(at(s, p.c, q), own.at[s, here], load.at[s, q]).start()

        each_part(one)

    for d in range(p.C - 1, 0, -1):
        for sign in (1, -1):
            s = p.k + sign * d

            @pl.when(inside(p, s))
            def _():
                share(s)

    share(p.k)


def line_sum_steps(p, part, rows, bufs, sems):
    own, inbox, relay, box, acc = bufs
    load, csend, crecv, zsend, rrecv, zrecv = sems
    size = rows // PARTS
    step = math.gcd(size, 128)
    piece = line_parts(p, part, rows)(0, 0, 0)

    def rows_of(q):
        return pl.ds(pl.multiple_of(q * size, size), size)

    def add(q, body):
        def one(j, carry):
            body(pl.ds(pl.multiple_of(q * size + j * step, step), step))
            return carry

        lax.fori_loop(0, size // step, one, 0)

    def pair(t, q):
        pltpu.make_async_copy(piece, own.at[t, rows_of(q)], load.at[t, q]).wait()
        pltpu.make_async_copy(piece, inbox.at[t, rows_of(q)], crecv.at[t, q]).wait()

    def at_distance(d):
        def onward(q):
            here = rows_of(q)
            for i, sign in enumerate((1, -1)):
                t = p.k + sign * d
                behind = inside(p, p.k - sign)

                @pl.when(inside(p, t))
                def _():
                    pair(t, q)

                    @pl.when(jnp.logical_not(behind))
                    def _():
                        def two(at):
                            own[t, at, :] = (own[t, at, :].astype(F32) + inbox[t, at, :].astype(F32)).astype(BF)

                        add(q, two)

                    @pl.when(behind)
                    def _():
                        pltpu.make_async_copy(piece, relay.at[t, here], rrecv.at[t, q]).wait()

                        def three(at):
                            both = own[t, at, :].astype(F32) + inbox[t, at, :].astype(F32)
                            own[t, at, :] = (both + relay[t, at, :].astype(F32)).astype(BF)

                        add(q, three)

                    src = own.at[t, here]
                    if d >= 2:
                        line_copy(p, src, relay.at[t, here], zsend.at[i, d, q], rrecv.at[t, q], p.k + sign, p.c).start()
                    else:
                        line_copy(p, src, box.at[i, here], zsend.at[i, d, q], zrecv.at[i, q], t, p.c).start()

        each_part(onward)

    def last(q):
        here = rows_of(q)
        pair(p.k, q)

        def first(at):
            acc[at, :] = own[p.k, at, :].astype(F32) + inbox[p.k, at, :].astype(F32)

        add(q, first)
        for i, sign in enumerate((1, -1)):

            @pl.when(inside(p, p.k - sign))
            def _():
                pltpu.make_async_copy(piece, box.at[i, here], zrecv.at[i, q]).wait()

                def more(at):
                    acc[at, :] += box[i, at, :].astype(F32)

                add(q, more)

            for d in range(1, p.C):

                @pl.when(inside(p, p.k + sign * d))
                def _():
                    pltpu.make_async_copy(piece, own.at[0, here], zsend.at[i, d, q]).wait()

        for s in range(p.C):
            pltpu.make_async_copy(piece, inbox.at[s, here], csend.at[s, q]).wait()

    return [functools.partial(at_distance, d) for d in range(p.C - 1, 0, -1)] + [lambda: each_part(last)]


def row_loop(rows, step, body):
    def one(i, carry):
        body(pl.ds(pl.multiple_of(i * step, step), step))
        return carry

    lax.fori_loop(0, rows // step, one, 0)


STEP = 64


def inv_rms(u):
    return lax.rsqrt(jnp.mean(u * u, axis=-1, keepdims=True) + EPSILON)


def swap_start(p, buf, out_ref, sems):
    @pl.when(p.moves)
    def _():
        swap_rows(p, buf, out_ref, sems.at[0], sems.at[1]).start()

    @pl.when(jnp.logical_not(p.moves))
    def _():
        out_ref[...] = buf[...]


def swap_end(p, buf, out_ref, sems):
    @pl.when(p.moves)
    def _():
        swap_rows(p, buf, out_ref, sems.at[0], sems.at[1]).wait()


def weave(gate_ref, up_ref, both_ref):
    ff = gate_ref.shape[1]
    t = math.gcd(ff, 256)
    for i in range(0, ff, t):
        both_ref[:, 2 * i : 2 * i + t] = gate_ref[:, i : i + t]
        both_ref[:, 2 * i + t : 2 * i + 2 * t] = up_ref[:, i : i + t]


def unweave_kernel(both_ref, gate_ref, up_ref):
    ff = gate_ref.shape[1]
    t = math.gcd(ff, 256)
    for i in range(0, ff, t):
        gate_ref[:, i : i + t] = both_ref[:, 2 * i : 2 * i + t].astype(F32)
        up_ref[:, i : i + t] = both_ref[:, 2 * i + t : 2 * i + 2 * t].astype(F32)


def input_kernel(
    wide, narrow, x_ref, gain_ref, shard, gate_ref, up_ref, own_ref, gathered, full, gu_ref, buf, swap, *sems
):
    p = Place(wide, narrow)
    rows = x_ref.shape[0]
    spread, line = sems[:4], (shard, full, shard.shape[0], *sems[4:])
    enter(p, line=True)

    @pl.when(p.moves)
    def _():
        swap_rows(p, x_ref, own_ref, swap.at[0], swap.at[1]).start()

    each_part(lambda q: line_push(p, *line, q))
    *steps, end = line_steps(p, *line)

    def share():
        def body(at):
            u = own_ref[at, :].astype(F32)
            buf[at, :] = (u * inv_rms(u) * gain_ref[...]).astype(BF)

        row_loop(rows, STEP, body)
        spread_start(p, buf, gathered, rows, *spread)

    @pl.when(jnp.logical_not(p.moves))
    def _():
        own_ref[...] = x_ref[...]
        share()

    weave(gate_ref, up_ref, gu_ref)
    steps[0]()

    @pl.when(p.moves)
    def _():
        swap_rows(p, x_ref, own_ref, swap.at[0], swap.at[1]).wait()
        share()

    for step in steps[1:-1]:
        step()
    spread_pass(p, buf, gathered, rows, *spread)
    steps[-1]()
    spread_end(p, buf, gathered, rows, *spread)
    end()


def turn(u):
    return pltpu.roll(u, u.shape[-1] // 2, 1)


def qkv_kernel(
    wide, narrow, qw, kw, fold, g_ref, x_ref, w_ref, cos_ref, sin_ref, qg_ref, kg_ref,
    own_ref, gathered, full, qproj_ref, kproj_ref, q_ref, kv_ref, w_buf, load, swap, *sems,
):
    p = Place(wide, narrow)
    rows = g_ref.shape[0]
    hd = cos_ref.shape[1]
    all_rows = x_ref.shape[0]
    size = all_rows // PARTS
    spread, line = sems[:4], (kv_ref, full, all_rows, *sems[4:])
    weights = pltpu.make_async_copy(w_ref.at[:, pl.ds(0, w_buf.shape[1])], w_buf, load)
    weights.start()
    enter(p, line=True)

    @pl.when(p.moves)
    def _():
        swap_rows(p, g_ref, own_ref, swap.at[0], swap.at[1]).start()

    @pl.when(jnp.logical_not(p.moves))
    def _():
        own_ref[...] = g_ref[...]
        spread_start(p, own_ref, gathered, rows, *spread)

    def project(q):
        at = pl.ds(pl.multiple_of(q * size, size), size)
        y = dg(x_ref[at, :], w_buf[...], NN)
        cos, sin = cos_ref[at, :], sin_ref[at, :]
        qproj_ref[at, :] = y[:, :qw]
        kproj_ref[at, :] = y[:, qw : qw + kw]

        def head(lo, gain):
            u = y[:, lo : lo + hd]
            v = u * inv_rms(u) * gain
            return v * cos + turn(v) * sin

        for h in range(kw // hd):
            kv_ref[at, 2 * h * hd : (2 * h + 1) * hd] = head(qw + h * hd, kg_ref[...]).astype(BF)
            kv_ref[at, (2 * h + 1) * hd : (2 * h + 2) * hd] = y[:, qw + kw + h * hd : qw + kw + (h + 1) * hd].astype(BF)
        line_push(p, *line, q)
        for h in range(qw // hd):
            q_ref[at, h * hd : (h + 1) * hd] = (head(h * hd, qg_ref[...]) * fold).astype(BF)

    weights.wait()
    each_part(project)
    *steps, end = line_steps(p, *line)
    steps[0]()

    @pl.when(p.moves)
    def _():
        swap_rows(p, g_ref, own_ref, swap.at[0], swap.at[1]).wait()
        spread_start(p, own_ref, gathered, rows, *spread)

    for step in steps[1:-1]:
        step()
    spread_pass(p, own_ref, gathered, rows, *spread)
    steps[-1]()
    spread_end(p, own_ref, gathered, rows, *spread)
    end()


def middle_kernel(wide, narrow, part, own_ref, gain_ref, mid_ref, gathered, buf, *refs):
    p = Place(wide, narrow)
    rows, dim = own_ref.shape
    bufs, sems, spread = split_refs(narrow, refs)
    enter(p)
    sum_start(p, part, rows, dim, bufs, sems)
    sum_pass(p, part, rows, dim, bufs, sems)
    sum_end(p, part, rows, dim, bufs, sems)

    def body(at):
        u = own_ref[at, :].astype(F32) + total(p, bufs, at)
        mid_ref[at, :] = u
        buf[at, :] = (u * inv_rms(u) * gain_ref[...]).astype(BF)

    row_loop(rows, STEP, body)
    spread_start(p, buf, gathered, rows, *spread)
    spread_pass(p, buf, gathered, rows, *spread)
    spread_end(p, buf, gathered, rows, *spread)


def split_refs(narrow, refs):
    bufs, sems = (3, 5) if narrow == 4 else (1, 3)
    return refs[:bufs], refs[bufs : bufs + sems], refs[bufs + sems :]


def norm_back(u, gain, cot):
    r = inv_rms(u)
    a = cot * gain
    du = r * a - u * (r * r * r) * jnp.mean(a * u, axis=-1, keepdims=True)
    return du, jnp.sum(cot * u * r, axis=0, keepdims=True)


def mlp_back_kernel(
    wide, narrow, low_ref, w_ref, x_ref, mid_ref, gain_ref, grad_ref, back_ref, rows_ref, dgain_ref, wgrad,
    low, w_buf, x_buf, stage, out, load, store, *refs
):
    p = Place(wide, narrow)
    rows, dim = mid_ref.shape
    half = dim // 2
    bufs, sems, _ = split_refs(narrow, refs)
    loads = [pltpu.make_async_copy(low_ref, low, load.at[0])]
    for i in range(2):
        at = pl.ds(i * half, half)
        loads.append(pltpu.make_async_copy(w_ref.at[at], w_buf.at[at], load.at[1 + i]))
    loads.append(pltpu.make_async_copy(x_ref, x_buf, load.at[3]))
    for copy in loads:
        copy.start()
    enter(p)
    for copy in loads[:3]:
        copy.wait()

    def product(j, i):
        a = low[pl.ds(pl.multiple_of(j * rows, rows), rows), :]
        return dg(a, w_buf[pl.ds(pl.multiple_of(i * half, half), half), :], NT).astype(BF)

    sum_start_of(p, product, out, rows, dim, bufs, sems)
    dgain_ref[...] = jnp.zeros_like(dgain_ref)
    loads[3].wait()
    tile = 256

    def write(i):
        return pltpu.make_async_copy(
            stage.at[lax.rem(i, 2)], wgrad.at[pl.ds(pl.multiple_of(i * tile, tile), tile)], store.at[lax.rem(i, 2)]
        )

    def grads(first, last):
        def one(i, carry):
            @pl.when(i >= 2)
            def _():
                write(i - 2).wait()

            stage[lax.rem(i, 2)] = dg(x_buf[:, pl.ds(pl.multiple_of(i * tile, tile), tile)], low[...], TN).astype(BF)
            write(i).start()
            return carry

        lax.fori_loop(first, last, one, 0)

    tiles = dim // tile
    early = 3
    grads(0, early)
    sum_pass(p, out, rows, dim, bufs, sems, loaded=narrow == 4)
    grads(early, tiles)
    sum_end(p, out, rows, dim, bufs, sems)

    def body(at):
        du, dgain = norm_back(mid_ref[at, :], gain_ref[...], total(p, bufs, at))
        back = grad_ref[at, :].astype(F32) + du
        back_ref[at, :] = back
        rows_ref[at, :] = back.astype(BF)
        dgain_ref[...] += dgain

    row_loop(rows, STEP, body)
    write(tiles - 2).wait()
    write(tiles - 1).wait()


def middle_back_kernel(
    wide, narrow, wo_at, groups, hd, rows_ref, hidden, w_ref, wo_ref, o_ref, gathered, next_ref, back_ref, delta_ref,
    h_buf, w_buf, wo_buf, o_buf, load, *spread
):
    p = Place(wide, narrow)
    rows = rows_ref.shape[0]
    pairs = ((hidden, h_buf), (w_ref, w_buf), (wo_ref.at[:, pl.ds(*wo_at)], wo_buf), (o_ref, o_buf))
    loads = [pltpu.make_async_copy(src, dst, load.at[i]) for i, (src, dst) in enumerate(pairs)]
    enter(p)
    spread_start(p, rows_ref, gathered, rows, *spread)
    for copy in loads:
        copy.start()
    for copy in loads[:2]:
        copy.wait()

    def down(at):
        next_ref[at, :] = dg(h_buf[at, :], w_buf[...], NT).astype(BF)

    row_loop(next_ref.shape[0], 256, down)
    for copy in loads[2:]:
        copy.wait()

    def on_slot(j):
        at = pl.ds(pl.multiple_of(j * rows, rows), rows)
        back = dg(gathered[at, :], wo_buf[...], NN).astype(BF)
        back_ref[at, :] = back
        lane = lax.broadcasted_iota(jnp.int32, (rows, hd), 1)
        out = jnp.zeros((rows, hd), F32)
        for h in range(back.shape[1] // hd):
            mine = slice(h * hd, (h + 1) * hd)
            row = 8 * (h // groups) + h % groups
            delta = jnp.sum(back[:, mine].astype(F32) * o_buf[at, mine], axis=1, keepdims=True)
            out = jnp.where(lane == row, delta, out)
        delta_ref[:, at] = jnp.transpose(out)[: delta_ref.shape[0]]

    spread_pass(p, rows_ref, gathered, rows, *spread)
    spread_end(p, rows_ref, gathered, rows, *spread, on_slot=on_slot)


def share_start(me, count, here, slots, sends, recvs, device):
    slots[me] = here[...]
    for t in range(count):

        @pl.when(me != t)
        def _():
            wide_at, narrow_at = device(t)
            to(here, slots.at[me], sends.at[t], recvs.at[me], wide_at, narrow_at).start()


def share_end(me, count, here, slots, sends, recvs):
    for t in range(count):

        @pl.when(me != t)
        def _():
            pltpu.make_async_copy(here, slots.at[t], sends.at[t]).wait()
            pltpu.make_async_copy(here, slots.at[t], recvs.at[t]).wait()

    out = slots[0]
    for t in range(1, count):
        out = out + slots[t]
    here[...] = out


def head_back(cot, u, gain, cos, sin):
    cot = cot * cos - turn(cot) * sin
    return norm_back(u, gain, cot)


def output_kernel(
    wide, narrow, part, mid_ref, dkv, dq, qproj, cos_ref, sin_ref, g_ref, x_ref, m_ref, a_ref,
    out_ref, kv_ref, low_ref, dgain_ref, wgrad_ref, buf, dq_buf, u_buf, x_buf, m_buf, a_buf, load, swap, *refs
):
    p = Place(wide, narrow)
    rows, dim = mid_ref.shape
    kv_rows = kv_ref.shape[0]
    width = low_ref.shape[1]
    hd = cos_ref.shape[1]
    bufs, sems, line = split_refs(narrow, refs)
    sums = (part, rows, dim, bufs, sems)
    chain = (p, dkv, kv_rows, line[:5], line[5:])
    pairs = ((dq, dq_buf), (qproj, u_buf), (x_ref, x_buf), (m_ref, m_buf), (a_ref, a_buf))
    loads = [pltpu.make_async_copy(src, dst, load.at[i]) for i, (src, dst) in enumerate(pairs)]
    enter(p, line=True)
    line_sum_start(*chain)
    sum_start(p, *sums)
    for copy in loads:
        copy.start()
    first, *steps, last = line_sum_steps(*chain)
    first()
    dgain_ref[...] = jnp.zeros_like(dgain_ref)
    for copy in loads[:2]:
        copy.wait()

    def through_heads(at):
        for h in range(width // hd):
            mine = slice(h * hd, (h + 1) * hd)
            du, dgain = head_back(dq_buf[at, mine], u_buf[at, mine], g_ref[...], cos_ref[at, :], sin_ref[at, :])
            low_ref[at, mine] = du.astype(BF)
            dgain_ref[...] += dgain

    row_loop(low_ref.shape[0], 128, through_heads)
    for copy in loads[2:]:
        copy.wait()

    def grads(first_tile, last_tile):
        def one(i, carry):
            at = pl.ds(pl.multiple_of(i * 256, 256), 256)
            wgrad_ref[at, :width] = dg(x_buf[:, at], low_ref[...], TN).astype(BF)
            wgrad_ref[at, width:] = dg(m_buf[:, at], a_buf[...], TN).astype(BF)
            return carry

        lax.fori_loop(first_tile, last_tile, one, 0)

    tiles = dim // 256
    grads(0, tiles // 2)
    sum_pass(p, *sums)
    steps[0]()
    sum_end(p, *sums)

    def body(at):
        buf[at, :] = (mid_ref[at, :] + total(p, bufs, at)).astype(BF)

    row_loop(rows, STEP, body)
    swap_start(p, buf, out_ref, swap)
    grads(tiles // 2, tiles)
    for step in steps[1:]:
        step()
    last()
    row_loop(kv_rows, 128, lambda at: kv_ref.__setitem__((at, slice(None)), line[4][at, :].astype(BF)))
    swap_end(p, buf, out_ref, swap)


def input_back_kernel(
    wide, narrow, qw, kw, own_ref, gain_ref, back_ref, gains_ref, wgrad, q_ref, kv_ref, proj_ref, cos_ref, sin_ref, kg_ref,
    w_ref, x_ref, out_ref, gsum_ref, wsum_ref, kvsum_ref,
    buf, far_buf, gbuf, gbuf2, low, part, kvgrad, w_buf, load, swap, gsend, grecv, gsend2, grecv2, *refs,
):
    p = Place(wide, narrow)
    rows, dim = own_ref.shape
    hd = cos_ref.shape[1]
    all_rows = x_ref.shape[0]
    w_rows = wsum_ref.shape[0]
    bufs, sems, line = split_refs(narrow, refs)
    sums = (part, rows, dim, bufs, sems)
    first_line = (p, wgrad, w_rows, (*line[:4], wsum_ref), line[4:10])
    second_line = (p, kvgrad, w_rows, (*line[10:14], kvsum_ref), line[14:])
    weights = pltpu.make_async_copy(w_ref.at[:, pl.ds(0, w_buf.shape[1])], w_buf, load)
    weights.start()
    enter(p, ring=True)
    line_sum_start(*first_line)
    gsum_ref[...] = gains_ref[...]
    size = min(all_rows, 256)
    weights.wait()

    def through_heads(at):
        low[at, :qw] = q_ref[at, :]
        for h in range(kw // hd):
            key = slice(2 * h * hd, (2 * h + 1) * hd)
            value = slice((2 * h + 1) * hd, (2 * h + 2) * hd)
            mine = slice(qw + h * hd, qw + (h + 1) * hd)
            du, dgain = head_back(
                kv_ref[at, key].astype(F32), proj_ref[at, h * hd : (h + 1) * hd], kg_ref[...], cos_ref[at, :], sin_ref[at, :]
            )
            low[at, mine] = du.astype(BF)
            low[at, qw + kw + h * hd : qw + kw + (h + 1) * hd] = kv_ref[at, value]
            gsum_ref[:, 2 * dim + hd :] += dgain
        part[at, :] = dg(low[at, :], w_buf[...], NT).astype(BF)

    row_loop(all_rows, size, through_heads)
    sum_start(p, *sums)
    first = line_sum_steps(*first_line)
    first[0]()

    def key_grads(at):
        kvgrad[at, :] = dg(x_ref[:, at], low[:, qw:], TN).astype(BF)

    row_loop(dim, 256, key_grads)
    line_sum_start(*second_line)
    second = line_sum_steps(*second_line)
    first[1]()
    sum_pass(p, *sums)
    second[0]()
    for step in first[2:-1]:
        step()
    sum_end(p, *sums)

    def body(at):
        du, dgain = norm_back(own_ref[at, :].astype(F32), gain_ref[...], total(p, bufs, at))
        grad = back_ref[at, :] + du
        out_ref[at, :] = grad
        buf[at, :] = grad.astype(BF)
        gsum_ref[:, :dim] += dgain

    row_loop(rows, STEP, body)

    @pl.when(p.moves)
    def _():
        swap_rows(p, buf, far_buf, swap.at[0], swap.at[1]).start()

    share_start(p.n, narrow, gsum_ref, gbuf, gsend, grecv, lambda t: (p.w, t))
    second[1]()
    first[-1]()
    share_end(p.n, narrow, gsum_ref, gbuf, gsend, grecv)
    share_start(p.w, wide, gsum_ref, gbuf2, gsend2, grecv2, lambda t: (t, p.n))
    for step in second[2:]:
        step()
    share_end(p.w, wide, gsum_ref, gbuf2, gsend2, grecv2)

    @pl.when(p.moves)
    def _():
        swap_rows(p, buf, far_buf, swap.at[0], swap.at[1]).wait()
        row_loop(rows, STEP, lambda at: out_ref.__setitem__((at, slice(None)), far_buf[at, :].astype(F32)))


VM = pl.BlockSpec(memory_space=pltpu.VMEM)


HB = pl.BlockSpec(memory_space=pl.ANY)


def comm_call(kernel, name, cid, out_shape, in_specs, out_specs, scratch, *args):
    return pl.pallas_call(
        kernel,
        out_shape=out_shape,
        in_specs=in_specs,
        out_specs=out_specs,
        scratch_shapes=scratch,
        compiler_params=pltpu.CompilerParams(collective_id=cid, has_side_effects=True, vmem_limit_bytes=60 << 20),
        cost_estimate=pl.CostEstimate(flops=0, bytes_accessed=160_000_000, transcendentals=0),
        name=name,
    )(*args)


def sds(shape, kind):
    return jax.ShapeDtypeStruct(shape, kind)


def plain(kernel, name, grid, in_specs, out_specs, out_shape, flops, nbytes, *args, scratch=(), aliases=None):
    return pl.pallas_call(
        kernel,
        out_shape=out_shape,
        grid=grid,
        in_specs=in_specs,
        out_specs=out_specs,
        scratch_shapes=scratch,
        input_output_aliases=aliases or {},
        compiler_params=pltpu.CompilerParams(vmem_limit_bytes=52 << 20),
        cost_estimate=pl.CostEstimate(flops=flops, bytes_accessed=nbytes, transcendentals=0),
        name=name,
    )(*args)


def whole(shape):
    return pl.BlockSpec(shape, lambda *i: (0,) * len(shape), pipeline_mode=pl.Buffered(1))


def by_rows(tm, width):
    return pl.BlockSpec((tm, width), lambda i: (i, 0))


def mlp_fwd_kernel(x_ref, w_ref, gu_ref, h_ref):
    t = h_ref.shape[1]
    y = dg(x_ref[...], w_ref[...], NN)
    gate, up = y[:, :t], y[:, t:]
    gu_ref[...] = y
    h_ref[...] = (gate * jax.nn.sigmoid(gate) * up).astype(BF)


def mlp_fwd(x, w, t):
    rows, dim = x.shape
    ff2 = w.shape[1]
    return plain(
        mlp_fwd_kernel, "mlp_fwd", (ff2 // (2 * t),),
        [whole((rows, dim)), pl.BlockSpec((dim, 2 * t), lambda i: (0, i))],
        [pl.BlockSpec((rows, 2 * t), lambda i: (0, i)), pl.BlockSpec((rows, t), lambda i: (0, i))],
        (sds((rows, ff2), F32), sds((rows, ff2 // 2), BF)),
        2 * rows * dim * ff2, rows * dim * 2 + dim * ff2 * 2 + rows * ff2 * 5, x, w,
    )


def mlp_bwd_kernel(g_ref, w_ref, gu_ref, out_ref):
    t = w_ref.shape[1]
    hb = dg(g_ref[...], w_ref[...], NN)
    gate, up = gu_ref[:, :t], gu_ref[:, t:]
    s = jax.nn.sigmoid(gate)
    gs = hb * s
    out_ref[:, :t] = (gs * up * (1.0 + gate * (1.0 - s))).astype(BF)
    out_ref[:, t:] = (gs * gate).astype(BF)


def mlp_bwd(g, w, gu, t):
    rows, dim = g.shape
    ff = w.shape[1]
    return plain(
        mlp_bwd_kernel, "mlp_bwd", (ff // t,),
        [whole((rows, dim)), pl.BlockSpec((dim, t), lambda i: (0, i)), pl.BlockSpec((rows, 2 * t), lambda i: (0, i))],
        pl.BlockSpec((rows, 2 * t), lambda i: (0, i)), sds((rows, 2 * ff), BF),
        2 * rows * dim * ff, rows * dim * 2 + dim * ff * 2 + rows * ff * 12, g, w, gu,
    )


def zero_kernel(o_ref):
    o_ref[...] = jnp.zeros_like(o_ref)


def zero_rows(shape):
    tm = 1024
    return plain(
        zero_kernel, "zero_rows", (shape[0] // tm,), [], by_rows(tm, shape[1]), sds(shape, BF), 0, 2 * shape[0] * shape[1]
    )


def fwd_kernel(groups, hd, tab, q_ref, kv_ref, o_ref, low_ref, lse_ref, acc, lsum):
    s = pl.program_id(1)
    block = q_ref.shape[0]
    diag, first, last = tab[2, s], tab[3, s], tab[4, s]

    @pl.when(first == 1)
    def _():
        acc[...] = jnp.zeros_like(acc)
        lsum[...] = jnp.zeros_like(lsum)

    def work(masked):
        k, v = kv_ref[:, :hd], kv_ref[:, hd:]
        for g in range(groups):
            at = slice(g * hd, (g + 1) * hd)
            scores = dg(q_ref[:, at], k, NT)
            if masked:
                row = lax.broadcasted_iota(jnp.int32, scores.shape, 0)
                col = lax.broadcasted_iota(jnp.int32, scores.shape, 1)
                scores = jnp.where(col <= row, scores, MASKED)
            probs = jnp.exp2(scores)
            part = probs[:, :128]
            for j in range(1, block // 128):
                part = part + probs[:, j * 128 : (j + 1) * 128]
            lsum[g] += part
            acc[:, at] += dg(probs.astype(BF), v, NN)

    @pl.when(diag == 0)
    def _():
        work(False)

    @pl.when(diag == 1)
    def _():
        work(True)

    @pl.when(last == 1)
    def _():
        lane = lax.broadcasted_iota(jnp.int32, (block, 128), 1)
        lse = jnp.zeros((block, 128), F32)
        for g in range(groups):
            at = slice(g * hd, (g + 1) * hd)
            l = jnp.sum(lsum[g], axis=1, keepdims=True)
            out = acc[:, at] / l
            o_ref[:, at] = out
            low_ref[:, at] = out.astype(BF)
            lse = jnp.where(lane == g, jnp.log2(l), lse)
        lse_ref[...] = jnp.transpose(lse)[: lse_ref.shape[0]]


def attn_fwd(tab, q, kv, groups, hd, block):
    rows, width = q.shape
    gw = groups * hd
    heads = width // gw
    steps = tab.shape[1]
    mine = pl.BlockSpec((block, gw), lambda h, s, t: (t[0, s], h))
    return pl.pallas_call(
        functools.partial(fwd_kernel, groups, hd),
        out_shape=(sds((rows, width), F32), sds((rows, width), BF), sds((8 * heads, rows), F32)),
        grid_spec=pltpu.PrefetchScalarGridSpec(
            num_scalar_prefetch=1,
            grid=(heads, steps),
            in_specs=[mine, pl.BlockSpec((block, 2 * hd), lambda h, s, t: (t[1, s], h))],
            out_specs=[mine, mine, pl.BlockSpec((8, block), lambda h, s, t: (h, t[0, s]))],
            scratch_shapes=[pltpu.VMEM((block, gw), F32), pltpu.VMEM((groups, block, 128), F32)],
        ),
        compiler_params=pltpu.CompilerParams(vmem_limit_bytes=48 << 20),
        cost_estimate=pl.CostEstimate(
            flops=heads * steps * block * block * gw * 4,
            bytes_accessed=heads * steps * block * hd * 8,
            transcendentals=heads * steps * block * block * groups,
        ),
        name="attn_fwd",
    )(tab, q, kv)


def bwd_kernel(groups, hd, tab, q_ref, do_ref, kv_ref, lse_ref, delta_ref, zeros, dq_ref, dkv_ref, dq_sum, dkv_sum):
    s = pl.program_id(1)
    block = q_ref.shape[0]
    qi, diag, first, last = tab[0, s], tab[2, s], tab[3, s], tab[4, s]

    @pl.when(s == 0)
    def _():
        dq_sum[...] = jnp.zeros_like(dq_sum)

    @pl.when(first == 1)
    def _():
        dkv_sum[...] = jnp.zeros_like(dkv_sum)

    def work(masked):
        k, v = kv_ref[:, :hd], kv_ref[:, hd:]
        for g in range(groups):
            at = slice(g * hd, (g + 1) * hd)
            q, do = q_ref[:, at], do_ref[:, at]
            scores = dg(k, q, NT) - lse_ref[g : g + 1, :]
            if masked:
                row = lax.broadcasted_iota(jnp.int32, scores.shape, 0)
                col = lax.broadcasted_iota(jnp.int32, scores.shape, 1)
                scores = jnp.where(row <= col, scores, MASKED)
            probs = jnp.exp2(scores)
            dots = dg(v, do, NT)
            dkv_sum[:, hd:] += dg(probs.astype(BF), do, NN)
            back = (probs * (dots - delta_ref[g : g + 1, :])).astype(BF)
            dkv_sum[:, :hd] += dg(back, q, NN)
            dq_sum[qi, :, at] += dg(back, k, TN)

    @pl.when(diag == 0)
    def _():
        work(False)

    @pl.when(diag == 1)
    def _():
        work(True)

    @pl.when(last == 1)
    def _():
        dkv_ref[:, :hd] = (dkv_sum[:, :hd] * math.log(2.0)).astype(BF)
        dkv_ref[:, hd:] = dkv_sum[:, hd:].astype(BF)

    @pl.when(s == pl.num_programs(1) - 1)
    def _():
        for i in range(dq_sum.shape[0]):
            dq_ref[i * block : (i + 1) * block, :] = dq_sum[i] * hd**-0.5


def attn_bwd(tab, q, do, kv, lse, delta, zeros, groups, hd, block):
    rows, width = q.shape
    gw = groups * hd
    heads = width // gw
    steps = tab.shape[1]
    mine = pl.BlockSpec((block, gw), lambda h, s, t: (t[0, s], h))
    keys = pl.BlockSpec((block, 2 * hd), lambda h, s, t: (t[1, s], h))
    stat = pl.BlockSpec((8, block), lambda h, s, t: (h, t[0, s]))
    return pl.pallas_call(
        functools.partial(bwd_kernel, groups, hd),
        out_shape=(sds((rows, width), F32), sds(kv.shape, BF)),
        grid_spec=pltpu.PrefetchScalarGridSpec(
            num_scalar_prefetch=1,
            grid=(heads, steps),
            in_specs=[mine, mine, keys, stat, stat, HB],
            out_specs=[pl.BlockSpec((rows, gw), lambda h, s, t: (0, h)), keys],
            scratch_shapes=[pltpu.VMEM((rows // block, block, gw), F32), pltpu.VMEM((block, 2 * hd), F32)],
        ),
        input_output_aliases={6: 1},
        compiler_params=pltpu.CompilerParams(vmem_limit_bytes=48 << 20),
        cost_estimate=pl.CostEstimate(
            flops=heads * steps * block * block * gw * 10,
            bytes_accessed=heads * steps * block * hd * 16,
            transcendentals=heads * steps * block * block * groups,
        ),
        name="attn_bwd",
    )(tab, q, do, kv, lse, delta, zeros)


def middle_chip(k, chips):
    return (k == chips // 2 - 1) | (k == chips // 2)


def place(w, chips):
    k, core = w // 2, w % 2
    return 4 * k + core, jnp.where(middle_chip(k, chips), 4 * k + 3, 4 * chips - 1 - 4 * k) - core


def block_row(b, chips):
    m, k = b % 4, b // 4
    early = m < 2
    k = jnp.where(early | middle_chip(k, chips), k, chips - 1 - k)
    core = jnp.where((m == 1) | (m == 2), 1, 0)
    return 2 * (2 * k + core) + jnp.where(early, 0, 1)


def tables(w, chips):
    a, b = place(w, chips)
    count = a + b + 2
    every = jnp.arange(4 * chips + 5, dtype=jnp.int32)
    s, idle = jnp.minimum(every, count - 1), every >= count
    in_a = s <= a
    key = jnp.where(in_a, s, s - a - 1)
    diag = jnp.where(in_a, s == a, s == count - 1)
    fwd = [jnp.where(in_a, 0, 1), block_row(key, chips), jnp.where(idle, 2, diag), ~idle & (key == 0), ~idle & diag]
    less, low = jnp.minimum(a, b), jnp.where(a < b, 0, 1)
    both = s < 2 * (less + 1)
    even = s % 2 == 0
    key = jnp.where(both, s // 2, s - (less + 1))
    query = jnp.where(both & even, low, 1 - low)
    diag = key == jnp.where(query == 0, a, b)
    bwd = [query, block_row(key, chips), jnp.where(idle, 2, diag), ~idle & (~both | even), ~idle & (~both | ~even)]
    return tuple(jnp.stack([row.astype(jnp.int32) for row in rows]) for rows in (fwd, bwd))


def rotation(positions, head_dim):
    steps_half = jnp.arange(head_dim // 2).astype(F32)
    inverse = jnp.exp(steps_half * (-2.0 * math.log(1000000.0) / head_dim))
    angles = positions.astype(F32)[:, None] * inverse[None, :]
    cos, sin = jnp.cos(angles), jnp.sin(angles)
    return jnp.concatenate([cos, cos], axis=1), jnp.concatenate([-sin, sin], axis=1)


def per_device(
    wide, narrow,
    layer_input, w_query, w_key, w_value, w_output, w_gate, w_up, w_down,
    attn_gain, mlp_gain, query_gain, key_gain, out_grad,
):
    hd = query_gain.shape[0]
    rows, dim = layer_input.shape
    all_rows = narrow * rows
    chips = wide // 2
    block = all_rows // 2
    qw, kw = w_query.shape[1], w_key.shape[1]
    ff = w_gate.shape[1]
    groups = qw // kw
    kv_heads = kw // hd
    w = lax.axis_index("wide")
    fwd_tab, bwd_tab = tables(w, chips)
    first, second = place(w, chips)
    at = jnp.arange(block, dtype=jnp.int32)
    positions = jnp.concatenate([first * block + at, second * block + at])
    cos_table, sin_table = rotation(positions, hd)

    def gather(shard):
        return lax.all_gather(shard, "wide", axis=0, tiled=True)

    def scatter(grad):
        return lax.psum_scatter(grad, "wide", scatter_dimension=0, tiled=True)

    t = math.gcd(ff, 256)

    spread_s = spread_sems(narrow)
    sum_s = [*sum_bufs(narrow, rows, dim), *sum_sems(narrow)]
    row_buf = pltpu.VMEM((rows, dim), BF)
    low_rows, full_rows, all_low = sds((rows, dim), BF), sds((rows, dim), F32), sds((all_rows, dim), BF)
    ring = functools.partial
    qg, kg = query_gain[None], key_gain[None]
    after = lax.optimization_barrier

    in_scratch = [DMA((2,)), *spread_s, *line_sems(chips)]
    shard = jnp.concatenate([w_query, w_key, w_value, w_output.T], axis=1)
    own, normed_all, w_attn, gu_shard = comm_call(
        ring(input_kernel, wide, narrow), "input_rows", 0,
        (low_rows, all_low, sds((dim, shard.shape[1]), BF), sds((w_gate.shape[0], 2 * ff), BF)),
        [VM, VM, HB, VM, VM], (VM, HB, HB, VM), [row_buf, *in_scratch],
        layer_input, attn_gain[None], shard, w_gate, w_up,
    )
    width = qw + 2 * kw
    grad_own, grad_all, kv, query_proj, key_proj, queries = comm_call(
        ring(qkv_kernel, wide, narrow, qw, kw, hd**-0.5 * math.log2(math.e)), "qkv_rows", 1,
        (low_rows, all_low, sds((wide * all_rows, 2 * kw), BF), sds((all_rows, qw), F32),
         sds((all_rows, kw), F32), sds((all_rows, qw), BF)),
        [VM, VM, HB, VM, VM, VM, VM], (VM, HB, HB, VM, VM, VM),
        [pltpu.VMEM((all_rows, 2 * kw), BF), pltpu.VMEM((dim, width), BF), DMA, *in_scratch],
        out_grad, normed_all, w_attn, cos_table, sin_table, qg, kg,
    )
    gu_shard, w_down, kv = after((gu_shard, w_down, kv))
    w_gu, w_d = gather(gu_shard), gather(w_down.T)
    attended, attended_low, lse = attn_fwd(fwd_tab, queries, kv, groups, hd, block)
    w_o = w_attn[:, qw + 2 * kw :]
    middle, normed_mlp = comm_call(
        ring(middle_kernel, wide, narrow), "middle_rows", 2, (full_rows, all_low), [HB, VM, VM], (VM, HB),
        [row_buf, *sum_s, *spread_s], dg(attended_low, w_o, NT).astype(BF), own, mlp_gain[None],
    )
    gate_up, hidden_low = mlp_fwd(normed_mlp, w_gu, t)
    grad_down = dg(grad_all, hidden_low, TN).astype(BF)
    w_d, _, zeros = after((w_d, grad_down, zero_rows(kv.shape)))
    gu_low = mlp_bwd(grad_all, w_d, gate_up, t)
    middle_back, middle_low, mlp_gain_part, grad_gu = comm_call(
        ring(mlp_back_kernel, wide, narrow), "mlp_back", 6,
        (full_rows, low_rows, sds((1, dim), F32), sds((dim, 2 * ff), BF)), [HB, HB, HB, VM, VM, VM], (VM, VM, VM, HB),
        [pltpu.VMEM((all_rows, 2 * ff), BF), pltpu.VMEM((dim, 2 * ff), BF), pltpu.VMEM((all_rows, dim), BF),
         pltpu.VMEM((2, 256, 2 * ff), BF), product_bufs(narrow, rows, dim), DMA((4,)), DMA((2,)), *sum_s],
        gu_low, w_gu, normed_mlp, middle, mlp_gain[None], grad_own,
    )
    grad_down, grad_gu = scatter(grad_down), scatter(grad_gu)
    middle_all, down_part, back, delta = comm_call(
        ring(middle_back_kernel, wide, narrow, (width, qw), groups, hd), "middle_back", 3,
        (all_low, all_low, sds((all_rows, qw), BF), sds((8 * kv_heads, all_rows), F32)),
        [VM, HB, HB, HB, HB], (VM, VM, VM, VM),
        [pltpu.VMEM((all_rows, ff), BF), pltpu.VMEM((dim, ff), BF), pltpu.VMEM((dim, qw), BF), pltpu.VMEM((all_rows, qw), F32),
         DMA((4,)), *spread_s],
        middle_low, hidden_low, w_d, w_attn, attended,
    )
    query_back, dkv = attn_bwd(bwd_tab, queries, back, kv, lse, delta, zeros, groups, hd, block)
    dkv, grad_down = after((dkv, grad_down))
    layer_output, kv_sum, q_low, query_gain_part, grad_qo = comm_call(
        ring(output_kernel, wide, narrow), "output_rows", 4,
        (low_rows, sds((all_rows, 2 * kw), BF), sds((all_rows, qw), BF), sds((1, hd), F32), sds((dim, 2 * qw), BF)),
        [HB, VM, HB, HB, HB, VM, VM, VM, HB, HB, HB], (VM, VM, VM, VM, VM),
        [row_buf, pltpu.VMEM((all_rows, qw), F32), pltpu.VMEM((all_rows, qw), F32), pltpu.VMEM((all_rows, dim), BF),
         pltpu.VMEM((all_rows, dim), BF), pltpu.VMEM((all_rows, qw), BF), DMA((5,)), DMA((2,)), *sum_s,
         *line_sum_bufs(chips, all_rows, 2 * kw), *line_sum_sems(chips)],
        down_part, middle, dkv, query_back, query_proj, cos_table, sin_table, qg, normed_all, middle_all, attended_low,
    )
    kv_sum, grad_gu = after((kv_sum, grad_gu))
    half = sds((dim // wide, ff), F32)
    grad_gate, grad_up = plain(
        unweave_kernel, "unweave", (1,), [whole(grad_gu.shape)], [whole(half.shape)] * 2, [half, half], 0, grad_gu.size * 6, grad_gu
    )
    gains = jnp.concatenate([jnp.zeros((1, dim), F32), mlp_gain_part, query_gain_part, jnp.zeros((1, hd), F32)], axis=1)
    w_rows = dim // wide
    input_grad, gain_sums, grad_qo, grad_kv = comm_call(
        ring(input_back_kernel, wide, narrow, qw, kw), "input_back", 5,
        (full_rows, sds(gains.shape, F32), sds((w_rows, 2 * qw), F32), sds((w_rows, 2 * kw), F32)),
        [VM, VM, VM, VM, HB, VM, VM, VM, VM, VM, VM, HB, VM],
        (VM, VM, VM, VM),
        [row_buf, row_buf, pltpu.VMEM((narrow, *gains.shape), F32), pltpu.VMEM((wide, *gains.shape), F32),
         pltpu.VMEM((all_rows, width), BF), pltpu.VMEM((all_rows, dim), BF), pltpu.VMEM((dim, 2 * kw), BF),
         pltpu.VMEM((dim, width), BF), DMA, DMA((2,)), DMA((narrow,)), DMA((narrow,)), DMA((wide,)), DMA((wide,)), *sum_s,
         *line_sum_bufs(chips, w_rows, 2 * qw)[:4], *line_sum_sems(chips),
         *line_sum_bufs(chips, w_rows, 2 * kw)[:4], *line_sum_sems(chips)],
        own, attn_gain[None], middle_back, gains, grad_qo, q_low, kv_sum, key_proj, cos_table, sin_table, kg, w_attn, normed_all,
    )
    g = gain_sums[0]
    return (
        layer_output, input_grad,
        grad_qo[:, :qw], grad_kv[:, :kw], grad_kv[:, kw:],
        grad_qo[:, qw:].T, grad_gate, grad_up,
        grad_down.T.astype(F32),
        g[:dim], g[dim : 2 * dim], g[2 * dim : 2 * dim + hd], g[2 * dim + hd :],
    )


def solution(mesh):
    rows = P(("wide", "narrow"), None)
    weight, turned = P("wide", "narrow"), P("narrow", "wide")
    return jax.shard_map(
        functools.partial(per_device, mesh.shape["wide"], mesh.shape["narrow"]),
        mesh=mesh,
        in_specs=(rows, weight, weight, weight, turned, weight, weight, turned, P(), P(), P(), P(), rows),
        out_specs=(rows, rows, weight, weight, weight, turned, weight, weight, turned, P(), P(), P(), P()),
        check_vma=False,
    )
```

```python
import functools
import math

import jax
import jax.numpy as jnp
from jax import lax
from jax.experimental import pallas as pl
from jax.experimental.pallas import tpu as pltpu
from jax.sharding import PartitionSpec as P

EPSILON = 1e-06
MASKED = -1e30
F32 = jnp.float32
BF = jnp.bfloat16
MESH = pl.DeviceIdType.MESH
NT = (((1,), (1,)), ((), ()))
NN = (((1,), (0,)), ((), ()))
TN = (((0,), (0,)), ((), ()))


def dg(a, b, dims):
    return lax.dot_general(a, b, dims, preferred_element_type=F32)
DMA = pltpu.SemaphoreType.DMA


class Place:
    def __init__(self, wide, narrow):
        self.W, self.N = wide, narrow
        self.C, self.half = wide // 2, narrow // 2
        self.w, self.n = lax.axis_index("wide"), lax.axis_index("narrow")
        self.k, self.c = self.w // 2, lax.rem(self.w, 2)
        late = (self.n >= self.half).astype(jnp.int32)
        self.group = lax.rem(self.c + late, 2)
        self.slot = jnp.where(self.group == 0, self.n, lax.rem(self.n + self.half, self.N))

    def owner(self, j):
        core = 1 if j >= self.half else 0
        n = jnp.where(self.c == 0, j, (j + self.half) % self.N)
        return core, n

    def owner_is_me(self, j):
        core, n = self.owner(j)
        return (self.c == core) & (self.n == n)


def enter(p, line=False, ring=False):
    barrier = pltpu.get_barrier_semaphore()

    def greet(device):
        pl.semaphore_signal(barrier, inc=1, device_id=device, device_id_type=MESH)

    for core in range(2):
        for n in range(p.N):

            @pl.when((p.c != core) | (p.n != n))
            def _():
                greet((2 * p.k + core, n))

    peers = 2 * p.N - 1
    if line or ring:
        for k in range(p.C):

            @pl.when(p.k != k)
            def _():
                greet((2 * k + p.c, p.n))
                if ring:
                    greet((2 * k + 1 - p.c, p.n))

        peers += (2 if ring else 1) * (p.C - 1)
    pl.semaphore_wait(barrier, peers)


def slot_of(p, n, group):
    return jnp.where(group == 0, n, lax.rem(n + p.half, p.N))


def neighbours(p):
    return p.n + 1 - 2 * lax.rem(p.n, 2), lax.rem(p.n + 2, 4), 3 - p.n


def to(src, dst, send, recv, wide, narrow):
    return pltpu.make_async_remote_copy(
        src_ref=src, dst_ref=dst, send_sem=send, recv_sem=recv, device_id=(wide, narrow), device_id_type=MESH
    )


def spread_sems(narrow):
    return [DMA((narrow, 2)), DMA((narrow, 2)), DMA((2,)), DMA((2,))]


def spread_start(p, src, gathered, rows, send, recv, local, onward):
    half = rows // 2
    view = lambda i: gathered.at[pl.ds(pl.multiple_of(p.slot * rows + i * half, half), half)]
    part = lambda i: src.at[pl.ds(i * half, half)]
    mine = p.group == p.c
    square = p.N == 4
    if square:
        nx, ny, _ = neighbours(p)
        targets = [(nx, (0, 1)), (ny, (1, 0))]
        order = [(t, q, i) for q in range(2) for t, halves in targets for i in (halves[q],)]
        for t, q, i in order:
            at = 0 if t is nx else 1
            to(part(i), view(i), send.at[at, i], recv.at[p.slot, i], 2 * p.k + p.group, t).start()
    else:
        for t in range(p.N):

            @pl.when(p.n != t)
            def _():
                for i in range(2):
                    to(part(i), view(i), send.at[t, i], recv.at[p.slot, i], 2 * p.k + p.group, t).start()

    @pl.when(mine)
    def _():
        for i in range(2):
            pltpu.make_async_copy(part(i), view(i), local.at[i]).start()

    @pl.when(jnp.logical_not(mine))
    def _():
        for i in range(2):
            to(part(i), view(i), local.at[i], recv.at[p.slot, i], 2 * p.k + p.group, p.n).start()


def spread_pass(p, src, gathered, rows, send, recv, local, onward):
    if p.N == 4:
        half = rows // 2
        piece = src.at[pl.ds(0, half)]
        nx, ny, _ = neighbours(p)
        for i, (n, other) in enumerate(((nx, ny), (ny, nx))):
            j = slot_of(p, n, p.c)
            here = gathered.at[pl.ds(pl.multiple_of(j * rows + i * half, half), half)]
            pltpu.make_async_copy(piece, here, recv.at[j, i]).wait()
            to(here, here, onward.at[i], recv.at[j, i], p.w, other).start()


def spread_end(p, src, gathered, rows, send, recv, local, onward, on_slot=lambda j: None):
    half = rows // 2
    piece = src.at[pl.ds(0, half)]
    mine = p.group == p.c
    at = lambda j, i: gathered.at[pl.ds(pl.multiple_of(j * rows + i * half, half), half)]

    def arrive(j, i):
        pltpu.make_async_copy(piece, at(j, i), recv.at[j, i]).wait()

    for i in range(2):
        pltpu.make_async_copy(piece, at(0, 0), local.at[i]).wait()
    here = slot_of(p, p.n, p.c)

    @pl.when(jnp.logical_not(mine))
    def _():
        arrive(here, 0)
        arrive(here, 1)

    on_slot(here)
    if p.N == 4:
        nx, ny, nd = neighbours(p)
        jx, jy, jd = (slot_of(p, n, p.c) for n in (nx, ny, nd))
        arrive(jx, 1)
        on_slot(jx)
        arrive(jy, 0)
        on_slot(jy)
        arrive(jd, 0)
        arrive(jd, 1)
        on_slot(jd)
        for i in range(2):
            pltpu.make_async_copy(piece, at(0, 0), onward.at[i]).wait()
            for t in range(2):
                pltpu.make_async_copy(piece, at(0, 0), send.at[t, i]).wait()
    else:
        for t in range(p.N):

            @pl.when(p.n != t)
            def _():
                for i in range(2):
                    pltpu.make_async_copy(piece, at(0, 0), send.at[t, i]).wait()
                    arrive(slot_of(p, t, p.c), i)
                on_slot(slot_of(p, t, p.c))


def sum_bufs(narrow, rows, dim):
    if narrow == 4:
        half = pltpu.VMEM((2, 2, rows, dim // 2), BF)
        return [half, half, pltpu.VMEM((2, rows, dim), BF)]
    return [pltpu.VMEM((narrow, rows, dim), BF)]


def sum_sems(narrow):
    if narrow == 4:
        return [DMA((2, 2)), DMA((2, 2)), DMA((2, 2)), DMA((4,)), DMA((4,))]
    return [DMA((narrow,)), DMA((narrow,)), DMA]


def pieces(p, part, rows, dim):
    half = dim // 2
    return lambda j, i: part.at[pl.ds(pl.multiple_of(j * rows, rows), rows), pl.ds(i * half, half)]


def sum_start(p, part, rows, dim, bufs, sems):
    if p.N != 4:
        (got,), (send, recv, local) = bufs, sems
        for j in range(p.N):
            core, n = p.owner(j)
            mine = p.owner_is_me(j)
            src = part.at[pl.ds(j * rows, rows)]

            @pl.when(mine)
            def _():
                pltpu.make_async_copy(src, got.at[p.n], local).start()

            @pl.when(jnp.logical_not(mine))
            def _():
                to(src, got.at[p.n], send.at[j], recv.at[p.n], 2 * p.k + core, n).start()

        return
    own, inbox, _ = bufs
    load, send, recv, _, _ = sems
    piece = pieces(p, part, rows, dim)
    nx, ny, nd = neighbours(p)
    across, here = slot_of(p, nd, p.c), slot_of(p, p.n, p.c)
    for i, n in enumerate((nx, ny)):
        to(piece(across, i), inbox.at[i, 0], send.at[i, 0], recv.at[i, 0], p.w, n).start()
    for i, n in enumerate((ny, nx)):
        pltpu.make_async_copy(piece(slot_of(p, n, p.c), i), own.at[i, 0], load.at[i, 0]).start()
    for i, n in enumerate((nx, ny)):
        to(piece(slot_of(p, n, p.c), i), inbox.at[i, 1], send.at[i, 1], recv.at[i, 1], p.w, n).start()
        pltpu.make_async_copy(piece(here, i), own.at[i, 1], load.at[i, 1]).start()


def product_bufs(narrow, rows, dim):
    shape = (4, rows, dim // 2) if narrow == 4 else (narrow * rows, dim)
    return pltpu.VMEM(shape, BF)


def sum_start_of(p, product, out, rows, dim, bufs, sems):
    half = dim // 2
    if p.N != 4:

        def one(j, carry):
            for i in range(2):
                out[pl.ds(pl.multiple_of(j * rows, rows), rows), i * half : (i + 1) * half] = product(j, i)
            return carry

        lax.fori_loop(0, p.N, one, 0)
        sum_start(p, out, rows, dim, bufs, sems)
        return
    own, inbox, _ = bufs
    _, send, recv, _, _ = sems
    nx, ny, nd = neighbours(p)
    across, jx, jy, here = (slot_of(p, n, p.c) for n in (nd, nx, ny, p.n))

    def one(t, carry):
        i = lax.rem(t, 2)
        q = lax.rem(t // 2, 2)
        beside = jnp.where(i == 0, jx, jy)
        other = jnp.where(i == 0, jy, jx)
        j = jnp.where(t < 4, jnp.where(q == 0, across, beside), jnp.where(q == 0, other, here))
        y = product(j, i)

        @pl.when(t < 4)
        def _():
            out[t] = y
            to(out.at[t], inbox.at[i, q], send.at[i, q], recv.at[i, q], p.w, jnp.where(i == 0, nx, ny)).start()

        @pl.when(t >= 4)
        def _():
            own[i, q] = y

        return carry

    lax.fori_loop(0, 8, one, 0)


def core_of(p, j):
    return (j >= p.half).astype(jnp.int32)


def sum_pass(p, part, rows, dim, bufs, sems, loaded=False):
    if p.N != 4:
        return
    own, inbox, box = bufs
    load, send, recv, send2, recv2 = sems
    piece = lambda j, i: own.at[0, 0]
    half = dim // 2
    nx, ny, _ = neighbours(p)
    cols = lambda i: pl.ds(i * half, half)

    def add(i, q):
        if not loaded:
            pltpu.make_async_copy(piece(0, 0), own.at[i, q], load.at[i, q]).wait()
        pltpu.make_async_copy(piece(0, 0), inbox.at[i, q], recv.at[i, q]).wait()

        def body(at):
            own[i, q, at, :] = (own[i, q, at, :].astype(F32) + inbox[i, q, at, :].astype(F32)).astype(BF)

        row_loop(rows, 64, body)

    for i, n in enumerate((ny, nx)):
        add(i, 0)
        j = slot_of(p, n, p.c)
        to(own.at[i, 0], box.at[1, :, cols(i)], send2.at[i], recv2.at[i], 2 * p.k + core_of(p, j), n).start()
    j = slot_of(p, p.n, p.c)
    keep = core_of(p, j) == p.c
    for i in range(2):
        add(i, 1)

        @pl.when(keep)
        def _():
            pltpu.make_async_copy(own.at[i, 1], box.at[0, :, cols(i)], send2.at[2 + i]).start()

        @pl.when(jnp.logical_not(keep))
        def _():
            to(own.at[i, 1], box.at[0, :, cols(i)], send2.at[2 + i], recv2.at[2 + i], 2 * p.k + core_of(p, j), p.n).start()


def sum_end(p, part, rows, dim, bufs, sems):
    if p.N != 4:
        (got,), (send, recv, local) = bufs, sems
        for t in range(p.N):
            mine = (p.group == p.c) & (p.n == t)

            @pl.when(mine)
            def _():
                pltpu.make_async_copy(part.at[pl.ds(0, rows)], got.at[t], local).wait()

            @pl.when(jnp.logical_not(mine))
            def _():
                pltpu.make_async_copy(part.at[pl.ds(0, rows)], got.at[t], recv.at[t]).wait()

        for j in range(p.N):

            @pl.when(jnp.logical_not(p.owner_is_me(j)))
            def _():
                pltpu.make_async_copy(part.at[pl.ds(j * rows, rows)], got.at[0], send.at[j]).wait()

        return
    own, inbox, box = bufs
    load, send, recv, send2, recv2 = sems
    piece = lambda j, i: own.at[0, 0]
    half = dim // 2
    cols = lambda i: pl.ds(i * half, half)
    for i in range(2):
        for q in range(2):
            pltpu.make_async_copy(piece(0, 0), inbox.at[i, q], send.at[i, q]).wait()
        pltpu.make_async_copy(own.at[i, 0], box.at[1, :, cols(i)], send2.at[i]).wait()
        pltpu.make_async_copy(own.at[i, 0], box.at[1, :, cols(i)], recv2.at[i]).wait()
        pltpu.make_async_copy(own.at[i, 1], box.at[0, :, cols(i)], send2.at[2 + i]).wait()

        @pl.when(p.group != p.c)
        def _():
            pltpu.make_async_copy(own.at[i, 1], box.at[0, :, cols(i)], recv2.at[2 + i]).wait()


def total(p, bufs, at):
    if p.N == 4:
        box = bufs[2]
        return box[0, at, :].astype(F32) + box[1, at, :].astype(F32)
    got = bufs[0]
    out = got[0, at, :].astype(F32)
    for t in range(1, p.N):
        out = out + got[t, at, :].astype(F32)
    return out


PARTS = 4


def line_sems(chips):
    return [DMA((2, chips, PARTS)), DMA((chips, PARTS)), DMA((chips, PARTS)), DMA((chips, PARTS)), DMA((PARTS,))]


def line_parts(p, full, rows):
    size = rows // PARTS

    def at(s, core, q=None):
        first = (2 * s + core) * rows
        if q is None:
            return full.at[pl.ds(pl.multiple_of(first, rows), rows)]
        return full.at[pl.ds(pl.multiple_of(first + q * size, size), size)]

    return at


def each_part(body):
    def one(q, carry):
        body(q)
        return carry

    lax.fori_loop(0, PARTS, one, 0)


def line_copy(p, src, dst, send, recv, k, core):
    return pltpu.make_async_remote_copy(
        src_ref=src, dst_ref=dst, send_sem=send, recv_sem=recv, device_id=(2 * k + core, p.n), device_id_type=MESH
    )


def inside(p, k):
    return (k >= 0) & (k < p.C)


BOTH, UP, DOWN = ((0, 1), (1, -1)), ((0, 1),), ((1, -1),)


def line_push(p, src, full, rows, zsend, zrecv, csend, crecv, local, q, ways=BOTH):
    size = rows // PARTS
    part = src.at[pl.ds(pl.multiple_of(q * size, size), size)]
    there = line_parts(p, full, rows)(p.k, p.c, q)
    for i, sign in ways:

        @pl.when(inside(p, p.k + sign))
        def _():
            line_copy(p, part, there, zsend.at[i, 0, q], zrecv.at[p.k, q], p.k + sign, p.c).start()

    line_copy(p, part, there, csend.at[p.k, q], crecv.at[p.k, q], p.k, 1 - p.c).start()
    pltpu.make_async_copy(part, there, local.at[q]).start()


def came(p, s, ways):
    if ways == BOTH:
        return s == s
    return s <= p.k if ways == UP else s >= p.k


def line_steps(p, src, full, rows, zsend, zrecv, csend, crecv, local, ways=BOTH):
    at = line_parts(p, full, rows)
    piece = src.at[pl.ds(0, rows // PARTS)]

    def at_distance(d):
        def onward(q):
            for i, sign in ways:
                s, t = p.k - sign * d, p.k + sign

                @pl.when(inside(p, s))
                def _():
                    here = at(s, p.c, q)
                    pltpu.make_async_copy(piece, here, zrecv.at[s, q]).wait()

                    @pl.when(inside(p, t))
                    def _():
                        line_copy(p, here, here, zsend.at[i, d, q], zrecv.at[s, q], t, p.c).start()

                    line_copy(p, here, here, csend.at[s, q], crecv.at[s, q], p.k, 1 - p.c).start()

        each_part(onward)

    def settle(q):
        here = at(p.k, p.c, q)
        pltpu.make_async_copy(piece, here, local.at[q]).wait()
        for s in range(p.C):

            @pl.when(came(p, jnp.int32(s), ways))
            def _():
                pltpu.make_async_copy(piece, here, csend.at[s, q]).wait()
                pltpu.make_async_copy(piece, at(s, 1 - p.c, q), crecv.at[s, q]).wait()

        for i, sign in ways:
            for d in range(p.C):

                @pl.when(inside(p, p.k - sign * d) & inside(p, p.k + sign))
                def _():
                    pltpu.make_async_copy(piece, here, zsend.at[i, d, q]).wait()

    return [functools.partial(at_distance, d) for d in range(1, p.C)] + [lambda: each_part(settle)]


def line_sum_bufs(chips, rows, width):
    return [pltpu.VMEM((chips, rows, width), BF)] * 3 + [pltpu.VMEM((2, rows, width), BF), pltpu.VMEM((rows, width), F32)]


def line_sum_sems(chips):
    return [
        DMA((chips, PARTS)), DMA((chips, PARTS)), DMA((chips, PARTS)), DMA((2, chips, PARTS)), DMA((chips, PARTS)),
        DMA((2, PARTS)),
    ]


OTHER = {BOTH: BOTH, UP: DOWN, DOWN: UP}


def line_sum_start(p, part, rows, bufs, sems, ways=BOTH):
    own, inbox, _, _, _ = bufs
    load, csend, crecv, _, _, _ = sems
    at = line_parts(p, part, rows)
    size = rows // PARTS

    def share(s):
        def one(q):
            here = pl.ds(pl.multiple_of(q * size, size), size)
            line_copy(p, at(s, 1 - p.c, q), inbox.at[s, here], csend.at[s, q], crecv.at[s, q], p.k, 1 - p.c).start()
            pltpu.make_async_copy(at(s, p.c, q), own.at[s, here], load.at[s, q]).start()

        each_part(one)

    for d in range(p.C - 1, 0, -1):
        for _, sign in ways:
            s = p.k + sign * d

            @pl.when(inside(p, s))
            def _():
                share(s)

    share(p.k)


def line_sum_steps(p, part, rows, bufs, sems, ways=BOTH):
    own, inbox, relay, box, acc = bufs
    load, csend, crecv, zsend, rrecv, zrecv = sems
    size = rows // PARTS
    step = math.gcd(size, 128)
    piece = line_parts(p, part, rows)(0, 0, 0)

    def rows_of(q):
        return pl.ds(pl.multiple_of(q * size, size), size)

    def add(q, body):
        def one(j, carry):
            body(pl.ds(pl.multiple_of(q * size + j * step, step), step))
            return carry

        lax.fori_loop(0, size // step, one, 0)

    def pair(t, q):
        pltpu.make_async_copy(piece, own.at[t, rows_of(q)], load.at[t, q]).wait()
        pltpu.make_async_copy(piece, inbox.at[t, rows_of(q)], crecv.at[t, q]).wait()

    def at_distance(d):
        def onward(q):
            here = rows_of(q)
            for i, sign in ways:
                t = p.k + sign * d
                behind = inside(p, p.k - sign)

                @pl.when(inside(p, t))
                def _():
                    pair(t, q)

                    @pl.when(jnp.logical_not(behind))
                    def _():
                        def two(at):
                            own[t, at, :] = (own[t, at, :].astype(F32) + inbox[t, at, :].astype(F32)).astype(BF)

                        add(q, two)

                    @pl.when(behind)
                    def _():
                        pltpu.make_async_copy(piece, relay.at[t, here], rrecv.at[t, q]).wait()

                        def three(at):
                            both = own[t, at, :].astype(F32) + inbox[t, at, :].astype(F32)
                            own[t, at, :] = (both + relay[t, at, :].astype(F32)).astype(BF)

                        add(q, three)

                    src = own.at[t, here]
                    if d >= 2:
                        line_copy(p, src, relay.at[t, here], zsend.at[i, d, q], rrecv.at[t, q], p.k + sign, p.c).start()
                    else:
                        line_copy(p, src, box.at[i, here], zsend.at[i, d, q], zrecv.at[i, q], t, p.c).start()

        each_part(onward)

    def last(q):
        here = rows_of(q)
        pair(p.k, q)

        def first(at):
            acc[at, :] = own[p.k, at, :].astype(F32) + inbox[p.k, at, :].astype(F32)

        add(q, first)
        for i, sign in ways:

            @pl.when(inside(p, p.k - sign))
            def _():
                pltpu.make_async_copy(piece, box.at[i, here], zrecv.at[i, q]).wait()

                def more(at):
                    acc[at, :] += box[i, at, :].astype(F32)

                add(q, more)

            for d in range(1, p.C):

                @pl.when(inside(p, p.k + sign * d))
                def _():
                    pltpu.make_async_copy(piece, own.at[0, here], zsend.at[i, d, q]).wait()

        for s in range(p.C):

            @pl.when(came(p, jnp.int32(s), OTHER[ways]))
            def _():
                pltpu.make_async_copy(piece, inbox.at[s, here], csend.at[s, q]).wait()


    return [functools.partial(at_distance, d) for d in range(p.C - 1, 0, -1)] + [lambda: each_part(last)]


def row_loop(rows, step, body):
    def one(i, carry):
        body(pl.ds(pl.multiple_of(i * step, step), step))
        return carry

    lax.fori_loop(0, rows // step, one, 0)


STEP = 64


def inv_rms(u):
    return lax.rsqrt(jnp.mean(u * u, axis=-1, keepdims=True) + EPSILON)


def weave(gate_ref, up_ref, both_ref):
    ff = gate_ref.shape[1]
    t = math.gcd(ff, 256)
    for i in range(0, ff, t):
        both_ref[:, 2 * i : 2 * i + t] = gate_ref[:, i : i + t]
        both_ref[:, 2 * i + t : 2 * i + 2 * t] = up_ref[:, i : i + t]


def unweave_kernel(both_ref, gate_ref, up_ref):
    ff = gate_ref.shape[1]
    t = math.gcd(ff, 256)
    for i in range(0, ff, t):
        gate_ref[:, i : i + t] = both_ref[:, 2 * i : 2 * i + t].astype(F32)
        up_ref[:, i : i + t] = both_ref[:, 2 * i + t : 2 * i + 2 * t].astype(F32)


def input_kernel(wide, narrow, x_ref, gain_ref, shard, gate_ref, up_ref, gathered, full, gu_ref, buf, *sems):
    p = Place(wide, narrow)
    rows = x_ref.shape[0]
    spread, line = sems[:4], (shard, full, shard.shape[0], *sems[4:])
    enter(p, line=True)
    each_part(lambda q: line_push(p, *line, q))
    *steps, end = line_steps(p, *line)

    def body(at):
        u = x_ref[at, :].astype(F32)
        buf[at, :] = (u * inv_rms(u) * gain_ref[...]).astype(BF)

    row_loop(rows, STEP, body)
    spread_start(p, buf, gathered, rows, *spread)
    weave(gate_ref, up_ref, gu_ref)
    steps[0]()
    spread_pass(p, buf, gathered, rows, *spread)
    for step in steps[1:]:
        step()
    spread_end(p, buf, gathered, rows, *spread)
    end()


def turn(u):
    return pltpu.roll(u, u.shape[-1] // 2, 1)


def qkv_kernel(
    wide, narrow, qw, kw, fold, g_ref, x_ref, w_ref, cos_ref, sin_ref, qg_ref, kg_ref,
    gathered, full, qproj_ref, kproj_ref, q_ref, kv_ref, w_buf, load, *sems,
):
    p = Place(wide, narrow)
    rows = g_ref.shape[0]
    hd = cos_ref.shape[1]
    all_rows = x_ref.shape[0]
    size = all_rows // 4
    spread, line = sems[:4], (kv_ref, full, all_rows, *sems[4:])
    weights = pltpu.make_async_copy(w_ref.at[:, pl.ds(0, w_buf.shape[1])], w_buf, load)
    weights.start()
    enter(p, line=True)
    def project(q):
        at = pl.ds(pl.multiple_of(q * size, size), size)
        y = dg(x_ref[at, :], w_buf[...], NN)
        cos, sin = cos_ref[at, :], sin_ref[at, :]
        qproj_ref[at, :] = y[:, :qw]
        kproj_ref[at, :] = y[:, qw : qw + kw]

        def head(lo, gain):
            u = y[:, lo : lo + hd]
            v = u * inv_rms(u) * gain
            return v * cos + turn(v) * sin

        for h in range(kw // hd):
            kv_ref[at, 2 * h * hd : (2 * h + 1) * hd] = head(qw + h * hd, kg_ref[...]).astype(BF)
            kv_ref[at, (2 * h + 1) * hd : (2 * h + 2) * hd] = y[:, qw + kw + h * hd : qw + kw + (h + 1) * hd].astype(BF)
        for i in range(PARTS // 4):
            line_push(p, *line, q * (PARTS // 4) + i, ways=UP)
        for h in range(qw // hd):
            q_ref[at, h * hd : (h + 1) * hd] = (head(h * hd, qg_ref[...]) * fold).astype(BF)

    weights.wait()

    def one(q, carry):
        project(q)
        return carry

    lax.fori_loop(0, 4, one, 0)
    spread_start(p, g_ref, gathered, rows, *spread)
    *steps, end = line_steps(p, *line, ways=UP)
    steps[0]()
    spread_pass(p, g_ref, gathered, rows, *spread)
    for step in steps[1:]:
        step()
    spread_end(p, g_ref, gathered, rows, *spread)
    end()


def middle_kernel(wide, narrow, part, own_ref, gain_ref, mid_ref, gathered, buf, *refs):
    p = Place(wide, narrow)
    rows, dim = own_ref.shape
    bufs, sems, spread = split_refs(narrow, refs)
    enter(p)
    sum_start(p, part, rows, dim, bufs, sems)
    sum_pass(p, part, rows, dim, bufs, sems)
    sum_end(p, part, rows, dim, bufs, sems)

    def body(at):
        u = own_ref[at, :].astype(F32) + total(p, bufs, at)
        mid_ref[at, :] = u
        buf[at, :] = (u * inv_rms(u) * gain_ref[...]).astype(BF)

    row_loop(rows, STEP, body)
    spread_start(p, buf, gathered, rows, *spread)
    spread_pass(p, buf, gathered, rows, *spread)
    spread_end(p, buf, gathered, rows, *spread)


def split_refs(narrow, refs):
    bufs, sems = (3, 5) if narrow == 4 else (1, 3)
    return refs[:bufs], refs[bufs : bufs + sems], refs[bufs + sems :]


def norm_back(u, gain, cot):
    r = inv_rms(u)
    a = cot * gain
    du = r * a - u * (r * r * r) * jnp.mean(a * u, axis=-1, keepdims=True)
    return du, jnp.sum(cot * u * r, axis=0, keepdims=True)


def mlp_back_kernel(
    wide, narrow, low_ref, w_ref, x_ref, mid_ref, gain_ref, grad_ref, back_ref, rows_ref, dgain_ref, wgrad,
    low, w_buf, x_buf, stage, out, load, store, *refs
):
    p = Place(wide, narrow)
    rows, dim = mid_ref.shape
    half = dim // 2
    bufs, sems, _ = split_refs(narrow, refs)
    loads = [pltpu.make_async_copy(low_ref, low, load.at[0])]
    for i in range(2):
        at = pl.ds(i * half, half)
        loads.append(pltpu.make_async_copy(w_ref.at[at], w_buf.at[at], load.at[1 + i]))
    loads.append(pltpu.make_async_copy(x_ref, x_buf, load.at[3]))
    for copy in loads:
        copy.start()
    enter(p)
    for copy in loads[:3]:
        copy.wait()

    def product(j, i):
        a = low[pl.ds(pl.multiple_of(j * rows, rows), rows), :]
        return dg(a, w_buf[pl.ds(pl.multiple_of(i * half, half), half), :], NT).astype(BF)

    sum_start_of(p, product, out, rows, dim, bufs, sems)
    dgain_ref[...] = jnp.zeros_like(dgain_ref)
    loads[3].wait()
    tile = 256

    def write(i):
        return pltpu.make_async_copy(
            stage.at[lax.rem(i, 2)], wgrad.at[pl.ds(pl.multiple_of(i * tile, tile), tile)], store.at[lax.rem(i, 2)]
        )

    def grads(first, last):
        def one(i, carry):
            @pl.when(i >= 2)
            def _():
                write(i - 2).wait()

            stage[lax.rem(i, 2)] = dg(x_buf[:, pl.ds(pl.multiple_of(i * tile, tile), tile)], low[...], TN).astype(BF)
            write(i).start()
            return carry

        lax.fori_loop(first, last, one, 0)

    tiles = dim // tile
    early = 3
    grads(0, early)
    sum_pass(p, out, rows, dim, bufs, sems, loaded=narrow == 4)
    grads(early, tiles)
    sum_end(p, out, rows, dim, bufs, sems)

    def body(at):
        du, dgain = norm_back(mid_ref[at, :], gain_ref[...], total(p, bufs, at))
        back = grad_ref[at, :].astype(F32) + du
        back_ref[at, :] = back
        rows_ref[at, :] = back.astype(BF)
        dgain_ref[...] += dgain

    row_loop(rows, STEP, body)
    write(tiles - 2).wait()
    write(tiles - 1).wait()


def middle_back_kernel(
    wide, narrow, wo_at, groups, hd, rows_ref, hidden, w_ref, wo_ref, o_ref, gathered, next_ref, back_ref, delta_ref,
    h_buf, w_buf, wo_buf, o_buf, load, *spread
):
    p = Place(wide, narrow)
    rows = rows_ref.shape[0]
    pairs = ((hidden, h_buf), (w_ref, w_buf), (wo_ref.at[:, pl.ds(*wo_at)], wo_buf), (o_ref, o_buf))
    loads = [pltpu.make_async_copy(src, dst, load.at[i]) for i, (src, dst) in enumerate(pairs)]
    enter(p)
    spread_start(p, rows_ref, gathered, rows, *spread)
    for copy in loads:
        copy.start()
    for copy in loads[:2]:
        copy.wait()

    def down(at):
        next_ref[at, :] = dg(h_buf[at, :], w_buf[...], NT).astype(BF)

    row_loop(next_ref.shape[0], 256, down)
    for copy in loads[2:]:
        copy.wait()

    def on_slot(j):
        at = pl.ds(pl.multiple_of(j * rows, rows), rows)
        back = dg(gathered[at, :], wo_buf[...], NN).astype(BF)
        back_ref[at, :] = back
        lane = lax.broadcasted_iota(jnp.int32, (rows, hd), 1)
        out = jnp.zeros((rows, hd), F32)
        for h in range(back.shape[1] // hd):
            mine = slice(h * hd, (h + 1) * hd)
            row = 8 * (h // groups) + h % groups
            delta = jnp.sum(back[:, mine].astype(F32) * o_buf[at, mine], axis=1, keepdims=True)
            out = jnp.where(lane == row, delta, out)
        delta_ref[:, at] = jnp.transpose(out)[: delta_ref.shape[0]]

    spread_pass(p, rows_ref, gathered, rows, *spread)
    spread_end(p, rows_ref, gathered, rows, *spread, on_slot=on_slot)


def share_start(me, count, here, slots, sends, recvs, device):
    slots[me] = here[...]
    for t in range(count):

        @pl.when(me != t)
        def _():
            wide_at, narrow_at = device(t)
            to(here, slots.at[me], sends.at[t], recvs.at[me], wide_at, narrow_at).start()


def share_end(me, count, here, slots, sends, recvs):
    for t in range(count):

        @pl.when(me != t)
        def _():
            pltpu.make_async_copy(here, slots.at[t], sends.at[t]).wait()
            pltpu.make_async_copy(here, slots.at[t], recvs.at[t]).wait()

    out = slots[0]
    for t in range(1, count):
        out = out + slots[t]
    here[...] = out


def head_back(cot, u, gain, cos, sin):
    cot = cot * cos - turn(cot) * sin
    return norm_back(u, gain, cot)


def output_kernel(
    wide, narrow, part, mid_ref, dkv, dq, qproj, cos_ref, sin_ref, g_ref, x_ref, m_ref, a_ref,
    out_ref, kv_ref, low_ref, dgain_ref, wgrad_ref, dq_buf, u_buf, x_buf, m_buf, a_buf, load, *refs
):
    p = Place(wide, narrow)
    rows, dim = mid_ref.shape
    kv_rows = kv_ref.shape[0]
    width = low_ref.shape[1]
    hd = cos_ref.shape[1]
    bufs, sems, line = split_refs(narrow, refs)
    sums = (part, rows, dim, bufs, sems)
    chain = (p, dkv, kv_rows, line[:5], line[5:])
    pairs = ((dq, dq_buf), (qproj, u_buf), (x_ref, x_buf), (m_ref, m_buf), (a_ref, a_buf))
    loads = [pltpu.make_async_copy(src, dst, load.at[i]) for i, (src, dst) in enumerate(pairs)]
    enter(p, line=True)
    line_sum_start(*chain, ways=DOWN)
    sum_start(p, *sums)
    for copy in loads:
        copy.start()
    first, *steps, last = line_sum_steps(*chain, ways=DOWN)
    first()
    dgain_ref[...] = jnp.zeros_like(dgain_ref)
    for copy in loads[:2]:
        copy.wait()

    def through_heads(at):
        for h in range(width // hd):
            mine = slice(h * hd, (h + 1) * hd)
            du, dgain = head_back(dq_buf[at, mine], u_buf[at, mine], g_ref[...], cos_ref[at, :], sin_ref[at, :])
            low_ref[at, mine] = du.astype(BF)
            dgain_ref[...] += dgain

    row_loop(low_ref.shape[0], 128, through_heads)
    for copy in loads[2:]:
        copy.wait()

    def grads(first_tile, last_tile):
        def one(i, carry):
            at = pl.ds(pl.multiple_of(i * 256, 256), 256)
            wgrad_ref[at, :width] = dg(x_buf[:, at], low_ref[...], TN).astype(BF)
            wgrad_ref[at, width:] = dg(m_buf[:, at], a_buf[...], TN).astype(BF)
            return carry

        lax.fori_loop(first_tile, last_tile, one, 0)

    tiles = dim // 256
    grads(0, tiles // 2)
    sum_pass(p, *sums)
    steps[0]()
    sum_end(p, *sums)

    def body(at):
        out_ref[at, :] = (mid_ref[at, :] + total(p, bufs, at)).astype(BF)

    row_loop(rows, STEP, body)
    grads(tiles // 2, tiles)
    for step in steps[1:]:
        step()
    last()
    row_loop(kv_rows, 128, lambda at: kv_ref.__setitem__((at, slice(None)), line[4][at, :].astype(BF)))


def input_back_kernel(
    wide, narrow, qw, kw, own_ref, gain_ref, back_ref, gains_ref, wgrad, q_ref, kv_ref, proj_ref, cos_ref, sin_ref, kg_ref,
    w_ref, x_ref, out_ref, gsum_ref, wsum_ref, kvsum_ref,
    gbuf, gbuf2, low, part, kvgrad, w_buf, load, gsend, grecv, gsend2, grecv2, *refs,
):
    p = Place(wide, narrow)
    rows, dim = own_ref.shape
    hd = cos_ref.shape[1]
    all_rows = x_ref.shape[0]
    w_rows = wsum_ref.shape[0]
    bufs, sems, line = split_refs(narrow, refs)
    sums = (part, rows, dim, bufs, sems)
    first_line = (p, wgrad, w_rows, (*line[:4], wsum_ref), line[4:10])
    second_line = (p, kvgrad, w_rows, (*line[10:14], kvsum_ref), line[14:])
    weights = pltpu.make_async_copy(w_ref.at[:, pl.ds(0, w_buf.shape[1])], w_buf, load)
    weights.start()
    enter(p, ring=True)
    line_sum_start(*first_line)
    gsum_ref[...] = gains_ref[...]
    size = min(all_rows, 256)
    first = line_sum_steps(*first_line)
    first[0]()
    weights.wait()

    def through_heads(at):
        low[at, :qw] = q_ref[at, :]
        for h in range(kw // hd):
            key = slice(2 * h * hd, (2 * h + 1) * hd)
            value = slice((2 * h + 1) * hd, (2 * h + 2) * hd)
            mine = slice(qw + h * hd, qw + (h + 1) * hd)
            du, dgain = head_back(
                kv_ref[at, key].astype(F32), proj_ref[at, h * hd : (h + 1) * hd], kg_ref[...], cos_ref[at, :], sin_ref[at, :]
            )
            low[at, mine] = du.astype(BF)
            low[at, qw + kw + h * hd : qw + kw + (h + 1) * hd] = kv_ref[at, value]
            gsum_ref[:, 2 * dim + hd :] += dgain
        part[at, :] = dg(low[at, :], w_buf[...], NT).astype(BF)

    row_loop(all_rows, size, through_heads)
    sum_start(p, *sums)
    first[1]()

    def key_grads(at):
        kvgrad[at, :] = dg(x_ref[:, at], low[:, qw:], TN).astype(BF)

    row_loop(dim, 256, key_grads)
    line_sum_start(*second_line)
    second = line_sum_steps(*second_line)
    second[0]()
    sum_pass(p, *sums)
    for step in first[2:-1]:
        step()
    sum_end(p, *sums)

    def body(at):
        du, dgain = norm_back(own_ref[at, :].astype(F32), gain_ref[...], total(p, bufs, at))
        out_ref[at, :] = back_ref[at, :] + du
        gsum_ref[:, :dim] += dgain

    row_loop(rows, STEP, body)

    share_start(p.n, narrow, gsum_ref, gbuf, gsend, grecv, lambda t: (p.w, t))
    second[1]()
    first[-1]()
    share_end(p.n, narrow, gsum_ref, gbuf, gsend, grecv)
    share_start(p.w, wide, gsum_ref, gbuf2, gsend2, grecv2, lambda t: (t, p.n))
    for step in second[2:]:
        step()
    share_end(p.w, wide, gsum_ref, gbuf2, gsend2, grecv2)


VM = pl.BlockSpec(memory_space=pltpu.VMEM)


HB = pl.BlockSpec(memory_space=pl.ANY)


def comm_call(kernel, name, cid, out_shape, in_specs, out_specs, scratch, *args):
    return pl.pallas_call(
        kernel,
        out_shape=out_shape,
        in_specs=in_specs,
        out_specs=out_specs,
        scratch_shapes=scratch,
        compiler_params=pltpu.CompilerParams(collective_id=cid, has_side_effects=True, vmem_limit_bytes=60 << 20),
        cost_estimate=pl.CostEstimate(flops=0, bytes_accessed=160_000_000, transcendentals=0),
        name=name,
    )(*args)


def sds(shape, kind):
    return jax.ShapeDtypeStruct(shape, kind)


def plain(kernel, name, grid, in_specs, out_specs, out_shape, flops, nbytes, *args, scratch=(), aliases=None):
    return pl.pallas_call(
        kernel,
        out_shape=out_shape,
        grid=grid,
        in_specs=in_specs,
        out_specs=out_specs,
        scratch_shapes=scratch,
        input_output_aliases=aliases or {},
        compiler_params=pltpu.CompilerParams(vmem_limit_bytes=52 << 20),
        cost_estimate=pl.CostEstimate(flops=flops, bytes_accessed=nbytes, transcendentals=0),
        name=name,
    )(*args)


def whole(shape):
    return pl.BlockSpec(shape, lambda *i: (0,) * len(shape), pipeline_mode=pl.Buffered(1))


def by_rows(tm, width):
    return pl.BlockSpec((tm, width), lambda i: (i, 0))


def mlp_fwd_kernel(x_ref, w_ref, gu_ref, h_ref):
    t = h_ref.shape[1]
    y = dg(x_ref[...], w_ref[...], NN)
    gate, up = y[:, :t], y[:, t:]
    gu_ref[...] = y
    h_ref[...] = (gate * jax.nn.sigmoid(gate) * up).astype(BF)


def mlp_fwd(x, w, t):
    rows, dim = x.shape
    ff2 = w.shape[1]
    return plain(
        mlp_fwd_kernel, "mlp_fwd", (ff2 // (2 * t),),
        [whole((rows, dim)), pl.BlockSpec((dim, 2 * t), lambda i: (0, i))],
        [pl.BlockSpec((rows, 2 * t), lambda i: (0, i)), pl.BlockSpec((rows, t), lambda i: (0, i))],
        (sds((rows, ff2), F32), sds((rows, ff2 // 2), BF)),
        2 * rows * dim * ff2, rows * dim * 2 + dim * ff2 * 2 + rows * ff2 * 5, x, w,
    )


def mlp_bwd_kernel(g_ref, w_ref, gu_ref, out_ref):
    t = w_ref.shape[1]
    hb = dg(g_ref[...], w_ref[...], NN)
    gate, up = gu_ref[:, :t], gu_ref[:, t:]
    s = jax.nn.sigmoid(gate)
    gs = hb * s
    out_ref[:, :t] = (gs * up * (1.0 + gate * (1.0 - s))).astype(BF)
    out_ref[:, t:] = (gs * gate).astype(BF)


def mlp_bwd(g, w, gu, t):
    rows, dim = g.shape
    ff = w.shape[1]
    return plain(
        mlp_bwd_kernel, "mlp_bwd", (ff // t,),
        [whole((rows, dim)), pl.BlockSpec((dim, t), lambda i: (0, i)), pl.BlockSpec((rows, 2 * t), lambda i: (0, i))],
        pl.BlockSpec((rows, 2 * t), lambda i: (0, i)), sds((rows, 2 * ff), BF),
        2 * rows * dim * ff, rows * dim * 2 + dim * ff * 2 + rows * ff * 12, g, w, gu,
    )


def fwd_kernel(groups, hd, tab, q_ref, kv_ref, o_ref, low_ref, lse_ref, acc, lsum):
    s = pl.program_id(1)
    block = q_ref.shape[0]
    diag, first, last = tab[2, s], tab[3, s], tab[4, s]

    @pl.when(first == 1)
    def _():
        acc[...] = jnp.zeros_like(acc)
        lsum[...] = jnp.zeros_like(lsum)

    def work(masked):
        k, v = kv_ref[:, :hd], kv_ref[:, hd:]
        for g in range(groups):
            at = slice(g * hd, (g + 1) * hd)
            scores = dg(q_ref[:, at], k, NT)
            if masked:
                row = lax.broadcasted_iota(jnp.int32, scores.shape, 0)
                col = lax.broadcasted_iota(jnp.int32, scores.shape, 1)
                scores = jnp.where(col <= row, scores, MASKED)
            probs = jnp.exp2(scores)
            part = probs[:, :128]
            for j in range(1, block // 128):
                part = part + probs[:, j * 128 : (j + 1) * 128]
            lsum[g] += part
            acc[:, at] += dg(probs.astype(BF), v, NN)

    @pl.when(diag == 0)
    def _():
        work(False)

    @pl.when(diag == 1)
    def _():
        work(True)

    @pl.when(last == 1)
    def _():
        lane = lax.broadcasted_iota(jnp.int32, (block, 128), 1)
        lse = jnp.zeros((block, 128), F32)
        for g in range(groups):
            at = slice(g * hd, (g + 1) * hd)
            l = jnp.sum(lsum[g], axis=1, keepdims=True)
            out = acc[:, at] / l
            o_ref[:, at] = out
            low_ref[:, at] = out.astype(BF)
            lse = jnp.where(lane == g, jnp.log2(l), lse)
        lse_ref[...] = jnp.transpose(lse)[: lse_ref.shape[0]]


def attn_fwd(tab, q, kv, groups, hd, block):
    rows, width = q.shape
    gw = groups * hd
    heads = width // gw
    steps = tab.shape[1]
    mine = pl.BlockSpec((block, gw), lambda h, s, t: (t[0, s], h))
    return pl.pallas_call(
        functools.partial(fwd_kernel, groups, hd),
        out_shape=(sds((rows, width), F32), sds((rows, width), BF), sds((8 * heads, rows), F32)),
        grid_spec=pltpu.PrefetchScalarGridSpec(
            num_scalar_prefetch=1,
            grid=(heads, steps),
            in_specs=[mine, pl.BlockSpec((block, 2 * hd), lambda h, s, t: (t[1, s], h))],
            out_specs=[mine, mine, pl.BlockSpec((8, block), lambda h, s, t: (h, t[0, s]))],
            scratch_shapes=[pltpu.VMEM((block, gw), F32), pltpu.VMEM((groups, block, 128), F32)],
        ),
        compiler_params=pltpu.CompilerParams(vmem_limit_bytes=48 << 20),
        cost_estimate=pl.CostEstimate(
            flops=heads * steps * block * block * gw * 4,
            bytes_accessed=heads * steps * block * hd * 8,
            transcendentals=heads * steps * block * block * groups,
        ),
        name="attn_fwd",
    )(tab, q, kv)


def bwd_kernel(groups, hd, tab, q_ref, do_ref, kv_ref, lse_ref, delta_ref, dq_ref, dkv_ref, dq_sum, dkv_sum):
    s = pl.program_id(1)
    block = q_ref.shape[0]
    qi, diag, first, last = tab[0, s], tab[2, s], tab[3, s], tab[4, s]

    @pl.when(s == 0)
    def _():
        dq_sum[...] = jnp.zeros_like(dq_sum)

    @pl.when(first == 1)
    def _():
        dkv_sum[...] = jnp.zeros_like(dkv_sum)

    def work(masked):
        k, v = kv_ref[:, :hd], kv_ref[:, hd:]
        for g in range(groups):
            at = slice(g * hd, (g + 1) * hd)
            q, do = q_ref[:, at], do_ref[:, at]
            scores = dg(k, q, NT) - lse_ref[g : g + 1, :]
            if masked:
                row = lax.broadcasted_iota(jnp.int32, scores.shape, 0)
                col = lax.broadcasted_iota(jnp.int32, scores.shape, 1)
                scores = jnp.where(row <= col, scores, MASKED)
            probs = jnp.exp2(scores)
            dots = dg(v, do, NT)
            dkv_sum[:, hd:] += dg(probs.astype(BF), do, NN)
            back = (probs * (dots - delta_ref[g : g + 1, :])).astype(BF)
            dkv_sum[:, :hd] += dg(back, q, NN)
            dq_sum[qi, :, at] += dg(back, k, TN)

    @pl.when(diag == 0)
    def _():
        work(False)

    @pl.when(diag == 1)
    def _():
        work(True)

    @pl.when(last == 1)
    def _():
        dkv_ref[:, :hd] = (dkv_sum[:, :hd] * math.log(2.0)).astype(BF)
        dkv_ref[:, hd:] = dkv_sum[:, hd:].astype(BF)

    @pl.when(s == pl.num_programs(1) - 1)
    def _():
        for i in range(dq_sum.shape[0]):
            dq_ref[i * block : (i + 1) * block, :] = dq_sum[i] * hd**-0.5


def attn_bwd(tab, q, do, kv, lse, delta, groups, hd, block):
    rows, width = q.shape
    gw = groups * hd
    heads = width // gw
    steps = tab.shape[1]
    mine = pl.BlockSpec((block, gw), lambda h, s, t: (t[0, s], h))
    keys = pl.BlockSpec((block, 2 * hd), lambda h, s, t: (t[1, s], h))
    stat = pl.BlockSpec((8, block), lambda h, s, t: (h, t[0, s]))
    return pl.pallas_call(
        functools.partial(bwd_kernel, groups, hd),
        out_shape=(sds((rows, width), F32), sds(kv.shape, BF)),
        grid_spec=pltpu.PrefetchScalarGridSpec(
            num_scalar_prefetch=1,
            grid=(heads, steps),
            in_specs=[mine, mine, keys, stat, stat],
            out_specs=[pl.BlockSpec((rows, gw), lambda h, s, t: (0, h)), keys],
            scratch_shapes=[pltpu.VMEM((rows // block, block, gw), F32), pltpu.VMEM((block, 2 * hd), F32)],
        ),
        compiler_params=pltpu.CompilerParams(vmem_limit_bytes=48 << 20),
        cost_estimate=pl.CostEstimate(
            flops=heads * steps * block * block * gw * 10,
            bytes_accessed=heads * steps * block * hd * 16,
            transcendentals=heads * steps * block * block * groups,
        ),
        name="attn_bwd",
    )(tab, q, do, kv, lse, delta)


def place(w):
    k, core = w // 2, w % 2
    return 4 * k + core, 4 * k + 3 - core


def block_row(b):
    m = b % 4
    core = jnp.where((m == 1) | (m == 2), 1, 0)
    return 2 * (2 * (b // 4) + core) + jnp.where(m < 2, 0, 1)


def tables(w, chips):
    a, b = place(w)
    count = a + b + 2
    every = jnp.arange(8 * chips - 2, dtype=jnp.int32)
    s, idle = jnp.minimum(every, count - 1), every >= count
    in_a = s <= a
    key = jnp.where(in_a, s, s - a - 1)
    diag = jnp.where(in_a, s == a, s == count - 1)
    fwd = [jnp.where(in_a, 0, 1), block_row(key), jnp.where(idle, 2, diag), ~idle & (key == 0), ~idle & diag]
    both = s < 2 * (a + 1)
    even = s % 2 == 0
    key = jnp.where(both, s // 2, s - (a + 1))
    query = jnp.where(both & even, 0, 1)
    diag = key == jnp.where(query == 0, a, b)
    zero = (every >= count) & (w % 2 == 1)
    key = jnp.where(zero, b + 1, key)
    only = zero & (every == count)
    bwd = [query, block_row(key), jnp.where(idle, 2, diag), only | ~idle & (~both | even), only | ~idle & (~both | ~even)]
    return tuple(jnp.stack([row.astype(jnp.int32) for row in rows]) for rows in (fwd, bwd))


def rotation(positions, head_dim):
    steps_half = jnp.arange(head_dim // 2).astype(F32)
    inverse = jnp.exp(steps_half * (-2.0 * math.log(1000000.0) / head_dim))
    angles = positions.astype(F32)[:, None] * inverse[None, :]
    cos, sin = jnp.cos(angles), jnp.sin(angles)
    return jnp.concatenate([cos, cos], axis=1), jnp.concatenate([-sin, sin], axis=1)


def per_device(
    wide, narrow,
    layer_input, w_query, w_key, w_value, w_output, w_gate, w_up, w_down,
    attn_gain, mlp_gain, query_gain, key_gain, out_grad,
):
    hd = query_gain.shape[0]
    rows, dim = layer_input.shape
    all_rows = narrow * rows
    chips = wide // 2
    block = all_rows // 2
    qw, kw = w_query.shape[1], w_key.shape[1]
    ff = w_gate.shape[1]
    groups = qw // kw
    kv_heads = kw // hd
    w = lax.axis_index("wide")
    fwd_tab, bwd_tab = tables(w, chips)
    first, second = place(w)
    at = jnp.arange(block, dtype=jnp.int32)
    positions = jnp.concatenate([first * block + at, second * block + at])
    cos_table, sin_table = rotation(positions, hd)

    def gather(shard):
        return lax.all_gather(shard, "wide", axis=0, tiled=True)

    def scatter(grad):
        return lax.psum_scatter(grad, "wide", scatter_dimension=0, tiled=True)

    t = math.gcd(ff, 256)

    spread_s = spread_sems(narrow)
    sum_s = [*sum_bufs(narrow, rows, dim), *sum_sems(narrow)]
    row_buf = pltpu.VMEM((rows, dim), BF)
    low_rows, full_rows, all_low = sds((rows, dim), BF), sds((rows, dim), F32), sds((all_rows, dim), BF)
    ring = functools.partial
    qg, kg = query_gain[None], key_gain[None]
    after = lax.optimization_barrier

    in_scratch = [*spread_s, *line_sems(chips)]
    shard = jnp.concatenate([w_query, w_key, w_value, w_output.T], axis=1)
    normed_all, w_attn, gu_shard = comm_call(
        ring(input_kernel, wide, narrow), "input_rows", 0,
        (all_low, sds((dim, shard.shape[1]), BF), sds((w_gate.shape[0], 2 * ff), BF)),
        [VM, VM, HB, VM, VM], (HB, HB, VM), [row_buf, *in_scratch],
        layer_input, attn_gain[None], shard, w_gate, w_up,
    )
    width = qw + 2 * kw
    grad_all, kv, query_proj, key_proj, queries = comm_call(
        ring(qkv_kernel, wide, narrow, qw, kw, hd**-0.5 * math.log2(math.e)), "qkv_rows", 1,
        (all_low, sds((wide * all_rows, 2 * kw), BF), sds((all_rows, qw), F32),
         sds((all_rows, kw), F32), sds((all_rows, qw), BF)),
        [VM, VM, HB, VM, VM, VM, VM], (HB, HB, VM, VM, VM),
        [pltpu.VMEM((all_rows, 2 * kw), BF), pltpu.VMEM((dim, width), BF), DMA, *in_scratch],
        out_grad, normed_all, w_attn, cos_table, sin_table, qg, kg,
    )
    gu_shard, w_down, kv = after((gu_shard, w_down, kv))
    w_gu, w_d = gather(gu_shard), gather(w_down.T)
    attended, attended_low, lse = attn_fwd(fwd_tab, queries, kv, groups, hd, block)
    w_o = w_attn[:, qw + 2 * kw :]
    middle, normed_mlp = comm_call(
        ring(middle_kernel, wide, narrow), "middle_rows", 2, (full_rows, all_low), [HB, VM, VM], (VM, HB),
        [row_buf, *sum_s, *spread_s], dg(attended_low, w_o, NT).astype(BF), layer_input, mlp_gain[None],
    )
    gate_up, hidden_low = mlp_fwd(normed_mlp, w_gu, t)
    grad_down = dg(grad_all, hidden_low, TN).astype(BF)
    w_d, _ = after((w_d, grad_down))
    gu_low = mlp_bwd(grad_all, w_d, gate_up, t)
    middle_back, middle_low, mlp_gain_part, grad_gu = comm_call(
        ring(mlp_back_kernel, wide, narrow), "mlp_back", 6,
        (full_rows, low_rows, sds((1, dim), F32), sds((dim, 2 * ff), BF)), [HB, HB, HB, VM, VM, VM], (VM, VM, VM, HB),
        [pltpu.VMEM((all_rows, 2 * ff), BF), pltpu.VMEM((dim, 2 * ff), BF), pltpu.VMEM((all_rows, dim), BF),
         pltpu.VMEM((2, 256, 2 * ff), BF), product_bufs(narrow, rows, dim), DMA((4,)), DMA((2,)), *sum_s],
        gu_low, w_gu, normed_mlp, middle, mlp_gain[None], out_grad,
    )
    grad_down, grad_gu = scatter(grad_down), scatter(grad_gu)
    middle_all, down_part, back, delta = comm_call(
        ring(middle_back_kernel, wide, narrow, (width, qw), groups, hd), "middle_back", 3,
        (all_low, all_low, sds((all_rows, qw), BF), sds((8 * kv_heads, all_rows), F32)),
        [VM, HB, HB, HB, HB], (VM, VM, VM, VM),
        [pltpu.VMEM((all_rows, ff), BF), pltpu.VMEM((dim, ff), BF), pltpu.VMEM((dim, qw), BF), pltpu.VMEM((all_rows, qw), F32),
         DMA((4,)), *spread_s],
        middle_low, hidden_low, w_d, w_attn, attended,
    )
    query_back, dkv = attn_bwd(bwd_tab, queries, back, kv, lse, delta, groups, hd, block)
    dkv, grad_down = after((dkv, grad_down))
    layer_output, kv_sum, q_low, query_gain_part, grad_qo = comm_call(
        ring(output_kernel, wide, narrow), "output_rows", 4,
        (low_rows, sds((all_rows, 2 * kw), BF), sds((all_rows, qw), BF), sds((1, hd), F32), sds((dim, 2 * qw), BF)),
        [HB, VM, HB, HB, HB, VM, VM, VM, HB, HB, HB], (VM, VM, VM, VM, VM),
        [pltpu.VMEM((all_rows, qw), F32), pltpu.VMEM((all_rows, qw), F32), pltpu.VMEM((all_rows, dim), BF),
         pltpu.VMEM((all_rows, dim), BF), pltpu.VMEM((all_rows, qw), BF), DMA((5,)), *sum_s,
         *line_sum_bufs(chips, all_rows, 2 * kw), *line_sum_sems(chips)],
        down_part, middle, dkv, query_back, query_proj, cos_table, sin_table, qg, normed_all, middle_all, attended_low,
    )
    kv_sum, grad_gu = after((kv_sum, grad_gu))
    half = sds((dim // wide, ff), F32)
    grad_gate, grad_up = plain(
        unweave_kernel, "unweave", (1,), [whole(grad_gu.shape)], [whole(half.shape)] * 2, [half, half], 0, grad_gu.size * 6, grad_gu
    )
    gains = jnp.concatenate([jnp.zeros((1, dim), F32), mlp_gain_part, query_gain_part, jnp.zeros((1, hd), F32)], axis=1)
    w_rows = dim // wide
    input_grad, gain_sums, grad_qo, grad_kv = comm_call(
        ring(input_back_kernel, wide, narrow, qw, kw), "input_back", 5,
        (full_rows, sds(gains.shape, F32), sds((w_rows, 2 * qw), F32), sds((w_rows, 2 * kw), F32)),
        [VM, VM, VM, VM, HB, VM, VM, VM, VM, VM, VM, HB, VM],
        (VM, VM, VM, VM),
        [pltpu.VMEM((narrow, *gains.shape), F32), pltpu.VMEM((wide, *gains.shape), F32),
         pltpu.VMEM((all_rows, width), BF), pltpu.VMEM((all_rows, dim), BF), pltpu.VMEM((dim, 2 * kw), BF),
         pltpu.VMEM((dim, width), BF), DMA, DMA((narrow,)), DMA((narrow,)), DMA((wide,)), DMA((wide,)), *sum_s,
         *line_sum_bufs(chips, w_rows, 2 * qw)[:4], *line_sum_sems(chips),
         *line_sum_bufs(chips, w_rows, 2 * kw)[:4], *line_sum_sems(chips)],
        layer_input, attn_gain[None], middle_back, gains, grad_qo, q_low, kv_sum, key_proj, cos_table, sin_table, kg, w_attn, normed_all,
    )
    g = gain_sums[0]
    return (
        layer_output, input_grad,
        grad_qo[:, :qw], grad_kv[:, :kw], grad_kv[:, kw:],
        grad_qo[:, qw:].T, grad_gate, grad_up,
        grad_down.T.astype(F32),
        g[:dim], g[dim : 2 * dim], g[2 * dim : 2 * dim + hd], g[2 * dim + hd :],
    )


def solution(mesh):
    rows = P(("wide", "narrow"), None)
    weight, turned = P("wide", "narrow"), P("narrow", "wide")
    return jax.shard_map(
        functools.partial(per_device, mesh.shape["wide"], mesh.shape["narrow"]),
        mesh=mesh,
        in_specs=(rows, weight, weight, weight, turned, weight, weight, turned, P(), P(), P(), P(), rows),
        out_specs=(rows, rows, weight, weight, weight, turned, weight, weight, turned, P(), P(), P(), P()),
        check_vma=False,
    )
```

```python
import functools
import math

import jax
import jax.numpy as jnp
from jax import lax
from jax.experimental import pallas as pl
from jax.experimental.pallas import tpu as pltpu
from jax.sharding import PartitionSpec as P

EPSILON = 1e-06
MASKED = -1e30
F32 = jnp.float32
BF = jnp.bfloat16
MESH = pl.DeviceIdType.MESH
NT = (((1,), (1,)), ((), ()))
NN = (((1,), (0,)), ((), ()))
TN = (((0,), (0,)), ((), ()))


def dg(a, b, dims):
    return lax.dot_general(a, b, dims, preferred_element_type=F32)
DMA = pltpu.SemaphoreType.DMA


class Place:
    def __init__(self, wide, narrow):
        self.W, self.N = wide, narrow
        self.C, self.half = wide // 2, narrow // 2
        self.w, self.n = lax.axis_index("wide"), lax.axis_index("narrow")
        self.k, self.c = self.w // 2, lax.rem(self.w, 2)
        late = (self.n >= self.half).astype(jnp.int32)
        self.group = lax.rem(self.c + late, 2)
        self.slot = jnp.where(self.group == 0, self.n, lax.rem(self.n + self.half, self.N))

    def owner(self, j):
        core = 1 if j >= self.half else 0
        n = jnp.where(self.c == 0, j, (j + self.half) % self.N)
        return core, n

    def owner_is_me(self, j):
        core, n = self.owner(j)
        return (self.c == core) & (self.n == n)


def enter(p, line=False, ring=False):
    barrier = pltpu.get_barrier_semaphore()

    def greet(device):
        pl.semaphore_signal(barrier, inc=1, device_id=device, device_id_type=MESH)

    for core in range(2):
        for n in range(p.N):

            @pl.when((p.c != core) | (p.n != n))
            def _():
                greet((2 * p.k + core, n))

    peers = 2 * p.N - 1
    if line or ring:
        for k in range(p.C):

            @pl.when(p.k != k)
            def _():
                greet((2 * k + p.c, p.n))
                if ring:
                    greet((2 * k + 1 - p.c, p.n))

        peers += (2 if ring else 1) * (p.C - 1)
    pl.semaphore_wait(barrier, peers)


def slot_of(p, n, group):
    return jnp.where(group == 0, n, lax.rem(n + p.half, p.N))


def neighbours(p):
    return p.n + 1 - 2 * lax.rem(p.n, 2), lax.rem(p.n + 2, 4), 3 - p.n


def to(src, dst, send, recv, wide, narrow):
    return pltpu.make_async_remote_copy(
        src_ref=src, dst_ref=dst, send_sem=send, recv_sem=recv, device_id=(wide, narrow), device_id_type=MESH
    )


def spread_sems(narrow):
    return [DMA((narrow, 2)), DMA((narrow, 2)), DMA((2,)), DMA((2,))]


def spread_start(p, src, gathered, rows, send, recv, local, onward):
    half = rows // 2
    view = lambda i: gathered.at[pl.ds(pl.multiple_of(p.slot * rows + i * half, half), half)]
    part = lambda i: src.at[pl.ds(i * half, half)]
    mine = p.group == p.c
    square = p.N == 4
    if square:
        nx, ny, _ = neighbours(p)
        targets = [(nx, (0, 1)), (ny, (1, 0))]
        order = [(t, q, i) for q in range(2) for t, halves in targets for i in (halves[q],)]
        for t, q, i in order:
            at = 0 if t is nx else 1
            to(part(i), view(i), send.at[at, i], recv.at[p.slot, i], 2 * p.k + p.group, t).start()
    else:
        for t in range(p.N):

            @pl.when(p.n != t)
            def _():
                for i in range(2):
                    to(part(i), view(i), send.at[t, i], recv.at[p.slot, i], 2 * p.k + p.group, t).start()

    @pl.when(mine)
    def _():
        for i in range(2):
            pltpu.make_async_copy(part(i), view(i), local.at[i]).start()

    @pl.when(jnp.logical_not(mine))
    def _():
        for i in range(2):
            to(part(i), view(i), local.at[i], recv.at[p.slot, i], 2 * p.k + p.group, p.n).start()


def spread_pass(p, src, gathered, rows, send, recv, local, onward):
    if p.N == 4:
        half = rows // 2
        piece = src.at[pl.ds(0, half)]
        nx, ny, _ = neighbours(p)
        for i, (n, other) in enumerate(((nx, ny), (ny, nx))):
            j = slot_of(p, n, p.c)
            here = gathered.at[pl.ds(pl.multiple_of(j * rows + i * half, half), half)]
            pltpu.make_async_copy(piece, here, recv.at[j, i]).wait()
            to(here, here, onward.at[i], recv.at[j, i], p.w, other).start()


def spread_end(p, src, gathered, rows, send, recv, local, onward, on_slot=lambda j: None):
    half = rows // 2
    piece = src.at[pl.ds(0, half)]
    mine = p.group == p.c
    at = lambda j, i: gathered.at[pl.ds(pl.multiple_of(j * rows + i * half, half), half)]

    def arrive(j, i):
        pltpu.make_async_copy(piece, at(j, i), recv.at[j, i]).wait()

    for i in range(2):
        pltpu.make_async_copy(piece, at(0, 0), local.at[i]).wait()
    here = slot_of(p, p.n, p.c)

    @pl.when(jnp.logical_not(mine))
    def _():
        arrive(here, 0)
        arrive(here, 1)

    on_slot(here)
    if p.N == 4:
        nx, ny, nd = neighbours(p)
        jx, jy, jd = (slot_of(p, n, p.c) for n in (nx, ny, nd))
        arrive(jx, 1)
        on_slot(jx)
        arrive(jy, 0)
        on_slot(jy)
        arrive(jd, 0)
        arrive(jd, 1)
        on_slot(jd)
        for i in range(2):
            pltpu.make_async_copy(piece, at(0, 0), onward.at[i]).wait()
            for t in range(2):
                pltpu.make_async_copy(piece, at(0, 0), send.at[t, i]).wait()
    else:
        for t in range(p.N):

            @pl.when(p.n != t)
            def _():
                for i in range(2):
                    pltpu.make_async_copy(piece, at(0, 0), send.at[t, i]).wait()
                    arrive(slot_of(p, t, p.c), i)
                on_slot(slot_of(p, t, p.c))


def sum_bufs(narrow, rows, dim):
    if narrow == 4:
        half = pltpu.VMEM((2, 2, rows, dim // 2), BF)
        return [half, half, pltpu.VMEM((2, rows, dim), BF)]
    return [pltpu.VMEM((narrow, rows, dim), BF)]


def sum_sems(narrow):
    if narrow == 4:
        return [DMA((2, 2)), DMA((2, 2)), DMA((2, 2)), DMA((4,)), DMA((4,))]
    return [DMA((narrow,)), DMA((narrow,)), DMA]


def pieces(p, part, rows, dim):
    half = dim // 2
    return lambda j, i: part.at[pl.ds(pl.multiple_of(j * rows, rows), rows), pl.ds(i * half, half)]


def sum_start(p, part, rows, dim, bufs, sems):
    if p.N != 4:
        (got,), (send, recv, local) = bufs, sems
        for j in range(p.N):
            core, n = p.owner(j)
            mine = p.owner_is_me(j)
            src = part.at[pl.ds(j * rows, rows)]

            @pl.when(mine)
            def _():
                pltpu.make_async_copy(src, got.at[p.n], local).start()

            @pl.when(jnp.logical_not(mine))
            def _():
                to(src, got.at[p.n], send.at[j], recv.at[p.n], 2 * p.k + core, n).start()

        return
    own, inbox, _ = bufs
    load, send, recv, _, _ = sems
    piece = pieces(p, part, rows, dim)
    nx, ny, nd = neighbours(p)
    across, here = slot_of(p, nd, p.c), slot_of(p, p.n, p.c)
    for i, n in enumerate((nx, ny)):
        to(piece(across, i), inbox.at[i, 0], send.at[i, 0], recv.at[i, 0], p.w, n).start()
    for i, n in enumerate((ny, nx)):
        pltpu.make_async_copy(piece(slot_of(p, n, p.c), i), own.at[i, 0], load.at[i, 0]).start()
    for i, n in enumerate((nx, ny)):
        to(piece(slot_of(p, n, p.c), i), inbox.at[i, 1], send.at[i, 1], recv.at[i, 1], p.w, n).start()
        pltpu.make_async_copy(piece(here, i), own.at[i, 1], load.at[i, 1]).start()


def product_bufs(narrow, rows, dim):
    shape = (4, rows, dim // 2) if narrow == 4 else (narrow * rows, dim)
    return pltpu.VMEM(shape, BF)


def sum_start_of(p, product, out, rows, dim, bufs, sems):
    half = dim // 2
    if p.N != 4:

        def one(j, carry):
            for i in range(2):
                out[pl.ds(pl.multiple_of(j * rows, rows), rows), i * half : (i + 1) * half] = product(j, i)
            return carry

        lax.fori_loop(0, p.N, one, 0)
        sum_start(p, out, rows, dim, bufs, sems)
        return
    own, inbox, _ = bufs
    _, send, recv, _, _ = sems
    nx, ny, nd = neighbours(p)
    across, jx, jy, here = (slot_of(p, n, p.c) for n in (nd, nx, ny, p.n))

    def one(t, carry):
        i = lax.rem(t, 2)
        q = lax.rem(t // 2, 2)
        beside = jnp.where(i == 0, jx, jy)
        other = jnp.where(i == 0, jy, jx)
        j = jnp.where(t < 4, jnp.where(q == 0, across, beside), jnp.where(q == 0, other, here))
        y = product(j, i)

        @pl.when(t < 4)
        def _():
            out[t] = y
            to(out.at[t], inbox.at[i, q], send.at[i, q], recv.at[i, q], p.w, jnp.where(i == 0, nx, ny)).start()

        @pl.when(t >= 4)
        def _():
            own[i, q] = y

        return carry

    lax.fori_loop(0, 8, one, 0)


def core_of(p, j):
    return (j >= p.half).astype(jnp.int32)


def sum_pass(p, part, rows, dim, bufs, sems, loaded=False):
    if p.N != 4:
        return
    own, inbox, box = bufs
    load, send, recv, send2, recv2 = sems
    piece = lambda j, i: own.at[0, 0]
    half = dim // 2
    nx, ny, _ = neighbours(p)
    cols = lambda i: pl.ds(i * half, half)

    def add(i, q):
        if not loaded:
            pltpu.make_async_copy(piece(0, 0), own.at[i, q], load.at[i, q]).wait()
        pltpu.make_async_copy(piece(0, 0), inbox.at[i, q], recv.at[i, q]).wait()

        def body(at):
            own[i, q, at, :] = (own[i, q, at, :].astype(F32) + inbox[i, q, at, :].astype(F32)).astype(BF)

        row_loop(rows, 64, body)

    for i, n in enumerate((ny, nx)):
        add(i, 0)
        j = slot_of(p, n, p.c)
        to(own.at[i, 0], box.at[1, :, cols(i)], send2.at[i], recv2.at[i], 2 * p.k + core_of(p, j), n).start()
    j = slot_of(p, p.n, p.c)
    keep = core_of(p, j) == p.c
    for i in range(2):
        add(i, 1)

        @pl.when(keep)
        def _():
            pltpu.make_async_copy(own.at[i, 1], box.at[0, :, cols(i)], send2.at[2 + i]).start()

        @pl.when(jnp.logical_not(keep))
        def _():
            to(own.at[i, 1], box.at[0, :, cols(i)], send2.at[2 + i], recv2.at[2 + i], 2 * p.k + core_of(p, j), p.n).start()


def sum_end(p, part, rows, dim, bufs, sems):
    if p.N != 4:
        (got,), (send, recv, local) = bufs, sems
        for t in range(p.N):
            mine = (p.group == p.c) & (p.n == t)

            @pl.when(mine)
            def _():
                pltpu.make_async_copy(part.at[pl.ds(0, rows)], got.at[t], local).wait()

            @pl.when(jnp.logical_not(mine))
            def _():
                pltpu.make_async_copy(part.at[pl.ds(0, rows)], got.at[t], recv.at[t]).wait()

        for j in range(p.N):

            @pl.when(jnp.logical_not(p.owner_is_me(j)))
            def _():
                pltpu.make_async_copy(part.at[pl.ds(j * rows, rows)], got.at[0], send.at[j]).wait()

        return
    own, inbox, box = bufs
    load, send, recv, send2, recv2 = sems
    piece = lambda j, i: own.at[0, 0]
    half = dim // 2
    cols = lambda i: pl.ds(i * half, half)
    for i in range(2):
        for q in range(2):
            pltpu.make_async_copy(piece(0, 0), inbox.at[i, q], send.at[i, q]).wait()
        pltpu.make_async_copy(own.at[i, 0], box.at[1, :, cols(i)], send2.at[i]).wait()
        pltpu.make_async_copy(own.at[i, 0], box.at[1, :, cols(i)], recv2.at[i]).wait()
        pltpu.make_async_copy(own.at[i, 1], box.at[0, :, cols(i)], send2.at[2 + i]).wait()

        @pl.when(p.group != p.c)
        def _():
            pltpu.make_async_copy(own.at[i, 1], box.at[0, :, cols(i)], recv2.at[2 + i]).wait()


def total(p, bufs, at):
    if p.N == 4:
        box = bufs[2]
        return box[0, at, :].astype(F32) + box[1, at, :].astype(F32)
    got = bufs[0]
    out = got[0, at, :].astype(F32)
    for t in range(1, p.N):
        out = out + got[t, at, :].astype(F32)
    return out


PARTS = 4


def line_sems(chips):
    return [DMA((2, chips, PARTS)), DMA((chips, PARTS)), DMA((chips, PARTS)), DMA((chips, PARTS)), DMA((PARTS,))]


def line_parts(p, full, rows):
    size = rows // PARTS

    def at(s, core, q=None):
        first = (2 * s + core) * rows
        if q is None:
            return full.at[pl.ds(pl.multiple_of(first, rows), rows)]
        return full.at[pl.ds(pl.multiple_of(first + q * size, size), size)]

    return at


def each_part(body):
    def one(q, carry):
        body(q)
        return carry

    lax.fori_loop(0, PARTS, one, 0)


def line_copy(p, src, dst, send, recv, k, core):
    return pltpu.make_async_remote_copy(
        src_ref=src, dst_ref=dst, send_sem=send, recv_sem=recv, device_id=(2 * k + core, p.n), device_id_type=MESH
    )


def inside(p, k):
    return (k >= 0) & (k < p.C)


BOTH, UP, DOWN = ((0, 1), (1, -1)), ((0, 1),), ((1, -1),)


def line_push(p, src, full, rows, zsend, zrecv, csend, crecv, local, q, ways=BOTH):
    size = rows // PARTS
    part = src.at[pl.ds(pl.multiple_of(q * size, size), size)]
    there = line_parts(p, full, rows)(p.k, p.c, q)
    for i, sign in ways:

        @pl.when(inside(p, p.k + sign))
        def _():
            line_copy(p, part, there, zsend.at[i, 0, q], zrecv.at[p.k, q], p.k + sign, p.c).start()

    line_copy(p, part, there, csend.at[p.k, q], crecv.at[p.k, q], p.k, 1 - p.c).start()
    pltpu.make_async_copy(part, there, local.at[q]).start()


def came(p, s, ways):
    if ways == BOTH:
        return s == s
    return s <= p.k if ways == UP else s >= p.k


def line_steps(p, src, full, rows, zsend, zrecv, csend, crecv, local, ways=BOTH):
    at = line_parts(p, full, rows)
    piece = src.at[pl.ds(0, rows // PARTS)]

    def at_distance(d):
        def onward(q):
            for i, sign in ways:
                s, t = p.k - sign * d, p.k + sign

                @pl.when(inside(p, s))
                def _():
                    here = at(s, p.c, q)
                    pltpu.make_async_copy(piece, here, zrecv.at[s, q]).wait()

                    @pl.when(inside(p, t))
                    def _():
                        line_copy(p, here, here, zsend.at[i, d, q], zrecv.at[s, q], t, p.c).start()

                    line_copy(p, here, here, csend.at[s, q], crecv.at[s, q], p.k, 1 - p.c).start()

        each_part(onward)

    def settle(q):
        here = at(p.k, p.c, q)
        pltpu.make_async_copy(piece, here, local.at[q]).wait()
        for s in range(p.C):

            @pl.when(came(p, jnp.int32(s), ways))
            def _():
                pltpu.make_async_copy(piece, here, csend.at[s, q]).wait()
                pltpu.make_async_copy(piece, at(s, 1 - p.c, q), crecv.at[s, q]).wait()

        for i, sign in ways:
            for d in range(p.C):

                @pl.when(inside(p, p.k - sign * d) & inside(p, p.k + sign))
                def _():
                    pltpu.make_async_copy(piece, here, zsend.at[i, d, q]).wait()

    return [functools.partial(at_distance, d) for d in range(1, p.C)] + [lambda: each_part(settle)]


def line_sum_bufs(chips, rows, width):
    return [pltpu.VMEM((chips, rows, width), BF)] * 3 + [pltpu.VMEM((2, rows, width), BF), pltpu.VMEM((rows, width), F32)]


def line_sum_sems(chips):
    return [
        DMA((chips, PARTS)), DMA((chips, PARTS)), DMA((chips, PARTS)), DMA((2, chips, PARTS)), DMA((chips, PARTS)),
        DMA((2, PARTS)),
    ]


OTHER = {BOTH: BOTH, UP: DOWN, DOWN: UP}


def line_sum_start(p, part, rows, bufs, sems, ways=BOTH):
    own, inbox, _, _, _ = bufs
    load, csend, crecv, _, _, _ = sems
    at = line_parts(p, part, rows)
    size = rows // PARTS

    def share(s):
        def one(q):
            here = pl.ds(pl.multiple_of(q * size, size), size)
            line_copy(p, at(s, 1 - p.c, q), inbox.at[s, here], csend.at[s, q], crecv.at[s, q], p.k, 1 - p.c).start()
            pltpu.make_async_copy(at(s, p.c, q), own.at[s, here], load.at[s, q]).start()

        each_part(one)

    for d in range(p.C - 1, 0, -1):
        for _, sign in ways:
            s = p.k + sign * d

            @pl.when(inside(p, s))
            def _():
                share(s)

    share(p.k)


def line_sum_steps(p, part, rows, bufs, sems, ways=BOTH):
    own, inbox, relay, box, acc = bufs
    load, csend, crecv, zsend, rrecv, zrecv = sems
    size = rows // PARTS
    step = math.gcd(size, 128)
    piece = line_parts(p, part, rows)(0, 0, 0)

    def rows_of(q):
        return pl.ds(pl.multiple_of(q * size, size), size)

    def add(q, body):
        def one(j, carry):
            body(pl.ds(pl.multiple_of(q * size + j * step, step), step))
            return carry

        lax.fori_loop(0, size // step, one, 0)

    def pair(t, q):
        pltpu.make_async_copy(piece, own.at[t, rows_of(q)], load.at[t, q]).wait()
        pltpu.make_async_copy(piece, inbox.at[t, rows_of(q)], crecv.at[t, q]).wait()

    def at_distance(d):
        def onward(q):
            here = rows_of(q)
            for i, sign in ways:
                t = p.k + sign * d
                behind = inside(p, p.k - sign)

                @pl.when(inside(p, t))
                def _():
                    pair(t, q)

                    @pl.when(jnp.logical_not(behind))
                    def _():
                        def two(at):
                            own[t, at, :] = (own[t, at, :].astype(F32) + inbox[t, at, :].astype(F32)).astype(BF)

                        add(q, two)

                    @pl.when(behind)
                    def _():
                        pltpu.make_async_copy(piece, relay.at[t, here], rrecv.at[t, q]).wait()

                        def three(at):
                            both = own[t, at, :].astype(F32) + inbox[t, at, :].astype(F32)
                            own[t, at, :] = (both + relay[t, at, :].astype(F32)).astype(BF)

                        add(q, three)

                    src = own.at[t, here]
                    if d >= 2:
                        line_copy(p, src, relay.at[t, here], zsend.at[i, d, q], rrecv.at[t, q], p.k + sign, p.c).start()
                    else:
                        line_copy(p, src, box.at[i, here], zsend.at[i, d, q], zrecv.at[i, q], t, p.c).start()

        each_part(onward)

    def last(q):
        here = rows_of(q)
        pair(p.k, q)

        def first(at):
            acc[at, :] = own[p.k, at, :].astype(F32) + inbox[p.k, at, :].astype(F32)

        add(q, first)
        for i, sign in ways:

            @pl.when(inside(p, p.k - sign))
            def _():
                pltpu.make_async_copy(piece, box.at[i, here], zrecv.at[i, q]).wait()

                def more(at):
                    acc[at, :] += box[i, at, :].astype(F32)

                add(q, more)

            for d in range(1, p.C):

                @pl.when(inside(p, p.k + sign * d))
                def _():
                    pltpu.make_async_copy(piece, own.at[0, here], zsend.at[i, d, q]).wait()

        for s in range(p.C):

            @pl.when(came(p, jnp.int32(s), OTHER[ways]))
            def _():
                pltpu.make_async_copy(piece, inbox.at[s, here], csend.at[s, q]).wait()


    return [functools.partial(at_distance, d) for d in range(p.C - 1, 0, -1)] + [lambda: each_part(last)]


def row_loop(rows, step, body):
    def one(i, carry):
        body(pl.ds(pl.multiple_of(i * step, step), step))
        return carry

    lax.fori_loop(0, rows // step, one, 0)


STEP = 64


def inv_rms(u):
    return lax.rsqrt(jnp.mean(u * u, axis=-1, keepdims=True) + EPSILON)


def weave(gate_ref, up_ref, both_ref):
    ff = gate_ref.shape[1]
    t = math.gcd(ff, 256)
    for i in range(0, ff, t):
        both_ref[:, 2 * i : 2 * i + t] = gate_ref[:, i : i + t]
        both_ref[:, 2 * i + t : 2 * i + 2 * t] = up_ref[:, i : i + t]


def unweave_kernel(both_ref, gate_ref, up_ref):
    ff = gate_ref.shape[1]
    t = math.gcd(ff, 256)
    for i in range(0, ff, t):
        gate_ref[:, i : i + t] = both_ref[:, 2 * i : 2 * i + t].astype(F32)
        up_ref[:, i : i + t] = both_ref[:, 2 * i + t : 2 * i + 2 * t].astype(F32)


def rotation(p, cos_ref, sin_ref):
    all_rows, hd = cos_ref.shape
    block, half, step = all_rows // 2, hd // 2, 64
    lane = lax.broadcasted_iota(jnp.int32, (step, hd), 1)
    column = jnp.where(lane < half, lane, lane - half).astype(F32)
    inverse = jnp.exp(column * (-2.0 * math.log(1000000.0) / hd))
    row = lax.broadcasted_iota(jnp.int32, (step, hd), 0)

    def body(i, carry):
        at = i * step
        first = jnp.where(at < block, (4 * p.k + p.c) * block + at, (4 * p.k + 3 - p.c) * block + at - block)
        angles = (first + row).astype(F32) * inverse
        here = pl.ds(pl.multiple_of(at, step), step)
        cos_ref[here, :] = jnp.cos(angles)
        sine = jnp.sin(angles)
        sin_ref[here, :] = jnp.where(lane < half, -sine, sine)
        return carry

    lax.fori_loop(0, all_rows // step, body, 0)


def input_kernel(
    wide, narrow, x_ref, gain_ref, shard, gate_ref, up_ref, gathered, full, gu_ref, cos_ref, sin_ref, buf, *sems
):
    p = Place(wide, narrow)
    rows = x_ref.shape[0]
    spread, line = sems[:4], (shard, full, shard.shape[0], *sems[4:])
    enter(p, line=True)
    each_part(lambda q: line_push(p, *line, q))
    *steps, end = line_steps(p, *line)

    def body(at):
        u = x_ref[at, :].astype(F32)
        buf[at, :] = (u * inv_rms(u) * gain_ref[...]).astype(BF)

    row_loop(rows, STEP, body)
    spread_start(p, buf, gathered, rows, *spread)
    weave(gate_ref, up_ref, gu_ref)
    steps[0]()
    rotation(p, cos_ref, sin_ref)
    spread_pass(p, buf, gathered, rows, *spread)
    for step in steps[1:]:
        step()
    spread_end(p, buf, gathered, rows, *spread)
    end()


def turn(u):
    return pltpu.roll(u, u.shape[-1] // 2, 1)


def qkv_kernel(
    wide, narrow, qw, kw, fold, g_ref, x_ref, w_ref, cos_ref, sin_ref, qg_ref, kg_ref,
    gathered, full, qproj_ref, kproj_ref, q_ref, kv_ref, w_buf, x_buf, load, *sems,
):
    p = Place(wide, narrow)
    rows = g_ref.shape[0]
    hd = cos_ref.shape[1]
    all_rows = x_ref.shape[0]
    size = all_rows // 4
    spread, line = sems[:4], (kv_ref, full, all_rows, *sems[4:])
    weights = pltpu.make_async_copy(w_ref.at[:, pl.ds(0, w_buf.shape[1])], w_buf, load.at[0])
    normed = pltpu.make_async_copy(x_ref, x_buf, load.at[1])
    normed.start()
    weights.start()
    enter(p, line=True)

    def project(q):
        at = pl.ds(pl.multiple_of(q * size, size), size)
        y = dg(x_buf[at, :], w_buf[...], NN)
        cos, sin = cos_ref[at, :], sin_ref[at, :]
        qproj_ref[at, :] = y[:, :qw]
        kproj_ref[at, :] = y[:, qw : qw + kw]

        def head(lo, gain):
            u = y[:, lo : lo + hd]
            v = u * inv_rms(u) * gain
            return v * cos + turn(v) * sin

        for h in range(kw // hd):
            kv_ref[at, 2 * h * hd : (2 * h + 1) * hd] = head(qw + h * hd, kg_ref[...]).astype(BF)
            kv_ref[at, (2 * h + 1) * hd : (2 * h + 2) * hd] = y[:, qw + kw + h * hd : qw + kw + (h + 1) * hd].astype(BF)
        for i in range(PARTS // 4):
            line_push(p, *line, q * (PARTS // 4) + i, ways=UP)
        for h in range(qw // hd):
            q_ref[at, h * hd : (h + 1) * hd] = (head(h * hd, qg_ref[...]) * fold).astype(BF)

    normed.wait()
    weights.wait()

    def one(q, carry):
        project(q)
        return carry

    lax.fori_loop(0, 4, one, 0)
    spread_start(p, g_ref, gathered, rows, *spread)
    *steps, end = line_steps(p, *line, ways=UP)
    steps[0]()
    spread_pass(p, g_ref, gathered, rows, *spread)
    for step in steps[1:]:
        step()
    spread_end(p, g_ref, gathered, rows, *spread)
    end()


def middle_kernel(wide, narrow, part, own_ref, gain_ref, mid_ref, gathered, buf, *refs):
    p = Place(wide, narrow)
    rows, dim = own_ref.shape
    bufs, sems, spread = split_refs(narrow, refs)
    enter(p)
    sum_start(p, part, rows, dim, bufs, sems)
    sum_pass(p, part, rows, dim, bufs, sems)
    sum_end(p, part, rows, dim, bufs, sems)

    def body(at):
        u = own_ref[at, :].astype(F32) + total(p, bufs, at)
        mid_ref[at, :] = u
        buf[at, :] = (u * inv_rms(u) * gain_ref[...]).astype(BF)

    row_loop(rows, STEP, body)
    spread_start(p, buf, gathered, rows, *spread)
    spread_pass(p, buf, gathered, rows, *spread)
    spread_end(p, buf, gathered, rows, *spread)


def split_refs(narrow, refs):
    bufs, sems = (3, 5) if narrow == 4 else (1, 3)
    return refs[:bufs], refs[bufs : bufs + sems], refs[bufs + sems :]


def norm_back(u, gain, cot):
    r = inv_rms(u)
    a = cot * gain
    du = r * a - u * (r * r * r) * jnp.mean(a * u, axis=-1, keepdims=True)
    return du, jnp.sum(cot * u * r, axis=0, keepdims=True)


def mlp_back_kernel(
    wide, narrow, g_ref, wd_ref, gu_ref, w_ref, x_ref, mid_ref, gain_ref, grad_ref, back_ref, rows_ref, dgain_ref, wgrad,
    g_buf, wd_buf, gu_buf, low, w_buf, x_buf, stage, out, load, tiles_in, store, *refs
):
    p = Place(wide, narrow)
    rows, dim = mid_ref.shape
    half = dim // 2
    t = wd_buf.shape[2]
    bufs, sems, _ = split_refs(narrow, refs)

    def tile_of(i):
        slot = lax.rem(i, 2)
        return (
            pltpu.make_async_copy(wd_ref.at[:, pl.ds(pl.multiple_of(i * t, t), t)], wd_buf.at[slot], tiles_in.at[0, slot]),
            pltpu.make_async_copy(gu_ref.at[:, pl.ds(pl.multiple_of(2 * i * t, t), 2 * t)], gu_buf.at[slot], tiles_in.at[1, slot]),
        )

    loads = [pltpu.make_async_copy(g_ref, g_buf, load.at[0])]
    for i in range(2):
        at = pl.ds(i * half, half)
        loads.append(pltpu.make_async_copy(w_ref.at[at], w_buf.at[at], load.at[1 + i]))
    loads.append(pltpu.make_async_copy(x_ref, x_buf, load.at[3]))
    loads[0].start()
    for copy in tile_of(0):
        copy.start()
    enter(p)
    loads[0].wait()
    count = wd_ref.shape[1] // t

    def gates(i, carry):
        @pl.when(i + 1 < count)
        def _():
            for copy in tile_of(i + 1):
                copy.start()

        for copy in tile_of(i):
            copy.wait()

        @pl.when(i == 0)
        def _():
            for copy in loads[1:]:
                copy.start()

        slot = lax.rem(i, 2)
        hb = dg(g_buf[...], wd_buf[slot], NN)
        gate, up = gu_buf[slot, :, :t], gu_buf[slot, :, t:]
        s = jax.nn.sigmoid(gate)
        gs = hb * s
        at = pl.multiple_of(2 * i * t, t)
        low[:, pl.ds(at, t)] = (gs * up * (1.0 + gate * (1.0 - s))).astype(BF)
        low[:, pl.ds(pl.multiple_of(at + t, t), t)] = (gs * gate).astype(BF)
        return carry

    lax.fori_loop(0, count, gates, 0)
    for copy in loads[1:3]:
        copy.wait()

    def product(j, i):
        a = low[pl.ds(pl.multiple_of(j * rows, rows), rows), :]
        return dg(a, w_buf[pl.ds(pl.multiple_of(i * half, half), half), :], NT).astype(BF)

    sum_start_of(p, product, out, rows, dim, bufs, sems)
    dgain_ref[...] = jnp.zeros_like(dgain_ref)
    loads[3].wait()
    tile = 256

    def write(i):
        return pltpu.make_async_copy(
            stage.at[lax.rem(i, 2)], wgrad.at[pl.ds(pl.multiple_of(i * tile, tile), tile)], store.at[lax.rem(i, 2)]
        )

    def grads(first, last):
        def one(i, carry):
            @pl.when(i >= 2)
            def _():
                write(i - 2).wait()

            stage[lax.rem(i, 2)] = dg(x_buf[:, pl.ds(pl.multiple_of(i * tile, tile), tile)], low[...], TN).astype(BF)
            write(i).start()
            return carry

        lax.fori_loop(first, last, one, 0)

    tiles = dim // tile
    early = 3
    grads(0, early)
    sum_pass(p, out, rows, dim, bufs, sems, loaded=narrow == 4)
    grads(early, tiles)
    sum_end(p, out, rows, dim, bufs, sems)

    def body(at):
        du, dgain = norm_back(mid_ref[at, :], gain_ref[...], total(p, bufs, at))
        back = grad_ref[at, :].astype(F32) + du
        back_ref[at, :] = back
        rows_ref[at, :] = back.astype(BF)
        dgain_ref[...] += dgain

    row_loop(rows, STEP, body)
    write(tiles - 2).wait()
    write(tiles - 1).wait()


def middle_back_kernel(
    wide, narrow, wo_at, groups, hd, rows_ref, hidden, w_ref, wo_ref, o_ref, gathered, next_ref, back_ref, delta_ref,
    h_buf, w_buf, wo_buf, o_buf, load, *spread
):
    p = Place(wide, narrow)
    rows = rows_ref.shape[0]
    pairs = ((hidden, h_buf), (w_ref, w_buf), (wo_ref.at[:, pl.ds(*wo_at)], wo_buf), (o_ref, o_buf))
    loads = [pltpu.make_async_copy(src, dst, load.at[i]) for i, (src, dst) in enumerate(pairs)]
    enter(p)
    spread_start(p, rows_ref, gathered, rows, *spread)
    for copy in loads:
        copy.start()
    for copy in loads[:2]:
        copy.wait()

    def down(at):
        next_ref[at, :] = dg(h_buf[at, :], w_buf[...], NT).astype(BF)

    row_loop(next_ref.shape[0], 256, down)
    for copy in loads[2:]:
        copy.wait()

    def on_slot(j):
        at = pl.ds(pl.multiple_of(j * rows, rows), rows)
        back = dg(gathered[at, :], wo_buf[...], NN).astype(BF)
        back_ref[at, :] = back
        lane = lax.broadcasted_iota(jnp.int32, (rows, hd), 1)
        out = jnp.zeros((rows, hd), F32)
        for h in range(back.shape[1] // hd):
            mine = slice(h * hd, (h + 1) * hd)
            row = 8 * (h // groups) + h % groups
            delta = jnp.sum(back[:, mine].astype(F32) * o_buf[at, mine], axis=1, keepdims=True)
            out = jnp.where(lane == row, delta, out)
        delta_ref[:, at] = jnp.transpose(out)[: delta_ref.shape[0]]

    spread_pass(p, rows_ref, gathered, rows, *spread)
    spread_end(p, rows_ref, gathered, rows, *spread, on_slot=on_slot)


def share_start(me, count, here, slots, sends, recvs, device):
    slots[me] = here[...]
    for t in range(count):

        @pl.when(me != t)
        def _():
            wide_at, narrow_at = device(t)
            to(here, slots.at[me], sends.at[t], recvs.at[me], wide_at, narrow_at).start()


def share_end(me, count, here, slots, sends, recvs):
    for t in range(count):

        @pl.when(me != t)
        def _():
            pltpu.make_async_copy(here, slots.at[t], sends.at[t]).wait()
            pltpu.make_async_copy(here, slots.at[t], recvs.at[t]).wait()

    out = slots[0]
    for t in range(1, count):
        out = out + slots[t]
    here[...] = out


def head_back(cot, u, gain, cos, sin):
    cot = cot * cos - turn(cot) * sin
    return norm_back(u, gain, cot)


def output_kernel(
    wide, narrow, part, mid_ref, dkv, dq, qproj, cos_ref, sin_ref, g_ref, x_ref, m_ref, a_ref,
    out_ref, kv_ref, low_ref, dgain_ref, wgrad_ref, dq_buf, u_buf, x_buf, m_buf, a_buf, load, *refs
):
    p = Place(wide, narrow)
    rows, dim = mid_ref.shape
    kv_rows = kv_ref.shape[0]
    width = low_ref.shape[1]
    hd = cos_ref.shape[1]
    bufs, sems, line = split_refs(narrow, refs)
    sums = (part, rows, dim, bufs, sems)
    chain = (p, dkv, kv_rows, line[:5], line[5:])
    pairs = ((dq, dq_buf), (qproj, u_buf), (x_ref, x_buf), (m_ref, m_buf), (a_ref, a_buf))
    loads = [pltpu.make_async_copy(src, dst, load.at[i]) for i, (src, dst) in enumerate(pairs)]
    enter(p, line=True)
    line_sum_start(*chain, ways=DOWN)
    sum_start(p, *sums)
    for copy in loads:
        copy.start()
    first, *steps, last = line_sum_steps(*chain, ways=DOWN)
    first()
    dgain_ref[...] = jnp.zeros_like(dgain_ref)
    for copy in loads[:2]:
        copy.wait()

    def through_heads(at):
        for h in range(width // hd):
            mine = slice(h * hd, (h + 1) * hd)
            du, dgain = head_back(dq_buf[at, mine], u_buf[at, mine], g_ref[...], cos_ref[at, :], sin_ref[at, :])
            low_ref[at, mine] = du.astype(BF)
            dgain_ref[...] += dgain

    row_loop(low_ref.shape[0], 128, through_heads)
    for copy in loads[2:]:
        copy.wait()

    def grads(first_tile, last_tile):
        def one(i, carry):
            at = pl.ds(pl.multiple_of(i * 256, 256), 256)
            wgrad_ref[at, :width] = dg(x_buf[:, at], low_ref[...], TN).astype(BF)
            wgrad_ref[at, width:] = dg(m_buf[:, at], a_buf[...], TN).astype(BF)
            return carry

        lax.fori_loop(first_tile, last_tile, one, 0)

    tiles = dim // 256
    grads(0, tiles // 2)
    sum_pass(p, *sums)
    steps[0]()
    sum_end(p, *sums)

    def body(at):
        out_ref[at, :] = (mid_ref[at, :] + total(p, bufs, at)).astype(BF)

    row_loop(rows, STEP, body)
    grads(tiles // 2, tiles)
    for step in steps[1:]:
        step()
    last()
    row_loop(kv_rows, 128, lambda at: kv_ref.__setitem__((at, slice(None)), line[4][at, :].astype(BF)))


def input_back_kernel(
    wide, narrow, qw, kw, own_ref, gain_ref, back_ref, gains_ref, wgrad, q_ref, kv_ref, proj_ref, cos_ref, sin_ref, kg_ref,
    w_ref, x_ref, out_ref, gsum_ref, wsum_ref, kvsum_ref,
    gbuf, gbuf2, low, part, kvgrad, w_buf, x_buf, load, gsend, grecv, gsend2, grecv2, *refs,
):
    p = Place(wide, narrow)
    rows, dim = own_ref.shape
    hd = cos_ref.shape[1]
    all_rows = x_ref.shape[0]
    w_rows = wsum_ref.shape[0]
    bufs, sems, line = split_refs(narrow, refs)
    sums = (part, rows, dim, bufs, sems)
    first_line = (p, wgrad, w_rows, (*line[:4], wsum_ref), line[4:10])
    second_line = (p, kvgrad, w_rows, (*line[10:14], kvsum_ref), line[14:])
    weights = pltpu.make_async_copy(w_ref.at[:, pl.ds(0, w_buf.shape[1])], w_buf, load.at[0])
    weights.start()
    normed = pltpu.make_async_copy(x_ref, x_buf, load.at[1])
    normed.start()
    enter(p, ring=True)
    line_sum_start(*first_line)
    gsum_ref[...] = gains_ref[...]
    size = min(all_rows, 256)
    first = line_sum_steps(*first_line)
    first[0]()
    weights.wait()

    def through_heads(at):
        low[at, :qw] = q_ref[at, :]
        for h in range(kw // hd):
            key = slice(2 * h * hd, (2 * h + 1) * hd)
            value = slice((2 * h + 1) * hd, (2 * h + 2) * hd)
            mine = slice(qw + h * hd, qw + (h + 1) * hd)
            du, dgain = head_back(
                kv_ref[at, key].astype(F32), proj_ref[at, h * hd : (h + 1) * hd], kg_ref[...], cos_ref[at, :], sin_ref[at, :]
            )
            low[at, mine] = du.astype(BF)
            low[at, qw + kw + h * hd : qw + kw + (h + 1) * hd] = kv_ref[at, value]
            gsum_ref[:, 2 * dim + hd :] += dgain
        part[at, :] = dg(low[at, :], w_buf[...], NT).astype(BF)

    row_loop(all_rows, size, through_heads)
    sum_start(p, *sums)
    first[1]()

    normed.wait()

    def key_grads(at):
        kvgrad[at, :] = dg(x_buf[:, at], low[:, qw:], TN).astype(BF)

    row_loop(dim, 256, key_grads)
    line_sum_start(*second_line)
    second = line_sum_steps(*second_line)
    second[0]()
    sum_pass(p, *sums)
    for step in first[2:-1]:
        step()
    sum_end(p, *sums)

    def body(at):
        du, dgain = norm_back(own_ref[at, :].astype(F32), gain_ref[...], total(p, bufs, at))
        out_ref[at, :] = back_ref[at, :] + du
        gsum_ref[:, :dim] += dgain

    row_loop(rows, STEP, body)

    share_start(p.n, narrow, gsum_ref, gbuf, gsend, grecv, lambda t: (p.w, t))
    second[1]()
    first[-1]()
    share_end(p.n, narrow, gsum_ref, gbuf, gsend, grecv)
    share_start(p.w, wide, gsum_ref, gbuf2, gsend2, grecv2, lambda t: (t, p.n))
    for step in second[2:]:
        step()
    share_end(p.w, wide, gsum_ref, gbuf2, gsend2, grecv2)


VM = pl.BlockSpec(memory_space=pltpu.VMEM)


HB = pl.BlockSpec(memory_space=pl.ANY)


def comm_call(kernel, name, cid, out_shape, in_specs, out_specs, scratch, *args):
    return pl.pallas_call(
        kernel,
        out_shape=out_shape,
        in_specs=in_specs,
        out_specs=out_specs,
        scratch_shapes=scratch,
        compiler_params=pltpu.CompilerParams(collective_id=cid, has_side_effects=True, vmem_limit_bytes=60 << 20),
        cost_estimate=pl.CostEstimate(flops=0, bytes_accessed=160_000_000, transcendentals=0),
        name=name,
    )(*args)


def sds(shape, kind):
    return jax.ShapeDtypeStruct(shape, kind)


def plain(kernel, name, grid, in_specs, out_specs, out_shape, flops, nbytes, *args, scratch=(), aliases=None):
    return pl.pallas_call(
        kernel,
        out_shape=out_shape,
        grid=grid,
        in_specs=in_specs,
        out_specs=out_specs,
        scratch_shapes=scratch,
        input_output_aliases=aliases or {},
        compiler_params=pltpu.CompilerParams(vmem_limit_bytes=52 << 20),
        cost_estimate=pl.CostEstimate(flops=flops, bytes_accessed=nbytes, transcendentals=0),
        name=name,
    )(*args)


def whole(shape):
    return pl.BlockSpec(shape, lambda *i: (0,) * len(shape), pipeline_mode=pl.Buffered(1))


def by_rows(tm, width):
    return pl.BlockSpec((tm, width), lambda i: (i, 0))


def mlp_fwd_kernel(x_ref, w_ref, gu_ref, h_ref):
    t = h_ref.shape[1]
    y = dg(x_ref[...], w_ref[...], NN)
    gate, up = y[:, :t], y[:, t:]
    gu_ref[...] = y
    h_ref[...] = (gate * jax.nn.sigmoid(gate) * up).astype(BF)


def mlp_fwd(x, w, t):
    rows, dim = x.shape
    ff2 = w.shape[1]
    return plain(
        mlp_fwd_kernel, "mlp_fwd", (ff2 // (2 * t),),
        [whole((rows, dim)), pl.BlockSpec((dim, 2 * t), lambda i: (0, i))],
        [pl.BlockSpec((rows, 2 * t), lambda i: (0, i)), pl.BlockSpec((rows, t), lambda i: (0, i))],
        (sds((rows, ff2), F32), sds((rows, ff2 // 2), BF)),
        2 * rows * dim * ff2, rows * dim * 2 + dim * ff2 * 2 + rows * ff2 * 5, x, w,
    )


def fwd_kernel(groups, hd, tab, q_ref, kv_ref, o_ref, low_ref, lse_ref, acc, lsum):
    s = pl.program_id(1)
    block = q_ref.shape[0]
    diag, first, last = tab[2, s], tab[3, s], tab[4, s]

    @pl.when(first == 1)
    def _():
        acc[...] = jnp.zeros_like(acc)
        lsum[...] = jnp.zeros_like(lsum)

    def work(masked):
        k, v = kv_ref[:, :hd], kv_ref[:, hd:]
        for g in range(groups):
            at = slice(g * hd, (g + 1) * hd)
            scores = dg(q_ref[:, at], k, NT)
            if masked:
                row = lax.broadcasted_iota(jnp.int32, scores.shape, 0)
                col = lax.broadcasted_iota(jnp.int32, scores.shape, 1)
                scores = jnp.where(col <= row, scores, MASKED)
            probs = jnp.exp2(scores)
            part = probs[:, :128]
            for j in range(1, block // 128):
                part = part + probs[:, j * 128 : (j + 1) * 128]
            lsum[g] += part
            acc[:, at] += dg(probs.astype(BF), v, NN)

    @pl.when(diag == 0)
    def _():
        work(False)

    @pl.when(diag == 1)
    def _():
        work(True)

    @pl.when(last == 1)
    def _():
        lane = lax.broadcasted_iota(jnp.int32, (block, 128), 1)
        lse = jnp.zeros((block, 128), F32)
        for g in range(groups):
            at = slice(g * hd, (g + 1) * hd)
            l = jnp.sum(lsum[g], axis=1, keepdims=True)
            out = acc[:, at] / l
            o_ref[:, at] = out
            low_ref[:, at] = out.astype(BF)
            lse = jnp.where(lane == g, jnp.log2(l), lse)
        lse_ref[...] = jnp.transpose(lse)[: lse_ref.shape[0]]


def attn_fwd(tab, q, kv, groups, hd, block):
    rows, width = q.shape
    gw = groups * hd
    heads = width // gw
    steps = tab.shape[1]
    mine = pl.BlockSpec((block, gw), lambda h, s, t: (t[0, s], h))
    return pl.pallas_call(
        functools.partial(fwd_kernel, groups, hd),
        out_shape=(sds((rows, width), F32), sds((rows, width), BF), sds((8 * heads, rows), F32)),
        grid_spec=pltpu.PrefetchScalarGridSpec(
            num_scalar_prefetch=1,
            grid=(heads, steps),
            in_specs=[mine, pl.BlockSpec((block, 2 * hd), lambda h, s, t: (t[1, s], h))],
            out_specs=[mine, mine, pl.BlockSpec((8, block), lambda h, s, t: (h, t[0, s]))],
            scratch_shapes=[pltpu.VMEM((block, gw), F32), pltpu.VMEM((groups, block, 128), F32)],
        ),
        compiler_params=pltpu.CompilerParams(vmem_limit_bytes=48 << 20),
        cost_estimate=pl.CostEstimate(
            flops=heads * steps * block * block * gw * 4,
            bytes_accessed=heads * steps * block * hd * 8,
            transcendentals=heads * steps * block * block * groups,
        ),
        name="attn_fwd",
    )(tab, q, kv)


def bwd_kernel(groups, hd, tab, q_ref, do_ref, kv_ref, lse_ref, delta_ref, dq_ref, dkv_ref, dq_sum, dkv_sum):
    s = pl.program_id(1)
    block = q_ref.shape[0]
    qi, diag, first, last = tab[0, s], tab[2, s], tab[3, s], tab[4, s]

    @pl.when(s == 0)
    def _():
        dq_sum[...] = jnp.zeros_like(dq_sum)

    @pl.when(first == 1)
    def _():
        dkv_sum[...] = jnp.zeros_like(dkv_sum)

    def work(masked):
        k, v = kv_ref[:, :hd], kv_ref[:, hd:]
        for g in range(groups):
            at = slice(g * hd, (g + 1) * hd)
            q, do = q_ref[:, at], do_ref[:, at]
            scores = dg(k, q, NT) - lse_ref[g : g + 1, :]
            if masked:
                row = lax.broadcasted_iota(jnp.int32, scores.shape, 0)
                col = lax.broadcasted_iota(jnp.int32, scores.shape, 1)
                scores = jnp.where(row <= col, scores, MASKED)
            probs = jnp.exp2(scores)
            dots = dg(v, do, NT)
            dkv_sum[:, hd:] += dg(probs.astype(BF), do, NN)
            back = (probs * (dots - delta_ref[g : g + 1, :])).astype(BF)
            dkv_sum[:, :hd] += dg(back, q, NN)
            dq_sum[qi, :, at] += dg(back, k, TN)

    @pl.when(diag == 0)
    def _():
        work(False)

    @pl.when(diag == 1)
    def _():
        work(True)

    @pl.when(last == 1)
    def _():
        dkv_ref[:, :hd] = (dkv_sum[:, :hd] * math.log(2.0)).astype(BF)
        dkv_ref[:, hd:] = dkv_sum[:, hd:].astype(BF)

    @pl.when(s == pl.num_programs(1) - 1)
    def _():
        for i in range(dq_sum.shape[0]):
            dq_ref[i * block : (i + 1) * block, :] = dq_sum[i] * hd**-0.5


def attn_bwd(tab, q, do, kv, lse, delta, groups, hd, block):
    rows, width = q.shape
    gw = groups * hd
    heads = width // gw
    steps = tab.shape[1]
    mine = pl.BlockSpec((block, gw), lambda h, s, t: (t[0, s], h))
    keys = pl.BlockSpec((block, 2 * hd), lambda h, s, t: (t[1, s], h))
    stat = pl.BlockSpec((8, block), lambda h, s, t: (h, t[0, s]))
    return pl.pallas_call(
        functools.partial(bwd_kernel, groups, hd),
        out_shape=(sds((rows, width), F32), sds(kv.shape, BF)),
        grid_spec=pltpu.PrefetchScalarGridSpec(
            num_scalar_prefetch=1,
            grid=(heads, steps),
            in_specs=[mine, mine, keys, stat, stat],
            out_specs=[pl.BlockSpec((rows, gw), lambda h, s, t: (0, h)), keys],
            scratch_shapes=[pltpu.VMEM((rows // block, block, gw), F32), pltpu.VMEM((block, 2 * hd), F32)],
        ),
        compiler_params=pltpu.CompilerParams(vmem_limit_bytes=48 << 20),
        cost_estimate=pl.CostEstimate(
            flops=heads * steps * block * block * gw * 10,
            bytes_accessed=heads * steps * block * hd * 16,
            transcendentals=heads * steps * block * block * groups,
        ),
        name="attn_bwd",
    )(tab, q, do, kv, lse, delta)


def place(w):
    k, core = w // 2, w % 2
    return 4 * k + core, 4 * k + 3 - core


def block_row(b):
    m = b % 4
    core = jnp.where((m == 1) | (m == 2), 1, 0)
    return 2 * (2 * (b // 4) + core) + jnp.where(m < 2, 0, 1)


def tables(w, chips):
    a, b = place(w)
    count = a + b + 2
    every = jnp.arange(8 * chips - 2, dtype=jnp.int32)
    s, idle = jnp.minimum(every, count - 1), every >= count
    in_a = s <= a
    key = jnp.where(in_a, s, s - a - 1)
    diag = jnp.where(in_a, s == a, s == count - 1)
    fwd = [jnp.where(in_a, 0, 1), block_row(key), jnp.where(idle, 2, diag), ~idle & (key == 0), ~idle & diag]
    both = s < 2 * (a + 1)
    even = s % 2 == 0
    key = jnp.where(both, s // 2, s - (a + 1))
    query = jnp.where(both & even, 0, 1)
    diag = key == jnp.where(query == 0, a, b)
    zero = (every >= count) & (w % 2 == 1)
    key = jnp.where(zero, b + 1, key)
    only = zero & (every == count)
    bwd = [query, block_row(key), jnp.where(idle, 2, diag), only | ~idle & (~both | even), only | ~idle & (~both | ~even)]
    return tuple(jnp.stack([row.astype(jnp.int32) for row in rows]) for rows in (fwd, bwd))


def per_device(
    wide, narrow,
    layer_input, w_query, w_key, w_value, w_output, w_gate, w_up, w_down,
    attn_gain, mlp_gain, query_gain, key_gain, out_grad,
):
    hd = query_gain.shape[0]
    rows, dim = layer_input.shape
    all_rows = narrow * rows
    chips = wide // 2
    block = all_rows // 2
    qw, kw = w_query.shape[1], w_key.shape[1]
    ff = w_gate.shape[1]
    groups = qw // kw
    kv_heads = kw // hd
    w = lax.axis_index("wide")
    fwd_tab, bwd_tab = tables(w, chips)
    def gather(shard):
        return lax.all_gather(shard, "wide", axis=0, tiled=True)

    def scatter(grad):
        return lax.psum_scatter(grad, "wide", scatter_dimension=0, tiled=True)

    t = math.gcd(ff, 256)

    spread_s = spread_sems(narrow)
    sum_s = [*sum_bufs(narrow, rows, dim), *sum_sems(narrow)]
    row_buf = pltpu.VMEM((rows, dim), BF)
    low_rows, full_rows, all_low = sds((rows, dim), BF), sds((rows, dim), F32), sds((all_rows, dim), BF)
    ring = functools.partial
    qg, kg = query_gain[None], key_gain[None]
    after = lax.optimization_barrier

    in_scratch = [*spread_s, *line_sems(chips)]
    shard = jnp.concatenate([w_query, w_key, w_value, w_output.T], axis=1)
    table = sds((all_rows, hd), F32)
    normed_all, w_attn, gu_shard, cos_table, sin_table = comm_call(
        ring(input_kernel, wide, narrow), "input_rows", 0,
        (all_low, sds((dim, shard.shape[1]), BF), sds((w_gate.shape[0], 2 * ff), BF), table, table),
        [VM, VM, HB, VM, VM], (HB, HB, VM, VM, VM), [row_buf, *in_scratch],
        layer_input, attn_gain[None], shard, w_gate, w_up,
    )
    width = qw + 2 * kw
    grad_all, kv, query_proj, key_proj, queries = comm_call(
        ring(qkv_kernel, wide, narrow, qw, kw, hd**-0.5 * math.log2(math.e)), "qkv_rows", 1,
        (all_low, sds((wide * all_rows, 2 * kw), BF), sds((all_rows, qw), F32),
         sds((all_rows, kw), F32), sds((all_rows, qw), BF)),
        [VM, HB, HB, VM, VM, VM, VM], (HB, HB, VM, VM, VM),
        [pltpu.VMEM((all_rows, 2 * kw), BF), pltpu.VMEM((dim, width), BF),
         pltpu.VMEM((all_rows, dim), BF), DMA((2,)), *in_scratch],
        out_grad, normed_all, w_attn, cos_table, sin_table, qg, kg,
    )
    gu_shard, w_down, kv = after((gu_shard, w_down, kv))
    w_gu, w_d = gather(gu_shard), gather(w_down.T)
    attended, attended_low, lse = attn_fwd(fwd_tab, queries, kv, groups, hd, block)
    w_o = w_attn[:, qw + 2 * kw :]
    middle, normed_mlp = comm_call(
        ring(middle_kernel, wide, narrow), "middle_rows", 2, (full_rows, all_low), [HB, VM, VM], (VM, HB),
        [row_buf, *sum_s, *spread_s], dg(attended_low, w_o, NT).astype(BF), layer_input, mlp_gain[None],
    )
    gate_up, hidden_low = mlp_fwd(normed_mlp, w_gu, t)
    grad_down = dg(grad_all, hidden_low, TN).astype(BF)
    w_d, _ = after((w_d, grad_down))
    middle_back, middle_low, mlp_gain_part, grad_gu = comm_call(
        ring(mlp_back_kernel, wide, narrow), "mlp_back", 6,
        (full_rows, low_rows, sds((1, dim), F32), sds((dim, 2 * ff), BF)), [HB, HB, HB, HB, HB, VM, VM, VM], (VM, VM, VM, HB),
        [pltpu.VMEM((all_rows, dim), BF), pltpu.VMEM((2, dim, t), BF), pltpu.VMEM((2, all_rows, 2 * t), F32),
         pltpu.VMEM((all_rows, 2 * ff), BF), pltpu.VMEM((dim, 2 * ff), BF), pltpu.VMEM((all_rows, dim), BF),
         pltpu.VMEM((2, 256, 2 * ff), BF), product_bufs(narrow, rows, dim), DMA((4,)), DMA((2, 2)), DMA((2,)), *sum_s],
        grad_all, w_d, gate_up, w_gu, normed_mlp, middle, mlp_gain[None], out_grad,
    )
    grad_down, grad_gu = scatter(grad_down), scatter(grad_gu)
    middle_all, down_part, back, delta = comm_call(
        ring(middle_back_kernel, wide, narrow, (width, qw), groups, hd), "middle_back", 3,
        (all_low, all_low, sds((all_rows, qw), BF), sds((8 * kv_heads, all_rows), F32)),
        [VM, HB, HB, HB, HB], (VM, VM, VM, VM),
        [pltpu.VMEM((all_rows, ff), BF), pltpu.VMEM((dim, ff), BF), pltpu.VMEM((dim, qw), BF), pltpu.VMEM((all_rows, qw), F32),
         DMA((4,)), *spread_s],
        middle_low, hidden_low, w_d, w_attn, attended,
    )
    query_back, dkv = attn_bwd(bwd_tab, queries, back, kv, lse, delta, groups, hd, block)
    dkv, grad_down = after((dkv, grad_down))
    layer_output, kv_sum, q_low, query_gain_part, grad_qo = comm_call(
        ring(output_kernel, wide, narrow), "output_rows", 4,
        (low_rows, sds((all_rows, 2 * kw), BF), sds((all_rows, qw), BF), sds((1, hd), F32), sds((dim, 2 * qw), BF)),
        [HB, VM, HB, HB, HB, VM, VM, VM, HB, HB, HB], (VM, VM, VM, VM, VM),
        [pltpu.VMEM((all_rows, qw), F32), pltpu.VMEM((all_rows, qw), F32), pltpu.VMEM((all_rows, dim), BF),
         pltpu.VMEM((all_rows, dim), BF), pltpu.VMEM((all_rows, qw), BF), DMA((5,)), *sum_s,
         *line_sum_bufs(chips, all_rows, 2 * kw), *line_sum_sems(chips)],
        down_part, middle, dkv, query_back, query_proj, cos_table, sin_table, qg, normed_all, middle_all, attended_low,
    )
    kv_sum, grad_gu = after((kv_sum, grad_gu))
    half = sds((dim // wide, ff), F32)
    grad_gate, grad_up = plain(
        unweave_kernel, "unweave", (1,), [whole(grad_gu.shape)], [whole(half.shape)] * 2, [half, half], 0, grad_gu.size * 6, grad_gu
    )
    gains = jnp.concatenate([jnp.zeros((1, dim), F32), mlp_gain_part, query_gain_part, jnp.zeros((1, hd), F32)], axis=1)
    w_rows = dim // wide
    input_grad, gain_sums, grad_qo, grad_kv = comm_call(
        ring(input_back_kernel, wide, narrow, qw, kw), "input_back", 5,
        (full_rows, sds(gains.shape, F32), sds((w_rows, 2 * qw), F32), sds((w_rows, 2 * kw), F32)),
        [VM, VM, VM, VM, HB, VM, VM, VM, VM, VM, VM, HB, HB],
        (VM, VM, VM, VM),
        [pltpu.VMEM((narrow, *gains.shape), F32), pltpu.VMEM((wide, *gains.shape), F32),
         pltpu.VMEM((all_rows, width), BF), pltpu.VMEM((all_rows, dim), BF), pltpu.VMEM((dim, 2 * kw), BF),
         pltpu.VMEM((dim, width), BF), pltpu.VMEM((all_rows, dim), BF), DMA((2,)), DMA((narrow,)), DMA((narrow,)), DMA((wide,)), DMA((wide,)), *sum_s,
         *line_sum_bufs(chips, w_rows, 2 * qw)[:4], *line_sum_sems(chips),
         *line_sum_bufs(chips, w_rows, 2 * kw)[:4], *line_sum_sems(chips)],
        layer_input, attn_gain[None], middle_back, gains, grad_qo, q_low, kv_sum, key_proj, cos_table, sin_table, kg, w_attn, normed_all,
    )
    g = gain_sums[0]
    return (
        layer_output, input_grad,
        grad_qo[:, :qw], grad_kv[:, :kw], grad_kv[:, kw:],
        grad_qo[:, qw:].T, grad_gate, grad_up,
        grad_down.T.astype(F32),
        g[:dim], g[dim : 2 * dim], g[2 * dim : 2 * dim + hd], g[2 * dim + hd :],
    )


def solution(mesh):
    rows = P(("wide", "narrow"), None)
    weight, turned = P("wide", "narrow"), P("narrow", "wide")
    return jax.shard_map(
        functools.partial(per_device, mesh.shape["wide"], mesh.shape["narrow"]),
        mesh=mesh,
        in_specs=(rows, weight, weight, weight, turned, weight, weight, turned, P(), P(), P(), P(), rows),
        out_specs=(rows, rows, weight, weight, weight, turned, weight, weight, turned, P(), P(), P(), P()),
        check_vma=False,
    )
```

```python
import functools
import math

import jax
import jax.numpy as jnp
from jax import lax
from jax.experimental import pallas as pl
from jax.experimental.pallas import tpu as pltpu
from jax.sharding import PartitionSpec as P

EPSILON = 1e-06
MASKED = -1e30
F32 = jnp.float32
BF = jnp.bfloat16
MESH = pl.DeviceIdType.MESH
NT = (((1,), (1,)), ((), ()))
NN = (((1,), (0,)), ((), ()))
TN = (((0,), (0,)), ((), ()))


def dg(a, b, dims):
    return lax.dot_general(a, b, dims, preferred_element_type=F32)
DMA = pltpu.SemaphoreType.DMA


class Place:
    def __init__(self, wide, narrow):
        self.W, self.N = wide, narrow
        self.C, self.half = wide // 2, narrow // 2
        self.w, self.n = lax.axis_index("wide"), lax.axis_index("narrow")
        self.k, self.c = self.w // 2, lax.rem(self.w, 2)
        late = (self.n >= self.half).astype(jnp.int32)
        self.group = lax.rem(self.c + late, 2)
        self.slot = jnp.where(self.group == 0, self.n, lax.rem(self.n + self.half, self.N))

    def owner(self, j):
        core = 1 if j >= self.half else 0
        n = jnp.where(self.c == 0, j, (j + self.half) % self.N)
        return core, n

    def owner_is_me(self, j):
        core, n = self.owner(j)
        return (self.c == core) & (self.n == n)


def enter(p, line=False, ring=False):
    barrier = pltpu.get_barrier_semaphore()

    def greet(device):
        pl.semaphore_signal(barrier, inc=1, device_id=device, device_id_type=MESH)

    for core in range(2):
        for n in range(p.N):

            @pl.when((p.c != core) | (p.n != n))
            def _():
                greet((2 * p.k + core, n))

    peers = 2 * p.N - 1
    if line or ring:
        for k in range(p.C):

            @pl.when(p.k != k)
            def _():
                greet((2 * k + p.c, p.n))
                if ring:
                    greet((2 * k + 1 - p.c, p.n))

        peers += (2 if ring else 1) * (p.C - 1)
    pl.semaphore_wait(barrier, peers)


def slot_of(p, n, group):
    return jnp.where(group == 0, n, lax.rem(n + p.half, p.N))


def neighbours(p):
    return p.n + 1 - 2 * lax.rem(p.n, 2), lax.rem(p.n + 2, 4), 3 - p.n


def to(src, dst, send, recv, wide, narrow):
    return pltpu.make_async_remote_copy(
        src_ref=src, dst_ref=dst, send_sem=send, recv_sem=recv, device_id=(wide, narrow), device_id_type=MESH
    )


def spread_sems(narrow):
    return [DMA((narrow, 2)), DMA((narrow, 2)), DMA((2,)), DMA((2,))]


def spread_start(p, src, gathered, rows, send, recv, local, onward):
    half = rows // 2
    view = lambda i: gathered.at[pl.ds(pl.multiple_of(p.slot * rows + i * half, half), half)]
    part = lambda i: src.at[pl.ds(i * half, half)]
    mine = p.group == p.c
    square = p.N == 4
    if square:
        nx, ny, _ = neighbours(p)
        targets = [(nx, (0, 1)), (ny, (1, 0))]
        order = [(t, q, i) for q in range(2) for t, halves in targets for i in (halves[q],)]
        for t, q, i in order:
            at = 0 if t is nx else 1
            to(part(i), view(i), send.at[at, i], recv.at[p.slot, i], 2 * p.k + p.group, t).start()
    else:
        for t in range(p.N):

            @pl.when(p.n != t)
            def _():
                for i in range(2):
                    to(part(i), view(i), send.at[t, i], recv.at[p.slot, i], 2 * p.k + p.group, t).start()

    @pl.when(mine)
    def _():
        for i in range(2):
            pltpu.make_async_copy(part(i), view(i), local.at[i]).start()

    @pl.when(jnp.logical_not(mine))
    def _():
        for i in range(2):
            to(part(i), view(i), local.at[i], recv.at[p.slot, i], 2 * p.k + p.group, p.n).start()


def spread_pass(p, src, gathered, rows, send, recv, local, onward):
    if p.N == 4:
        half = rows // 2
        piece = src.at[pl.ds(0, half)]
        nx, ny, _ = neighbours(p)
        for i, (n, other) in enumerate(((nx, ny), (ny, nx))):
            j = slot_of(p, n, p.c)
            here = gathered.at[pl.ds(pl.multiple_of(j * rows + i * half, half), half)]
            pltpu.make_async_copy(piece, here, recv.at[j, i]).wait()
            to(here, here, onward.at[i], recv.at[j, i], p.w, other).start()


def spread_end(p, src, gathered, rows, send, recv, local, onward, on_slot=lambda j: None):
    half = rows // 2
    piece = src.at[pl.ds(0, half)]
    mine = p.group == p.c
    at = lambda j, i: gathered.at[pl.ds(pl.multiple_of(j * rows + i * half, half), half)]

    def arrive(j, i):
        pltpu.make_async_copy(piece, at(j, i), recv.at[j, i]).wait()

    for i in range(2):
        pltpu.make_async_copy(piece, at(0, 0), local.at[i]).wait()
    here = slot_of(p, p.n, p.c)

    @pl.when(jnp.logical_not(mine))
    def _():
        arrive(here, 0)
        arrive(here, 1)

    on_slot(here)
    if p.N == 4:
        nx, ny, nd = neighbours(p)
        jx, jy, jd = (slot_of(p, n, p.c) for n in (nx, ny, nd))
        arrive(jx, 1)
        on_slot(jx)
        arrive(jy, 0)
        on_slot(jy)
        arrive(jd, 0)
        arrive(jd, 1)
        on_slot(jd)
        for i in range(2):
            pltpu.make_async_copy(piece, at(0, 0), onward.at[i]).wait()
            for t in range(2):
                pltpu.make_async_copy(piece, at(0, 0), send.at[t, i]).wait()
    else:
        for t in range(p.N):

            @pl.when(p.n != t)
            def _():
                for i in range(2):
                    pltpu.make_async_copy(piece, at(0, 0), send.at[t, i]).wait()
                    arrive(slot_of(p, t, p.c), i)
                on_slot(slot_of(p, t, p.c))


def sum_bufs(narrow, rows, dim):
    if narrow == 4:
        half = pltpu.VMEM((2, 2, rows, dim // 2), BF)
        return [half, half, pltpu.VMEM((2, rows, dim), BF)]
    return [pltpu.VMEM((narrow, rows, dim), BF)]


def sum_sems(narrow):
    if narrow == 4:
        return [DMA((2, 2)), DMA((2, 2)), DMA((2, 2)), DMA((4,)), DMA((4,))]
    return [DMA((narrow,)), DMA((narrow,)), DMA]


def pieces(p, part, rows, dim):
    half = dim // 2
    return lambda j, i: part.at[pl.ds(pl.multiple_of(j * rows, rows), rows), pl.ds(i * half, half)]


def sum_start(p, part, rows, dim, bufs, sems):
    if p.N != 4:
        (got,), (send, recv, local) = bufs, sems
        for j in range(p.N):
            core, n = p.owner(j)
            mine = p.owner_is_me(j)
            src = part.at[pl.ds(j * rows, rows)]

            @pl.when(mine)
            def _():
                pltpu.make_async_copy(src, got.at[p.n], local).start()

            @pl.when(jnp.logical_not(mine))
            def _():
                to(src, got.at[p.n], send.at[j], recv.at[p.n], 2 * p.k + core, n).start()

        return
    own, inbox, _ = bufs
    load, send, recv, _, _ = sems
    piece = pieces(p, part, rows, dim)
    nx, ny, nd = neighbours(p)
    across, here = slot_of(p, nd, p.c), slot_of(p, p.n, p.c)
    for i, n in enumerate((nx, ny)):
        to(piece(across, i), inbox.at[i, 0], send.at[i, 0], recv.at[i, 0], p.w, n).start()
    for i, n in enumerate((ny, nx)):
        pltpu.make_async_copy(piece(slot_of(p, n, p.c), i), own.at[i, 0], load.at[i, 0]).start()
    for i, n in enumerate((nx, ny)):
        to(piece(slot_of(p, n, p.c), i), inbox.at[i, 1], send.at[i, 1], recv.at[i, 1], p.w, n).start()
        pltpu.make_async_copy(piece(here, i), own.at[i, 1], load.at[i, 1]).start()


def product_bufs(narrow, rows, dim):
    shape = (4, rows, dim // 2) if narrow == 4 else (narrow * rows, dim)
    return pltpu.VMEM(shape, BF)


def sum_start_of(p, product, out, rows, dim, bufs, sems):
    half = dim // 2
    if p.N != 4:

        def one(j, carry):
            for i in range(2):
                out[pl.ds(pl.multiple_of(j * rows, rows), rows), i * half : (i + 1) * half] = product(j, i)
            return carry

        lax.fori_loop(0, p.N, one, 0)
        sum_start(p, out, rows, dim, bufs, sems)
        return
    own, inbox, _ = bufs
    _, send, recv, _, _ = sems
    nx, ny, nd = neighbours(p)
    across, jx, jy, here = (slot_of(p, n, p.c) for n in (nd, nx, ny, p.n))

    def one(t, carry):
        i = lax.rem(t, 2)
        q = lax.rem(t // 2, 2)
        beside = jnp.where(i == 0, jx, jy)
        other = jnp.where(i == 0, jy, jx)
        j = jnp.where(t < 4, jnp.where(q == 0, across, beside), jnp.where(q == 0, other, here))
        y = product(j, i)

        @pl.when(t < 4)
        def _():
            out[t] = y
            to(out.at[t], inbox.at[i, q], send.at[i, q], recv.at[i, q], p.w, jnp.where(i == 0, nx, ny)).start()

        @pl.when(t >= 4)
        def _():
            own[i, q] = y

        return carry

    lax.fori_loop(0, 8, one, 0)


def core_of(p, j):
    return (j >= p.half).astype(jnp.int32)


def sum_pass(p, part, rows, dim, bufs, sems, loaded=False):
    if p.N != 4:
        return
    own, inbox, box = bufs
    load, send, recv, send2, recv2 = sems
    piece = lambda j, i: own.at[0, 0]
    half = dim // 2
    nx, ny, _ = neighbours(p)
    cols = lambda i: pl.ds(i * half, half)

    def add(i, q):
        if not loaded:
            pltpu.make_async_copy(piece(0, 0), own.at[i, q], load.at[i, q]).wait()
        pltpu.make_async_copy(piece(0, 0), inbox.at[i, q], recv.at[i, q]).wait()

        def body(at):
            own[i, q, at, :] = (own[i, q, at, :].astype(F32) + inbox[i, q, at, :].astype(F32)).astype(BF)

        row_loop(rows, 64, body)

    for i, n in enumerate((ny, nx)):
        add(i, 0)
        j = slot_of(p, n, p.c)
        to(own.at[i, 0], box.at[1, :, cols(i)], send2.at[i], recv2.at[i], 2 * p.k + core_of(p, j), n).start()
    j = slot_of(p, p.n, p.c)
    keep = core_of(p, j) == p.c
    for i in range(2):
        add(i, 1)

        @pl.when(keep)
        def _():
            pltpu.make_async_copy(own.at[i, 1], box.at[0, :, cols(i)], send2.at[2 + i]).start()

        @pl.when(jnp.logical_not(keep))
        def _():
            to(own.at[i, 1], box.at[0, :, cols(i)], send2.at[2 + i], recv2.at[2 + i], 2 * p.k + core_of(p, j), p.n).start()


def sum_end(p, part, rows, dim, bufs, sems):
    if p.N != 4:
        (got,), (send, recv, local) = bufs, sems
        for t in range(p.N):
            mine = (p.group == p.c) & (p.n == t)

            @pl.when(mine)
            def _():
                pltpu.make_async_copy(part.at[pl.ds(0, rows)], got.at[t], local).wait()

            @pl.when(jnp.logical_not(mine))
            def _():
                pltpu.make_async_copy(part.at[pl.ds(0, rows)], got.at[t], recv.at[t]).wait()

        for j in range(p.N):

            @pl.when(jnp.logical_not(p.owner_is_me(j)))
            def _():
                pltpu.make_async_copy(part.at[pl.ds(j * rows, rows)], got.at[0], send.at[j]).wait()

        return
    own, inbox, box = bufs
    load, send, recv, send2, recv2 = sems
    piece = lambda j, i: own.at[0, 0]
    half = dim // 2
    cols = lambda i: pl.ds(i * half, half)
    for i in range(2):
        for q in range(2):
            pltpu.make_async_copy(piece(0, 0), inbox.at[i, q], send.at[i, q]).wait()
        pltpu.make_async_copy(own.at[i, 0], box.at[1, :, cols(i)], send2.at[i]).wait()
        pltpu.make_async_copy(own.at[i, 0], box.at[1, :, cols(i)], recv2.at[i]).wait()
        pltpu.make_async_copy(own.at[i, 1], box.at[0, :, cols(i)], send2.at[2 + i]).wait()

        @pl.when(p.group != p.c)
        def _():
            pltpu.make_async_copy(own.at[i, 1], box.at[0, :, cols(i)], recv2.at[2 + i]).wait()


def total(p, bufs, at):
    if p.N == 4:
        box = bufs[2]
        return box[0, at, :].astype(F32) + box[1, at, :].astype(F32)
    got = bufs[0]
    out = got[0, at, :].astype(F32)
    for t in range(1, p.N):
        out = out + got[t, at, :].astype(F32)
    return out


PARTS = 4


def line_sems(chips):
    return [DMA((2, chips, PARTS)), DMA((chips, PARTS)), DMA((chips, PARTS)), DMA((chips, PARTS)), DMA((PARTS,))]


def line_parts(p, full, rows):
    size = rows // PARTS

    def at(s, core, q=None):
        first = (2 * s + core) * rows
        if q is None:
            return full.at[pl.ds(pl.multiple_of(first, rows), rows)]
        return full.at[pl.ds(pl.multiple_of(first + q * size, size), size)]

    return at


def each_part(body):
    def one(q, carry):
        body(q)
        return carry

    lax.fori_loop(0, PARTS, one, 0)


def line_copy(p, src, dst, send, recv, k, core):
    return pltpu.make_async_remote_copy(
        src_ref=src, dst_ref=dst, send_sem=send, recv_sem=recv, device_id=(2 * k + core, p.n), device_id_type=MESH
    )


def inside(p, k):
    return (k >= 0) & (k < p.C)


BOTH, UP, DOWN = ((0, 1), (1, -1)), ((0, 1),), ((1, -1),)


def line_push(p, src, full, rows, zsend, zrecv, csend, crecv, local, q, ways=BOTH):
    size = rows // PARTS
    part = src.at[pl.ds(pl.multiple_of(q * size, size), size)]
    there = line_parts(p, full, rows)(p.k, p.c, q)
    for i, sign in ways:

        @pl.when(inside(p, p.k + sign))
        def _():
            line_copy(p, part, there, zsend.at[i, 0, q], zrecv.at[p.k, q], p.k + sign, p.c).start()

    line_copy(p, part, there, csend.at[p.k, q], crecv.at[p.k, q], p.k, 1 - p.c).start()
    pltpu.make_async_copy(part, there, local.at[q]).start()


def came(p, s, ways):
    if ways == BOTH:
        return s == s
    return s <= p.k if ways == UP else s >= p.k


def line_steps(p, src, full, rows, zsend, zrecv, csend, crecv, local, ways=BOTH):
    at = line_parts(p, full, rows)
    piece = src.at[pl.ds(0, rows // PARTS)]

    def at_distance(d):
        def onward(q):
            for i, sign in ways:
                s, t = p.k - sign * d, p.k + sign

                @pl.when(inside(p, s))
                def _():
                    here = at(s, p.c, q)
                    pltpu.make_async_copy(piece, here, zrecv.at[s, q]).wait()

                    @pl.when(inside(p, t))
                    def _():
                        line_copy(p, here, here, zsend.at[i, d, q], zrecv.at[s, q], t, p.c).start()

                    line_copy(p, here, here, csend.at[s, q], crecv.at[s, q], p.k, 1 - p.c).start()

        each_part(onward)

    def settle(q):
        here = at(p.k, p.c, q)
        pltpu.make_async_copy(piece, here, local.at[q]).wait()
        for s in range(p.C):

            @pl.when(came(p, jnp.int32(s), ways))
            def _():
                pltpu.make_async_copy(piece, here, csend.at[s, q]).wait()
                pltpu.make_async_copy(piece, at(s, 1 - p.c, q), crecv.at[s, q]).wait()

        for i, sign in ways:
            for d in range(p.C):

                @pl.when(inside(p, p.k - sign * d) & inside(p, p.k + sign))
                def _():
                    pltpu.make_async_copy(piece, here, zsend.at[i, d, q]).wait()

    return [functools.partial(at_distance, d) for d in range(1, p.C)] + [lambda: each_part(settle)]


def line_sum_bufs(chips, rows, width):
    return [pltpu.VMEM((chips, rows, width), BF)] * 3 + [pltpu.VMEM((2, rows, width), BF), pltpu.VMEM((rows, width), F32)]


def line_sum_sems(chips):
    return [
        DMA((chips, PARTS)), DMA((chips, PARTS)), DMA((chips, PARTS)), DMA((2, chips, PARTS)), DMA((chips, PARTS)),
        DMA((2, PARTS)),
    ]


OTHER = {BOTH: BOTH, UP: DOWN, DOWN: UP}


def line_sum_start(p, part, rows, bufs, sems, ways=BOTH):
    own, inbox, _, _, _ = bufs
    load, csend, crecv, _, _, _ = sems
    at = line_parts(p, part, rows)
    size = rows // PARTS

    def share(s):
        def one(q):
            here = pl.ds(pl.multiple_of(q * size, size), size)
            line_copy(p, at(s, 1 - p.c, q), inbox.at[s, here], csend.at[s, q], crecv.at[s, q], p.k, 1 - p.c).start()
            pltpu.make_async_copy(at(s, p.c, q), own.at[s, here], load.at[s, q]).start()

        each_part(one)

    for d in range(p.C - 1, 0, -1):
        for _, sign in ways:
            s = p.k + sign * d

            @pl.when(inside(p, s))
            def _():
                share(s)

    share(p.k)


def line_sum_steps(p, part, rows, bufs, sems, ways=BOTH):
    own, inbox, relay, box, acc = bufs
    load, csend, crecv, zsend, rrecv, zrecv = sems
    size = rows // PARTS
    step = math.gcd(size, 128)
    piece = line_parts(p, part, rows)(0, 0, 0)

    def rows_of(q):
        return pl.ds(pl.multiple_of(q * size, size), size)

    def add(q, body):
        def one(j, carry):
            body(pl.ds(pl.multiple_of(q * size + j * step, step), step))
            return carry

        lax.fori_loop(0, size // step, one, 0)

    def pair(t, q):
        pltpu.make_async_copy(piece, own.at[t, rows_of(q)], load.at[t, q]).wait()
        pltpu.make_async_copy(piece, inbox.at[t, rows_of(q)], crecv.at[t, q]).wait()

    def at_distance(d):
        def onward(q):
            here = rows_of(q)
            for i, sign in ways:
                t = p.k + sign * d
                behind = inside(p, p.k - sign)

                @pl.when(inside(p, t))
                def _():
                    pair(t, q)

                    @pl.when(jnp.logical_not(behind))
                    def _():
                        def two(at):
                            own[t, at, :] = (own[t, at, :].astype(F32) + inbox[t, at, :].astype(F32)).astype(BF)

                        add(q, two)

                    @pl.when(behind)
                    def _():
                        pltpu.make_async_copy(piece, relay.at[t, here], rrecv.at[t, q]).wait()

                        def three(at):
                            both = own[t, at, :].astype(F32) + inbox[t, at, :].astype(F32)
                            own[t, at, :] = (both + relay[t, at, :].astype(F32)).astype(BF)

                        add(q, three)

                    src = own.at[t, here]
                    if d >= 2:
                        line_copy(p, src, relay.at[t, here], zsend.at[i, d, q], rrecv.at[t, q], p.k + sign, p.c).start()
                    else:
                        line_copy(p, src, box.at[i, here], zsend.at[i, d, q], zrecv.at[i, q], t, p.c).start()

        each_part(onward)

    def last(q):
        here = rows_of(q)
        pair(p.k, q)

        def first(at):
            acc[at, :] = own[p.k, at, :].astype(F32) + inbox[p.k, at, :].astype(F32)

        add(q, first)
        for i, sign in ways:

            @pl.when(inside(p, p.k - sign))
            def _():
                pltpu.make_async_copy(piece, box.at[i, here], zrecv.at[i, q]).wait()

                def more(at):
                    acc[at, :] += box[i, at, :].astype(F32)

                add(q, more)

            for d in range(1, p.C):

                @pl.when(inside(p, p.k + sign * d))
                def _():
                    pltpu.make_async_copy(piece, own.at[0, here], zsend.at[i, d, q]).wait()

        for s in range(p.C):

            @pl.when(came(p, jnp.int32(s), OTHER[ways]))
            def _():
                pltpu.make_async_copy(piece, inbox.at[s, here], csend.at[s, q]).wait()


    return [functools.partial(at_distance, d) for d in range(p.C - 1, 0, -1)] + [lambda: each_part(last)]


def row_loop(rows, step, body):
    def one(i, carry):
        body(pl.ds(pl.multiple_of(i * step, step), step))
        return carry

    lax.fori_loop(0, rows // step, one, 0)


STEP = 64


def inv_rms(u):
    return lax.rsqrt(jnp.mean(u * u, axis=-1, keepdims=True) + EPSILON)


def weave(gate_ref, up_ref, both_ref):
    ff = gate_ref.shape[1]
    t = math.gcd(ff, 256)
    for i in range(0, ff, t):
        both_ref[:, 2 * i : 2 * i + t] = gate_ref[:, i : i + t]
        both_ref[:, 2 * i + t : 2 * i + 2 * t] = up_ref[:, i : i + t]


def finish_kernel(both_ref, down_ref, qo_ref, kv_ref, gate_out, up_out, down_out, q_out, k_out, v_out, o_out):
    ff = gate_out.shape[1]
    t = math.gcd(ff, 256)
    for i in range(0, ff, t):
        gate_out[:, i : i + t] = both_ref[:, 2 * i : 2 * i + t].astype(F32)
        up_out[:, i : i + t] = both_ref[:, 2 * i + t : 2 * i + 2 * t].astype(F32)
    down_out[...] = jnp.transpose(down_ref[...].astype(F32))
    qw, kw = q_out.shape[1], k_out.shape[1]
    q_out[...] = qo_ref[:, :qw]
    o_out[...] = jnp.transpose(qo_ref[:, qw:])
    k_out[...] = kv_ref[:, :kw]
    v_out[...] = kv_ref[:, kw:]


def rotation(p, cos_ref, sin_ref):
    all_rows, hd = cos_ref.shape
    block, half, step = all_rows // 2, hd // 2, 64
    lane = lax.broadcasted_iota(jnp.int32, (step, hd), 1)
    column = jnp.where(lane < half, lane, lane - half).astype(F32)
    inverse = jnp.exp(column * (-2.0 * math.log(1000000.0) / hd))
    row = lax.broadcasted_iota(jnp.int32, (step, hd), 0)

    def body(i, carry):
        at = i * step
        first = jnp.where(at < block, (4 * p.k + p.c) * block + at, (4 * p.k + 3 - p.c) * block + at - block)
        angles = (first + row).astype(F32) * inverse
        here = pl.ds(pl.multiple_of(at, step), step)
        cos_ref[here, :] = jnp.cos(angles)
        sine = jnp.sin(angles)
        sin_ref[here, :] = jnp.where(lane < half, -sine, sine)
        return carry

    lax.fori_loop(0, all_rows // step, body, 0)


def input_kernel(
    wide, narrow, x_ref, gain_ref, shard, gate_ref, up_ref, gathered, full, gu_ref, cos_ref, sin_ref, buf, *sems
):
    p = Place(wide, narrow)
    rows = x_ref.shape[0]
    spread, line = sems[:4], (shard, full, shard.shape[0], *sems[4:])
    enter(p, line=True)
    each_part(lambda q: line_push(p, *line, q))
    *steps, end = line_steps(p, *line)

    def body(at):
        u = x_ref[at, :].astype(F32)
        buf[at, :] = (u * inv_rms(u) * gain_ref[...]).astype(BF)

    row_loop(rows, STEP, body)
    spread_start(p, buf, gathered, rows, *spread)
    weave(gate_ref, up_ref, gu_ref)
    steps[0]()
    rotation(p, cos_ref, sin_ref)
    spread_pass(p, buf, gathered, rows, *spread)
    for step in steps[1:]:
        step()
    spread_end(p, buf, gathered, rows, *spread)
    end()


def turn(u):
    return pltpu.roll(u, u.shape[-1] // 2, 1)


def qkv_kernel(
    wide, narrow, qw, kw, fold, g_ref, x_ref, w_ref, cos_ref, sin_ref, qg_ref, kg_ref,
    gathered, full, qproj_ref, kproj_ref, q_ref, kv_ref, w_buf, x_buf, load, *sems,
):
    p = Place(wide, narrow)
    rows = g_ref.shape[0]
    hd = cos_ref.shape[1]
    all_rows = x_ref.shape[0]
    size = all_rows // 4
    spread, line = sems[:4], (kv_ref, full, all_rows, *sems[4:])
    weights = pltpu.make_async_copy(w_ref.at[:, pl.ds(0, w_buf.shape[1])], w_buf, load.at[0])
    normed = pltpu.make_async_copy(x_ref, x_buf, load.at[1])
    normed.start()
    weights.start()
    enter(p, line=True)

    def project(q):
        at = pl.ds(pl.multiple_of(q * size, size), size)
        y = dg(x_buf[at, :], w_buf[...], NN)
        cos, sin = cos_ref[at, :], sin_ref[at, :]
        qproj_ref[at, :] = y[:, :qw]
        kproj_ref[at, :] = y[:, qw : qw + kw]

        def head(lo, gain):
            u = y[:, lo : lo + hd]
            v = u * inv_rms(u) * gain
            return v * cos + turn(v) * sin

        for h in range(kw // hd):
            kv_ref[at, 2 * h * hd : (2 * h + 1) * hd] = head(qw + h * hd, kg_ref[...]).astype(BF)
            kv_ref[at, (2 * h + 1) * hd : (2 * h + 2) * hd] = y[:, qw + kw + h * hd : qw + kw + (h + 1) * hd].astype(BF)
        for i in range(PARTS // 4):
            line_push(p, *line, q * (PARTS // 4) + i, ways=UP)
        for h in range(qw // hd):
            q_ref[at, h * hd : (h + 1) * hd] = (head(h * hd, qg_ref[...]) * fold).astype(BF)

    normed.wait()
    weights.wait()

    def one(q, carry):
        project(q)
        return carry

    lax.fori_loop(0, 4, one, 0)
    spread_start(p, g_ref, gathered, rows, *spread)
    *steps, end = line_steps(p, *line, ways=UP)
    steps[0]()
    spread_pass(p, g_ref, gathered, rows, *spread)
    for step in steps[1:]:
        step()
    spread_end(p, g_ref, gathered, rows, *spread)
    end()


def middle_kernel(wide, narrow, part, own_ref, gain_ref, mid_ref, gathered, buf, *refs):
    p = Place(wide, narrow)
    rows, dim = own_ref.shape
    bufs, sems, spread = split_refs(narrow, refs)
    enter(p)
    sum_start(p, part, rows, dim, bufs, sems)
    sum_pass(p, part, rows, dim, bufs, sems)
    sum_end(p, part, rows, dim, bufs, sems)

    def body(at):
        u = own_ref[at, :].astype(F32) + total(p, bufs, at)
        mid_ref[at, :] = u
        buf[at, :] = (u * inv_rms(u) * gain_ref[...]).astype(BF)

    row_loop(rows, STEP, body)
    spread_start(p, buf, gathered, rows, *spread)
    spread_pass(p, buf, gathered, rows, *spread)
    spread_end(p, buf, gathered, rows, *spread)


def split_refs(narrow, refs):
    bufs, sems = (3, 5) if narrow == 4 else (1, 3)
    return refs[:bufs], refs[bufs : bufs + sems], refs[bufs + sems :]


def norm_back(u, gain, cot):
    r = inv_rms(u)
    a = cot * gain
    du = r * a - u * (r * r * r) * jnp.mean(a * u, axis=-1, keepdims=True)
    return du, jnp.sum(cot * u * r, axis=0, keepdims=True)


def mlp_back_kernel(
    wide, narrow, g_ref, wd_ref, gu_ref, w_ref, x_ref, mid_ref, gain_ref, grad_ref, back_ref, rows_ref, dgain_ref, wgrad,
    g_buf, wd_buf, gu_buf, low, w_buf, x_buf, stage, out, load, tiles_in, store, *refs
):
    p = Place(wide, narrow)
    rows, dim = mid_ref.shape
    half = dim // 2
    t = wd_buf.shape[2]
    bufs, sems, _ = split_refs(narrow, refs)

    def tile_of(i):
        slot = lax.rem(i, 2)
        return (
            pltpu.make_async_copy(wd_ref.at[:, pl.ds(pl.multiple_of(i * t, t), t)], wd_buf.at[slot], tiles_in.at[0, slot]),
            pltpu.make_async_copy(gu_ref.at[:, pl.ds(pl.multiple_of(2 * i * t, t), 2 * t)], gu_buf.at[slot], tiles_in.at[1, slot]),
        )

    loads = [pltpu.make_async_copy(g_ref, g_buf, load.at[0])]
    for i in range(2):
        at = pl.ds(i * half, half)
        loads.append(pltpu.make_async_copy(w_ref.at[at], w_buf.at[at], load.at[1 + i]))
    loads.append(pltpu.make_async_copy(x_ref, x_buf, load.at[3]))
    loads[0].start()
    for copy in tile_of(0):
        copy.start()
    enter(p)
    loads[0].wait()
    count = wd_ref.shape[1] // t

    def gates(i, carry):
        @pl.when(i + 1 < count)
        def _():
            for copy in tile_of(i + 1):
                copy.start()

        for copy in tile_of(i):
            copy.wait()

        @pl.when(i == 0)
        def _():
            for copy in loads[1:]:
                copy.start()

        slot = lax.rem(i, 2)
        hb = dg(g_buf[...], wd_buf[slot], NN)
        gate, up = gu_buf[slot, :, :t], gu_buf[slot, :, t:]
        s = jax.nn.sigmoid(gate)
        gs = hb * s
        at = pl.multiple_of(2 * i * t, t)
        low[:, pl.ds(at, t)] = (gs * up * (1.0 + gate * (1.0 - s))).astype(BF)
        low[:, pl.ds(pl.multiple_of(at + t, t), t)] = (gs * gate).astype(BF)
        return carry

    lax.fori_loop(0, count, gates, 0)
    for copy in loads[1:3]:
        copy.wait()

    def product(j, i):
        a = low[pl.ds(pl.multiple_of(j * rows, rows), rows), :]
        return dg(a, w_buf[pl.ds(pl.multiple_of(i * half, half), half), :], NT).astype(BF)

    sum_start_of(p, product, out, rows, dim, bufs, sems)
    dgain_ref[...] = jnp.zeros_like(dgain_ref)
    loads[3].wait()
    tile = 256

    def write(i):
        return pltpu.make_async_copy(
            stage.at[lax.rem(i, 2)], wgrad.at[pl.ds(pl.multiple_of(i * tile, tile), tile)], store.at[lax.rem(i, 2)]
        )

    def grads(first, last):
        def one(i, carry):
            @pl.when(i >= 2)
            def _():
                write(i - 2).wait()

            stage[lax.rem(i, 2)] = dg(x_buf[:, pl.ds(pl.multiple_of(i * tile, tile), tile)], low[...], TN).astype(BF)
            write(i).start()
            return carry

        lax.fori_loop(first, last, one, 0)

    tiles = dim // tile
    early = 3
    grads(0, early)
    sum_pass(p, out, rows, dim, bufs, sems, loaded=narrow == 4)
    grads(early, tiles)
    sum_end(p, out, rows, dim, bufs, sems)

    def body(at):
        du, dgain = norm_back(mid_ref[at, :], gain_ref[...], total(p, bufs, at))
        back = grad_ref[at, :].astype(F32) + du
        back_ref[at, :] = back
        rows_ref[at, :] = back.astype(BF)
        dgain_ref[...] += dgain

    row_loop(rows, STEP, body)
    write(tiles - 2).wait()
    write(tiles - 1).wait()


def middle_back_kernel(
    wide, narrow, wo_at, groups, hd, rows_ref, hidden, w_ref, wo_ref, o_ref, all_ref, next_ref, back_ref, delta_ref,
    gathered, next_buf, h_buf, w_buf, wo_buf, o_buf, load, store, next_store, *spread
):
    p = Place(wide, narrow)
    rows = rows_ref.shape[0]
    pairs = ((hidden, h_buf), (w_ref, w_buf), (wo_ref.at[:, pl.ds(*wo_at)], wo_buf), (o_ref, o_buf))
    loads = [pltpu.make_async_copy(src, dst, load.at[i]) for i, (src, dst) in enumerate(pairs)]
    enter(p)
    spread_start(p, rows_ref, gathered, rows, *spread)
    for copy in loads:
        copy.start()
    for copy in loads[:2]:
        copy.wait()

    def write_next(i):
        at = pl.ds(pl.multiple_of(i * 256, 256), 256)
        return pltpu.make_async_copy(next_buf.at[at], next_ref.at[at], next_store.at[i])

    def write_slot(j):
        at = pl.ds(pl.multiple_of(j * rows, rows), rows)
        return pltpu.make_async_copy(gathered.at[at], all_ref.at[at], store.at[j])

    def downs(first, last):
        def one(i, carry):
            at = pl.ds(pl.multiple_of(i * 256, 256), 256)
            next_buf[at, :] = dg(h_buf[at, :], w_buf[...], NT).astype(BF)
            write_next(i).start()
            return carry

        lax.fori_loop(first, last, one, 0)

    blocks = next_buf.shape[0] // 256
    downs(0, blocks // 2)

    def on_slot(j):
        at = pl.ds(pl.multiple_of(j * rows, rows), rows)
        write_slot(j).start()
        back = dg(gathered[at, :], wo_buf[...], NN).astype(BF)
        back_ref[at, :] = back
        lane = lax.broadcasted_iota(jnp.int32, (rows, hd), 1)
        out = jnp.zeros((rows, hd), F32)
        for h in range(back.shape[1] // hd):
            mine = slice(h * hd, (h + 1) * hd)
            row = 8 * (h // groups) + h % groups
            delta = jnp.sum(back[:, mine].astype(F32) * o_buf[at, mine], axis=1, keepdims=True)
            out = jnp.where(lane == row, delta, out)
        delta_ref[:, at] = jnp.transpose(out)[: delta_ref.shape[0]]

    spread_pass(p, rows_ref, gathered, rows, *spread)
    downs(blocks // 2, blocks)
    for copy in loads[2:]:
        copy.wait()
    spread_end(p, rows_ref, gathered, rows, *spread, on_slot=on_slot)
    for i in range(blocks):
        write_next(i).wait()
    for j in range(p.N):
        write_slot(j).wait()


def share_start(me, count, here, slots, sends, recvs, device):
    slots[me] = here[...]
    for t in range(count):

        @pl.when(me != t)
        def _():
            wide_at, narrow_at = device(t)
            to(here, slots.at[me], sends.at[t], recvs.at[me], wide_at, narrow_at).start()


def share_end(me, count, here, slots, sends, recvs):
    for t in range(count):

        @pl.when(me != t)
        def _():
            pltpu.make_async_copy(here, slots.at[t], sends.at[t]).wait()
            pltpu.make_async_copy(here, slots.at[t], recvs.at[t]).wait()

    out = slots[0]
    for t in range(1, count):
        out = out + slots[t]
    here[...] = out


def head_back(cot, u, gain, cos, sin):
    cot = cot * cos - turn(cot) * sin
    return norm_back(u, gain, cot)


def output_kernel(
    wide, narrow, part, mid_ref, dkv, dq, qproj, cos_ref, sin_ref, g_ref, x_ref, m_ref, a_ref,
    out_ref, kv_ref, low_ref, dgain_ref, wgrad_out, wgrad_ref, dq_buf, u_buf, x_buf, m_buf, a_buf, load, store, *refs
):
    p = Place(wide, narrow)
    rows, dim = mid_ref.shape
    kv_rows = kv_ref.shape[0]
    width = low_ref.shape[1]
    hd = cos_ref.shape[1]
    bufs, sems, line = split_refs(narrow, refs)
    sums = (part, rows, dim, bufs, sems)
    chain = (p, dkv, kv_rows, line[:5], line[5:])
    pairs = ((dq, dq_buf), (qproj, u_buf), (x_ref, x_buf), (m_ref, m_buf), (a_ref, a_buf))
    loads = [pltpu.make_async_copy(src, dst, load.at[i]) for i, (src, dst) in enumerate(pairs)]
    enter(p, line=True)
    line_sum_start(*chain, ways=DOWN)
    sum_start(p, *sums)
    for copy in loads:
        copy.start()
    first, *steps, last = line_sum_steps(*chain, ways=DOWN)
    first()
    dgain_ref[...] = jnp.zeros_like(dgain_ref)
    for copy in loads[:2]:
        copy.wait()

    def through_heads(at):
        for h in range(width // hd):
            mine = slice(h * hd, (h + 1) * hd)
            du, dgain = head_back(dq_buf[at, mine], u_buf[at, mine], g_ref[...], cos_ref[at, :], sin_ref[at, :])
            low_ref[at, mine] = du.astype(BF)
            dgain_ref[...] += dgain

    row_loop(low_ref.shape[0], 128, through_heads)
    for copy in loads[2:]:
        copy.wait()

    def write(i):
        at = pl.ds(pl.multiple_of(i * 256, 256), 256)
        return pltpu.make_async_copy(wgrad_ref.at[at], wgrad_out.at[at], store.at[i])

    def grads(first_tile, last_tile):
        def one(i, carry):
            at = pl.ds(pl.multiple_of(i * 256, 256), 256)
            wgrad_ref[at, :width] = dg(x_buf[:, at], low_ref[...], TN).astype(BF)
            wgrad_ref[at, width:] = dg(m_buf[:, at], a_buf[...], TN).astype(BF)
            write(i).start()
            return carry

        lax.fori_loop(first_tile, last_tile, one, 0)

    tiles = dim // 256
    grads(0, tiles // 2)
    sum_pass(p, *sums)
    steps[0]()
    grads(tiles // 2, tiles)
    sum_end(p, *sums)

    def body(at):
        out_ref[at, :] = (mid_ref[at, :] + total(p, bufs, at)).astype(BF)

    row_loop(rows, STEP, body)
    for step in steps[1:]:
        step()
    last()
    row_loop(kv_rows, 128, lambda at: kv_ref.__setitem__((at, slice(None)), line[4][at, :].astype(BF)))
    for i in range(tiles):
        write(i).wait()


def input_back_kernel(
    wide, narrow, qw, kw, own_ref, gain_ref, back_ref, gains_ref, wgrad, q_ref, kv_ref, proj_ref, cos_ref, sin_ref, kg_ref,
    w_ref, x_ref, out_ref, gsum_ref, wsum_ref, kvsum_ref,
    gbuf, gbuf2, low, part, kvgrad, w_buf, x_buf, load, gsend, grecv, gsend2, grecv2, *refs,
):
    p = Place(wide, narrow)
    rows, dim = own_ref.shape
    hd = cos_ref.shape[1]
    all_rows = x_ref.shape[0]
    w_rows = wsum_ref.shape[0]
    bufs, sems, line = split_refs(narrow, refs)
    sums = (part, rows, dim, bufs, sems)
    first_line = (p, wgrad, w_rows, (*line[:4], wsum_ref), line[4:10])
    second_line = (p, kvgrad, w_rows, (*line[10:14], kvsum_ref), line[14:])
    weights = pltpu.make_async_copy(w_ref.at[:, pl.ds(0, w_buf.shape[1])], w_buf, load.at[0])
    weights.start()
    normed = pltpu.make_async_copy(x_ref, x_buf, load.at[1])
    normed.start()
    enter(p, ring=True)
    line_sum_start(*first_line)
    gsum_ref[...] = gains_ref[...]
    size = min(all_rows, 256)
    first = line_sum_steps(*first_line)
    first[0]()
    weights.wait()

    def through_heads(at):
        low[at, :qw] = q_ref[at, :]
        for h in range(kw // hd):
            key = slice(2 * h * hd, (2 * h + 1) * hd)
            value = slice((2 * h + 1) * hd, (2 * h + 2) * hd)
            mine = slice(qw + h * hd, qw + (h + 1) * hd)
            du, dgain = head_back(
                kv_ref[at, key].astype(F32), proj_ref[at, h * hd : (h + 1) * hd], kg_ref[...], cos_ref[at, :], sin_ref[at, :]
            )
            low[at, mine] = du.astype(BF)
            low[at, qw + kw + h * hd : qw + kw + (h + 1) * hd] = kv_ref[at, value]
            gsum_ref[:, 2 * dim + hd :] += dgain
        part[at, :] = dg(low[at, :], w_buf[...], NT).astype(BF)

    row_loop(all_rows, size, through_heads)
    sum_start(p, *sums)
    first[1]()

    normed.wait()

    def key_grads(at):
        kvgrad[at, :] = dg(x_buf[:, at], low[:, qw:], TN).astype(BF)

    row_loop(dim, 256, key_grads)
    line_sum_start(*second_line)
    second = line_sum_steps(*second_line)
    second[0]()
    for step in first[2:-1]:
        step()
    sum_pass(p, *sums)
    for step in second[1:-1]:
        step()
    sum_end(p, *sums)

    def body(at):
        du, dgain = norm_back(own_ref[at, :].astype(F32), gain_ref[...], total(p, bufs, at))
        out_ref[at, :] = back_ref[at, :] + du
        gsum_ref[:, :dim] += dgain

    row_loop(rows, STEP, body)

    share_start(p.n, narrow, gsum_ref, gbuf, gsend, grecv, lambda t: (p.w, t))
    first[-1]()
    share_end(p.n, narrow, gsum_ref, gbuf, gsend, grecv)
    share_start(p.w, wide, gsum_ref, gbuf2, gsend2, grecv2, lambda t: (t, p.n))
    second[-1]()
    share_end(p.w, wide, gsum_ref, gbuf2, gsend2, grecv2)


VM = pl.BlockSpec(memory_space=pltpu.VMEM)


HB = pl.BlockSpec(memory_space=pl.ANY)


def comm_call(kernel, name, cid, out_shape, in_specs, out_specs, scratch, *args):
    return pl.pallas_call(
        kernel,
        out_shape=out_shape,
        in_specs=in_specs,
        out_specs=out_specs,
        scratch_shapes=scratch,
        compiler_params=pltpu.CompilerParams(collective_id=cid, has_side_effects=True, vmem_limit_bytes=60 << 20),
        cost_estimate=pl.CostEstimate(flops=0, bytes_accessed=160_000_000, transcendentals=0),
        name=name,
    )(*args)


def sds(shape, kind):
    return jax.ShapeDtypeStruct(shape, kind)


def plain(kernel, name, grid, in_specs, out_specs, out_shape, flops, nbytes, *args, scratch=(), aliases=None):
    return pl.pallas_call(
        kernel,
        out_shape=out_shape,
        grid=grid,
        in_specs=in_specs,
        out_specs=out_specs,
        scratch_shapes=scratch,
        input_output_aliases=aliases or {},
        compiler_params=pltpu.CompilerParams(vmem_limit_bytes=52 << 20),
        cost_estimate=pl.CostEstimate(flops=flops, bytes_accessed=nbytes, transcendentals=0),
        name=name,
    )(*args)


def whole(shape):
    return pl.BlockSpec(shape, lambda *i: (0,) * len(shape), pipeline_mode=pl.Buffered(1))


def by_rows(tm, width):
    return pl.BlockSpec((tm, width), lambda i: (i, 0))


def mlp_fwd_kernel(x_ref, w_ref, gu_ref, h_ref):
    t = h_ref.shape[1]
    y = dg(x_ref[...], w_ref[...], NN)
    gate, up = y[:, :t], y[:, t:]
    gu_ref[...] = y
    h_ref[...] = (gate * jax.nn.sigmoid(gate) * up).astype(BF)


def mlp_fwd(x, w, t):
    rows, dim = x.shape
    ff2 = w.shape[1]
    return plain(
        mlp_fwd_kernel, "mlp_fwd", (ff2 // (2 * t),),
        [whole((rows, dim)), pl.BlockSpec((dim, 2 * t), lambda i: (0, i))],
        [pl.BlockSpec((rows, 2 * t), lambda i: (0, i)), pl.BlockSpec((rows, t), lambda i: (0, i))],
        (sds((rows, ff2), F32), sds((rows, ff2 // 2), BF)),
        2 * rows * dim * ff2, rows * dim * 2 + dim * ff2 * 2 + rows * ff2 * 5, x, w,
    )


def fwd_kernel(groups, hd, tab, q_ref, kv_ref, o_ref, low_ref, lse_ref, acc, lsum):
    s = pl.program_id(1)
    block = q_ref.shape[0]
    diag, first, last = tab[2, s], tab[3, s], tab[4, s]

    @pl.when(first == 1)
    def _():
        acc[...] = jnp.zeros_like(acc)
        lsum[...] = jnp.zeros_like(lsum)

    def work(masked):
        k, v = kv_ref[:, :hd], kv_ref[:, hd:]
        for g in range(groups):
            at = slice(g * hd, (g + 1) * hd)
            scores = dg(q_ref[:, at], k, NT)
            if masked:
                row = lax.broadcasted_iota(jnp.int32, scores.shape, 0)
                col = lax.broadcasted_iota(jnp.int32, scores.shape, 1)
                scores = jnp.where(col <= row, scores, MASKED)
            probs = jnp.exp2(scores)
            part = probs[:, :128]
            for j in range(1, block // 128):
                part = part + probs[:, j * 128 : (j + 1) * 128]
            lsum[g] += part
            acc[:, at] += dg(probs.astype(BF), v, NN)

    @pl.when(diag == 0)
    def _():
        work(False)

    @pl.when(diag == 1)
    def _():
        work(True)

    @pl.when(last == 1)
    def _():
        lane = lax.broadcasted_iota(jnp.int32, (block, 128), 1)
        lse = jnp.zeros((block, 128), F32)
        for g in range(groups):
            at = slice(g * hd, (g + 1) * hd)
            l = jnp.sum(lsum[g], axis=1, keepdims=True)
            out = acc[:, at] / l
            o_ref[:, at] = out
            low_ref[:, at] = out.astype(BF)
            lse = jnp.where(lane == g, jnp.log2(l), lse)
        lse_ref[...] = jnp.transpose(lse)[: lse_ref.shape[0]]


def attn_fwd(tab, q, kv, groups, hd, block):
    rows, width = q.shape
    gw = groups * hd
    heads = width // gw
    steps = tab.shape[1]
    mine = pl.BlockSpec((block, gw), lambda h, s, t: (t[0, s], h))
    return pl.pallas_call(
        functools.partial(fwd_kernel, groups, hd),
        out_shape=(sds((rows, width), F32), sds((rows, width), BF), sds((8 * heads, rows), F32)),
        grid_spec=pltpu.PrefetchScalarGridSpec(
            num_scalar_prefetch=1,
            grid=(heads, steps),
            in_specs=[mine, pl.BlockSpec((block, 2 * hd), lambda h, s, t: (t[1, s], h))],
            out_specs=[mine, mine, pl.BlockSpec((8, block), lambda h, s, t: (h, t[0, s]))],
            scratch_shapes=[pltpu.VMEM((block, gw), F32), pltpu.VMEM((groups, block, 128), F32)],
        ),
        compiler_params=pltpu.CompilerParams(vmem_limit_bytes=48 << 20),
        cost_estimate=pl.CostEstimate(
            flops=heads * steps * block * block * gw * 4,
            bytes_accessed=heads * steps * block * hd * 8,
            transcendentals=heads * steps * block * block * groups,
        ),
        name="attn_fwd",
    )(tab, q, kv)


def bwd_kernel(groups, hd, tab, q_ref, do_ref, kv_ref, lse_ref, delta_ref, dq_ref, dkv_ref, dq_sum, dkv_sum):
    s = pl.program_id(1)
    block = q_ref.shape[0]
    qi, diag, first, last = tab[0, s], tab[2, s], tab[3, s], tab[4, s]

    @pl.when(s == 0)
    def _():
        dq_sum[...] = jnp.zeros_like(dq_sum)

    @pl.when(first == 1)
    def _():
        dkv_sum[...] = jnp.zeros_like(dkv_sum)

    def work(masked):
        k, v = kv_ref[:, :hd], kv_ref[:, hd:]
        for g in range(groups):
            at = slice(g * hd, (g + 1) * hd)
            q, do = q_ref[:, at], do_ref[:, at]
            scores = dg(k, q, NT) - lse_ref[g : g + 1, :]
            if masked:
                row = lax.broadcasted_iota(jnp.int32, scores.shape, 0)
                col = lax.broadcasted_iota(jnp.int32, scores.shape, 1)
                scores = jnp.where(row <= col, scores, MASKED)
            probs = jnp.exp2(scores)
            dots = dg(v, do, NT)
            dkv_sum[:, hd:] += dg(probs.astype(BF), do, NN)
            back = (probs * (dots - delta_ref[g : g + 1, :])).astype(BF)
            dkv_sum[:, :hd] += dg(back, q, NN)
            dq_sum[qi, :, at] += dg(back, k, TN)

    @pl.when(diag == 0)
    def _():
        work(False)

    @pl.when(diag == 1)
    def _():
        work(True)

    @pl.when(last == 1)
    def _():
        dkv_ref[:, :hd] = (dkv_sum[:, :hd] * math.log(2.0)).astype(BF)
        dkv_ref[:, hd:] = dkv_sum[:, hd:].astype(BF)

    @pl.when(s == pl.num_programs(1) - 1)
    def _():
        for i in range(dq_sum.shape[0]):
            dq_ref[i * block : (i + 1) * block, :] = dq_sum[i] * hd**-0.5


def attn_bwd(tab, q, do, kv, lse, delta, groups, hd, block):
    rows, width = q.shape
    gw = groups * hd
    heads = width // gw
    steps = tab.shape[1]
    mine = pl.BlockSpec((block, gw), lambda h, s, t: (t[0, s], h))
    keys = pl.BlockSpec((block, 2 * hd), lambda h, s, t: (t[1, s], h))
    stat = pl.BlockSpec((8, block), lambda h, s, t: (h, t[0, s]))
    return pl.pallas_call(
        functools.partial(bwd_kernel, groups, hd),
        out_shape=(sds((rows, width), F32), sds(kv.shape, BF)),
        grid_spec=pltpu.PrefetchScalarGridSpec(
            num_scalar_prefetch=1,
            grid=(heads, steps),
            in_specs=[mine, mine, keys, stat, stat],
            out_specs=[pl.BlockSpec((rows, gw), lambda h, s, t: (0, h)), keys],
            scratch_shapes=[pltpu.VMEM((rows // block, block, gw), F32), pltpu.VMEM((block, 2 * hd), F32)],
        ),
        compiler_params=pltpu.CompilerParams(vmem_limit_bytes=48 << 20),
        cost_estimate=pl.CostEstimate(
            flops=heads * steps * block * block * gw * 10,
            bytes_accessed=heads * steps * block * hd * 16,
            transcendentals=heads * steps * block * block * groups,
        ),
        name="attn_bwd",
    )(tab, q, do, kv, lse, delta)


def place(w):
    k, core = w // 2, w % 2
    return 4 * k + core, 4 * k + 3 - core


def block_row(b):
    m = b % 4
    core = jnp.where((m == 1) | (m == 2), 1, 0)
    return 2 * (2 * (b // 4) + core) + jnp.where(m < 2, 0, 1)


def tables(w, chips):
    a, b = place(w)
    count = a + b + 2
    every = jnp.arange(8 * chips - 2, dtype=jnp.int32)
    s, idle = jnp.minimum(every, count - 1), every >= count
    in_a = s <= a
    key = jnp.where(in_a, s, s - a - 1)
    diag = jnp.where(in_a, s == a, s == count - 1)
    fwd = [jnp.where(in_a, 0, 1), block_row(key), jnp.where(idle, 2, diag), ~idle & (key == 0), ~idle & diag]
    both = s < 2 * (a + 1)
    even = s % 2 == 0
    key = jnp.where(both, s // 2, s - (a + 1))
    query = jnp.where(both & even, 0, 1)
    diag = key == jnp.where(query == 0, a, b)
    zero = (every >= count) & (w % 2 == 1)
    key = jnp.where(zero, b + 1, key)
    only = zero & (every == count)
    bwd = [query, block_row(key), jnp.where(idle, 2, diag), only | ~idle & (~both | even), only | ~idle & (~both | ~even)]
    return tuple(jnp.stack([row.astype(jnp.int32) for row in rows]) for rows in (fwd, bwd))


def per_device(
    wide, narrow,
    layer_input, w_query, w_key, w_value, w_output, w_gate, w_up, w_down,
    attn_gain, mlp_gain, query_gain, key_gain, out_grad,
):
    hd = query_gain.shape[0]
    rows, dim = layer_input.shape
    all_rows = narrow * rows
    chips = wide // 2
    block = all_rows // 2
    qw, kw = w_query.shape[1], w_key.shape[1]
    ff = w_gate.shape[1]
    groups = qw // kw
    kv_heads = kw // hd
    w = lax.axis_index("wide")
    fwd_tab, bwd_tab = tables(w, chips)
    def gather(shard):
        return lax.all_gather(shard, "wide", axis=0, tiled=True)

    def scatter(grad):
        return lax.psum_scatter(grad, "wide", scatter_dimension=0, tiled=True)

    t = math.gcd(ff, 256)

    spread_s = spread_sems(narrow)
    sum_s = [*sum_bufs(narrow, rows, dim), *sum_sems(narrow)]
    row_buf = pltpu.VMEM((rows, dim), BF)
    low_rows, full_rows, all_low = sds((rows, dim), BF), sds((rows, dim), F32), sds((all_rows, dim), BF)
    ring = functools.partial
    qg, kg = query_gain[None], key_gain[None]
    after = lax.optimization_barrier

    in_scratch = [*spread_s, *line_sems(chips)]
    shard = jnp.concatenate([w_query, w_key, w_value, w_output.T], axis=1)
    table = sds((all_rows, hd), F32)
    normed_all, w_attn, gu_shard, cos_table, sin_table = comm_call(
        ring(input_kernel, wide, narrow), "input_rows", 0,
        (all_low, sds((dim, shard.shape[1]), BF), sds((w_gate.shape[0], 2 * ff), BF), table, table),
        [VM, VM, HB, VM, VM], (HB, HB, VM, VM, VM), [row_buf, *in_scratch],
        layer_input, attn_gain[None], shard, w_gate, w_up,
    )
    width = qw + 2 * kw
    grad_all, kv, query_proj, key_proj, queries = comm_call(
        ring(qkv_kernel, wide, narrow, qw, kw, hd**-0.5 * math.log2(math.e)), "qkv_rows", 1,
        (all_low, sds((wide * all_rows, 2 * kw), BF), sds((all_rows, qw), F32),
         sds((all_rows, kw), F32), sds((all_rows, qw), BF)),
        [VM, HB, HB, VM, VM, VM, VM], (HB, HB, VM, VM, VM),
        [pltpu.VMEM((all_rows, 2 * kw), BF), pltpu.VMEM((dim, width), BF),
         pltpu.VMEM((all_rows, dim), BF), DMA((2,)), *in_scratch],
        out_grad, normed_all, w_attn, cos_table, sin_table, qg, kg,
    )
    gu_shard, w_down, kv = after((gu_shard, w_down, kv))
    w_gu, w_d = gather(gu_shard), gather(w_down.T)
    attended, attended_low, lse = attn_fwd(fwd_tab, queries, kv, groups, hd, block)
    w_o = w_attn[:, qw + 2 * kw :]
    middle, normed_mlp = comm_call(
        ring(middle_kernel, wide, narrow), "middle_rows", 2, (full_rows, all_low), [HB, VM, VM], (VM, HB),
        [row_buf, *sum_s, *spread_s], dg(attended_low, w_o, NT).astype(BF), layer_input, mlp_gain[None],
    )
    gate_up, hidden_low = mlp_fwd(normed_mlp, w_gu, t)
    grad_down = dg(grad_all, hidden_low, TN).astype(BF)
    w_d, _ = after((w_d, grad_down))
    middle_back, middle_low, mlp_gain_part, grad_gu = comm_call(
        ring(mlp_back_kernel, wide, narrow), "mlp_back", 6,
        (full_rows, low_rows, sds((1, dim), F32), sds((dim, 2 * ff), BF)), [HB, HB, HB, HB, HB, VM, VM, VM], (VM, VM, VM, HB),
        [pltpu.VMEM((all_rows, dim), BF), pltpu.VMEM((2, dim, t), BF), pltpu.VMEM((2, all_rows, 2 * t), F32),
         pltpu.VMEM((all_rows, 2 * ff), BF), pltpu.VMEM((dim, 2 * ff), BF), pltpu.VMEM((all_rows, dim), BF),
         pltpu.VMEM((2, 256, 2 * ff), BF), product_bufs(narrow, rows, dim), DMA((4,)), DMA((2, 2)), DMA((2,)), *sum_s],
        grad_all, w_d, gate_up, w_gu, normed_mlp, middle, mlp_gain[None], out_grad,
    )
    grad_down, grad_gu = scatter(grad_down), scatter(grad_gu)
    middle_all, down_part, back, delta = comm_call(
        ring(middle_back_kernel, wide, narrow, (width, qw), groups, hd), "middle_back", 3,
        (all_low, all_low, sds((all_rows, qw), BF), sds((8 * kv_heads, all_rows), F32)),
        [VM, HB, HB, HB, HB], (HB, HB, VM, VM),
        [pltpu.VMEM((all_rows, dim), BF), pltpu.VMEM((all_rows, dim), BF), pltpu.VMEM((all_rows, ff), BF), pltpu.VMEM((dim, ff), BF), pltpu.VMEM((dim, qw), BF), pltpu.VMEM((all_rows, qw), F32),
         DMA((4,)), DMA((narrow,)), DMA((all_rows // 256,)), *spread_s],
        middle_low, hidden_low, w_d, w_attn, attended,
    )
    query_back, dkv = attn_bwd(bwd_tab, queries, back, kv, lse, delta, groups, hd, block)
    dkv, grad_down = after((dkv, grad_down))
    layer_output, kv_sum, q_low, query_gain_part, grad_qo = comm_call(
        ring(output_kernel, wide, narrow), "output_rows", 4,
        (low_rows, sds((all_rows, 2 * kw), BF), sds((all_rows, qw), BF), sds((1, hd), F32), sds((dim, 2 * qw), BF)),
        [HB, VM, HB, HB, HB, VM, VM, VM, HB, HB, HB], (VM, VM, VM, VM, HB),
        [pltpu.VMEM((dim, 2 * qw), BF), pltpu.VMEM((all_rows, qw), F32), pltpu.VMEM((all_rows, qw), F32), pltpu.VMEM((all_rows, dim), BF),
         pltpu.VMEM((all_rows, dim), BF), pltpu.VMEM((all_rows, qw), BF), DMA((5,)), DMA((dim // 256,)), *sum_s,
         *line_sum_bufs(chips, all_rows, 2 * kw), *line_sum_sems(chips)],
        down_part, middle, dkv, query_back, query_proj, cos_table, sin_table, qg, normed_all, middle_all, attended_low,
    )
    kv_sum, grad_gu = after((kv_sum, grad_gu))
    gains = jnp.concatenate([jnp.zeros((1, dim), F32), mlp_gain_part, query_gain_part, jnp.zeros((1, hd), F32)], axis=1)
    w_rows = dim // wide
    input_grad, gain_sums, grad_qo, grad_kv = comm_call(
        ring(input_back_kernel, wide, narrow, qw, kw), "input_back", 5,
        (full_rows, sds(gains.shape, F32), sds((w_rows, 2 * qw), F32), sds((w_rows, 2 * kw), F32)),
        [VM, VM, VM, VM, HB, VM, VM, VM, VM, VM, VM, HB, HB],
        (VM, VM, VM, VM),
        [pltpu.VMEM((narrow, *gains.shape), F32), pltpu.VMEM((wide, *gains.shape), F32),
         pltpu.VMEM((all_rows, width), BF), pltpu.VMEM((all_rows, dim), BF), pltpu.VMEM((dim, 2 * kw), BF),
         pltpu.VMEM((dim, width), BF), pltpu.VMEM((all_rows, dim), BF), DMA((2,)), DMA((narrow,)), DMA((narrow,)), DMA((wide,)), DMA((wide,)), *sum_s,
         *line_sum_bufs(chips, w_rows, 2 * qw)[:4], *line_sum_sems(chips),
         *line_sum_bufs(chips, w_rows, 2 * kw)[:4], *line_sum_sems(chips)],
        layer_input, attn_gain[None], middle_back, gains, grad_qo, q_low, kv_sum, key_proj, cos_table, sin_table, kg, w_attn, normed_all,
    )
    tm = min(w_rows, 128)
    turned = lambda height: pl.BlockSpec((height, tm), lambda i: (0, i))
    grads = plain(
        finish_kernel, "finish", (w_rows // tm,),
        [by_rows(tm, 2 * ff), by_rows(tm, ff), by_rows(tm, 2 * qw), by_rows(tm, 2 * kw)],
        [by_rows(tm, ff), by_rows(tm, ff), turned(ff), by_rows(tm, qw), by_rows(tm, kw), by_rows(tm, kw), turned(qw)],
        [sds(shape, F32) for shape in (w_gate.shape, w_up.shape, w_down.shape, w_query.shape, w_key.shape, w_value.shape,
                                       w_output.shape)],
        0, 10 * dim // wide * (3 * ff + qw), grad_gu, grad_down, grad_qo, grad_kv,
    )
    grad_gate, grad_up, grad_down, grad_query, grad_key, grad_value, grad_output = grads
    g = gain_sums[0]
    return (
        layer_output, input_grad, grad_query, grad_key, grad_value, grad_output, grad_gate, grad_up, grad_down,
        g[:dim], g[dim : 2 * dim], g[2 * dim : 2 * dim + hd], g[2 * dim + hd :],
    )


def solution(mesh):
    rows = P(("wide", "narrow"), None)
    weight, turned = P("wide", "narrow"), P("narrow", "wide")
    return jax.shard_map(
        functools.partial(per_device, mesh.shape["wide"], mesh.shape["narrow"]),
        mesh=mesh,
        in_specs=(rows, weight, weight, weight, turned, weight, weight, turned, P(), P(), P(), P(), rows),
        out_specs=(rows, rows, weight, weight, weight, turned, weight, weight, turned, P(), P(), P(), P()),
        check_vma=False,
    )
```

```python
import functools
import math

import jax
import jax.numpy as jnp
from jax import lax
from jax.experimental import pallas as pl
from jax.experimental.pallas import tpu as pltpu
from jax.sharding import PartitionSpec as P

EPSILON = 1e-06
MASKED = -1e30
F32 = jnp.float32
BF = jnp.bfloat16
MESH = pl.DeviceIdType.MESH
NT = (((1,), (1,)), ((), ()))
NN = (((1,), (0,)), ((), ()))
TN = (((0,), (0,)), ((), ()))


def dg(a, b, dims):
    return lax.dot_general(a, b, dims, preferred_element_type=F32)
DMA = pltpu.SemaphoreType.DMA


class Place:
    def __init__(self, wide, narrow):
        self.W, self.N = wide, narrow
        self.C, self.half = wide // 2, narrow // 2
        self.w, self.n = lax.axis_index("wide"), lax.axis_index("narrow")
        self.k, self.c = self.w // 2, lax.rem(self.w, 2)
        late = (self.n >= self.half).astype(jnp.int32)
        self.group = lax.rem(self.c + late, 2)
        self.slot = jnp.where(self.group == 0, self.n, lax.rem(self.n + self.half, self.N))

    def owner(self, j):
        core = 1 if j >= self.half else 0
        n = jnp.where(self.c == 0, j, (j + self.half) % self.N)
        return core, n

    def owner_is_me(self, j):
        core, n = self.owner(j)
        return (self.c == core) & (self.n == n)


def enter(p, line=False, ring=False):
    barrier = pltpu.get_barrier_semaphore()

    def greet(device):
        pl.semaphore_signal(barrier, inc=1, device_id=device, device_id_type=MESH)

    for core in range(2):
        for n in range(p.N):

            @pl.when((p.c != core) | (p.n != n))
            def _():
                greet((2 * p.k + core, n))

    peers = 2 * p.N - 1
    if line or ring:
        for k in range(p.C):

            @pl.when(p.k != k)
            def _():
                greet((2 * k + p.c, p.n))
                if ring:
                    greet((2 * k + 1 - p.c, p.n))

        peers += (2 if ring else 1) * (p.C - 1)
    pl.semaphore_wait(barrier, peers)


def slot_of(p, n, group):
    return jnp.where(group == 0, n, lax.rem(n + p.half, p.N))


def neighbours(p):
    return p.n + 1 - 2 * lax.rem(p.n, 2), lax.rem(p.n + 2, 4), 3 - p.n


def to(src, dst, send, recv, wide, narrow):
    return pltpu.make_async_remote_copy(
        src_ref=src, dst_ref=dst, send_sem=send, recv_sem=recv, device_id=(wide, narrow), device_id_type=MESH
    )


def spread_sems(narrow):
    return [DMA((narrow, 2)), DMA((narrow, 2)), DMA((2,)), DMA((2,))]


def spread_start(p, src, gathered, rows, send, recv, local, onward):
    half = rows // 2
    view = lambda i: gathered.at[pl.ds(pl.multiple_of(p.slot * rows + i * half, half), half)]
    part = lambda i: src.at[pl.ds(i * half, half)]
    mine = p.group == p.c
    square = p.N == 4
    if square:
        nx, ny, _ = neighbours(p)
        targets = [(nx, (0, 1)), (ny, (1, 0))]
        order = [(t, q, i) for q in range(2) for t, halves in targets for i in (halves[q],)]
        for t, q, i in order:
            at = 0 if t is nx else 1
            to(part(i), view(i), send.at[at, i], recv.at[p.slot, i], 2 * p.k + p.group, t).start()
    else:
        for t in range(p.N):

            @pl.when(p.n != t)
            def _():
                for i in range(2):
                    to(part(i), view(i), send.at[t, i], recv.at[p.slot, i], 2 * p.k + p.group, t).start()

    @pl.when(mine)
    def _():
        for i in range(2):
            pltpu.make_async_copy(part(i), view(i), local.at[i]).start()

    @pl.when(jnp.logical_not(mine))
    def _():
        for i in range(2):
            to(part(i), view(i), local.at[i], recv.at[p.slot, i], 2 * p.k + p.group, p.n).start()


def spread_pass(p, src, gathered, rows, send, recv, local, onward):
    if p.N == 4:
        half = rows // 2
        piece = src.at[pl.ds(0, half)]
        nx, ny, _ = neighbours(p)
        for i, (n, other) in enumerate(((nx, ny), (ny, nx))):
            j = slot_of(p, n, p.c)
            here = gathered.at[pl.ds(pl.multiple_of(j * rows + i * half, half), half)]
            pltpu.make_async_copy(piece, here, recv.at[j, i]).wait()
            to(here, here, onward.at[i], recv.at[j, i], p.w, other).start()


def spread_end(p, src, gathered, rows, send, recv, local, onward, on_slot=lambda j: None):
    half = rows // 2
    piece = src.at[pl.ds(0, half)]
    mine = p.group == p.c
    at = lambda j, i: gathered.at[pl.ds(pl.multiple_of(j * rows + i * half, half), half)]

    def arrive(j, i):
        pltpu.make_async_copy(piece, at(j, i), recv.at[j, i]).wait()

    for i in range(2):
        pltpu.make_async_copy(piece, at(0, 0), local.at[i]).wait()
    here = slot_of(p, p.n, p.c)

    @pl.when(jnp.logical_not(mine))
    def _():
        arrive(here, 0)
        arrive(here, 1)

    on_slot(here)
    if p.N == 4:
        nx, ny, nd = neighbours(p)
        jx, jy, jd = (slot_of(p, n, p.c) for n in (nx, ny, nd))
        arrive(jx, 1)
        on_slot(jx)
        arrive(jy, 0)
        on_slot(jy)
        arrive(jd, 0)
        arrive(jd, 1)
        on_slot(jd)
        for i in range(2):
            pltpu.make_async_copy(piece, at(0, 0), onward.at[i]).wait()
            for t in range(2):
                pltpu.make_async_copy(piece, at(0, 0), send.at[t, i]).wait()
    else:
        for t in range(p.N):

            @pl.when(p.n != t)
            def _():
                for i in range(2):
                    pltpu.make_async_copy(piece, at(0, 0), send.at[t, i]).wait()
                    arrive(slot_of(p, t, p.c), i)
                on_slot(slot_of(p, t, p.c))


def sum_bufs(narrow, rows, dim):
    if narrow == 4:
        half = pltpu.VMEM((2, 2, rows, dim // 2), BF)
        return [half, half, pltpu.VMEM((2, rows, dim), BF)]
    return [pltpu.VMEM((narrow, rows, dim), BF)]


def sum_sems(narrow):
    if narrow == 4:
        return [DMA((2, 2)), DMA((2, 2)), DMA((2, 2)), DMA((4,)), DMA((4,))]
    return [DMA((narrow,)), DMA((narrow,)), DMA]


def pieces(p, part, rows, dim):
    half = dim // 2
    return lambda j, i: part.at[pl.ds(pl.multiple_of(j * rows, rows), rows), pl.ds(i * half, half)]


def sum_start(p, part, rows, dim, bufs, sems):
    if p.N != 4:
        (got,), (send, recv, local) = bufs, sems
        for j in range(p.N):
            core, n = p.owner(j)
            mine = p.owner_is_me(j)
            src = part.at[pl.ds(j * rows, rows)]

            @pl.when(mine)
            def _():
                pltpu.make_async_copy(src, got.at[p.n], local).start()

            @pl.when(jnp.logical_not(mine))
            def _():
                to(src, got.at[p.n], send.at[j], recv.at[p.n], 2 * p.k + core, n).start()

        return
    own, inbox, _ = bufs
    load, send, recv, _, _ = sems
    piece = pieces(p, part, rows, dim)
    nx, ny, nd = neighbours(p)
    across, here = slot_of(p, nd, p.c), slot_of(p, p.n, p.c)
    for i, n in enumerate((nx, ny)):
        to(piece(across, i), inbox.at[i, 0], send.at[i, 0], recv.at[i, 0], p.w, n).start()
    for i, n in enumerate((ny, nx)):
        pltpu.make_async_copy(piece(slot_of(p, n, p.c), i), own.at[i, 0], load.at[i, 0]).start()
    for i, n in enumerate((nx, ny)):
        to(piece(slot_of(p, n, p.c), i), inbox.at[i, 1], send.at[i, 1], recv.at[i, 1], p.w, n).start()
        pltpu.make_async_copy(piece(here, i), own.at[i, 1], load.at[i, 1]).start()


def product_bufs(narrow, rows, dim):
    shape = (4, rows, dim // 2) if narrow == 4 else (narrow * rows, dim)
    return pltpu.VMEM(shape, BF)


def sum_start_of(p, product, out, rows, dim, bufs, sems):
    half = dim // 2
    if p.N != 4:

        def one(j, carry):
            for i in range(2):
                out[pl.ds(pl.multiple_of(j * rows, rows), rows), i * half : (i + 1) * half] = product(j, i)
            return carry

        lax.fori_loop(0, p.N, one, 0)
        sum_start(p, out, rows, dim, bufs, sems)
        return
    own, inbox, _ = bufs
    _, send, recv, _, _ = sems
    nx, ny, nd = neighbours(p)
    across, jx, jy, here = (slot_of(p, n, p.c) for n in (nd, nx, ny, p.n))

    def one(t, carry):
        i = lax.rem(t, 2)
        q = lax.rem(t // 2, 2)
        beside = jnp.where(i == 0, jx, jy)
        other = jnp.where(i == 0, jy, jx)
        j = jnp.where(t < 4, jnp.where(q == 0, across, beside), jnp.where(q == 0, other, here))
        y = product(j, i)

        @pl.when(t < 4)
        def _():
            out[t] = y
            to(out.at[t], inbox.at[i, q], send.at[i, q], recv.at[i, q], p.w, jnp.where(i == 0, nx, ny)).start()

        @pl.when(t >= 4)
        def _():
            own[i, q] = y

        return carry

    lax.fori_loop(0, 8, one, 0)


def core_of(p, j):
    return (j >= p.half).astype(jnp.int32)


def sum_pass(p, part, rows, dim, bufs, sems, loaded=False):
    if p.N != 4:
        return
    own, inbox, box = bufs
    load, send, recv, send2, recv2 = sems
    piece = lambda j, i: own.at[0, 0]
    half = dim // 2
    nx, ny, _ = neighbours(p)
    cols = lambda i: pl.ds(i * half, half)

    def add(i, q):
        if not loaded:
            pltpu.make_async_copy(piece(0, 0), own.at[i, q], load.at[i, q]).wait()
        pltpu.make_async_copy(piece(0, 0), inbox.at[i, q], recv.at[i, q]).wait()

        def body(at):
            own[i, q, at, :] = (own[i, q, at, :].astype(F32) + inbox[i, q, at, :].astype(F32)).astype(BF)

        row_loop(rows, 64, body)

    for i, n in enumerate((ny, nx)):
        add(i, 0)
        j = slot_of(p, n, p.c)
        to(own.at[i, 0], box.at[1, :, cols(i)], send2.at[i], recv2.at[i], 2 * p.k + core_of(p, j), n).start()
    j = slot_of(p, p.n, p.c)
    keep = core_of(p, j) == p.c
    for i in range(2):
        add(i, 1)

        @pl.when(keep)
        def _():
            pltpu.make_async_copy(own.at[i, 1], box.at[0, :, cols(i)], send2.at[2 + i]).start()

        @pl.when(jnp.logical_not(keep))
        def _():
            to(own.at[i, 1], box.at[0, :, cols(i)], send2.at[2 + i], recv2.at[2 + i], 2 * p.k + core_of(p, j), p.n).start()


def sum_end(p, part, rows, dim, bufs, sems):
    if p.N != 4:
        (got,), (send, recv, local) = bufs, sems
        for t in range(p.N):
            mine = (p.group == p.c) & (p.n == t)

            @pl.when(mine)
            def _():
                pltpu.make_async_copy(part.at[pl.ds(0, rows)], got.at[t], local).wait()

            @pl.when(jnp.logical_not(mine))
            def _():
                pltpu.make_async_copy(part.at[pl.ds(0, rows)], got.at[t], recv.at[t]).wait()

        for j in range(p.N):

            @pl.when(jnp.logical_not(p.owner_is_me(j)))
            def _():
                pltpu.make_async_copy(part.at[pl.ds(j * rows, rows)], got.at[0], send.at[j]).wait()

        return
    own, inbox, box = bufs
    load, send, recv, send2, recv2 = sems
    piece = lambda j, i: own.at[0, 0]
    half = dim // 2
    cols = lambda i: pl.ds(i * half, half)
    for i in range(2):
        for q in range(2):
            pltpu.make_async_copy(piece(0, 0), inbox.at[i, q], send.at[i, q]).wait()
        pltpu.make_async_copy(own.at[i, 0], box.at[1, :, cols(i)], send2.at[i]).wait()
        pltpu.make_async_copy(own.at[i, 0], box.at[1, :, cols(i)], recv2.at[i]).wait()
        pltpu.make_async_copy(own.at[i, 1], box.at[0, :, cols(i)], send2.at[2 + i]).wait()

        @pl.when(p.group != p.c)
        def _():
            pltpu.make_async_copy(own.at[i, 1], box.at[0, :, cols(i)], recv2.at[2 + i]).wait()


def total(p, bufs, at):
    if p.N == 4:
        box = bufs[2]
        return box[0, at, :].astype(F32) + box[1, at, :].astype(F32)
    got = bufs[0]
    out = got[0, at, :].astype(F32)
    for t in range(1, p.N):
        out = out + got[t, at, :].astype(F32)
    return out


PARTS = 4


def line_sems(chips):
    return [DMA((2, chips, PARTS)), DMA((chips, PARTS)), DMA((chips, PARTS)), DMA((chips, PARTS)), DMA((PARTS,))]


def line_parts(p, full, rows):
    size = rows // PARTS

    def at(s, core, q=None):
        first = (2 * s + core) * rows
        if q is None:
            return full.at[pl.ds(pl.multiple_of(first, rows), rows)]
        return full.at[pl.ds(pl.multiple_of(first + q * size, size), size)]

    return at


def each_part(body):
    def one(q, carry):
        body(q)
        return carry

    lax.fori_loop(0, PARTS, one, 0)


def line_copy(p, src, dst, send, recv, k, core):
    return pltpu.make_async_remote_copy(
        src_ref=src, dst_ref=dst, send_sem=send, recv_sem=recv, device_id=(2 * k + core, p.n), device_id_type=MESH
    )


def inside(p, k):
    return (k >= 0) & (k < p.C)


BOTH, UP, DOWN = ((0, 1), (1, -1)), ((0, 1),), ((1, -1),)


def line_push(p, src, full, rows, zsend, zrecv, csend, crecv, local, q, ways=BOTH):
    size = rows // PARTS
    part = src.at[pl.ds(pl.multiple_of(q * size, size), size)]
    there = line_parts(p, full, rows)(p.k, p.c, q)
    for i, sign in ways:

        @pl.when(inside(p, p.k + sign))
        def _():
            line_copy(p, part, there, zsend.at[i, 0, q], zrecv.at[p.k, q], p.k + sign, p.c).start()

    line_copy(p, part, there, csend.at[p.k, q], crecv.at[p.k, q], p.k, 1 - p.c).start()
    pltpu.make_async_copy(part, there, local.at[q]).start()


def came(p, s, ways):
    if ways == BOTH:
        return s == s
    return s <= p.k if ways == UP else s >= p.k


def line_steps(p, src, full, rows, zsend, zrecv, csend, crecv, local, ways=BOTH):
    at = line_parts(p, full, rows)
    piece = src.at[pl.ds(0, rows // PARTS)]

    def at_distance(d):
        def onward(q):
            for i, sign in ways:
                s, t = p.k - sign * d, p.k + sign

                @pl.when(inside(p, s))
                def _():
                    here = at(s, p.c, q)
                    pltpu.make_async_copy(piece, here, zrecv.at[s, q]).wait()

                    @pl.when(inside(p, t))
                    def _():
                        line_copy(p, here, here, zsend.at[i, d, q], zrecv.at[s, q], t, p.c).start()

                    line_copy(p, here, here, csend.at[s, q], crecv.at[s, q], p.k, 1 - p.c).start()

        each_part(onward)

    def settle(q):
        here = at(p.k, p.c, q)
        pltpu.make_async_copy(piece, here, local.at[q]).wait()
        for s in range(p.C):

            @pl.when(came(p, jnp.int32(s), ways))
            def _():
                pltpu.make_async_copy(piece, here, csend.at[s, q]).wait()
                pltpu.make_async_copy(piece, at(s, 1 - p.c, q), crecv.at[s, q]).wait()

        for i, sign in ways:
            for d in range(p.C):

                @pl.when(inside(p, p.k - sign * d) & inside(p, p.k + sign))
                def _():
                    pltpu.make_async_copy(piece, here, zsend.at[i, d, q]).wait()

    return [functools.partial(at_distance, d) for d in range(1, p.C)] + [lambda: each_part(settle)]


def line_sum_bufs(chips, rows, width):
    return [pltpu.VMEM((chips, rows, width), BF)] * 3 + [pltpu.VMEM((2, rows, width), BF), pltpu.VMEM((rows, width), F32)]


def line_sum_sems(chips):
    return [
        DMA((chips, PARTS)), DMA((chips, PARTS)), DMA((chips, PARTS)), DMA((2, chips, PARTS)), DMA((chips, PARTS)),
        DMA((2, PARTS)),
    ]


OTHER = {BOTH: BOTH, UP: DOWN, DOWN: UP}


def line_sum_start(p, part, rows, bufs, sems, ways=BOTH):
    own, inbox, _, _, _ = bufs
    load, csend, crecv, _, _, _ = sems
    at = line_parts(p, part, rows)
    size = rows // PARTS

    def share(s):
        def one(q):
            here = pl.ds(pl.multiple_of(q * size, size), size)
            line_copy(p, at(s, 1 - p.c, q), inbox.at[s, here], csend.at[s, q], crecv.at[s, q], p.k, 1 - p.c).start()
            pltpu.make_async_copy(at(s, p.c, q), own.at[s, here], load.at[s, q]).start()

        each_part(one)

    for d in range(p.C - 1, 0, -1):
        for _, sign in ways:
            s = p.k + sign * d

            @pl.when(inside(p, s))
            def _():
                share(s)

    share(p.k)


def line_sum_steps(p, part, rows, bufs, sems, ways=BOTH):
    own, inbox, relay, box, acc = bufs
    load, csend, crecv, zsend, rrecv, zrecv = sems
    size = rows // PARTS
    step = math.gcd(size, 128)
    piece = line_parts(p, part, rows)(0, 0, 0)

    def rows_of(q):
        return pl.ds(pl.multiple_of(q * size, size), size)

    def add(q, body):
        def one(j, carry):
            body(pl.ds(pl.multiple_of(q * size + j * step, step), step))
            return carry

        lax.fori_loop(0, size // step, one, 0)

    def pair(t, q):
        pltpu.make_async_copy(piece, own.at[t, rows_of(q)], load.at[t, q]).wait()
        pltpu.make_async_copy(piece, inbox.at[t, rows_of(q)], crecv.at[t, q]).wait()

    def at_distance(d):
        def onward(q):
            here = rows_of(q)
            for i, sign in ways:
                t = p.k + sign * d
                behind = inside(p, p.k - sign)

                @pl.when(inside(p, t))
                def _():
                    pair(t, q)

                    @pl.when(jnp.logical_not(behind))
                    def _():
                        def two(at):
                            own[t, at, :] = (own[t, at, :].astype(F32) + inbox[t, at, :].astype(F32)).astype(BF)

                        add(q, two)

                    @pl.when(behind)
                    def _():
                        pltpu.make_async_copy(piece, relay.at[t, here], rrecv.at[t, q]).wait()

                        def three(at):
                            both = own[t, at, :].astype(F32) + inbox[t, at, :].astype(F32)
                            own[t, at, :] = (both + relay[t, at, :].astype(F32)).astype(BF)

                        add(q, three)

                    src = own.at[t, here]
                    if d >= 2:
                        line_copy(p, src, relay.at[t, here], zsend.at[i, d, q], rrecv.at[t, q], p.k + sign, p.c).start()
                    else:
                        line_copy(p, src, box.at[i, here], zsend.at[i, d, q], zrecv.at[i, q], t, p.c).start()

        each_part(onward)

    def last(q):
        here = rows_of(q)
        pair(p.k, q)

        def first(at):
            acc[at, :] = own[p.k, at, :].astype(F32) + inbox[p.k, at, :].astype(F32)

        add(q, first)
        for i, sign in ways:

            @pl.when(inside(p, p.k - sign))
            def _():
                pltpu.make_async_copy(piece, box.at[i, here], zrecv.at[i, q]).wait()

                def more(at):
                    acc[at, :] += box[i, at, :].astype(F32)

                add(q, more)

            for d in range(1, p.C):

                @pl.when(inside(p, p.k + sign * d))
                def _():
                    pltpu.make_async_copy(piece, own.at[0, here], zsend.at[i, d, q]).wait()

        for s in range(p.C):

            @pl.when(came(p, jnp.int32(s), OTHER[ways]))
            def _():
                pltpu.make_async_copy(piece, inbox.at[s, here], csend.at[s, q]).wait()


    return [functools.partial(at_distance, d) for d in range(p.C - 1, 0, -1)] + [lambda: each_part(last)]


def row_loop(rows, step, body):
    def one(i, carry):
        body(pl.ds(pl.multiple_of(i * step, step), step))
        return carry

    lax.fori_loop(0, rows // step, one, 0)


STEP = 64


def inv_rms(u):
    return lax.rsqrt(jnp.mean(u * u, axis=-1, keepdims=True) + EPSILON)


def weave(gate_ref, up_ref, both_ref):
    ff = gate_ref.shape[1]
    t = math.gcd(ff, 256)
    for i in range(0, ff, t):
        both_ref[:, 2 * i : 2 * i + t] = gate_ref[:, i : i + t]
        both_ref[:, 2 * i + t : 2 * i + 2 * t] = up_ref[:, i : i + t]


def finish_kernel(both_ref, down_ref, qo_ref, kv_ref, gate_out, up_out, down_out, q_out, k_out, v_out, o_out):
    ff = gate_out.shape[1]
    t = math.gcd(ff, 256)
    for i in range(0, ff, t):
        gate_out[:, i : i + t] = both_ref[:, 2 * i : 2 * i + t].astype(F32)
        up_out[:, i : i + t] = both_ref[:, 2 * i + t : 2 * i + 2 * t].astype(F32)
    down_out[...] = jnp.transpose(down_ref[...].astype(F32))
    qw, kw = q_out.shape[1], k_out.shape[1]
    q_out[...] = qo_ref[:, :qw]
    o_out[...] = jnp.transpose(qo_ref[:, qw:])
    k_out[...] = kv_ref[:, :kw]
    v_out[...] = kv_ref[:, kw:]


def rotation(p, cos_ref, sin_ref):
    all_rows, hd = cos_ref.shape
    block, half, step = all_rows // 2, hd // 2, 64
    lane = lax.broadcasted_iota(jnp.int32, (step, hd), 1)
    column = jnp.where(lane < half, lane, lane - half).astype(F32)
    inverse = jnp.exp(column * (-2.0 * math.log(1000000.0) / hd))
    row = lax.broadcasted_iota(jnp.int32, (step, hd), 0)

    def body(i, carry):
        at = i * step
        first = jnp.where(at < block, (4 * p.k + p.c) * block + at, (4 * p.k + 3 - p.c) * block + at - block)
        angles = (first + row).astype(F32) * inverse
        here = pl.ds(pl.multiple_of(at, step), step)
        cos_ref[here, :] = jnp.cos(angles)
        sine = jnp.sin(angles)
        sin_ref[here, :] = jnp.where(lane < half, -sine, sine)
        return carry

    lax.fori_loop(0, all_rows // step, body, 0)


def input_kernel(
    wide, narrow, x_ref, gain_ref, wq_ref, wk_ref, wv_ref, wo_ref, gate_ref, up_ref, down_ref,
    gathered, full, gu_ref, d_ref, cos_ref, sin_ref, buf, shard, *sems
):
    p = Place(wide, narrow)
    rows = x_ref.shape[0]
    lo = 0
    for w_ref in (wq_ref, wk_ref, wv_ref):
        shard[:, lo : lo + w_ref.shape[1]] = w_ref[...]
        lo += w_ref.shape[1]
    shard[:, lo:] = jnp.transpose(wo_ref[...])
    spread, line = sems[:4], (shard, full, shard.shape[0], *sems[4:])
    enter(p, line=True)
    each_part(lambda q: line_push(p, *line, q))
    *steps, end = line_steps(p, *line)

    def body(at):
        u = x_ref[at, :].astype(F32)
        buf[at, :] = (u * inv_rms(u) * gain_ref[...]).astype(BF)

    row_loop(rows, STEP, body)
    spread_start(p, buf, gathered, rows, *spread)
    weave(gate_ref, up_ref, gu_ref)
    d_ref[...] = jnp.transpose(down_ref[...])
    steps[0]()
    rotation(p, cos_ref, sin_ref)
    spread_pass(p, buf, gathered, rows, *spread)
    for step in steps[1:]:
        step()
    spread_end(p, buf, gathered, rows, *spread)
    end()


def turn(u):
    return pltpu.roll(u, u.shape[-1] // 2, 1)


def qkv_kernel(
    wide, narrow, qw, kw, fold, g_ref, x_ref, w_ref, cos_ref, sin_ref, qg_ref, kg_ref,
    gathered, full, qproj_ref, kproj_ref, q_ref, kv_ref, w_buf, x_buf, load, *sems,
):
    p = Place(wide, narrow)
    rows = g_ref.shape[0]
    hd = cos_ref.shape[1]
    all_rows = x_ref.shape[0]
    size = all_rows // 4
    spread, line = sems[:4], (kv_ref, full, all_rows, *sems[4:])
    weights = pltpu.make_async_copy(w_ref.at[:, pl.ds(0, w_buf.shape[1])], w_buf, load.at[0])
    normed = pltpu.make_async_copy(x_ref, x_buf, load.at[1])
    normed.start()
    weights.start()
    enter(p, line=True)

    def project(q):
        at = pl.ds(pl.multiple_of(q * size, size), size)
        y = dg(x_buf[at, :], w_buf[...], NN)
        cos, sin = cos_ref[at, :], sin_ref[at, :]
        qproj_ref[at, :] = y[:, :qw]
        kproj_ref[at, :] = y[:, qw : qw + kw]

        def head(lo, gain):
            u = y[:, lo : lo + hd]
            v = u * inv_rms(u) * gain
            return v * cos + turn(v) * sin

        for h in range(kw // hd):
            kv_ref[at, 2 * h * hd : (2 * h + 1) * hd] = head(qw + h * hd, kg_ref[...]).astype(BF)
            kv_ref[at, (2 * h + 1) * hd : (2 * h + 2) * hd] = y[:, qw + kw + h * hd : qw + kw + (h + 1) * hd].astype(BF)
        for i in range(PARTS // 4):
            line_push(p, *line, q * (PARTS // 4) + i, ways=UP)
        for h in range(qw // hd):
            q_ref[at, h * hd : (h + 1) * hd] = (head(h * hd, qg_ref[...]) * fold).astype(BF)

    normed.wait()
    weights.wait()

    def one(q, carry):
        project(q)
        return carry

    lax.fori_loop(0, 4, one, 0)
    spread_start(p, g_ref, gathered, rows, *spread)
    *steps, end = line_steps(p, *line, ways=UP)
    steps[0]()
    spread_pass(p, g_ref, gathered, rows, *spread)
    for step in steps[1:]:
        step()
    spread_end(p, g_ref, gathered, rows, *spread)
    end()


def middle_kernel(wide, narrow, part, own_ref, gain_ref, mid_ref, gathered, buf, *refs):
    p = Place(wide, narrow)
    rows, dim = own_ref.shape
    bufs, sems, spread = split_refs(narrow, refs)
    enter(p)
    sum_start(p, part, rows, dim, bufs, sems)
    sum_pass(p, part, rows, dim, bufs, sems)
    sum_end(p, part, rows, dim, bufs, sems)

    def body(at):
        u = own_ref[at, :].astype(F32) + total(p, bufs, at)
        mid_ref[at, :] = u
        buf[at, :] = (u * inv_rms(u) * gain_ref[...]).astype(BF)

    row_loop(rows, STEP, body)
    spread_start(p, buf, gathered, rows, *spread)
    spread_pass(p, buf, gathered, rows, *spread)
    spread_end(p, buf, gathered, rows, *spread)


def split_refs(narrow, refs):
    bufs, sems = (3, 5) if narrow == 4 else (1, 3)
    return refs[:bufs], refs[bufs : bufs + sems], refs[bufs + sems :]


def norm_back(u, gain, cot):
    r = inv_rms(u)
    a = cot * gain
    du = r * a - u * (r * r * r) * jnp.mean(a * u, axis=-1, keepdims=True)
    return du, jnp.sum(cot * u * r, axis=0, keepdims=True)


def mlp_back_kernel(
    wide, narrow, g_ref, wd_ref, gu_ref, w_ref, x_ref, mid_ref, gain_ref, grad_ref, back_ref, rows_ref, dgain_ref, wgrad,
    g_buf, wd_buf, gu_buf, low, w_buf, x_buf, mid_buf, grad_buf, stage, out, load, tiles_in, store, *refs
):
    p = Place(wide, narrow)
    rows, dim = mid_ref.shape
    half = dim // 2
    t = wd_buf.shape[2]
    bufs, sems, _ = split_refs(narrow, refs)

    def tile_of(i):
        slot = lax.rem(i, 2)
        return (
            pltpu.make_async_copy(wd_ref.at[:, pl.ds(pl.multiple_of(i * t, t), t)], wd_buf.at[slot], tiles_in.at[0, slot]),
            pltpu.make_async_copy(gu_ref.at[:, pl.ds(pl.multiple_of(2 * i * t, t), 2 * t)], gu_buf.at[slot], tiles_in.at[1, slot]),
        )

    loads = [pltpu.make_async_copy(g_ref, g_buf, load.at[0])]
    for i in range(2):
        at = pl.ds(i * half, half)
        loads.append(pltpu.make_async_copy(w_ref.at[at], w_buf.at[at], load.at[1 + i]))
    loads.append(pltpu.make_async_copy(x_ref, x_buf, load.at[3]))
    loads.append(pltpu.make_async_copy(mid_ref, mid_buf, load.at[4]))
    loads.append(pltpu.make_async_copy(grad_ref, grad_buf, load.at[5]))
    loads[0].start()
    for copy in tile_of(0):
        copy.start()
    enter(p)
    loads[0].wait()
    count = wd_ref.shape[1] // t

    def gates(i, carry):
        @pl.when(i + 1 < count)
        def _():
            for copy in tile_of(i + 1):
                copy.start()

        for copy in tile_of(i):
            copy.wait()

        @pl.when(i == 0)
        def _():
            for copy in loads[1:3]:
                copy.start()

        slot = lax.rem(i, 2)
        hb = dg(g_buf[...], wd_buf[slot], NN)
        at = pl.multiple_of(2 * i * t, t)
        low[:, pl.ds(at, t)] = (hb * gu_buf[slot, :, :t]).astype(BF)
        low[:, pl.ds(pl.multiple_of(at + t, t), t)] = (hb * gu_buf[slot, :, t:]).astype(BF)
        return carry

    lax.fori_loop(0, count, gates, 0)
    for copy in loads[3:]:
        copy.start()
    for copy in loads[1:3]:
        copy.wait()

    def product(j, i):
        a = low[pl.ds(pl.multiple_of(j * rows, rows), rows), :]
        return dg(a, w_buf[pl.ds(pl.multiple_of(i * half, half), half), :], NT).astype(BF)

    sum_start_of(p, product, out, rows, dim, bufs, sems)
    dgain_ref[...] = jnp.zeros_like(dgain_ref)
    loads[3].wait()
    tile = 256

    def write(i):
        return pltpu.make_async_copy(
            stage.at[lax.rem(i, 2)], wgrad.at[pl.ds(pl.multiple_of(i * tile, tile), tile)], store.at[lax.rem(i, 2)]
        )

    def grads(first, last):
        def one(i, carry):
            @pl.when(i >= 2)
            def _():
                write(i - 2).wait()

            stage[lax.rem(i, 2)] = dg(x_buf[:, pl.ds(pl.multiple_of(i * tile, tile), tile)], low[...], TN).astype(BF)
            write(i).start()
            return carry

        lax.fori_loop(first, last, one, 0)

    tiles = dim // tile
    early = 3
    grads(0, early)
    sum_pass(p, out, rows, dim, bufs, sems, loaded=narrow == 4)
    grads(early, tiles)
    sum_end(p, out, rows, dim, bufs, sems)
    for copy in loads[4:]:
        copy.wait()

    def body(at):
        du, dgain = norm_back(mid_buf[at, :], gain_ref[...], total(p, bufs, at))
        back = grad_buf[at, :].astype(F32) + du
        back_ref[at, :] = back
        rows_ref[at, :] = back.astype(BF)
        dgain_ref[...] += dgain

    row_loop(rows, STEP, body)
    write(tiles - 2).wait()
    write(tiles - 1).wait()


def middle_back_kernel(
    wide, narrow, wo_at, groups, hd, rows_ref, hidden, w_ref, wo_ref, o_ref, all_ref, next_ref, back_ref, delta_ref,
    gathered, next_buf, h_buf, w_buf, wo_buf, o_buf, load, store, next_store, *spread
):
    p = Place(wide, narrow)
    rows = rows_ref.shape[0]
    pairs = ((hidden, h_buf), (w_ref, w_buf), (wo_ref.at[:, pl.ds(*wo_at)], wo_buf), (o_ref, o_buf))
    loads = [pltpu.make_async_copy(src, dst, load.at[i]) for i, (src, dst) in enumerate(pairs)]
    enter(p)
    spread_start(p, rows_ref, gathered, rows, *spread)
    for copy in loads:
        copy.start()
    for copy in loads[:2]:
        copy.wait()

    def write_next(i):
        at = pl.ds(pl.multiple_of(i * 256, 256), 256)
        return pltpu.make_async_copy(next_buf.at[at], next_ref.at[at], next_store.at[i])

    def write_slot(j):
        at = pl.ds(pl.multiple_of(j * rows, rows), rows)
        return pltpu.make_async_copy(gathered.at[at], all_ref.at[at], store.at[j])

    def downs(first, last):
        def one(i, carry):
            at = pl.ds(pl.multiple_of(i * 256, 256), 256)
            next_buf[at, :] = dg(h_buf[at, :], w_buf[...], NT).astype(BF)
            write_next(i).start()
            return carry

        lax.fori_loop(first, last, one, 0)

    blocks = next_buf.shape[0] // 256
    downs(0, blocks // 2)

    def on_slot(j):
        at = pl.ds(pl.multiple_of(j * rows, rows), rows)
        write_slot(j).start()
        back = dg(gathered[at, :], wo_buf[...], NN).astype(BF)
        back_ref[at, :] = back
        lane = lax.broadcasted_iota(jnp.int32, (rows, hd), 1)
        out = jnp.zeros((rows, hd), F32)
        for h in range(back.shape[1] // hd):
            mine = slice(h * hd, (h + 1) * hd)
            row = 8 * (h // groups) + h % groups
            delta = jnp.sum(back[:, mine].astype(F32) * o_buf[at, mine], axis=1, keepdims=True)
            out = jnp.where(lane == row, delta, out)
        delta_ref[:, at] = jnp.transpose(out)[: delta_ref.shape[0]]

    spread_pass(p, rows_ref, gathered, rows, *spread)
    downs(blocks // 2, blocks)
    for copy in loads[2:]:
        copy.wait()
    spread_end(p, rows_ref, gathered, rows, *spread, on_slot=on_slot)
    for i in range(blocks):
        write_next(i).wait()
    for j in range(p.N):
        write_slot(j).wait()


def share_start(me, count, here, slots, sends, recvs, device):
    slots[me] = here[...]
    for t in range(count):

        @pl.when(me != t)
        def _():
            wide_at, narrow_at = device(t)
            to(here, slots.at[me], sends.at[t], recvs.at[me], wide_at, narrow_at).start()


def share_end(me, count, here, slots, sends, recvs):
    for t in range(count):

        @pl.when(me != t)
        def _():
            pltpu.make_async_copy(here, slots.at[t], sends.at[t]).wait()
            pltpu.make_async_copy(here, slots.at[t], recvs.at[t]).wait()

    out = slots[0]
    for t in range(1, count):
        out = out + slots[t]
    here[...] = out


def head_back(cot, u, gain, cos, sin):
    cot = cot * cos - turn(cot) * sin
    return norm_back(u, gain, cot)


def output_kernel(
    wide, narrow, part, mid_ref, dkv, dq, qproj, cos_ref, sin_ref, g_ref, x_ref, m_ref, a_ref,
    out_ref, kv_ref, low_ref, dgain_ref, wgrad_out, wgrad_ref, dq_buf, u_buf, x_buf, m_buf, a_buf, load, store, *refs
):
    p = Place(wide, narrow)
    rows, dim = mid_ref.shape
    kv_rows = kv_ref.shape[0]
    width = low_ref.shape[1]
    hd = cos_ref.shape[1]
    bufs, sems, line = split_refs(narrow, refs)
    sums = (part, rows, dim, bufs, sems)
    chain = (p, dkv, kv_rows, line[:5], line[5:])
    pairs = ((dq, dq_buf), (qproj, u_buf), (x_ref, x_buf), (m_ref, m_buf), (a_ref, a_buf))
    loads = [pltpu.make_async_copy(src, dst, load.at[i]) for i, (src, dst) in enumerate(pairs)]
    enter(p, line=True)
    line_sum_start(*chain, ways=DOWN)
    sum_start(p, *sums)
    for copy in loads:
        copy.start()
    first, *steps, last = line_sum_steps(*chain, ways=DOWN)
    first()
    dgain_ref[...] = jnp.zeros_like(dgain_ref)
    for copy in loads[:2]:
        copy.wait()

    def through_heads(at):
        for h in range(width // hd):
            mine = slice(h * hd, (h + 1) * hd)
            du, dgain = head_back(dq_buf[at, mine], u_buf[at, mine], g_ref[...], cos_ref[at, :], sin_ref[at, :])
            low_ref[at, mine] = du.astype(BF)
            dgain_ref[...] += dgain

    row_loop(low_ref.shape[0], 128, through_heads)
    for copy in loads[2:]:
        copy.wait()

    def write(i):
        at = pl.ds(pl.multiple_of(i * 256, 256), 256)
        return pltpu.make_async_copy(wgrad_ref.at[at], wgrad_out.at[at], store.at[i])

    def grads(first_tile, last_tile):
        def one(i, carry):
            at = pl.ds(pl.multiple_of(i * 256, 256), 256)
            wgrad_ref[at, :width] = dg(x_buf[:, at], low_ref[...], TN).astype(BF)
            wgrad_ref[at, width:] = dg(m_buf[:, at], a_buf[...], TN).astype(BF)
            write(i).start()
            return carry

        lax.fori_loop(first_tile, last_tile, one, 0)

    tiles = dim // 256
    grads(0, tiles // 2)
    sum_pass(p, *sums)
    steps[0]()
    grads(tiles // 2, tiles)
    sum_end(p, *sums)

    def body(at):
        out_ref[at, :] = (mid_ref[at, :] + total(p, bufs, at)).astype(BF)

    row_loop(rows, STEP, body)
    for step in steps[1:]:
        step()
    last()
    row_loop(kv_rows, 128, lambda at: kv_ref.__setitem__((at, slice(None)), line[4][at, :].astype(BF)))
    for i in range(tiles):
        write(i).wait()


def input_back_kernel(
    wide, narrow, qw, kw, own_ref, gain_ref, back_ref, gains_ref, wgrad, q_ref, kv_ref, proj_ref, cos_ref, sin_ref, kg_ref,
    w_ref, x_ref, out_ref, gsum_ref, wsum_ref, kvsum_ref,
    gbuf, gbuf2, low, part, kvgrad, w_buf, x_buf, own_buf, back_buf, load, gsend, grecv, gsend2, grecv2, *refs,
):
    p = Place(wide, narrow)
    rows, dim = own_ref.shape
    hd = cos_ref.shape[1]
    all_rows = x_ref.shape[0]
    w_rows = wsum_ref.shape[0]
    bufs, sems, line = split_refs(narrow, refs)
    sums = (part, rows, dim, bufs, sems)
    first_line = (p, wgrad, w_rows, (*line[:4], wsum_ref), line[4:10])
    second_line = (p, kvgrad, w_rows, (*line[10:14], kvsum_ref), line[14:])
    weights = pltpu.make_async_copy(w_ref.at[:, pl.ds(0, w_buf.shape[1])], w_buf, load.at[0])
    weights.start()
    normed = pltpu.make_async_copy(x_ref, x_buf, load.at[1])
    normed.start()
    later = [pltpu.make_async_copy(own_ref, own_buf, load.at[2]), pltpu.make_async_copy(back_ref, back_buf, load.at[3])]
    for copy in later:
        copy.start()
    enter(p, ring=True)
    line_sum_start(*first_line)
    gsum_ref[...] = gains_ref[...]
    size = min(all_rows, 256)
    first = line_sum_steps(*first_line)
    first[0]()
    weights.wait()

    def through_heads(at):
        low[at, :qw] = q_ref[at, :]
        for h in range(kw // hd):
            key = slice(2 * h * hd, (2 * h + 1) * hd)
            value = slice((2 * h + 1) * hd, (2 * h + 2) * hd)
            mine = slice(qw + h * hd, qw + (h + 1) * hd)
            du, dgain = head_back(
                kv_ref[at, key].astype(F32), proj_ref[at, h * hd : (h + 1) * hd], kg_ref[...], cos_ref[at, :], sin_ref[at, :]
            )
            low[at, mine] = du.astype(BF)
            low[at, qw + kw + h * hd : qw + kw + (h + 1) * hd] = kv_ref[at, value]
            gsum_ref[:, 2 * dim + hd :] += dgain
        part[at, :] = dg(low[at, :], w_buf[...], NT).astype(BF)

    row_loop(all_rows, size, through_heads)
    sum_start(p, *sums)
    first[1]()

    normed.wait()

    def key_grads(at):
        kvgrad[at, :] = dg(x_buf[:, at], low[:, qw:], TN).astype(BF)

    row_loop(dim, 256, key_grads)
    line_sum_start(*second_line)
    second = line_sum_steps(*second_line)
    second[0]()
    for step in first[2:-1]:
        step()
    sum_pass(p, *sums)
    for step in second[1:-1]:
        step()
    sum_end(p, *sums)
    for copy in later:
        copy.wait()

    def body(at):
        du, dgain = norm_back(own_buf[at, :].astype(F32), gain_ref[...], total(p, bufs, at))
        out_ref[at, :] = back_buf[at, :] + du
        gsum_ref[:, :dim] += dgain

    row_loop(rows, STEP, body)

    share_start(p.n, narrow, gsum_ref, gbuf, gsend, grecv, lambda t: (p.w, t))
    first[-1]()
    share_end(p.n, narrow, gsum_ref, gbuf, gsend, grecv)
    share_start(p.w, wide, gsum_ref, gbuf2, gsend2, grecv2, lambda t: (t, p.n))
    second[-1]()
    share_end(p.w, wide, gsum_ref, gbuf2, gsend2, grecv2)


VM = pl.BlockSpec(memory_space=pltpu.VMEM)


HB = pl.BlockSpec(memory_space=pl.ANY)


def comm_call(kernel, name, cid, out_shape, in_specs, out_specs, scratch, *args):
    return pl.pallas_call(
        kernel,
        out_shape=out_shape,
        in_specs=in_specs,
        out_specs=out_specs,
        scratch_shapes=scratch,
        compiler_params=pltpu.CompilerParams(collective_id=cid, has_side_effects=True, vmem_limit_bytes=60 << 20),
        cost_estimate=pl.CostEstimate(flops=0, bytes_accessed=160_000_000, transcendentals=0),
        name=name,
    )(*args)


def sds(shape, kind):
    return jax.ShapeDtypeStruct(shape, kind)


def plain(kernel, name, grid, in_specs, out_specs, out_shape, flops, nbytes, *args, scratch=(), aliases=None):
    return pl.pallas_call(
        kernel,
        out_shape=out_shape,
        grid=grid,
        in_specs=in_specs,
        out_specs=out_specs,
        scratch_shapes=scratch,
        input_output_aliases=aliases or {},
        compiler_params=pltpu.CompilerParams(vmem_limit_bytes=52 << 20),
        cost_estimate=pl.CostEstimate(flops=flops, bytes_accessed=nbytes, transcendentals=0),
        name=name,
    )(*args)


def whole(shape):
    return pl.BlockSpec(shape, lambda *i: (0,) * len(shape), pipeline_mode=pl.Buffered(1))


def by_rows(tm, width):
    return pl.BlockSpec((tm, width), lambda i: (i, 0))


def mlp_fwd_kernel(x_ref, w_ref, gu_ref, h_ref):
    t = h_ref.shape[1]
    y = dg(x_ref[...], w_ref[...], NN)
    gate, up = y[:, :t], y[:, t:]
    s = jax.nn.sigmoid(gate)
    silu = gate * s
    h_ref[...] = (silu * up).astype(BF)
    gu_ref[:, :t] = (up * s * (1.0 + gate * (1.0 - s))).astype(BF)
    gu_ref[:, t:] = silu.astype(BF)


def mlp_fwd(x, w, t):
    rows, dim = x.shape
    ff2 = w.shape[1]
    return plain(
        mlp_fwd_kernel, "mlp_fwd", (ff2 // (2 * t),),
        [whole((rows, dim)), pl.BlockSpec((dim, 2 * t), lambda i: (0, i))],
        [pl.BlockSpec((rows, 2 * t), lambda i: (0, i)), pl.BlockSpec((rows, t), lambda i: (0, i))],
        (sds((rows, ff2), BF), sds((rows, ff2 // 2), BF)),
        2 * rows * dim * ff2, rows * dim * 2 + dim * ff2 * 2 + rows * ff2 * 3, x, w,
    )


def fwd_kernel(groups, hd, tab, q_ref, kv_ref, o_ref, low_ref, lse_ref, acc, lsum):
    s = pl.program_id(1)
    block = q_ref.shape[0]
    diag, first, last = tab[2, s], tab[3, s], tab[4, s]

    @pl.when(first == 1)
    def _():
        acc[...] = jnp.zeros_like(acc)
        lsum[...] = jnp.zeros_like(lsum)

    def work(masked):
        k, v = kv_ref[:, :hd], kv_ref[:, hd:]
        for g in range(groups):
            at = slice(g * hd, (g + 1) * hd)
            scores = dg(q_ref[:, at], k, NT)
            if masked:
                row = lax.broadcasted_iota(jnp.int32, scores.shape, 0)
                col = lax.broadcasted_iota(jnp.int32, scores.shape, 1)
                scores = jnp.where(col <= row, scores, MASKED)
            probs = jnp.exp2(scores)
            part = probs[:, :128]
            for j in range(1, block // 128):
                part = part + probs[:, j * 128 : (j + 1) * 128]
            lsum[g] += part
            acc[:, at] += dg(probs.astype(BF), v, NN)

    @pl.when(diag == 0)
    def _():
        work(False)

    @pl.when(diag == 1)
    def _():
        work(True)

    @pl.when(last == 1)
    def _():
        lane = lax.broadcasted_iota(jnp.int32, (block, 128), 1)
        lse = jnp.zeros((block, 128), F32)
        for g in range(groups):
            at = slice(g * hd, (g + 1) * hd)
            l = jnp.sum(lsum[g], axis=1, keepdims=True)
            out = acc[:, at] / l
            o_ref[:, at] = out
            low_ref[:, at] = out.astype(BF)
            lse = jnp.where(lane == g, jnp.log2(l), lse)
        lse_ref[...] = jnp.transpose(lse)[: lse_ref.shape[0]]


def attn_fwd(tab, q, kv, groups, hd, block):
    rows, width = q.shape
    gw = groups * hd
    heads = width // gw
    steps = tab.shape[1]
    mine = pl.BlockSpec((block, gw), lambda h, s, t: (t[0, s], h))
    return pl.pallas_call(
        functools.partial(fwd_kernel, groups, hd),
        out_shape=(sds((rows, width), F32), sds((rows, width), BF), sds((8 * heads, rows), F32)),
        grid_spec=pltpu.PrefetchScalarGridSpec(
            num_scalar_prefetch=1,
            grid=(heads, steps),
            in_specs=[mine, pl.BlockSpec((block, 2 * hd), lambda h, s, t: (t[1, s], h))],
            out_specs=[mine, mine, pl.BlockSpec((8, block), lambda h, s, t: (h, t[0, s]))],
            scratch_shapes=[pltpu.VMEM((block, gw), F32), pltpu.VMEM((groups, block, 128), F32)],
        ),
        compiler_params=pltpu.CompilerParams(vmem_limit_bytes=48 << 20),
        cost_estimate=pl.CostEstimate(
            flops=heads * steps * block * block * gw * 4,
            bytes_accessed=heads * steps * block * hd * 8,
            transcendentals=heads * steps * block * block * groups,
        ),
        name="attn_fwd",
    )(tab, q, kv)


def bwd_kernel(groups, hd, tab, q_ref, do_ref, kv_ref, lse_ref, delta_ref, dq_ref, dkv_ref, dq_sum, dkv_sum):
    s = pl.program_id(1)
    block = q_ref.shape[0]
    qi, diag, first, last = tab[0, s], tab[2, s], tab[3, s], tab[4, s]

    @pl.when(s == 0)
    def _():
        dq_sum[...] = jnp.zeros_like(dq_sum)

    @pl.when(first == 1)
    def _():
        dkv_sum[...] = jnp.zeros_like(dkv_sum)

    def work(masked):
        k, v = kv_ref[:, :hd], kv_ref[:, hd:]
        for g in range(groups):
            at = slice(g * hd, (g + 1) * hd)
            q, do = q_ref[:, at], do_ref[:, at]
            scores = dg(k, q, NT) - lse_ref[g : g + 1, :]
            if masked:
                row = lax.broadcasted_iota(jnp.int32, scores.shape, 0)
                col = lax.broadcasted_iota(jnp.int32, scores.shape, 1)
                scores = jnp.where(row <= col, scores, MASKED)
            probs = jnp.exp2(scores)
            dots = dg(v, do, NT)
            dkv_sum[:, hd:] += dg(probs.astype(BF), do, NN)
            back = (probs * (dots - delta_ref[g : g + 1, :])).astype(BF)
            dkv_sum[:, :hd] += dg(back, q, NN)
            dq_sum[qi, :, at] += dg(back, k, TN)

    @pl.when(diag == 0)
    def _():
        work(False)

    @pl.when(diag == 1)
    def _():
        work(True)

    @pl.when(last == 1)
    def _():
        dkv_ref[:, :hd] = (dkv_sum[:, :hd] * math.log(2.0)).astype(BF)
        dkv_ref[:, hd:] = dkv_sum[:, hd:].astype(BF)

    @pl.when(s == pl.num_programs(1) - 1)
    def _():
        for i in range(dq_sum.shape[0]):
            dq_ref[i * block : (i + 1) * block, :] = dq_sum[i] * hd**-0.5


def attn_bwd(tab, q, do, kv, lse, delta, groups, hd, block):
    rows, width = q.shape
    gw = groups * hd
    heads = width // gw
    steps = tab.shape[1]
    mine = pl.BlockSpec((block, gw), lambda h, s, t: (t[0, s], h))
    keys = pl.BlockSpec((block, 2 * hd), lambda h, s, t: (t[1, s], h))
    stat = pl.BlockSpec((8, block), lambda h, s, t: (h, t[0, s]))
    return pl.pallas_call(
        functools.partial(bwd_kernel, groups, hd),
        out_shape=(sds((rows, width), F32), sds(kv.shape, BF)),
        grid_spec=pltpu.PrefetchScalarGridSpec(
            num_scalar_prefetch=1,
            grid=(heads, steps),
            in_specs=[mine, mine, keys, stat, stat],
            out_specs=[pl.BlockSpec((rows, gw), lambda h, s, t: (0, h)), keys],
            scratch_shapes=[pltpu.VMEM((rows // block, block, gw), F32), pltpu.VMEM((block, 2 * hd), F32)],
        ),
        compiler_params=pltpu.CompilerParams(vmem_limit_bytes=48 << 20),
        cost_estimate=pl.CostEstimate(
            flops=heads * steps * block * block * gw * 10,
            bytes_accessed=heads * steps * block * hd * 16,
            transcendentals=heads * steps * block * block * groups,
        ),
        name="attn_bwd",
    )(tab, q, do, kv, lse, delta)


def place(w):
    k, core = w // 2, w % 2
    return 4 * k + core, 4 * k + 3 - core


def block_row(b):
    m = b % 4
    core = jnp.where((m == 1) | (m == 2), 1, 0)
    return 2 * (2 * (b // 4) + core) + jnp.where(m < 2, 0, 1)


def tables(w, chips):
    a, b = place(w)
    count = a + b + 2
    every = jnp.arange(8 * chips - 2, dtype=jnp.int32)
    s, idle = jnp.minimum(every, count - 1), every >= count
    in_a = s <= a
    key = jnp.where(in_a, s, s - a - 1)
    diag = jnp.where(in_a, s == a, s == count - 1)
    fwd = [jnp.where(in_a, 0, 1), block_row(key), jnp.where(idle, 2, diag), ~idle & (key == 0), ~idle & diag]
    both = s < 2 * (a + 1)
    even = s % 2 == 0
    key = jnp.where(both, s // 2, s - (a + 1))
    query = jnp.where(both & even, 0, 1)
    diag = key == jnp.where(query == 0, a, b)
    zero = (every >= count) & (w % 2 == 1)
    key = jnp.where(zero, b + 1, key)
    only = zero & (every == count)
    bwd = [query, block_row(key), jnp.where(idle, 2, diag), only | ~idle & (~both | even), only | ~idle & (~both | ~even)]
    return tuple(jnp.stack([row.astype(jnp.int32) for row in rows]) for rows in (fwd, bwd))


def per_device(
    wide, narrow,
    layer_input, w_query, w_key, w_value, w_output, w_gate, w_up, w_down,
    attn_gain, mlp_gain, query_gain, key_gain, out_grad,
):
    hd = query_gain.shape[0]
    rows, dim = layer_input.shape
    all_rows = narrow * rows
    chips = wide // 2
    block = all_rows // 2
    qw, kw = w_query.shape[1], w_key.shape[1]
    ff = w_gate.shape[1]
    groups = qw // kw
    kv_heads = kw // hd
    w = lax.axis_index("wide")
    fwd_tab, bwd_tab = tables(w, chips)
    def gather(shard):
        return lax.all_gather(shard, "wide", axis=0, tiled=True)

    def scatter(grad):
        return lax.psum_scatter(grad, "wide", scatter_dimension=0, tiled=True)

    t = math.gcd(ff, 256)

    spread_s = spread_sems(narrow)
    sum_s = [*sum_bufs(narrow, rows, dim), *sum_sems(narrow)]
    row_buf = pltpu.VMEM((rows, dim), BF)
    low_rows, full_rows, all_low = sds((rows, dim), BF), sds((rows, dim), F32), sds((all_rows, dim), BF)
    ring = functools.partial
    qg, kg = query_gain[None], key_gain[None]
    after = lax.optimization_barrier

    in_scratch = [*spread_s, *line_sems(chips)]
    table = sds((all_rows, hd), F32)
    s_rows, s_cols = w_query.shape[0], 2 * qw + 2 * kw
    normed_all, w_attn, gu_shard, d_shard, cos_table, sin_table = comm_call(
        ring(input_kernel, wide, narrow), "input_rows", 0,
        (all_low, sds((dim, s_cols), BF), sds((s_rows, 2 * ff), BF), sds((s_rows, ff), BF), table, table),
        [VM] * 9, (HB, HB, VM, VM, VM, VM), [row_buf, pltpu.VMEM((s_rows, s_cols), BF), *in_scratch],
        layer_input, attn_gain[None], w_query, w_key, w_value, w_output, w_gate, w_up, w_down,
    )
    width = qw + 2 * kw
    grad_all, kv, query_proj, key_proj, queries = comm_call(
        ring(qkv_kernel, wide, narrow, qw, kw, hd**-0.5 * math.log2(math.e)), "qkv_rows", 1,
        (all_low, sds((wide * all_rows, 2 * kw), BF), sds((all_rows, qw), F32),
         sds((all_rows, kw), F32), sds((all_rows, qw), BF)),
        [VM, HB, HB, VM, VM, VM, VM], (HB, HB, VM, VM, VM),
        [pltpu.VMEM((all_rows, 2 * kw), BF), pltpu.VMEM((dim, width), BF),
         pltpu.VMEM((all_rows, dim), BF), DMA((2,)), *in_scratch],
        out_grad, normed_all, w_attn, cos_table, sin_table, qg, kg,
    )
    gu_shard, d_shard, kv = after((gu_shard, d_shard, kv))
    w_gu, w_d = gather(gu_shard), gather(d_shard)
    attended, attended_low, lse = attn_fwd(fwd_tab, queries, kv, groups, hd, block)
    w_o = w_attn[:, qw + 2 * kw :]
    middle, normed_mlp = comm_call(
        ring(middle_kernel, wide, narrow), "middle_rows", 2, (full_rows, all_low), [HB, VM, VM], (VM, HB),
        [row_buf, *sum_s, *spread_s], dg(attended_low, w_o, NT).astype(BF), layer_input, mlp_gain[None],
    )
    factors, hidden_low = mlp_fwd(normed_mlp, w_gu, t)
    grad_down = dg(grad_all, hidden_low, TN).astype(BF)
    w_d, _ = after((w_d, grad_down))
    middle_back, middle_low, mlp_gain_part, grad_gu = comm_call(
        ring(mlp_back_kernel, wide, narrow), "mlp_back", 6,
        (full_rows, low_rows, sds((1, dim), F32), sds((dim, 2 * ff), BF)), [HB, HB, HB, HB, HB, HB, VM, HB], (VM, VM, VM, HB),
        [pltpu.VMEM((all_rows, dim), BF), pltpu.VMEM((2, dim, t), BF), pltpu.VMEM((2, all_rows, 2 * t), BF),
         pltpu.VMEM((all_rows, 2 * ff), BF), pltpu.VMEM((dim, 2 * ff), BF), pltpu.VMEM((all_rows, dim), BF),
         pltpu.VMEM((rows, dim), F32), row_buf, pltpu.VMEM((2, 256, 2 * ff), BF), product_bufs(narrow, rows, dim), DMA((6,)), DMA((2, 2)), DMA((2,)), *sum_s],
        grad_all, w_d, factors, w_gu, normed_mlp, middle, mlp_gain[None], out_grad,
    )
    grad_down, grad_gu = scatter(grad_down), scatter(grad_gu)
    middle_all, down_part, back, delta = comm_call(
        ring(middle_back_kernel, wide, narrow, (width, qw), groups, hd), "middle_back", 3,
        (all_low, all_low, sds((all_rows, qw), BF), sds((8 * kv_heads, all_rows), F32)),
        [VM, HB, HB, HB, HB], (HB, HB, VM, VM),
        [pltpu.VMEM((all_rows, dim), BF), pltpu.VMEM((all_rows, dim), BF), pltpu.VMEM((all_rows, ff), BF), pltpu.VMEM((dim, ff), BF), pltpu.VMEM((dim, qw), BF), pltpu.VMEM((all_rows, qw), F32),
         DMA((4,)), DMA((narrow,)), DMA((all_rows // 256,)), *spread_s],
        middle_low, hidden_low, w_d, w_attn, attended,
    )
    query_back, dkv = attn_bwd(bwd_tab, queries, back, kv, lse, delta, groups, hd, block)
    dkv, grad_down = after((dkv, grad_down))
    layer_output, kv_sum, q_low, query_gain_part, grad_qo = comm_call(
        ring(output_kernel, wide, narrow), "output_rows", 4,
        (low_rows, sds((all_rows, 2 * kw), BF), sds((all_rows, qw), BF), sds((1, hd), F32), sds((dim, 2 * qw), BF)),
        [HB, VM, HB, HB, HB, VM, VM, VM, HB, HB, HB], (VM, VM, VM, VM, HB),
        [pltpu.VMEM((dim, 2 * qw), BF), pltpu.VMEM((all_rows, qw), F32), pltpu.VMEM((all_rows, qw), F32), pltpu.VMEM((all_rows, dim), BF),
         pltpu.VMEM((all_rows, dim), BF), pltpu.VMEM((all_rows, qw), BF), DMA((5,)), DMA((dim // 256,)), *sum_s,
         *line_sum_bufs(chips, all_rows, 2 * kw), *line_sum_sems(chips)],
        down_part, middle, dkv, query_back, query_proj, cos_table, sin_table, qg, normed_all, middle_all, attended_low,
    )
    kv_sum, grad_gu = after((kv_sum, grad_gu))
    gains = jnp.concatenate([jnp.zeros((1, dim), F32), mlp_gain_part, query_gain_part, jnp.zeros((1, hd), F32)], axis=1)
    w_rows = dim // wide
    input_grad, gain_sums, grad_qo, grad_kv = comm_call(
        ring(input_back_kernel, wide, narrow, qw, kw), "input_back", 5,
        (full_rows, sds(gains.shape, F32), sds((w_rows, 2 * qw), F32), sds((w_rows, 2 * kw), F32)),
        [HB, VM, HB, VM, HB, VM, VM, VM, VM, VM, VM, HB, HB],
        (VM, VM, VM, VM),
        [pltpu.VMEM((narrow, *gains.shape), F32), pltpu.VMEM((wide, *gains.shape), F32),
         pltpu.VMEM((all_rows, width), BF), pltpu.VMEM((all_rows, dim), BF), pltpu.VMEM((dim, 2 * kw), BF),
         pltpu.VMEM((dim, width), BF), pltpu.VMEM((all_rows, dim), BF),
         row_buf, pltpu.VMEM((rows, dim), F32), DMA((4,)), DMA((narrow,)), DMA((narrow,)), DMA((wide,)), DMA((wide,)), *sum_s,
         *line_sum_bufs(chips, w_rows, 2 * qw)[:4], *line_sum_sems(chips),
         *line_sum_bufs(chips, w_rows, 2 * kw)[:4], *line_sum_sems(chips)],
        layer_input, attn_gain[None], middle_back, gains, grad_qo, q_low, kv_sum, key_proj, cos_table, sin_table, kg, w_attn, normed_all,
    )
    tm = min(w_rows, 128)
    turned = lambda height: pl.BlockSpec((height, tm), lambda i: (0, i))
    grads = plain(
        finish_kernel, "finish", (w_rows // tm,),
        [by_rows(tm, 2 * ff), by_rows(tm, ff), by_rows(tm, 2 * qw), by_rows(tm, 2 * kw)],
        [by_rows(tm, ff), by_rows(tm, ff), turned(ff), by_rows(tm, qw), by_rows(tm, kw), by_rows(tm, kw), turned(qw)],
        [sds(shape, F32) for shape in (w_gate.shape, w_up.shape, w_down.shape, w_query.shape, w_key.shape, w_value.shape,
                                       w_output.shape)],
        0, 10 * dim // wide * (3 * ff + qw), grad_gu, grad_down, grad_qo, grad_kv,
    )
    grad_gate, grad_up, grad_down, grad_query, grad_key, grad_value, grad_output = grads
    g = gain_sums[0]
    return (
        layer_output, input_grad, grad_query, grad_key, grad_value, grad_output, grad_gate, grad_up, grad_down,
        g[:dim], g[dim : 2 * dim], g[2 * dim : 2 * dim + hd], g[2 * dim + hd :],
    )


def solution(mesh):
    rows = P(("wide", "narrow"), None)
    weight, turned = P("wide", "narrow"), P("narrow", "wide")
    return jax.shard_map(
        functools.partial(per_device, mesh.shape["wide"], mesh.shape["narrow"]),
        mesh=mesh,
        in_specs=(rows, weight, weight, weight, turned, weight, weight, turned, P(), P(), P(), P(), rows),
        out_specs=(rows, rows, weight, weight, weight, turned, weight, weight, turned, P(), P(), P(), P()),
        check_vma=False,
    )
```

```python
import functools
import math

import jax
import jax.numpy as jnp
from jax import lax
from jax.experimental import pallas as pl
from jax.experimental.pallas import tpu as pltpu
from jax.sharding import PartitionSpec as P

EPSILON = 1e-06
MASKED = -1e30
F32 = jnp.float32
BF = jnp.bfloat16
MESH = pl.DeviceIdType.MESH
NT = (((1,), (1,)), ((), ()))
NN = (((1,), (0,)), ((), ()))
TN = (((0,), (0,)), ((), ()))


def dg(a, b, dims):
    return lax.dot_general(a, b, dims, preferred_element_type=F32)
DMA = pltpu.SemaphoreType.DMA


class Place:
    def __init__(self, wide, narrow):
        self.W, self.N = wide, narrow
        self.C, self.half = wide // 2, narrow // 2
        self.w, self.n = lax.axis_index("wide"), lax.axis_index("narrow")
        self.k, self.c = self.w // 2, lax.rem(self.w, 2)
        late = (self.n >= self.half).astype(jnp.int32)
        self.group = lax.rem(self.c + late, 2)
        self.slot = jnp.where(self.group == 0, self.n, lax.rem(self.n + self.half, self.N))

    def owner(self, j):
        core = 1 if j >= self.half else 0
        n = jnp.where(self.c == 0, j, (j + self.half) % self.N)
        return core, n

    def owner_is_me(self, j):
        core, n = self.owner(j)
        return (self.c == core) & (self.n == n)


def enter(p, line=False, ring=False):
    barrier = pltpu.get_barrier_semaphore()

    def greet(device):
        pl.semaphore_signal(barrier, inc=1, device_id=device, device_id_type=MESH)

    for core in range(2):
        for n in range(p.N):

            @pl.when((p.c != core) | (p.n != n))
            def _():
                greet((2 * p.k + core, n))

    peers = 2 * p.N - 1
    if line or ring:
        for k in range(p.C):

            @pl.when(p.k != k)
            def _():
                greet((2 * k + p.c, p.n))
                if ring:
                    greet((2 * k + 1 - p.c, p.n))

        peers += (2 if ring else 1) * (p.C - 1)
    pl.semaphore_wait(barrier, peers)


def slot_of(p, n, group):
    return jnp.where(group == 0, n, lax.rem(n + p.half, p.N))


def neighbours(p):
    return p.n + 1 - 2 * lax.rem(p.n, 2), lax.rem(p.n + 2, 4), 3 - p.n


def to(src, dst, send, recv, wide, narrow):
    return pltpu.make_async_remote_copy(
        src_ref=src, dst_ref=dst, send_sem=send, recv_sem=recv, device_id=(wide, narrow), device_id_type=MESH
    )


def spread_sems(narrow):
    return [DMA((narrow, 2)), DMA((narrow, 2)), DMA((2,)), DMA((2,))]


def spread_start(p, src, gathered, rows, send, recv, local, onward):
    half = rows // 2
    view = lambda i: gathered.at[pl.ds(pl.multiple_of(p.slot * rows + i * half, half), half)]
    part = lambda i: src.at[pl.ds(i * half, half)]
    mine = p.group == p.c
    square = p.N == 4
    if square:
        nx, ny, _ = neighbours(p)
        targets = [(nx, (0, 1)), (ny, (1, 0))]
        order = [(t, q, i) for q in range(2) for t, halves in targets for i in (halves[q],)]
        for t, q, i in order:
            at = 0 if t is nx else 1
            to(part(i), view(i), send.at[at, i], recv.at[p.slot, i], 2 * p.k + p.group, t).start()
    else:
        for t in range(p.N):

            @pl.when(p.n != t)
            def _():
                for i in range(2):
                    to(part(i), view(i), send.at[t, i], recv.at[p.slot, i], 2 * p.k + p.group, t).start()

    @pl.when(mine)
    def _():
        for i in range(2):
            pltpu.make_async_copy(part(i), view(i), local.at[i]).start()

    @pl.when(jnp.logical_not(mine))
    def _():
        for i in range(2):
            to(part(i), view(i), local.at[i], recv.at[p.slot, i], 2 * p.k + p.group, p.n).start()


def spread_pass(p, src, gathered, rows, send, recv, local, onward):
    if p.N == 4:
        half = rows // 2
        piece = src.at[pl.ds(0, half)]
        nx, ny, _ = neighbours(p)
        for i, (n, other) in enumerate(((nx, ny), (ny, nx))):
            j = slot_of(p, n, p.c)
            here = gathered.at[pl.ds(pl.multiple_of(j * rows + i * half, half), half)]
            pltpu.make_async_copy(piece, here, recv.at[j, i]).wait()
            to(here, here, onward.at[i], recv.at[j, i], p.w, other).start()


def spread_end(p, src, gathered, rows, send, recv, local, onward, on_slot=lambda j: None):
    half = rows // 2
    piece = src.at[pl.ds(0, half)]
    mine = p.group == p.c
    at = lambda j, i: gathered.at[pl.ds(pl.multiple_of(j * rows + i * half, half), half)]

    def arrive(j, i):
        pltpu.make_async_copy(piece, at(j, i), recv.at[j, i]).wait()

    for i in range(2):
        pltpu.make_async_copy(piece, at(0, 0), local.at[i]).wait()
    here = slot_of(p, p.n, p.c)

    @pl.when(jnp.logical_not(mine))
    def _():
        arrive(here, 0)
        arrive(here, 1)

    on_slot(here)
    if p.N == 4:
        nx, ny, nd = neighbours(p)
        jx, jy, jd = (slot_of(p, n, p.c) for n in (nx, ny, nd))
        arrive(jx, 1)
        on_slot(jx)
        arrive(jy, 0)
        on_slot(jy)
        arrive(jd, 0)
        arrive(jd, 1)
        on_slot(jd)
        for i in range(2):
            pltpu.make_async_copy(piece, at(0, 0), onward.at[i]).wait()
            for t in range(2):
                pltpu.make_async_copy(piece, at(0, 0), send.at[t, i]).wait()
    else:
        for t in range(p.N):

            @pl.when(p.n != t)
            def _():
                for i in range(2):
                    pltpu.make_async_copy(piece, at(0, 0), send.at[t, i]).wait()
                    arrive(slot_of(p, t, p.c), i)
                on_slot(slot_of(p, t, p.c))


def sum_bufs(narrow, rows, dim):
    if narrow == 4:
        half = pltpu.VMEM((2, 2, rows, dim // 2), BF)
        return [half, half, pltpu.VMEM((2, rows, dim), BF)]
    return [pltpu.VMEM((narrow, rows, dim), BF)]


def sum_sems(narrow):
    if narrow == 4:
        return [DMA((2, 2)), DMA((2, 2)), DMA((2, 2)), DMA((4,)), DMA((4,))]
    return [DMA((narrow,)), DMA((narrow,)), DMA]


def pieces(p, part, rows, dim):
    half = dim // 2
    return lambda j, i: part.at[pl.ds(pl.multiple_of(j * rows, rows), rows), pl.ds(i * half, half)]


def sum_start(p, part, rows, dim, bufs, sems):
    if p.N != 4:
        (got,), (send, recv, local) = bufs, sems
        for j in range(p.N):
            core, n = p.owner(j)
            mine = p.owner_is_me(j)
            src = part.at[pl.ds(j * rows, rows)]

            @pl.when(mine)
            def _():
                pltpu.make_async_copy(src, got.at[p.n], local).start()

            @pl.when(jnp.logical_not(mine))
            def _():
                to(src, got.at[p.n], send.at[j], recv.at[p.n], 2 * p.k + core, n).start()

        return
    own, inbox, _ = bufs
    load, send, recv, _, _ = sems
    piece = pieces(p, part, rows, dim)
    nx, ny, nd = neighbours(p)
    across, here = slot_of(p, nd, p.c), slot_of(p, p.n, p.c)
    for i, n in enumerate((nx, ny)):
        to(piece(across, i), inbox.at[i, 0], send.at[i, 0], recv.at[i, 0], p.w, n).start()
    for i, n in enumerate((ny, nx)):
        pltpu.make_async_copy(piece(slot_of(p, n, p.c), i), own.at[i, 0], load.at[i, 0]).start()
    for i, n in enumerate((nx, ny)):
        to(piece(slot_of(p, n, p.c), i), inbox.at[i, 1], send.at[i, 1], recv.at[i, 1], p.w, n).start()
        pltpu.make_async_copy(piece(here, i), own.at[i, 1], load.at[i, 1]).start()


def product_bufs(narrow, rows, dim):
    shape = (4, rows, dim // 2) if narrow == 4 else (narrow * rows, dim)
    return pltpu.VMEM(shape, BF)


def sum_start_of(p, product, out, rows, dim, bufs, sems):
    half = dim // 2
    if p.N != 4:

        def one(j, carry):
            for i in range(2):
                out[pl.ds(pl.multiple_of(j * rows, rows), rows), i * half : (i + 1) * half] = product(j, i)
            return carry

        lax.fori_loop(0, p.N, one, 0)
        sum_start(p, out, rows, dim, bufs, sems)
        return
    own, inbox, _ = bufs
    _, send, recv, _, _ = sems
    nx, ny, nd = neighbours(p)
    across, jx, jy, here = (slot_of(p, n, p.c) for n in (nd, nx, ny, p.n))

    def one(t, carry):
        i = lax.rem(t, 2)
        q = lax.rem(t // 2, 2)
        beside = jnp.where(i == 0, jx, jy)
        other = jnp.where(i == 0, jy, jx)
        j = jnp.where(t < 4, jnp.where(q == 0, across, beside), jnp.where(q == 0, other, here))
        y = product(j, i)

        @pl.when(t < 4)
        def _():
            out[t] = y
            to(out.at[t], inbox.at[i, q], send.at[i, q], recv.at[i, q], p.w, jnp.where(i == 0, nx, ny)).start()

        @pl.when(t >= 4)
        def _():
            own[i, q] = y

        return carry

    lax.fori_loop(0, 8, one, 0)


def core_of(p, j):
    return (j >= p.half).astype(jnp.int32)


def sum_pass(p, part, rows, dim, bufs, sems, loaded=False):
    if p.N != 4:
        return
    own, inbox, box = bufs
    load, send, recv, send2, recv2 = sems
    piece = lambda j, i: own.at[0, 0]
    half = dim // 2
    nx, ny, _ = neighbours(p)
    cols = lambda i: pl.ds(i * half, half)

    def add(i, q):
        if not loaded:
            pltpu.make_async_copy(piece(0, 0), own.at[i, q], load.at[i, q]).wait()
        pltpu.make_async_copy(piece(0, 0), inbox.at[i, q], recv.at[i, q]).wait()

        def body(at):
            own[i, q, at, :] = (own[i, q, at, :].astype(F32) + inbox[i, q, at, :].astype(F32)).astype(BF)

        row_loop(rows, 64, body)

    for i, n in enumerate((ny, nx)):
        add(i, 0)
        j = slot_of(p, n, p.c)
        to(own.at[i, 0], box.at[1, :, cols(i)], send2.at[i], recv2.at[i], 2 * p.k + core_of(p, j), n).start()
    j = slot_of(p, p.n, p.c)
    keep = core_of(p, j) == p.c
    for i in range(2):
        add(i, 1)

        @pl.when(keep)
        def _():
            pltpu.make_async_copy(own.at[i, 1], box.at[0, :, cols(i)], send2.at[2 + i]).start()

        @pl.when(jnp.logical_not(keep))
        def _():
            to(own.at[i, 1], box.at[0, :, cols(i)], send2.at[2 + i], recv2.at[2 + i], 2 * p.k + core_of(p, j), p.n).start()


def sum_end(p, part, rows, dim, bufs, sems):
    if p.N != 4:
        (got,), (send, recv, local) = bufs, sems
        for t in range(p.N):
            mine = (p.group == p.c) & (p.n == t)

            @pl.when(mine)
            def _():
                pltpu.make_async_copy(part.at[pl.ds(0, rows)], got.at[t], local).wait()

            @pl.when(jnp.logical_not(mine))
            def _():
                pltpu.make_async_copy(part.at[pl.ds(0, rows)], got.at[t], recv.at[t]).wait()

        for j in range(p.N):

            @pl.when(jnp.logical_not(p.owner_is_me(j)))
            def _():
                pltpu.make_async_copy(part.at[pl.ds(j * rows, rows)], got.at[0], send.at[j]).wait()

        return
    own, inbox, box = bufs
    load, send, recv, send2, recv2 = sems
    piece = lambda j, i: own.at[0, 0]
    half = dim // 2
    cols = lambda i: pl.ds(i * half, half)
    for i in range(2):
        for q in range(2):
            pltpu.make_async_copy(piece(0, 0), inbox.at[i, q], send.at[i, q]).wait()
        pltpu.make_async_copy(own.at[i, 0], box.at[1, :, cols(i)], send2.at[i]).wait()
        pltpu.make_async_copy(own.at[i, 0], box.at[1, :, cols(i)], recv2.at[i]).wait()
        pltpu.make_async_copy(own.at[i, 1], box.at[0, :, cols(i)], send2.at[2 + i]).wait()

        @pl.when(p.group != p.c)
        def _():
            pltpu.make_async_copy(own.at[i, 1], box.at[0, :, cols(i)], recv2.at[2 + i]).wait()


def total(p, bufs, at):
    if p.N == 4:
        box = bufs[2]
        return box[0, at, :].astype(F32) + box[1, at, :].astype(F32)
    got = bufs[0]
    out = got[0, at, :].astype(F32)
    for t in range(1, p.N):
        out = out + got[t, at, :].astype(F32)
    return out


PARTS = 4


def line_sems(chips):
    return [DMA((2, chips, PARTS)), DMA((chips, PARTS)), DMA((chips, PARTS)), DMA((chips, PARTS)), DMA((PARTS,))]


def line_parts(p, full, rows):
    size = rows // PARTS

    def at(s, core, q=None):
        first = (2 * s + core) * rows
        if q is None:
            return full.at[pl.ds(pl.multiple_of(first, rows), rows)]
        return full.at[pl.ds(pl.multiple_of(first + q * size, size), size)]

    return at


def each_part(body):
    def one(q, carry):
        body(q)
        return carry

    lax.fori_loop(0, PARTS, one, 0)


def line_copy(p, src, dst, send, recv, k, core):
    return pltpu.make_async_remote_copy(
        src_ref=src, dst_ref=dst, send_sem=send, recv_sem=recv, device_id=(2 * k + core, p.n), device_id_type=MESH
    )


def inside(p, k):
    return (k >= 0) & (k < p.C)


BOTH, UP, DOWN = ((0, 1), (1, -1)), ((0, 1),), ((1, -1),)


def line_push(p, src, full, rows, zsend, zrecv, csend, crecv, local, q, ways=BOTH):
    size = rows // PARTS
    part = src.at[pl.ds(pl.multiple_of(q * size, size), size)]
    there = line_parts(p, full, rows)(p.k, p.c, q)
    for i, sign in ways:

        @pl.when(inside(p, p.k + sign))
        def _():
            line_copy(p, part, there, zsend.at[i, 0, q], zrecv.at[p.k, q], p.k + sign, p.c).start()

    line_copy(p, part, there, csend.at[p.k, q], crecv.at[p.k, q], p.k, 1 - p.c).start()
    pltpu.make_async_copy(part, there, local.at[q]).start()


def came(p, s, ways):
    if ways == BOTH:
        return s == s
    return s <= p.k if ways == UP else s >= p.k


def line_steps(p, src, full, rows, zsend, zrecv, csend, crecv, local, ways=BOTH):
    at = line_parts(p, full, rows)
    piece = src.at[pl.ds(0, rows // PARTS)]

    def at_distance(d):
        def onward(q):
            for i, sign in ways:
                s, t = p.k - sign * d, p.k + sign

                @pl.when(inside(p, s))
                def _():
                    here = at(s, p.c, q)
                    pltpu.make_async_copy(piece, here, zrecv.at[s, q]).wait()

                    @pl.when(inside(p, t))
                    def _():
                        line_copy(p, here, here, zsend.at[i, d, q], zrecv.at[s, q], t, p.c).start()

                    line_copy(p, here, here, csend.at[s, q], crecv.at[s, q], p.k, 1 - p.c).start()

        each_part(onward)

    def settle(q):
        here = at(p.k, p.c, q)
        pltpu.make_async_copy(piece, here, local.at[q]).wait()
        for s in range(p.C):

            @pl.when(came(p, jnp.int32(s), ways))
            def _():
                pltpu.make_async_copy(piece, here, csend.at[s, q]).wait()
                pltpu.make_async_copy(piece, at(s, 1 - p.c, q), crecv.at[s, q]).wait()

        for i, sign in ways:
            for d in range(p.C):

                @pl.when(inside(p, p.k - sign * d) & inside(p, p.k + sign))
                def _():
                    pltpu.make_async_copy(piece, here, zsend.at[i, d, q]).wait()

    return [functools.partial(at_distance, d) for d in range(1, p.C)] + [lambda: each_part(settle)]


def line_sum_bufs(chips, rows, width):
    return [pltpu.VMEM((chips, rows, width), BF)] * 3 + [pltpu.VMEM((2, rows, width), BF), pltpu.VMEM((rows, width), F32)]


def line_sum_sems(chips):
    return [
        DMA((chips, PARTS)), DMA((chips, PARTS)), DMA((chips, PARTS)), DMA((2, chips, PARTS)), DMA((chips, PARTS)),
        DMA((2, PARTS)),
    ]


OTHER = {BOTH: BOTH, UP: DOWN, DOWN: UP}


def line_sum_start(p, part, rows, bufs, sems, ways=BOTH):
    own, inbox, _, _, _ = bufs
    load, csend, crecv, _, _, _ = sems
    at = line_parts(p, part, rows)
    size = rows // PARTS

    def share(s):
        def one(q):
            here = pl.ds(pl.multiple_of(q * size, size), size)
            line_copy(p, at(s, 1 - p.c, q), inbox.at[s, here], csend.at[s, q], crecv.at[s, q], p.k, 1 - p.c).start()
            pltpu.make_async_copy(at(s, p.c, q), own.at[s, here], load.at[s, q]).start()

        each_part(one)

    for d in range(p.C - 1, 0, -1):
        for _, sign in ways:
            s = p.k + sign * d

            @pl.when(inside(p, s))
            def _():
                share(s)

    share(p.k)


def line_sum_steps(p, part, rows, bufs, sems, ways=BOTH):
    own, inbox, relay, box, acc = bufs
    load, csend, crecv, zsend, rrecv, zrecv = sems
    size = rows // PARTS
    step = math.gcd(size, 128)
    piece = line_parts(p, part, rows)(0, 0, 0)

    def rows_of(q):
        return pl.ds(pl.multiple_of(q * size, size), size)

    def add(q, body):
        def one(j, carry):
            body(pl.ds(pl.multiple_of(q * size + j * step, step), step))
            return carry

        lax.fori_loop(0, size // step, one, 0)

    def pair(t, q):
        pltpu.make_async_copy(piece, own.at[t, rows_of(q)], load.at[t, q]).wait()
        pltpu.make_async_copy(piece, inbox.at[t, rows_of(q)], crecv.at[t, q]).wait()

    def at_distance(d):
        def onward(q):
            here = rows_of(q)
            for i, sign in ways:
                t = p.k + sign * d
                behind = inside(p, p.k - sign)

                @pl.when(inside(p, t))
                def _():
                    pair(t, q)

                    @pl.when(jnp.logical_not(behind))
                    def _():
                        def two(at):
                            own[t, at, :] = (own[t, at, :].astype(F32) + inbox[t, at, :].astype(F32)).astype(BF)

                        add(q, two)

                    @pl.when(behind)
                    def _():
                        pltpu.make_async_copy(piece, relay.at[t, here], rrecv.at[t, q]).wait()

                        def three(at):
                            both = own[t, at, :].astype(F32) + inbox[t, at, :].astype(F32)
                            own[t, at, :] = (both + relay[t, at, :].astype(F32)).astype(BF)

                        add(q, three)

                    src = own.at[t, here]
                    if d >= 2:
                        line_copy(p, src, relay.at[t, here], zsend.at[i, d, q], rrecv.at[t, q], p.k + sign, p.c).start()
                    else:
                        line_copy(p, src, box.at[i, here], zsend.at[i, d, q], zrecv.at[i, q], t, p.c).start()

        each_part(onward)

    def last(q):
        here = rows_of(q)
        pair(p.k, q)

        def first(at):
            acc[at, :] = own[p.k, at, :].astype(F32) + inbox[p.k, at, :].astype(F32)

        add(q, first)
        for i, sign in ways:

            @pl.when(inside(p, p.k - sign))
            def _():
                pltpu.make_async_copy(piece, box.at[i, here], zrecv.at[i, q]).wait()

                def more(at):
                    acc[at, :] += box[i, at, :].astype(F32)

                add(q, more)

            for d in range(1, p.C):

                @pl.when(inside(p, p.k + sign * d))
                def _():
                    pltpu.make_async_copy(piece, own.at[0, here], zsend.at[i, d, q]).wait()

        for s in range(p.C):

            @pl.when(came(p, jnp.int32(s), OTHER[ways]))
            def _():
                pltpu.make_async_copy(piece, inbox.at[s, here], csend.at[s, q]).wait()


    return [functools.partial(at_distance, d) for d in range(p.C - 1, 0, -1)] + [lambda: each_part(last)]


def row_loop(rows, step, body):
    def one(i, carry):
        body(pl.ds(pl.multiple_of(i * step, step), step))
        return carry

    lax.fori_loop(0, rows // step, one, 0)


STEP = 64


def inv_rms(u):
    return lax.rsqrt(jnp.mean(u * u, axis=-1, keepdims=True) + EPSILON)


def weave(gate_ref, up_ref, both_ref):
    ff = gate_ref.shape[1]
    t = math.gcd(ff, 256)
    for i in range(0, ff, t):
        both_ref[:, 2 * i : 2 * i + t] = gate_ref[:, i : i + t]
        both_ref[:, 2 * i + t : 2 * i + 2 * t] = up_ref[:, i : i + t]


def finish_kernel(both_ref, down_ref, qo_ref, kv_ref, gate_out, up_out, down_out, q_out, k_out, v_out, o_out):
    ff = gate_out.shape[1]
    t = math.gcd(ff, 256)
    for i in range(0, ff, t):
        gate_out[:, i : i + t] = both_ref[:, 2 * i : 2 * i + t].astype(F32)
        up_out[:, i : i + t] = both_ref[:, 2 * i + t : 2 * i + 2 * t].astype(F32)
    down_out[...] = jnp.transpose(down_ref[...].astype(F32))
    qw, kw = q_out.shape[1], k_out.shape[1]
    q_out[...] = qo_ref[:, :qw]
    o_out[...] = jnp.transpose(qo_ref[:, qw:])
    k_out[...] = kv_ref[:, :kw]
    v_out[...] = kv_ref[:, kw:]


def rotation(p, cos_ref, sin_ref):
    all_rows, hd = cos_ref.shape
    block, half, step = all_rows // 2, hd // 2, 64
    lane = lax.broadcasted_iota(jnp.int32, (step, hd), 1)
    column = jnp.where(lane < half, lane, lane - half).astype(F32)
    inverse = jnp.exp(column * (-2.0 * math.log(1000000.0) / hd))
    row = lax.broadcasted_iota(jnp.int32, (step, hd), 0)

    def body(i, carry):
        at = i * step
        first = jnp.where(at < block, (4 * p.k + p.c) * block + at, (4 * p.k + 3 - p.c) * block + at - block)
        angles = (first + row).astype(F32) * inverse
        here = pl.ds(pl.multiple_of(at, step), step)
        cos_ref[here, :] = jnp.cos(angles)
        sine = jnp.sin(angles)
        sin_ref[here, :] = jnp.where(lane < half, -sine, sine)
        return carry

    lax.fori_loop(0, all_rows // step, body, 0)


def input_kernel(
    wide, narrow, x_ref, gain_ref, wq_ref, wk_ref, wv_ref, wo_ref, gate_ref, up_ref, down_ref,
    gathered, full, gu_ref, d_ref, cos_ref, sin_ref, buf, shard, *sems
):
    p = Place(wide, narrow)
    rows = x_ref.shape[0]
    lo = 0
    for w_ref in (wq_ref, wk_ref, wv_ref):
        shard[:, lo : lo + w_ref.shape[1]] = w_ref[...]
        lo += w_ref.shape[1]
    shard[:, lo:] = jnp.transpose(wo_ref[...])
    spread, line = sems[:4], (shard, full, shard.shape[0], *sems[4:])
    enter(p, line=True)
    each_part(lambda q: line_push(p, *line, q))
    *steps, end = line_steps(p, *line)

    def body(at):
        u = x_ref[at, :].astype(F32)
        buf[at, :] = (u * inv_rms(u) * gain_ref[...]).astype(BF)

    row_loop(rows, STEP, body)
    spread_start(p, buf, gathered, rows, *spread)
    weave(gate_ref, up_ref, gu_ref)
    d_ref[...] = jnp.transpose(down_ref[...])
    steps[0]()
    rotation(p, cos_ref, sin_ref)
    spread_pass(p, buf, gathered, rows, *spread)
    for step in steps[1:]:
        step()
    spread_end(p, buf, gathered, rows, *spread)
    end()


def turn(u):
    return pltpu.roll(u, u.shape[-1] // 2, 1)


def qkv_kernel(
    wide, narrow, qw, kw, fold, g_ref, x_ref, w_ref, cos_ref, sin_ref, qg_ref, kg_ref,
    gathered, full, qproj_out, kproj_out, q_out, qproj_ref, kproj_ref, q_ref, kv_ref, w_buf, x_buf, load, store, *sems,
):
    p = Place(wide, narrow)
    rows = g_ref.shape[0]
    hd = cos_ref.shape[1]
    all_rows = x_ref.shape[0]
    size = all_rows // 4
    spread, line = sems[:4], (kv_ref, full, all_rows, *sems[4:])
    weights = pltpu.make_async_copy(w_ref.at[:, pl.ds(0, w_buf.shape[1])], w_buf, load.at[0])
    normed = pltpu.make_async_copy(x_ref, x_buf, load.at[1])
    normed.start()
    weights.start()
    enter(p, line=True)

    def project(q):
        at = pl.ds(pl.multiple_of(q * size, size), size)
        y = dg(x_buf[at, :], w_buf[...], NN)
        cos, sin = cos_ref[at, :], sin_ref[at, :]
        qproj_ref[at, :] = y[:, :qw]
        kproj_ref[at, :] = y[:, qw : qw + kw]

        def head(lo, gain):
            u = y[:, lo : lo + hd]
            v = u * inv_rms(u) * gain
            return v * cos + turn(v) * sin

        for h in range(kw // hd):
            kv_ref[at, 2 * h * hd : (2 * h + 1) * hd] = head(qw + h * hd, kg_ref[...]).astype(BF)
            kv_ref[at, (2 * h + 1) * hd : (2 * h + 2) * hd] = y[:, qw + kw + h * hd : qw + kw + (h + 1) * hd].astype(BF)
        for i in range(PARTS // 4):
            line_push(p, *line, q * (PARTS // 4) + i, ways=UP)
        for h in range(qw // hd):
            q_ref[at, h * hd : (h + 1) * hd] = (head(h * hd, qg_ref[...]) * fold).astype(BF)

    normed.wait()
    weights.wait()

    def one(q, carry):
        project(q)
        return carry

    lax.fori_loop(0, 4, one, 0)
    pairs = ((qproj_ref, qproj_out), (kproj_ref, kproj_out), (q_ref, q_out))
    stores = [pltpu.make_async_copy(src, dst, store.at[i]) for i, (src, dst) in enumerate(pairs)]
    spread_start(p, g_ref, gathered, rows, *spread)
    for copy in stores:
        copy.start()
    *steps, end = line_steps(p, *line, ways=UP)
    steps[0]()
    spread_pass(p, g_ref, gathered, rows, *spread)
    for step in steps[1:]:
        step()
    spread_end(p, g_ref, gathered, rows, *spread)
    end()
    for copy in stores:
        copy.wait()


def middle_kernel(wide, narrow, part, own_ref, gain_ref, mid_ref, gathered, buf, *refs):
    p = Place(wide, narrow)
    rows, dim = own_ref.shape
    bufs, sems, spread = split_refs(narrow, refs)
    enter(p)
    sum_start(p, part, rows, dim, bufs, sems)
    sum_pass(p, part, rows, dim, bufs, sems)
    sum_end(p, part, rows, dim, bufs, sems)

    def body(at):
        u = own_ref[at, :].astype(F32) + total(p, bufs, at)
        mid_ref[at, :] = u
        buf[at, :] = (u * inv_rms(u) * gain_ref[...]).astype(BF)

    row_loop(rows, STEP, body)
    spread_start(p, buf, gathered, rows, *spread)
    spread_pass(p, buf, gathered, rows, *spread)
    spread_end(p, buf, gathered, rows, *spread)


def split_refs(narrow, refs):
    bufs, sems = (3, 5) if narrow == 4 else (1, 3)
    return refs[:bufs], refs[bufs : bufs + sems], refs[bufs + sems :]


def norm_back(u, gain, cot):
    r = inv_rms(u)
    a = cot * gain
    du = r * a - u * (r * r * r) * jnp.mean(a * u, axis=-1, keepdims=True)
    return du, jnp.sum(cot * u * r, axis=0, keepdims=True)


def mlp_back_kernel(
    wide, narrow, g_ref, wd_ref, gu_ref, w_ref, x_ref, mid_ref, gain_ref, grad_ref, back_out, rows_ref, dgain_ref, wgrad,
    g_buf, wd_buf, gu_buf, low, w_buf, x_buf, mid_buf, grad_buf, back_ref, stage, out, load, tiles_in, store, leave, *refs
):
    p = Place(wide, narrow)
    rows, dim = mid_ref.shape
    half = dim // 2
    t = wd_buf.shape[2]
    bufs, sems, _ = split_refs(narrow, refs)

    def tile_of(i):
        slot = lax.rem(i, 2)
        return (
            pltpu.make_async_copy(wd_ref.at[:, pl.ds(pl.multiple_of(i * t, t), t)], wd_buf.at[slot], tiles_in.at[0, slot]),
            pltpu.make_async_copy(gu_ref.at[:, pl.ds(pl.multiple_of(2 * i * t, t), 2 * t)], gu_buf.at[slot], tiles_in.at[1, slot]),
        )

    loads = [pltpu.make_async_copy(g_ref, g_buf, load.at[0])]
    for i in range(2):
        at = pl.ds(i * half, half)
        loads.append(pltpu.make_async_copy(w_ref.at[at], w_buf.at[at], load.at[1 + i]))
    loads.append(pltpu.make_async_copy(x_ref, x_buf, load.at[3]))
    loads.append(pltpu.make_async_copy(mid_ref, mid_buf, load.at[4]))
    loads.append(pltpu.make_async_copy(grad_ref, grad_buf, load.at[5]))
    loads[0].start()
    for copy in tile_of(0):
        copy.start()
    enter(p)
    loads[0].wait()
    count = wd_ref.shape[1] // t

    def gates(i, carry):
        @pl.when(i + 1 < count)
        def _():
            for copy in tile_of(i + 1):
                copy.start()

        for copy in tile_of(i):
            copy.wait()

        @pl.when(i == 0)
        def _():
            for copy in loads[1:3]:
                copy.start()

        slot = lax.rem(i, 2)
        hb = dg(g_buf[...], wd_buf[slot], NN)
        at = pl.multiple_of(2 * i * t, t)
        low[:, pl.ds(at, t)] = (hb * gu_buf[slot, :, :t]).astype(BF)
        low[:, pl.ds(pl.multiple_of(at + t, t), t)] = (hb * gu_buf[slot, :, t:]).astype(BF)
        return carry

    lax.fori_loop(0, count, gates, 0)
    for copy in loads[3:]:
        copy.start()
    for copy in loads[1:3]:
        copy.wait()

    def product(j, i):
        a = low[pl.ds(pl.multiple_of(j * rows, rows), rows), :]
        return dg(a, w_buf[pl.ds(pl.multiple_of(i * half, half), half), :], NT).astype(BF)

    sum_start_of(p, product, out, rows, dim, bufs, sems)
    dgain_ref[...] = jnp.zeros_like(dgain_ref)
    loads[3].wait()
    tile = 256

    def write(i):
        return pltpu.make_async_copy(
            stage.at[lax.rem(i, 2)], wgrad.at[pl.ds(pl.multiple_of(i * tile, tile), tile)], store.at[lax.rem(i, 2)]
        )

    def grads(first, last):
        def one(i, carry):
            @pl.when(i >= 2)
            def _():
                write(i - 2).wait()

            stage[lax.rem(i, 2)] = dg(x_buf[:, pl.ds(pl.multiple_of(i * tile, tile), tile)], low[...], TN).astype(BF)
            write(i).start()
            return carry

        lax.fori_loop(first, last, one, 0)

    tiles = dim // tile
    early = 3
    grads(0, early)
    sum_pass(p, out, rows, dim, bufs, sems, loaded=narrow == 4)
    grads(early, tiles)
    sum_end(p, out, rows, dim, bufs, sems)
    for copy in loads[4:]:
        copy.wait()

    def body(at):
        du, dgain = norm_back(mid_buf[at, :], gain_ref[...], total(p, bufs, at))
        back = grad_buf[at, :].astype(F32) + du
        back_ref[at, :] = back
        pltpu.make_async_copy(back_ref.at[at], back_out.at[at], leave).start()
        rows_ref[at, :] = back.astype(BF)
        dgain_ref[...] += dgain

    row_loop(rows, STEP, body)
    pltpu.make_async_copy(back_ref, back_out, leave).wait()
    write(tiles - 2).wait()
    write(tiles - 1).wait()


def middle_back_kernel(
    wide, narrow, wo_at, groups, hd, rows_ref, hidden, w_ref, wo_ref, o_ref, all_ref, next_ref, back_ref, delta_ref,
    gathered, next_buf, h_buf, w_buf, wo_buf, o_buf, load, store, next_store, *spread
):
    p = Place(wide, narrow)
    rows = rows_ref.shape[0]
    pairs = ((hidden, h_buf), (w_ref, w_buf), (wo_ref.at[:, pl.ds(*wo_at)], wo_buf), (o_ref, o_buf))
    loads = [pltpu.make_async_copy(src, dst, load.at[i]) for i, (src, dst) in enumerate(pairs)]
    enter(p)
    spread_start(p, rows_ref, gathered, rows, *spread)
    for copy in loads:
        copy.start()
    for copy in loads[:2]:
        copy.wait()

    def write_next(i):
        at = pl.ds(pl.multiple_of(i * 256, 256), 256)
        return pltpu.make_async_copy(next_buf.at[at], next_ref.at[at], next_store.at[i])

    def write_slot(j):
        at = pl.ds(pl.multiple_of(j * rows, rows), rows)
        return pltpu.make_async_copy(gathered.at[at], all_ref.at[at], store.at[j])

    def downs(first, last):
        def one(i, carry):
            at = pl.ds(pl.multiple_of(i * 256, 256), 256)
            next_buf[at, :] = dg(h_buf[at, :], w_buf[...], NT).astype(BF)
            write_next(i).start()
            return carry

        lax.fori_loop(first, last, one, 0)

    blocks = next_buf.shape[0] // 256
    downs(0, blocks // 2)

    def on_slot(j):
        at = pl.ds(pl.multiple_of(j * rows, rows), rows)
        write_slot(j).start()
        back = dg(gathered[at, :], wo_buf[...], NN).astype(BF)
        back_ref[at, :] = back
        lane = lax.broadcasted_iota(jnp.int32, (rows, hd), 1)
        out = jnp.zeros((rows, hd), F32)
        for h in range(back.shape[1] // hd):
            mine = slice(h * hd, (h + 1) * hd)
            row = 8 * (h // groups) + h % groups
            delta = jnp.sum(back[:, mine].astype(F32) * o_buf[at, mine], axis=1, keepdims=True)
            out = jnp.where(lane == row, delta, out)
        delta_ref[:, at] = jnp.transpose(out)[: delta_ref.shape[0]]

    spread_pass(p, rows_ref, gathered, rows, *spread)
    downs(blocks // 2, blocks)
    for copy in loads[2:]:
        copy.wait()
    spread_end(p, rows_ref, gathered, rows, *spread, on_slot=on_slot)
    for i in range(blocks):
        write_next(i).wait()
    for j in range(p.N):
        write_slot(j).wait()


def share_start(me, count, here, slots, sends, recvs, device):
    slots[me] = here[...]
    for t in range(count):

        @pl.when(me != t)
        def _():
            wide_at, narrow_at = device(t)
            to(here, slots.at[me], sends.at[t], recvs.at[me], wide_at, narrow_at).start()


def share_end(me, count, here, slots, sends, recvs):
    for t in range(count):

        @pl.when(me != t)
        def _():
            pltpu.make_async_copy(here, slots.at[t], sends.at[t]).wait()
            pltpu.make_async_copy(here, slots.at[t], recvs.at[t]).wait()

    out = slots[0]
    for t in range(1, count):
        out = out + slots[t]
    here[...] = out


def head_back(cot, u, gain, cos, sin):
    cot = cot * cos - turn(cot) * sin
    return norm_back(u, gain, cot)


def output_kernel(
    wide, narrow, part, mid_ref, dkv, dq, qproj, cos_ref, sin_ref, g_ref, x_ref, m_ref, a_ref,
    out_ref, kv_ref, low_ref, dgain_ref, wgrad_out, wgrad_ref, dq_buf, u_buf, x_buf, m_buf, a_buf, load, store, *refs
):
    p = Place(wide, narrow)
    rows, dim = mid_ref.shape
    kv_rows = kv_ref.shape[0]
    width = low_ref.shape[1]
    hd = cos_ref.shape[1]
    bufs, sems, line = split_refs(narrow, refs)
    sums = (part, rows, dim, bufs, sems)
    chain = (p, dkv, kv_rows, line[:5], line[5:])
    pairs = ((dq, dq_buf), (qproj, u_buf), (x_ref, x_buf), (m_ref, m_buf), (a_ref, a_buf))
    loads = [pltpu.make_async_copy(src, dst, load.at[i]) for i, (src, dst) in enumerate(pairs)]
    enter(p, line=True)
    line_sum_start(*chain, ways=DOWN)
    sum_start(p, *sums)
    for copy in loads:
        copy.start()
    first, *steps, last = line_sum_steps(*chain, ways=DOWN)
    first()
    dgain_ref[...] = jnp.zeros_like(dgain_ref)
    for copy in loads[:2]:
        copy.wait()

    def through_heads(at):
        for h in range(width // hd):
            mine = slice(h * hd, (h + 1) * hd)
            du, dgain = head_back(dq_buf[at, mine], u_buf[at, mine], g_ref[...], cos_ref[at, :], sin_ref[at, :])
            low_ref[at, mine] = du.astype(BF)
            dgain_ref[...] += dgain

    row_loop(low_ref.shape[0], 128, through_heads)
    for copy in loads[2:]:
        copy.wait()

    def write(i):
        at = pl.ds(pl.multiple_of(i * 256, 256), 256)
        return pltpu.make_async_copy(wgrad_ref.at[at], wgrad_out.at[at], store.at[i])

    def grads(first_tile, last_tile):
        def one(i, carry):
            at = pl.ds(pl.multiple_of(i * 256, 256), 256)
            wgrad_ref[at, :width] = dg(x_buf[:, at], low_ref[...], TN).astype(BF)
            wgrad_ref[at, width:] = dg(m_buf[:, at], a_buf[...], TN).astype(BF)
            write(i).start()
            return carry

        lax.fori_loop(first_tile, last_tile, one, 0)

    tiles = dim // 256
    grads(0, tiles // 2)
    sum_pass(p, *sums)
    steps[0]()
    grads(tiles // 2, tiles)
    sum_end(p, *sums)

    def body(at):
        out_ref[at, :] = (mid_ref[at, :] + total(p, bufs, at)).astype(BF)

    row_loop(rows, STEP, body)
    for step in steps[1:]:
        step()
    last()
    row_loop(kv_rows, 128, lambda at: kv_ref.__setitem__((at, slice(None)), line[4][at, :].astype(BF)))
    for i in range(tiles):
        write(i).wait()


def input_back_kernel(
    wide, narrow, qw, kw, own_ref, gain_ref, back_ref, mlp_ref, qg_ref, wgrad, q_ref, kv_ref, proj_ref, cos_ref, sin_ref, kg_ref,
    w_ref, x_ref, out_ref, gsum_ref, wsum_ref, kvsum_ref,
    gbuf, gbuf2, low, part, kvgrad, w_buf, x_buf, own_buf, back_buf, load, gsend, grecv, gsend2, grecv2, *refs,
):
    p = Place(wide, narrow)
    rows, dim = own_ref.shape
    hd = cos_ref.shape[1]
    all_rows = x_ref.shape[0]
    w_rows = wsum_ref.shape[0]
    bufs, sems, line = split_refs(narrow, refs)
    sums = (part, rows, dim, bufs, sems)
    first_line = (p, wgrad, w_rows, (*line[:4], wsum_ref), line[4:10])
    second_line = (p, kvgrad, w_rows, (*line[10:14], kvsum_ref), line[14:])
    weights = pltpu.make_async_copy(w_ref.at[:, pl.ds(0, w_buf.shape[1])], w_buf, load.at[0])
    weights.start()
    normed = pltpu.make_async_copy(x_ref, x_buf, load.at[1])
    normed.start()
    later = [pltpu.make_async_copy(own_ref, own_buf, load.at[2]), pltpu.make_async_copy(back_ref, back_buf, load.at[3])]
    for copy in later:
        copy.start()
    enter(p, ring=True)
    line_sum_start(*first_line)
    gsum_ref[...] = jnp.zeros_like(gsum_ref)
    gsum_ref[:, dim : 2 * dim] = mlp_ref[...]
    gsum_ref[:, 2 * dim : 2 * dim + hd] = qg_ref[...]
    size = min(all_rows, 256)
    first = line_sum_steps(*first_line)
    first[0]()
    weights.wait()

    def through_heads(at):
        low[at, :qw] = q_ref[at, :]
        for h in range(kw // hd):
            key = slice(2 * h * hd, (2 * h + 1) * hd)
            value = slice((2 * h + 1) * hd, (2 * h + 2) * hd)
            mine = slice(qw + h * hd, qw + (h + 1) * hd)
            du, dgain = head_back(
                kv_ref[at, key].astype(F32), proj_ref[at, h * hd : (h + 1) * hd], kg_ref[...], cos_ref[at, :], sin_ref[at, :]
            )
            low[at, mine] = du.astype(BF)
            low[at, qw + kw + h * hd : qw + kw + (h + 1) * hd] = kv_ref[at, value]
            gsum_ref[:, 2 * dim + hd :] += dgain
        part[at, :] = dg(low[at, :], w_buf[...], NT).astype(BF)

    row_loop(all_rows, size, through_heads)
    sum_start(p, *sums)
    first[1]()

    normed.wait()

    def key_grads(at):
        kvgrad[at, :] = dg(x_buf[:, at], low[:, qw:], TN).astype(BF)

    row_loop(dim, 256, key_grads)
    line_sum_start(*second_line)
    second = line_sum_steps(*second_line)
    second[0]()
    for step in first[2:-1]:
        step()
    sum_pass(p, *sums)
    for step in second[1:-1]:
        step()
    sum_end(p, *sums)
    for copy in later:
        copy.wait()

    def body(at):
        du, dgain = norm_back(own_buf[at, :].astype(F32), gain_ref[...], total(p, bufs, at))
        out_ref[at, :] = back_buf[at, :] + du
        gsum_ref[:, :dim] += dgain

    row_loop(rows, STEP, body)

    share_start(p.n, narrow, gsum_ref, gbuf, gsend, grecv, lambda t: (p.w, t))
    first[-1]()
    share_end(p.n, narrow, gsum_ref, gbuf, gsend, grecv)
    share_start(p.w, wide, gsum_ref, gbuf2, gsend2, grecv2, lambda t: (t, p.n))
    second[-1]()
    share_end(p.w, wide, gsum_ref, gbuf2, gsend2, grecv2)


VM = pl.BlockSpec(memory_space=pltpu.VMEM)


HB = pl.BlockSpec(memory_space=pl.ANY)


def comm_call(kernel, name, cid, out_shape, in_specs, out_specs, scratch, *args):
    return pl.pallas_call(
        kernel,
        out_shape=out_shape,
        in_specs=in_specs,
        out_specs=out_specs,
        scratch_shapes=scratch,
        compiler_params=pltpu.CompilerParams(collective_id=cid, has_side_effects=True, vmem_limit_bytes=60 << 20),
        cost_estimate=pl.CostEstimate(flops=0, bytes_accessed=160_000_000, transcendentals=0),
        name=name,
    )(*args)


def sds(shape, kind):
    return jax.ShapeDtypeStruct(shape, kind)


def plain(kernel, name, grid, in_specs, out_specs, out_shape, flops, nbytes, *args, scratch=(), aliases=None):
    return pl.pallas_call(
        kernel,
        out_shape=out_shape,
        grid=grid,
        in_specs=in_specs,
        out_specs=out_specs,
        scratch_shapes=scratch,
        input_output_aliases=aliases or {},
        compiler_params=pltpu.CompilerParams(vmem_limit_bytes=52 << 20),
        cost_estimate=pl.CostEstimate(flops=flops, bytes_accessed=nbytes, transcendentals=0),
        name=name,
    )(*args)


def whole(shape):
    return pl.BlockSpec(shape, lambda *i: (0,) * len(shape), pipeline_mode=pl.Buffered(1))


def by_rows(tm, width):
    return pl.BlockSpec((tm, width), lambda i: (i, 0))


def mlp_fwd_kernel(x_ref, w_ref, gu_ref, h_ref):
    t = h_ref.shape[1]
    y = dg(x_ref[...], w_ref[...], NN)
    gate, up = y[:, :t], y[:, t:]
    s = jax.nn.sigmoid(gate)
    silu = gate * s
    h_ref[...] = (silu * up).astype(BF)
    gu_ref[:, :t] = (up * s * (1.0 + gate * (1.0 - s))).astype(BF)
    gu_ref[:, t:] = silu.astype(BF)


def mlp_fwd(x, w, t):
    rows, dim = x.shape
    ff2 = w.shape[1]
    return plain(
        mlp_fwd_kernel, "mlp_fwd", (ff2 // (2 * t),),
        [whole((rows, dim)), pl.BlockSpec((dim, 2 * t), lambda i: (0, i))],
        [pl.BlockSpec((rows, 2 * t), lambda i: (0, i)), pl.BlockSpec((rows, t), lambda i: (0, i))],
        (sds((rows, ff2), BF), sds((rows, ff2 // 2), BF)),
        2 * rows * dim * ff2, rows * dim * 2 + dim * ff2 * 2 + rows * ff2 * 3, x, w,
    )


def fwd_kernel(groups, hd, tab, q_ref, kv_ref, o_ref, low_ref, lse_ref, acc, lsum):
    s = pl.program_id(1)
    block = q_ref.shape[0]
    diag, first, last = tab[2, s], tab[3, s], tab[4, s]

    @pl.when(first == 1)
    def _():
        acc[...] = jnp.zeros_like(acc)
        lsum[...] = jnp.zeros_like(lsum)

    def work(masked):
        k, v = kv_ref[:, :hd], kv_ref[:, hd:]
        for g in range(groups):
            at = slice(g * hd, (g + 1) * hd)
            scores = dg(q_ref[:, at], k, NT)
            if masked:
                row = lax.broadcasted_iota(jnp.int32, scores.shape, 0)
                col = lax.broadcasted_iota(jnp.int32, scores.shape, 1)
                scores = jnp.where(col <= row, scores, MASKED)
            probs = jnp.exp2(scores)
            part = probs[:, :128]
            for j in range(1, block // 128):
                part = part + probs[:, j * 128 : (j + 1) * 128]
            lsum[g] += part
            acc[:, at] += dg(probs.astype(BF), v, NN)

    @pl.when(diag == 0)
    def _():
        work(False)

    @pl.when(diag == 1)
    def _():
        work(True)

    @pl.when(last == 1)
    def _():
        lane = lax.broadcasted_iota(jnp.int32, (block, 128), 1)
        lse = jnp.zeros((block, 128), F32)
        for g in range(groups):
            at = slice(g * hd, (g + 1) * hd)
            l = jnp.sum(lsum[g], axis=1, keepdims=True)
            out = acc[:, at] / l
            o_ref[:, at] = out
            low_ref[:, at] = out.astype(BF)
            lse = jnp.where(lane == g, jnp.log2(l), lse)
        lse_ref[...] = jnp.transpose(lse)[: lse_ref.shape[0]]


def attn_fwd(tab, q, kv, groups, hd, block):
    rows, width = q.shape
    gw = groups * hd
    heads = width // gw
    steps = tab.shape[1]
    mine = pl.BlockSpec((block, gw), lambda h, s, t: (t[0, s], h))
    return pl.pallas_call(
        functools.partial(fwd_kernel, groups, hd),
        out_shape=(sds((rows, width), F32), sds((rows, width), BF), sds((8 * heads, rows), F32)),
        grid_spec=pltpu.PrefetchScalarGridSpec(
            num_scalar_prefetch=1,
            grid=(heads, steps),
            in_specs=[mine, pl.BlockSpec((block, 2 * hd), lambda h, s, t: (t[1, s], h))],
            out_specs=[mine, mine, pl.BlockSpec((8, block), lambda h, s, t: (h, t[0, s]))],
            scratch_shapes=[pltpu.VMEM((block, gw), F32), pltpu.VMEM((groups, block, 128), F32)],
        ),
        compiler_params=pltpu.CompilerParams(vmem_limit_bytes=48 << 20),
        cost_estimate=pl.CostEstimate(
            flops=heads * steps * block * block * gw * 4,
            bytes_accessed=heads * steps * block * hd * 8,
            transcendentals=heads * steps * block * block * groups,
        ),
        name="attn_fwd",
    )(tab, q, kv)


def bwd_kernel(groups, hd, tab, q_ref, do_ref, kv_ref, lse_ref, delta_ref, dq_ref, dkv_ref, dq_sum, dkv_sum):
    s = pl.program_id(1)
    block = q_ref.shape[0]
    qi, diag, first, last = tab[0, s], tab[2, s], tab[3, s], tab[4, s]

    @pl.when(s == 0)
    def _():
        dq_sum[...] = jnp.zeros_like(dq_sum)

    @pl.when(first == 1)
    def _():
        dkv_sum[...] = jnp.zeros_like(dkv_sum)

    def work(masked):
        k, v = kv_ref[:, :hd], kv_ref[:, hd:]
        for g in range(groups):
            at = slice(g * hd, (g + 1) * hd)
            q, do = q_ref[:, at], do_ref[:, at]
            scores = dg(k, q, NT) - lse_ref[g : g + 1, :]
            if masked:
                row = lax.broadcasted_iota(jnp.int32, scores.shape, 0)
                col = lax.broadcasted_iota(jnp.int32, scores.shape, 1)
                scores = jnp.where(row <= col, scores, MASKED)
            probs = jnp.exp2(scores)
            dots = dg(v, do, NT)
            dkv_sum[:, hd:] += dg(probs.astype(BF), do, NN)
            back = (probs * (dots - delta_ref[g : g + 1, :])).astype(BF)
            dkv_sum[:, :hd] += dg(back, q, NN)
            dq_sum[qi, :, at] += dg(back, k, TN)

    @pl.when(diag == 0)
    def _():
        work(False)

    @pl.when(diag == 1)
    def _():
        work(True)

    @pl.when(last == 1)
    def _():
        dkv_ref[:, :hd] = (dkv_sum[:, :hd] * math.log(2.0)).astype(BF)
        dkv_ref[:, hd:] = dkv_sum[:, hd:].astype(BF)

    @pl.when(s == pl.num_programs(1) - 1)
    def _():
        for i in range(dq_sum.shape[0]):
            dq_ref[i * block : (i + 1) * block, :] = dq_sum[i] * hd**-0.5


def attn_bwd(tab, q, do, kv, lse, delta, groups, hd, block):
    rows, width = q.shape
    gw = groups * hd
    heads = width // gw
    steps = tab.shape[1]
    mine = pl.BlockSpec((block, gw), lambda h, s, t: (t[0, s], h))
    keys = pl.BlockSpec((block, 2 * hd), lambda h, s, t: (t[1, s], h))
    stat = pl.BlockSpec((8, block), lambda h, s, t: (h, t[0, s]))
    return pl.pallas_call(
        functools.partial(bwd_kernel, groups, hd),
        out_shape=(sds((rows, width), F32), sds(kv.shape, BF)),
        grid_spec=pltpu.PrefetchScalarGridSpec(
            num_scalar_prefetch=1,
            grid=(heads, steps),
            in_specs=[mine, mine, keys, stat, stat],
            out_specs=[pl.BlockSpec((rows, gw), lambda h, s, t: (0, h)), keys],
            scratch_shapes=[pltpu.VMEM((rows // block, block, gw), F32), pltpu.VMEM((block, 2 * hd), F32)],
        ),
        compiler_params=pltpu.CompilerParams(vmem_limit_bytes=48 << 20),
        cost_estimate=pl.CostEstimate(
            flops=heads * steps * block * block * gw * 10,
            bytes_accessed=heads * steps * block * hd * 16,
            transcendentals=heads * steps * block * block * groups,
        ),
        name="attn_bwd",
    )(tab, q, do, kv, lse, delta)


def place(w):
    k, core = w // 2, w % 2
    return 4 * k + core, 4 * k + 3 - core


def block_row(b):
    m = b % 4
    core = jnp.where((m == 1) | (m == 2), 1, 0)
    return 2 * (2 * (b // 4) + core) + jnp.where(m < 2, 0, 1)


def tables(w, chips):
    a, b = place(w)
    count = a + b + 2
    every = jnp.arange(8 * chips - 2, dtype=jnp.int32)
    s, idle = jnp.minimum(every, count - 1), every >= count
    in_a = s <= a
    key = jnp.where(in_a, s, s - a - 1)
    diag = jnp.where(in_a, s == a, s == count - 1)
    fwd = [jnp.where(in_a, 0, 1), block_row(key), jnp.where(idle, 2, diag), ~idle & (key == 0), ~idle & diag]
    both = s < 2 * (a + 1)
    even = s % 2 == 0
    key = jnp.where(both, s // 2, s - (a + 1))
    query = jnp.where(both & even, 0, 1)
    diag = key == jnp.where(query == 0, a, b)
    zero = (every >= count) & (w % 2 == 1)
    key = jnp.where(zero, b + 1, key)
    only = zero & (every == count)
    bwd = [query, block_row(key), jnp.where(idle, 2, diag), only | ~idle & (~both | even), only | ~idle & (~both | ~even)]
    return tuple(jnp.stack([row.astype(jnp.int32) for row in rows]) for rows in (fwd, bwd))


def per_device(
    wide, narrow,
    layer_input, w_query, w_key, w_value, w_output, w_gate, w_up, w_down,
    attn_gain, mlp_gain, query_gain, key_gain, out_grad,
):
    hd = query_gain.shape[0]
    rows, dim = layer_input.shape
    all_rows = narrow * rows
    chips = wide // 2
    block = all_rows // 2
    qw, kw = w_query.shape[1], w_key.shape[1]
    ff = w_gate.shape[1]
    groups = qw // kw
    kv_heads = kw // hd
    w = lax.axis_index("wide")
    fwd_tab, bwd_tab = tables(w, chips)
    def gather(shard):
        return lax.all_gather(shard, "wide", axis=0, tiled=True)

    def scatter(grad):
        return lax.psum_scatter(grad, "wide", scatter_dimension=0, tiled=True)

    t = math.gcd(ff, 256)

    spread_s = spread_sems(narrow)
    sum_s = [*sum_bufs(narrow, rows, dim), *sum_sems(narrow)]
    row_buf = pltpu.VMEM((rows, dim), BF)
    low_rows, full_rows, all_low = sds((rows, dim), BF), sds((rows, dim), F32), sds((all_rows, dim), BF)
    ring = functools.partial
    qg, kg = query_gain[None], key_gain[None]
    after = lax.optimization_barrier

    in_scratch = [*spread_s, *line_sems(chips)]
    table = sds((all_rows, hd), F32)
    s_rows, s_cols = w_query.shape[0], 2 * qw + 2 * kw
    normed_all, w_attn, gu_shard, d_shard, cos_table, sin_table = comm_call(
        ring(input_kernel, wide, narrow), "input_rows", 0,
        (all_low, sds((dim, s_cols), BF), sds((s_rows, 2 * ff), BF), sds((s_rows, ff), BF), table, table),
        [VM] * 9, (HB, HB, VM, VM, VM, VM), [row_buf, pltpu.VMEM((s_rows, s_cols), BF), *in_scratch],
        layer_input, attn_gain[None], w_query, w_key, w_value, w_output, w_gate, w_up, w_down,
    )
    width = qw + 2 * kw
    grad_all, kv, query_proj, key_proj, queries = comm_call(
        ring(qkv_kernel, wide, narrow, qw, kw, hd**-0.5 * math.log2(math.e)), "qkv_rows", 1,
        (all_low, sds((wide * all_rows, 2 * kw), BF), sds((all_rows, qw), F32),
         sds((all_rows, kw), F32), sds((all_rows, qw), BF)),
        [VM, HB, HB, VM, VM, VM, VM], (HB, HB, HB, HB, HB),
        [pltpu.VMEM((all_rows, qw), F32), pltpu.VMEM((all_rows, kw), F32), pltpu.VMEM((all_rows, qw), BF),
         pltpu.VMEM((all_rows, 2 * kw), BF), pltpu.VMEM((dim, width), BF),
         pltpu.VMEM((all_rows, dim), BF), DMA((2,)), DMA((3,)), *in_scratch],
        out_grad, normed_all, w_attn, cos_table, sin_table, qg, kg,
    )
    gu_shard, d_shard, kv = after((gu_shard, d_shard, kv))
    w_gu, w_d = gather(gu_shard), gather(d_shard)
    attended, attended_low, lse = attn_fwd(fwd_tab, queries, kv, groups, hd, block)
    w_o = w_attn[:, qw + 2 * kw :]
    middle, normed_mlp = comm_call(
        ring(middle_kernel, wide, narrow), "middle_rows", 2, (full_rows, all_low), [HB, VM, VM], (VM, HB),
        [row_buf, *sum_s, *spread_s], dg(attended_low, w_o, NT).astype(BF), layer_input, mlp_gain[None],
    )
    factors, hidden_low = mlp_fwd(normed_mlp, w_gu, t)
    grad_down = dg(grad_all, hidden_low, TN).astype(BF)
    w_d, _ = after((w_d, grad_down))
    middle_back, middle_low, mlp_gain_part, grad_gu = comm_call(
        ring(mlp_back_kernel, wide, narrow), "mlp_back", 6,
        (full_rows, low_rows, sds((1, dim), F32), sds((dim, 2 * ff), BF)), [HB, HB, HB, HB, HB, HB, VM, HB], (HB, VM, VM, HB),
        [pltpu.VMEM((all_rows, dim), BF), pltpu.VMEM((2, dim, t), BF), pltpu.VMEM((2, all_rows, 2 * t), BF),
         pltpu.VMEM((all_rows, 2 * ff), BF), pltpu.VMEM((dim, 2 * ff), BF), pltpu.VMEM((all_rows, dim), BF),
         pltpu.VMEM((rows, dim), F32), row_buf, pltpu.VMEM((rows, dim), F32), pltpu.VMEM((2, 256, 2 * ff), BF),
         product_bufs(narrow, rows, dim), DMA((6,)), DMA((2, 2)), DMA((2,)), DMA, *sum_s],
        grad_all, w_d, factors, w_gu, normed_mlp, middle, mlp_gain[None], out_grad,
    )
    grad_down, grad_gu = scatter(grad_down), scatter(grad_gu)
    middle_all, down_part, back, delta = comm_call(
        ring(middle_back_kernel, wide, narrow, (width, qw), groups, hd), "middle_back", 3,
        (all_low, all_low, sds((all_rows, qw), BF), sds((8 * kv_heads, all_rows), F32)),
        [VM, HB, HB, HB, HB], (HB, HB, VM, VM),
        [pltpu.VMEM((all_rows, dim), BF), pltpu.VMEM((all_rows, dim), BF), pltpu.VMEM((all_rows, ff), BF), pltpu.VMEM((dim, ff), BF), pltpu.VMEM((dim, qw), BF), pltpu.VMEM((all_rows, qw), F32),
         DMA((4,)), DMA((narrow,)), DMA((all_rows // 256,)), *spread_s],
        middle_low, hidden_low, w_d, w_attn, attended,
    )
    query_back, dkv = attn_bwd(bwd_tab, queries, back, kv, lse, delta, groups, hd, block)
    dkv, grad_down = after((dkv, grad_down))
    layer_output, kv_sum, q_low, query_gain_part, grad_qo = comm_call(
        ring(output_kernel, wide, narrow), "output_rows", 4,
        (low_rows, sds((all_rows, 2 * kw), BF), sds((all_rows, qw), BF), sds((1, hd), F32), sds((dim, 2 * qw), BF)),
        [HB, VM, HB, HB, HB, VM, VM, VM, HB, HB, HB], (VM, VM, VM, VM, HB),
        [pltpu.VMEM((dim, 2 * qw), BF), pltpu.VMEM((all_rows, qw), F32), pltpu.VMEM((all_rows, qw), F32), pltpu.VMEM((all_rows, dim), BF),
         pltpu.VMEM((all_rows, dim), BF), pltpu.VMEM((all_rows, qw), BF), DMA((5,)), DMA((dim // 256,)), *sum_s,
         *line_sum_bufs(chips, all_rows, 2 * kw), *line_sum_sems(chips)],
        down_part, middle, dkv, query_back, query_proj, cos_table, sin_table, qg, normed_all, middle_all, attended_low,
    )
    kv_sum, grad_gu = after((kv_sum, grad_gu))
    gains = sds((1, 2 * dim + 2 * hd), F32)
    w_rows = dim // wide
    input_grad, gain_sums, grad_qo, grad_kv = comm_call(
        ring(input_back_kernel, wide, narrow, qw, kw), "input_back", 5,
        (full_rows, gains, sds((w_rows, 2 * qw), F32), sds((w_rows, 2 * kw), F32)),
        [HB, VM, HB, VM, VM, HB, VM, VM, VM, VM, VM, VM, HB, HB],
        (VM, VM, VM, VM),
        [pltpu.VMEM((narrow, *gains.shape), F32), pltpu.VMEM((wide, *gains.shape), F32),
         pltpu.VMEM((all_rows, width), BF), pltpu.VMEM((all_rows, dim), BF), pltpu.VMEM((dim, 2 * kw), BF),
         pltpu.VMEM((dim, width), BF), pltpu.VMEM((all_rows, dim), BF),
         row_buf, pltpu.VMEM((rows, dim), F32), DMA((4,)), DMA((narrow,)), DMA((narrow,)), DMA((wide,)), DMA((wide,)), *sum_s,
         *line_sum_bufs(chips, w_rows, 2 * qw)[:4], *line_sum_sems(chips),
         *line_sum_bufs(chips, w_rows, 2 * kw)[:4], *line_sum_sems(chips)],
        layer_input, attn_gain[None], middle_back, mlp_gain_part, query_gain_part, grad_qo, q_low, kv_sum, key_proj, cos_table, sin_table, kg, w_attn, normed_all,
    )
    tm = min(w_rows, 128)
    turned = lambda height: pl.BlockSpec((height, tm), lambda i: (0, i))
    grads = plain(
        finish_kernel, "finish", (w_rows // tm,),
        [by_rows(tm, 2 * ff), by_rows(tm, ff), by_rows(tm, 2 * qw), by_rows(tm, 2 * kw)],
        [by_rows(tm, ff), by_rows(tm, ff), turned(ff), by_rows(tm, qw), by_rows(tm, kw), by_rows(tm, kw), turned(qw)],
        [sds(shape, F32) for shape in (w_gate.shape, w_up.shape, w_down.shape, w_query.shape, w_key.shape, w_value.shape,
                                       w_output.shape)],
        0, 10 * dim // wide * (3 * ff + qw), grad_gu, grad_down, grad_qo, grad_kv,
    )
    grad_gate, grad_up, grad_down, grad_query, grad_key, grad_value, grad_output = grads
    g = gain_sums[0]
    return (
        layer_output, input_grad, grad_query, grad_key, grad_value, grad_output, grad_gate, grad_up, grad_down,
        g[:dim], g[dim : 2 * dim], g[2 * dim : 2 * dim + hd], g[2 * dim + hd :],
    )


def solution(mesh):
    rows = P(("wide", "narrow"), None)
    weight, turned = P("wide", "narrow"), P("narrow", "wide")
    return jax.shard_map(
        functools.partial(per_device, mesh.shape["wide"], mesh.shape["narrow"]),
        mesh=mesh,
        in_specs=(rows, weight, weight, weight, turned, weight, weight, turned, P(), P(), P(), P(), rows),
        out_specs=(rows, rows, weight, weight, weight, turned, weight, weight, turned, P(), P(), P(), P()),
        check_vma=False,
    )
```

```python
import functools
import math

import jax
import jax.numpy as jnp
from jax import lax
from jax.experimental import pallas as pl
from jax.experimental.pallas import tpu as pltpu
from jax.sharding import PartitionSpec as P

EPSILON = 1e-06
MASKED = -1e30
F32 = jnp.float32
BF = jnp.bfloat16
MESH = pl.DeviceIdType.MESH
NT = (((1,), (1,)), ((), ()))
NN = (((1,), (0,)), ((), ()))
TN = (((0,), (0,)), ((), ()))


def dg(a, b, dims):
    return lax.dot_general(a, b, dims, preferred_element_type=F32)
DMA = pltpu.SemaphoreType.DMA


class Place:
    def __init__(self, wide, narrow):
        self.W, self.N = wide, narrow
        self.C, self.half = wide // 2, narrow // 2
        self.w, self.n = lax.axis_index("wide"), lax.axis_index("narrow")
        self.k, self.c = self.w // 2, lax.rem(self.w, 2)
        late = (self.n >= self.half).astype(jnp.int32)
        self.group = lax.rem(self.c + late, 2)
        self.slot = jnp.where(self.group == 0, self.n, lax.rem(self.n + self.half, self.N))

    def owner(self, j):
        core = 1 if j >= self.half else 0
        n = jnp.where(self.c == 0, j, (j + self.half) % self.N)
        return core, n

    def owner_is_me(self, j):
        core, n = self.owner(j)
        return (self.c == core) & (self.n == n)


def enter(p, line=False, ring=False):
    barrier = pltpu.get_barrier_semaphore()

    def greet(device):
        pl.semaphore_signal(barrier, inc=1, device_id=device, device_id_type=MESH)

    for core in range(2):
        for n in range(p.N):

            @pl.when((p.c != core) | (p.n != n))
            def _():
                greet((2 * p.k + core, n))

    peers = 2 * p.N - 1
    if line or ring:
        for k in range(p.C):

            @pl.when(p.k != k)
            def _():
                greet((2 * k + p.c, p.n))
                if ring:
                    greet((2 * k + 1 - p.c, p.n))

        peers += (2 if ring else 1) * (p.C - 1)
    pl.semaphore_wait(barrier, peers)


def slot_of(p, n, group):
    return jnp.where(group == 0, n, lax.rem(n + p.half, p.N))


def neighbours(p):
    return p.n + 1 - 2 * lax.rem(p.n, 2), lax.rem(p.n + 2, 4), 3 - p.n


def to(src, dst, send, recv, wide, narrow):
    return pltpu.make_async_remote_copy(
        src_ref=src, dst_ref=dst, send_sem=send, recv_sem=recv, device_id=(wide, narrow), device_id_type=MESH
    )


def spread_sems(narrow):
    return [DMA((narrow, 2)), DMA((narrow, 2)), DMA((2,)), DMA((2,))]


def spread_start(p, src, gathered, rows, send, recv, local, onward):
    half = rows // 2
    view = lambda i: gathered.at[pl.ds(pl.multiple_of(p.slot * rows + i * half, half), half)]
    part = lambda i: src.at[pl.ds(i * half, half)]
    mine = p.group == p.c
    square = p.N == 4
    if square:
        nx, ny, _ = neighbours(p)
        targets = [(nx, (0, 1)), (ny, (1, 0))]
        order = [(t, q, i) for q in range(2) for t, halves in targets for i in (halves[q],)]
        for t, q, i in order:
            at = 0 if t is nx else 1
            to(part(i), view(i), send.at[at, i], recv.at[p.slot, i], 2 * p.k + p.group, t).start()
    else:
        for t in range(p.N):

            @pl.when(p.n != t)
            def _():
                for i in range(2):
                    to(part(i), view(i), send.at[t, i], recv.at[p.slot, i], 2 * p.k + p.group, t).start()

    @pl.when(mine)
    def _():
        for i in range(2):
            pltpu.make_async_copy(part(i), view(i), local.at[i]).start()

    @pl.when(jnp.logical_not(mine))
    def _():
        for i in range(2):
            to(part(i), view(i), local.at[i], recv.at[p.slot, i], 2 * p.k + p.group, p.n).start()


def spread_pass(p, src, gathered, rows, send, recv, local, onward):
    if p.N == 4:
        half = rows // 2
        piece = src.at[pl.ds(0, half)]
        nx, ny, _ = neighbours(p)
        for i, (n, other) in enumerate(((nx, ny), (ny, nx))):
            j = slot_of(p, n, p.c)
            here = gathered.at[pl.ds(pl.multiple_of(j * rows + i * half, half), half)]
            pltpu.make_async_copy(piece, here, recv.at[j, i]).wait()
            to(here, here, onward.at[i], recv.at[j, i], p.w, other).start()


def spread_end(p, src, gathered, rows, send, recv, local, onward, on_slot=lambda j: None):
    half = rows // 2
    piece = src.at[pl.ds(0, half)]
    mine = p.group == p.c
    at = lambda j, i: gathered.at[pl.ds(pl.multiple_of(j * rows + i * half, half), half)]

    def arrive(j, i):
        pltpu.make_async_copy(piece, at(j, i), recv.at[j, i]).wait()

    for i in range(2):
        pltpu.make_async_copy(piece, at(0, 0), local.at[i]).wait()
    here = slot_of(p, p.n, p.c)

    @pl.when(jnp.logical_not(mine))
    def _():
        arrive(here, 0)
        arrive(here, 1)

    on_slot(here)
    if p.N == 4:
        nx, ny, nd = neighbours(p)
        jx, jy, jd = (slot_of(p, n, p.c) for n in (nx, ny, nd))
        arrive(jx, 1)
        on_slot(jx)
        arrive(jy, 0)
        on_slot(jy)
        arrive(jd, 0)
        arrive(jd, 1)
        on_slot(jd)
        for i in range(2):
            pltpu.make_async_copy(piece, at(0, 0), onward.at[i]).wait()
            for t in range(2):
                pltpu.make_async_copy(piece, at(0, 0), send.at[t, i]).wait()
    else:
        for t in range(p.N):

            @pl.when(p.n != t)
            def _():
                for i in range(2):
                    pltpu.make_async_copy(piece, at(0, 0), send.at[t, i]).wait()
                    arrive(slot_of(p, t, p.c), i)
                on_slot(slot_of(p, t, p.c))


def sum_bufs(narrow, rows, dim):
    if narrow == 4:
        half = pltpu.VMEM((2, 2, rows, dim // 2), BF)
        return [half, half, pltpu.VMEM((2, rows, dim), BF)]
    return [pltpu.VMEM((narrow, rows, dim), BF)]


def sum_sems(narrow):
    if narrow == 4:
        return [DMA((2, 2)), DMA((2, 2)), DMA((2, 2)), DMA((4,)), DMA((4,))]
    return [DMA((narrow,)), DMA((narrow,)), DMA]


def pieces(p, part, rows, dim):
    half = dim // 2
    return lambda j, i: part.at[pl.ds(pl.multiple_of(j * rows, rows), rows), pl.ds(i * half, half)]


def sum_start(p, part, rows, dim, bufs, sems):
    if p.N != 4:
        (got,), (send, recv, local) = bufs, sems
        for j in range(p.N):
            core, n = p.owner(j)
            mine = p.owner_is_me(j)
            src = part.at[pl.ds(j * rows, rows)]

            @pl.when(mine)
            def _():
                pltpu.make_async_copy(src, got.at[p.n], local).start()

            @pl.when(jnp.logical_not(mine))
            def _():
                to(src, got.at[p.n], send.at[j], recv.at[p.n], 2 * p.k + core, n).start()

        return
    own, inbox, _ = bufs
    load, send, recv, _, _ = sems
    piece = pieces(p, part, rows, dim)
    nx, ny, nd = neighbours(p)
    across, here = slot_of(p, nd, p.c), slot_of(p, p.n, p.c)
    for i, n in enumerate((nx, ny)):
        to(piece(across, i), inbox.at[i, 0], send.at[i, 0], recv.at[i, 0], p.w, n).start()
    for i, n in enumerate((ny, nx)):
        pltpu.make_async_copy(piece(slot_of(p, n, p.c), i), own.at[i, 0], load.at[i, 0]).start()
    for i, n in enumerate((nx, ny)):
        to(piece(slot_of(p, n, p.c), i), inbox.at[i, 1], send.at[i, 1], recv.at[i, 1], p.w, n).start()
        pltpu.make_async_copy(piece(here, i), own.at[i, 1], load.at[i, 1]).start()


def product_bufs(narrow, rows, dim):
    shape = (4, rows, dim // 2) if narrow == 4 else (narrow * rows, dim)
    return pltpu.VMEM(shape, BF)


def sum_start_of(p, product, out, rows, dim, bufs, sems):
    half = dim // 2
    if p.N != 4:

        def one(j, carry):
            for i in range(2):
                out[pl.ds(pl.multiple_of(j * rows, rows), rows), i * half : (i + 1) * half] = product(j, i)
            return carry

        lax.fori_loop(0, p.N, one, 0)
        sum_start(p, out, rows, dim, bufs, sems)
        return
    own, inbox, _ = bufs
    _, send, recv, _, _ = sems
    nx, ny, nd = neighbours(p)
    across, jx, jy, here = (slot_of(p, n, p.c) for n in (nd, nx, ny, p.n))

    def one(t, carry):
        i = lax.rem(t, 2)
        q = lax.rem(t // 2, 2)
        beside = jnp.where(i == 0, jx, jy)
        other = jnp.where(i == 0, jy, jx)
        j = jnp.where(t < 4, jnp.where(q == 0, across, beside), jnp.where(q == 0, other, here))
        y = product(j, i)

        @pl.when(t < 4)
        def _():
            out[t] = y
            to(out.at[t], inbox.at[i, q], send.at[i, q], recv.at[i, q], p.w, jnp.where(i == 0, nx, ny)).start()

        @pl.when(t >= 4)
        def _():
            own[i, q] = y

        return carry

    lax.fori_loop(0, 8, one, 0)


def core_of(p, j):
    return (j >= p.half).astype(jnp.int32)


def sum_pass(p, part, rows, dim, bufs, sems, loaded=False):
    if p.N != 4:
        return
    own, inbox, box = bufs
    load, send, recv, send2, recv2 = sems
    piece = lambda j, i: own.at[0, 0]
    half = dim // 2
    nx, ny, _ = neighbours(p)
    cols = lambda i: pl.ds(i * half, half)

    def add(i, q):
        if not loaded:
            pltpu.make_async_copy(piece(0, 0), own.at[i, q], load.at[i, q]).wait()
        pltpu.make_async_copy(piece(0, 0), inbox.at[i, q], recv.at[i, q]).wait()

        def body(at):
            own[i, q, at, :] = (own[i, q, at, :].astype(F32) + inbox[i, q, at, :].astype(F32)).astype(BF)

        row_loop(rows, 64, body)

    for i, n in enumerate((ny, nx)):
        add(i, 0)
        j = slot_of(p, n, p.c)
        to(own.at[i, 0], box.at[1, :, cols(i)], send2.at[i], recv2.at[i], 2 * p.k + core_of(p, j), n).start()
    j = slot_of(p, p.n, p.c)
    keep = core_of(p, j) == p.c
    for i in range(2):
        add(i, 1)

        @pl.when(keep)
        def _():
            pltpu.make_async_copy(own.at[i, 1], box.at[0, :, cols(i)], send2.at[2 + i]).start()

        @pl.when(jnp.logical_not(keep))
        def _():
            to(own.at[i, 1], box.at[0, :, cols(i)], send2.at[2 + i], recv2.at[2 + i], 2 * p.k + core_of(p, j), p.n).start()


def sum_end(p, part, rows, dim, bufs, sems):
    if p.N != 4:
        (got,), (send, recv, local) = bufs, sems
        for t in range(p.N):
            mine = (p.group == p.c) & (p.n == t)

            @pl.when(mine)
            def _():
                pltpu.make_async_copy(part.at[pl.ds(0, rows)], got.at[t], local).wait()

            @pl.when(jnp.logical_not(mine))
            def _():
                pltpu.make_async_copy(part.at[pl.ds(0, rows)], got.at[t], recv.at[t]).wait()

        for j in range(p.N):

            @pl.when(jnp.logical_not(p.owner_is_me(j)))
            def _():
                pltpu.make_async_copy(part.at[pl.ds(j * rows, rows)], got.at[0], send.at[j]).wait()

        return
    own, inbox, box = bufs
    load, send, recv, send2, recv2 = sems
    piece = lambda j, i: own.at[0, 0]
    half = dim // 2
    cols = lambda i: pl.ds(i * half, half)
    for i in range(2):
        for q in range(2):
            pltpu.make_async_copy(piece(0, 0), inbox.at[i, q], send.at[i, q]).wait()
        pltpu.make_async_copy(own.at[i, 0], box.at[1, :, cols(i)], send2.at[i]).wait()
        pltpu.make_async_copy(own.at[i, 0], box.at[1, :, cols(i)], recv2.at[i]).wait()
        pltpu.make_async_copy(own.at[i, 1], box.at[0, :, cols(i)], send2.at[2 + i]).wait()

        @pl.when(p.group != p.c)
        def _():
            pltpu.make_async_copy(own.at[i, 1], box.at[0, :, cols(i)], recv2.at[2 + i]).wait()


def total(p, bufs, at):
    if p.N == 4:
        box = bufs[2]
        return box[0, at, :].astype(F32) + box[1, at, :].astype(F32)
    got = bufs[0]
    out = got[0, at, :].astype(F32)
    for t in range(1, p.N):
        out = out + got[t, at, :].astype(F32)
    return out


PARTS = 4


def line_sems(chips):
    return [DMA((2, chips, PARTS)), DMA((chips, PARTS)), DMA((chips, PARTS)), DMA((chips, PARTS)), DMA((PARTS,))]


def line_parts(p, full, rows):
    size = rows // PARTS

    def at(s, core, q=None):
        first = (2 * s + core) * rows
        if q is None:
            return full.at[pl.ds(pl.multiple_of(first, rows), rows)]
        return full.at[pl.ds(pl.multiple_of(first + q * size, size), size)]

    return at


def each_part(body):
    def one(q, carry):
        body(q)
        return carry

    lax.fori_loop(0, PARTS, one, 0)


def line_copy(p, src, dst, send, recv, k, core):
    return pltpu.make_async_remote_copy(
        src_ref=src, dst_ref=dst, send_sem=send, recv_sem=recv, device_id=(2 * k + core, p.n), device_id_type=MESH
    )


def inside(p, k):
    return (k >= 0) & (k < p.C)


BOTH, UP, DOWN = ((0, 1), (1, -1)), ((0, 1),), ((1, -1),)


def line_push(p, src, full, rows, zsend, zrecv, csend, crecv, local, q, ways=BOTH):
    size = rows // PARTS
    part = src.at[pl.ds(pl.multiple_of(q * size, size), size)]
    there = line_parts(p, full, rows)(p.k, p.c, q)
    for i, sign in ways:

        @pl.when(inside(p, p.k + sign))
        def _():
            line_copy(p, part, there, zsend.at[i, 0, q], zrecv.at[p.k, q], p.k + sign, p.c).start()

    line_copy(p, part, there, csend.at[p.k, q], crecv.at[p.k, q], p.k, 1 - p.c).start()
    pltpu.make_async_copy(part, there, local.at[q]).start()


def came(p, s, ways):
    if ways == BOTH:
        return s == s
    return s <= p.k if ways == UP else s >= p.k


def line_steps(p, src, full, rows, zsend, zrecv, csend, crecv, local, ways=BOTH):
    at = line_parts(p, full, rows)
    piece = src.at[pl.ds(0, rows // PARTS)]

    def at_distance(d):
        def onward(q):
            for i, sign in ways:
                s, t = p.k - sign * d, p.k + sign

                @pl.when(inside(p, s))
                def _():
                    here = at(s, p.c, q)
                    pltpu.make_async_copy(piece, here, zrecv.at[s, q]).wait()

                    @pl.when(inside(p, t))
                    def _():
                        line_copy(p, here, here, zsend.at[i, d, q], zrecv.at[s, q], t, p.c).start()

                    line_copy(p, here, here, csend.at[s, q], crecv.at[s, q], p.k, 1 - p.c).start()

        each_part(onward)

    def settle(q):
        here = at(p.k, p.c, q)
        pltpu.make_async_copy(piece, here, local.at[q]).wait()
        for s in range(p.C):

            @pl.when(came(p, jnp.int32(s), ways))
            def _():
                pltpu.make_async_copy(piece, here, csend.at[s, q]).wait()
                pltpu.make_async_copy(piece, at(s, 1 - p.c, q), crecv.at[s, q]).wait()

        for i, sign in ways:
            for d in range(p.C):

                @pl.when(inside(p, p.k - sign * d) & inside(p, p.k + sign))
                def _():
                    pltpu.make_async_copy(piece, here, zsend.at[i, d, q]).wait()

    return [functools.partial(at_distance, d) for d in range(1, p.C)] + [lambda: each_part(settle)]


def line_sum_bufs(chips, rows, width):
    return [pltpu.VMEM((chips, rows, width), BF)] * 3 + [pltpu.VMEM((2, rows, width), BF), pltpu.VMEM((rows, width), F32)]


def line_sum_sems(chips):
    return [
        DMA((chips, PARTS)), DMA((chips, PARTS)), DMA((chips, PARTS)), DMA((2, chips, PARTS)), DMA((chips, PARTS)),
        DMA((2, PARTS)),
    ]


OTHER = {BOTH: BOTH, UP: DOWN, DOWN: UP}


def line_sum_start(p, part, rows, bufs, sems, ways=BOTH):
    own, inbox, _, _, _ = bufs
    load, csend, crecv, _, _, _ = sems
    at = line_parts(p, part, rows)
    size = rows // PARTS

    def share(s):
        def one(q):
            here = pl.ds(pl.multiple_of(q * size, size), size)
            line_copy(p, at(s, 1 - p.c, q), inbox.at[s, here], csend.at[s, q], crecv.at[s, q], p.k, 1 - p.c).start()
            pltpu.make_async_copy(at(s, p.c, q), own.at[s, here], load.at[s, q]).start()

        each_part(one)

    for d in range(p.C - 1, 0, -1):
        for _, sign in ways:
            s = p.k + sign * d

            @pl.when(inside(p, s))
            def _():
                share(s)

    share(p.k)


def line_sum_steps(p, part, rows, bufs, sems, ways=BOTH):
    own, inbox, relay, box, acc = bufs
    load, csend, crecv, zsend, rrecv, zrecv = sems
    size = rows // PARTS
    step = math.gcd(size, 128)
    piece = line_parts(p, part, rows)(0, 0, 0)

    def rows_of(q):
        return pl.ds(pl.multiple_of(q * size, size), size)

    def add(q, body):
        def one(j, carry):
            body(pl.ds(pl.multiple_of(q * size + j * step, step), step))
            return carry

        lax.fori_loop(0, size // step, one, 0)

    def pair(t, q):
        pltpu.make_async_copy(piece, own.at[t, rows_of(q)], load.at[t, q]).wait()
        pltpu.make_async_copy(piece, inbox.at[t, rows_of(q)], crecv.at[t, q]).wait()

    def at_distance(d):
        def onward(q):
            here = rows_of(q)
            for i, sign in ways:
                t = p.k + sign * d
                behind = inside(p, p.k - sign)

                @pl.when(inside(p, t))
                def _():
                    pair(t, q)

                    @pl.when(jnp.logical_not(behind))
                    def _():
                        def two(at):
                            own[t, at, :] = (own[t, at, :].astype(F32) + inbox[t, at, :].astype(F32)).astype(BF)

                        add(q, two)

                    @pl.when(behind)
                    def _():
                        pltpu.make_async_copy(piece, relay.at[t, here], rrecv.at[t, q]).wait()

                        def three(at):
                            both = own[t, at, :].astype(F32) + inbox[t, at, :].astype(F32)
                            own[t, at, :] = (both + relay[t, at, :].astype(F32)).astype(BF)

                        add(q, three)

                    src = own.at[t, here]
                    if d >= 2:
                        line_copy(p, src, relay.at[t, here], zsend.at[i, d, q], rrecv.at[t, q], p.k + sign, p.c).start()
                    else:
                        line_copy(p, src, box.at[i, here], zsend.at[i, d, q], zrecv.at[i, q], t, p.c).start()

        each_part(onward)

    def last(q):
        here = rows_of(q)
        pair(p.k, q)

        def first(at):
            acc[at, :] = own[p.k, at, :].astype(F32) + inbox[p.k, at, :].astype(F32)

        add(q, first)
        for i, sign in ways:

            @pl.when(inside(p, p.k - sign))
            def _():
                pltpu.make_async_copy(piece, box.at[i, here], zrecv.at[i, q]).wait()

                def more(at):
                    acc[at, :] += box[i, at, :].astype(F32)

                add(q, more)

            for d in range(1, p.C):

                @pl.when(inside(p, p.k + sign * d))
                def _():
                    pltpu.make_async_copy(piece, own.at[0, here], zsend.at[i, d, q]).wait()

        for s in range(p.C):

            @pl.when(came(p, jnp.int32(s), OTHER[ways]))
            def _():
                pltpu.make_async_copy(piece, inbox.at[s, here], csend.at[s, q]).wait()


    return [functools.partial(at_distance, d) for d in range(p.C - 1, 0, -1)] + [lambda: each_part(last)]


def row_loop(rows, step, body):
    def one(i, carry):
        body(pl.ds(pl.multiple_of(i * step, step), step))
        return carry

    lax.fori_loop(0, rows // step, one, 0)


STEP = 64


def inv_rms(u):
    return lax.rsqrt(jnp.mean(u * u, axis=-1, keepdims=True) + EPSILON)


def weave(gate_ref, up_ref, both_ref):
    ff = gate_ref.shape[1]
    t = math.gcd(ff, 256)
    for i in range(0, ff, t):
        both_ref[:, 2 * i : 2 * i + t] = gate_ref[:, i : i + t]
        both_ref[:, 2 * i + t : 2 * i + 2 * t] = up_ref[:, i : i + t]


def finish_kernel(both_ref, down_ref, qo_ref, kv_ref, gate_out, up_out, down_out, q_out, k_out, v_out, o_out):
    ff = gate_out.shape[1]
    t = math.gcd(ff, 256)
    for i in range(0, ff, t):
        gate_out[:, i : i + t] = both_ref[:, 2 * i : 2 * i + t].astype(F32)
        up_out[:, i : i + t] = both_ref[:, 2 * i + t : 2 * i + 2 * t].astype(F32)
    down_out[...] = jnp.transpose(down_ref[...].astype(F32))
    qw, kw = q_out.shape[1], k_out.shape[1]
    q_out[...] = qo_ref[:, :qw]
    o_out[...] = jnp.transpose(qo_ref[:, qw:])
    k_out[...] = kv_ref[:, :kw]
    v_out[...] = kv_ref[:, kw:]


def rotation(p, cos_ref, sin_ref):
    all_rows, hd = cos_ref.shape
    block, half, step = all_rows // 2, hd // 2, 64
    lane = lax.broadcasted_iota(jnp.int32, (step, hd), 1)
    column = jnp.where(lane < half, lane, lane - half).astype(F32)
    inverse = jnp.exp(column * (-2.0 * math.log(1000000.0) / hd))
    row = lax.broadcasted_iota(jnp.int32, (step, hd), 0)

    def body(i, carry):
        at = i * step
        first = jnp.where(at < block, (4 * p.k + p.c) * block + at, (4 * p.k + 3 - p.c) * block + at - block)
        angles = (first + row).astype(F32) * inverse
        here = pl.ds(pl.multiple_of(at, step), step)
        cos_ref[here, :] = jnp.cos(angles)
        sine = jnp.sin(angles)
        sin_ref[here, :] = jnp.where(lane < half, -sine, sine)
        return carry

    lax.fori_loop(0, all_rows // step, body, 0)


def input_kernel(
    wide, narrow, x_ref, gain_ref, wq_ref, wk_ref, wv_ref, wo_ref, gate_ref, up_ref, down_ref,
    gathered, full, gu_out, d_out, cos_out, sin_out, gu_ref, d_ref, cos_ref, sin_ref, buf, shard, store, *sems
):
    p = Place(wide, narrow)
    rows = x_ref.shape[0]
    lo = 0
    for w_ref in (wq_ref, wk_ref, wv_ref):
        shard[:, lo : lo + w_ref.shape[1]] = w_ref[...]
        lo += w_ref.shape[1]
    shard[:, lo:] = jnp.transpose(wo_ref[...])
    spread, line = sems[:4], (shard, full, shard.shape[0], *sems[4:])
    enter(p, line=True)
    each_part(lambda q: line_push(p, *line, q))
    *steps, end = line_steps(p, *line)

    def body(at):
        u = x_ref[at, :].astype(F32)
        buf[at, :] = (u * inv_rms(u) * gain_ref[...]).astype(BF)

    row_loop(rows, STEP, body)
    spread_start(p, buf, gathered, rows, *spread)
    weave(gate_ref, up_ref, gu_ref)
    d_ref[...] = jnp.transpose(down_ref[...])
    steps[0]()
    rotation(p, cos_ref, sin_ref)
    pairs = ((gu_ref, gu_out), (d_ref, d_out), (cos_ref, cos_out), (sin_ref, sin_out))
    stores = [pltpu.make_async_copy(src, dst, store.at[i]) for i, (src, dst) in enumerate(pairs)]
    for copy in stores:
        copy.start()
    spread_pass(p, buf, gathered, rows, *spread)
    for step in steps[1:]:
        step()
    spread_end(p, buf, gathered, rows, *spread)
    end()
    for copy in stores:
        copy.wait()


def turn(u):
    return pltpu.roll(u, u.shape[-1] // 2, 1)


def qkv_kernel(
    wide, narrow, qw, kw, fold, g_ref, x_ref, w_ref, cos_ref, sin_ref, qg_ref, kg_ref,
    gathered, full, qproj_out, kproj_out, q_out, qproj_ref, kproj_ref, q_ref, kv_ref, w_buf, x_buf, load, store, *sems,
):
    p = Place(wide, narrow)
    rows = g_ref.shape[0]
    hd = cos_ref.shape[1]
    all_rows = x_ref.shape[0]
    size = all_rows // 4
    spread, line = sems[:4], (kv_ref, full, all_rows, *sems[4:])
    weights = pltpu.make_async_copy(w_ref.at[:, pl.ds(0, w_buf.shape[1])], w_buf, load.at[0])
    normed = pltpu.make_async_copy(x_ref, x_buf, load.at[1])
    normed.start()
    weights.start()
    enter(p, line=True)

    def project(q):
        at = pl.ds(pl.multiple_of(q * size, size), size)
        y = dg(x_buf[at, :], w_buf[...], NN)
        cos, sin = cos_ref[at, :], sin_ref[at, :]
        qproj_ref[at, :] = y[:, :qw]
        kproj_ref[at, :] = y[:, qw : qw + kw]

        def head(lo, gain):
            u = y[:, lo : lo + hd]
            v = u * inv_rms(u) * gain
            return v * cos + turn(v) * sin

        for h in range(kw // hd):
            kv_ref[at, 2 * h * hd : (2 * h + 1) * hd] = head(qw + h * hd, kg_ref[...]).astype(BF)
            kv_ref[at, (2 * h + 1) * hd : (2 * h + 2) * hd] = y[:, qw + kw + h * hd : qw + kw + (h + 1) * hd].astype(BF)
        for i in range(PARTS // 4):
            line_push(p, *line, q * (PARTS // 4) + i, ways=UP)
        for h in range(qw // hd):
            q_ref[at, h * hd : (h + 1) * hd] = (head(h * hd, qg_ref[...]) * fold).astype(BF)

    normed.wait()
    weights.wait()

    def one(q, carry):
        project(q)
        return carry

    lax.fori_loop(0, 4, one, 0)
    pairs = ((qproj_ref, qproj_out), (kproj_ref, kproj_out), (q_ref, q_out))
    stores = [pltpu.make_async_copy(src, dst, store.at[i]) for i, (src, dst) in enumerate(pairs)]
    spread_start(p, g_ref, gathered, rows, *spread)
    for copy in stores:
        copy.start()
    *steps, end = line_steps(p, *line, ways=UP)
    steps[0]()
    spread_pass(p, g_ref, gathered, rows, *spread)
    for step in steps[1:]:
        step()
    spread_end(p, g_ref, gathered, rows, *spread)
    end()
    for copy in stores:
        copy.wait()


def middle_kernel(wide, narrow, part, own_ref, gain_ref, mid_ref, gathered, buf, *refs):
    p = Place(wide, narrow)
    rows, dim = own_ref.shape
    bufs, sems, spread = split_refs(narrow, refs)
    enter(p)
    sum_start(p, part, rows, dim, bufs, sems)
    sum_pass(p, part, rows, dim, bufs, sems)
    sum_end(p, part, rows, dim, bufs, sems)

    def body(at):
        u = own_ref[at, :].astype(F32) + total(p, bufs, at)
        mid_ref[at, :] = u
        buf[at, :] = (u * inv_rms(u) * gain_ref[...]).astype(BF)

    row_loop(rows, STEP, body)
    spread_start(p, buf, gathered, rows, *spread)
    spread_pass(p, buf, gathered, rows, *spread)
    spread_end(p, buf, gathered, rows, *spread)


def split_refs(narrow, refs):
    bufs, sems = (3, 5) if narrow == 4 else (1, 3)
    return refs[:bufs], refs[bufs : bufs + sems], refs[bufs + sems :]


def norm_back(u, gain, cot):
    r = inv_rms(u)
    a = cot * gain
    du = r * a - u * (r * r * r) * jnp.mean(a * u, axis=-1, keepdims=True)
    return du, jnp.sum(cot * u * r, axis=0, keepdims=True)


def mlp_back_kernel(
    wide, narrow, g_ref, wd_ref, gu_ref, w_ref, x_ref, mid_ref, gain_ref, grad_ref, back_out, rows_ref, dgain_ref, wgrad,
    g_buf, wd_buf, gu_buf, low, w_buf, x_buf, mid_buf, grad_buf, back_ref, stage, out, load, tiles_in, store, leave, *refs
):
    p = Place(wide, narrow)
    rows, dim = mid_ref.shape
    half = dim // 2
    t = wd_buf.shape[2]
    bufs, sems, _ = split_refs(narrow, refs)

    def tile_of(i):
        slot = lax.rem(i, 2)
        return (
            pltpu.make_async_copy(wd_ref.at[:, pl.ds(pl.multiple_of(i * t, t), t)], wd_buf.at[slot], tiles_in.at[0, slot]),
            pltpu.make_async_copy(gu_ref.at[:, pl.ds(pl.multiple_of(2 * i * t, t), 2 * t)], gu_buf.at[slot], tiles_in.at[1, slot]),
        )

    loads = [pltpu.make_async_copy(g_ref, g_buf, load.at[0])]
    for i in range(2):
        at = pl.ds(i * half, half)
        loads.append(pltpu.make_async_copy(w_ref.at[at], w_buf.at[at], load.at[1 + i]))
    loads.append(pltpu.make_async_copy(x_ref, x_buf, load.at[3]))
    loads.append(pltpu.make_async_copy(mid_ref, mid_buf, load.at[4]))
    loads.append(pltpu.make_async_copy(grad_ref, grad_buf, load.at[5]))
    loads[0].start()
    for copy in tile_of(0):
        copy.start()
    enter(p)
    loads[0].wait()
    count = wd_ref.shape[1] // t

    def gates(i, carry):
        @pl.when(i + 1 < count)
        def _():
            for copy in tile_of(i + 1):
                copy.start()

        for copy in tile_of(i):
            copy.wait()

        @pl.when(i == 0)
        def _():
            for copy in loads[1:3]:
                copy.start()

        slot = lax.rem(i, 2)
        hb = dg(g_buf[...], wd_buf[slot], NN)
        at = pl.multiple_of(2 * i * t, t)
        low[:, pl.ds(at, t)] = (hb * gu_buf[slot, :, :t]).astype(BF)
        low[:, pl.ds(pl.multiple_of(at + t, t), t)] = (hb * gu_buf[slot, :, t:]).astype(BF)
        return carry

    lax.fori_loop(0, count, gates, 0)
    for copy in loads[3:]:
        copy.start()
    for copy in loads[1:3]:
        copy.wait()

    def product(j, i):
        a = low[pl.ds(pl.multiple_of(j * rows, rows), rows), :]
        return dg(a, w_buf[pl.ds(pl.multiple_of(i * half, half), half), :], NT).astype(BF)

    sum_start_of(p, product, out, rows, dim, bufs, sems)
    dgain_ref[...] = jnp.zeros_like(dgain_ref)
    loads[3].wait()
    tile = 256

    def write(i):
        return pltpu.make_async_copy(
            stage.at[lax.rem(i, 2)], wgrad.at[pl.ds(pl.multiple_of(i * tile, tile), tile)], store.at[lax.rem(i, 2)]
        )

    def grads(first, last):
        def one(i, carry):
            @pl.when(i >= 2)
            def _():
                write(i - 2).wait()

            stage[lax.rem(i, 2)] = dg(x_buf[:, pl.ds(pl.multiple_of(i * tile, tile), tile)], low[...], TN).astype(BF)
            write(i).start()
            return carry

        lax.fori_loop(first, last, one, 0)

    tiles = dim // tile
    early = 3
    grads(0, early)
    sum_pass(p, out, rows, dim, bufs, sems, loaded=narrow == 4)
    grads(early, tiles)
    sum_end(p, out, rows, dim, bufs, sems)
    for copy in loads[4:]:
        copy.wait()

    def body(at):
        du, dgain = norm_back(mid_buf[at, :], gain_ref[...], total(p, bufs, at))
        back = grad_buf[at, :].astype(F32) + du
        back_ref[at, :] = back
        pltpu.make_async_copy(back_ref.at[at], back_out.at[at], leave).start()
        rows_ref[at, :] = back.astype(BF)
        dgain_ref[...] += dgain

    row_loop(rows, STEP, body)
    pltpu.make_async_copy(back_ref, back_out, leave).wait()
    write(tiles - 2).wait()
    write(tiles - 1).wait()


def middle_back_kernel(
    wide, narrow, wo_at, groups, hd, rows_ref, hidden, w_ref, wo_ref, o_ref, all_ref, next_ref, back_ref, delta_ref,
    gathered, next_buf, h_buf, w_buf, wo_buf, o_buf, load, store, next_store, *spread
):
    p = Place(wide, narrow)
    rows = rows_ref.shape[0]
    pairs = ((hidden, h_buf), (w_ref, w_buf), (wo_ref.at[:, pl.ds(*wo_at)], wo_buf), (o_ref, o_buf))
    loads = [pltpu.make_async_copy(src, dst, load.at[i]) for i, (src, dst) in enumerate(pairs)]
    enter(p)
    spread_start(p, rows_ref, gathered, rows, *spread)
    for copy in loads:
        copy.start()
    for copy in loads[:2]:
        copy.wait()

    def write_next(i):
        at = pl.ds(pl.multiple_of(i * 256, 256), 256)
        return pltpu.make_async_copy(next_buf.at[at], next_ref.at[at], next_store.at[i])

    def write_slot(j):
        at = pl.ds(pl.multiple_of(j * rows, rows), rows)
        return pltpu.make_async_copy(gathered.at[at], all_ref.at[at], store.at[j])

    def downs(first, last):
        def one(i, carry):
            at = pl.ds(pl.multiple_of(i * 256, 256), 256)
            next_buf[at, :] = dg(h_buf[at, :], w_buf[...], NT).astype(BF)
            write_next(i).start()
            return carry

        lax.fori_loop(first, last, one, 0)

    blocks = next_buf.shape[0] // 256
    downs(0, blocks // 2)

    def on_slot(j):
        at = pl.ds(pl.multiple_of(j * rows, rows), rows)
        write_slot(j).start()
        back = dg(gathered[at, :], wo_buf[...], NN).astype(BF)
        back_ref[at, :] = back
        lane = lax.broadcasted_iota(jnp.int32, (rows, hd), 1)
        out = jnp.zeros((rows, hd), F32)
        for h in range(back.shape[1] // hd):
            mine = slice(h * hd, (h + 1) * hd)
            row = 8 * (h // groups) + h % groups
            delta = jnp.sum(back[:, mine].astype(F32) * o_buf[at, mine], axis=1, keepdims=True)
            out = jnp.where(lane == row, delta, out)
        delta_ref[:, at] = jnp.transpose(out)[: delta_ref.shape[0]]

    spread_pass(p, rows_ref, gathered, rows, *spread)
    downs(blocks // 2, blocks)
    for copy in loads[2:]:
        copy.wait()
    spread_end(p, rows_ref, gathered, rows, *spread, on_slot=on_slot)
    for i in range(blocks):
        write_next(i).wait()
    for j in range(p.N):
        write_slot(j).wait()


def share_start(me, count, here, slots, sends, recvs, device):
    slots[me] = here[...]
    for t in range(count):

        @pl.when(me != t)
        def _():
            wide_at, narrow_at = device(t)
            to(here, slots.at[me], sends.at[t], recvs.at[me], wide_at, narrow_at).start()


def share_end(me, count, here, slots, sends, recvs):
    for t in range(count):

        @pl.when(me != t)
        def _():
            pltpu.make_async_copy(here, slots.at[t], sends.at[t]).wait()
            pltpu.make_async_copy(here, slots.at[t], recvs.at[t]).wait()

    out = slots[0]
    for t in range(1, count):
        out = out + slots[t]
    here[...] = out


def head_back(cot, u, gain, cos, sin):
    cot = cot * cos - turn(cot) * sin
    return norm_back(u, gain, cot)


def output_kernel(
    wide, narrow, part, mid_ref, dkv, dq, qproj, cos_ref, sin_ref, g_ref, x_ref, m_ref, a_ref,
    out_out, kv_ref, low_out, dgain_ref, wgrad_out, out_ref, low_ref, wgrad_ref, dq_buf, u_buf, x_buf, m_buf, a_buf, load, store, leave, *refs
):
    p = Place(wide, narrow)
    rows, dim = mid_ref.shape
    kv_rows = kv_ref.shape[0]
    width = low_ref.shape[1]
    hd = cos_ref.shape[1]
    bufs, sems, line = split_refs(narrow, refs)
    sums = (part, rows, dim, bufs, sems)
    chain = (p, dkv, kv_rows, line[:5], line[5:])
    pairs = ((dq, dq_buf), (qproj, u_buf), (x_ref, x_buf), (m_ref, m_buf), (a_ref, a_buf))
    loads = [pltpu.make_async_copy(src, dst, load.at[i]) for i, (src, dst) in enumerate(pairs)]
    enter(p, line=True)
    line_sum_start(*chain, ways=DOWN)
    sum_start(p, *sums)
    for copy in loads:
        copy.start()
    first, *steps, last = line_sum_steps(*chain, ways=DOWN)
    first()
    dgain_ref[...] = jnp.zeros_like(dgain_ref)
    for copy in loads[:2]:
        copy.wait()

    def through_heads(at):
        for h in range(width // hd):
            mine = slice(h * hd, (h + 1) * hd)
            du, dgain = head_back(dq_buf[at, mine], u_buf[at, mine], g_ref[...], cos_ref[at, :], sin_ref[at, :])
            low_ref[at, mine] = du.astype(BF)
            dgain_ref[...] += dgain

    row_loop(low_ref.shape[0], 128, through_heads)
    low_store = pltpu.make_async_copy(low_ref, low_out, leave.at[0])
    low_store.start()
    for copy in loads[2:]:
        copy.wait()

    def write(i):
        at = pl.ds(pl.multiple_of(i * 256, 256), 256)
        return pltpu.make_async_copy(wgrad_ref.at[at], wgrad_out.at[at], store.at[i])

    def grads(first_tile, last_tile):
        def one(i, carry):
            at = pl.ds(pl.multiple_of(i * 256, 256), 256)
            wgrad_ref[at, :width] = dg(x_buf[:, at], low_ref[...], TN).astype(BF)
            wgrad_ref[at, width:] = dg(m_buf[:, at], a_buf[...], TN).astype(BF)
            write(i).start()
            return carry

        lax.fori_loop(first_tile, last_tile, one, 0)

    tiles = dim // 256
    grads(0, tiles // 2)
    sum_pass(p, *sums)
    steps[0]()
    grads(tiles // 2, tiles)
    sum_end(p, *sums)

    def body(at):
        out_ref[at, :] = (mid_ref[at, :] + total(p, bufs, at)).astype(BF)

    row_loop(rows, STEP, body)
    out_store = pltpu.make_async_copy(out_ref, out_out, leave.at[1])
    out_store.start()
    for step in steps[1:]:
        step()
    last()
    row_loop(kv_rows, 128, lambda at: kv_ref.__setitem__((at, slice(None)), line[4][at, :].astype(BF)))
    for i in range(tiles):
        write(i).wait()
    low_store.wait()
    out_store.wait()


def input_back_kernel(
    wide, narrow, qw, kw, own_ref, gain_ref, back_ref, mlp_ref, qg_ref, wgrad, q_ref, kv_ref, proj_ref, cos_ref, sin_ref, kg_ref,
    w_ref, x_ref, out_out, gsum_ref, wsum_ref, kvsum_ref,
    gbuf, gbuf2, low, part, kvgrad, w_buf, x_buf, own_buf, back_buf, out_ref, load, leave, gsend, grecv, gsend2, grecv2, *refs,
):
    p = Place(wide, narrow)
    rows, dim = own_ref.shape
    hd = cos_ref.shape[1]
    all_rows = x_ref.shape[0]
    w_rows = wsum_ref.shape[0]
    bufs, sems, line = split_refs(narrow, refs)
    sums = (part, rows, dim, bufs, sems)
    first_line = (p, wgrad, w_rows, (*line[:4], wsum_ref), line[4:10])
    second_line = (p, kvgrad, w_rows, (*line[10:14], kvsum_ref), line[14:])
    weights = pltpu.make_async_copy(w_ref.at[:, pl.ds(0, w_buf.shape[1])], w_buf, load.at[0])
    weights.start()
    normed = pltpu.make_async_copy(x_ref, x_buf, load.at[1])
    normed.start()
    later = [pltpu.make_async_copy(own_ref, own_buf, load.at[2]), pltpu.make_async_copy(back_ref, back_buf, load.at[3])]
    for copy in later:
        copy.start()
    enter(p, ring=True)
    line_sum_start(*first_line)
    gsum_ref[...] = jnp.zeros_like(gsum_ref)
    gsum_ref[:, dim : 2 * dim] = mlp_ref[...]
    gsum_ref[:, 2 * dim : 2 * dim + hd] = qg_ref[...]
    size = min(all_rows, 256)
    first = line_sum_steps(*first_line)
    first[0]()
    weights.wait()

    def through_heads(at):
        low[at, :qw] = q_ref[at, :]
        for h in range(kw // hd):
            key = slice(2 * h * hd, (2 * h + 1) * hd)
            value = slice((2 * h + 1) * hd, (2 * h + 2) * hd)
            mine = slice(qw + h * hd, qw + (h + 1) * hd)
            du, dgain = head_back(
                kv_ref[at, key].astype(F32), proj_ref[at, h * hd : (h + 1) * hd], kg_ref[...], cos_ref[at, :], sin_ref[at, :]
            )
            low[at, mine] = du.astype(BF)
            low[at, qw + kw + h * hd : qw + kw + (h + 1) * hd] = kv_ref[at, value]
            gsum_ref[:, 2 * dim + hd :] += dgain
        part[at, :] = dg(low[at, :], w_buf[...], NT).astype(BF)

    row_loop(all_rows, size, through_heads)
    sum_start(p, *sums)
    first[1]()

    normed.wait()

    def key_grads(at):
        kvgrad[at, :] = dg(x_buf[:, at], low[:, qw:], TN).astype(BF)

    row_loop(dim, 256, key_grads)
    line_sum_start(*second_line)
    second = line_sum_steps(*second_line)
    second[0]()
    for step in first[2:-1]:
        step()
    sum_pass(p, *sums)
    for step in second[1:-1]:
        step()
    sum_end(p, *sums)
    for copy in later:
        copy.wait()

    def body(at):
        du, dgain = norm_back(own_buf[at, :].astype(F32), gain_ref[...], total(p, bufs, at))
        out_ref[at, :] = back_buf[at, :] + du
        gsum_ref[:, :dim] += dgain

    row_loop(rows, STEP, body)
    out_store = pltpu.make_async_copy(out_ref, out_out, leave)
    out_store.start()

    share_start(p.n, narrow, gsum_ref, gbuf, gsend, grecv, lambda t: (p.w, t))
    first[-1]()
    share_end(p.n, narrow, gsum_ref, gbuf, gsend, grecv)
    share_start(p.w, wide, gsum_ref, gbuf2, gsend2, grecv2, lambda t: (t, p.n))
    second[-1]()
    share_end(p.w, wide, gsum_ref, gbuf2, gsend2, grecv2)
    out_store.wait()


VM = pl.BlockSpec(memory_space=pltpu.VMEM)


HB = pl.BlockSpec(memory_space=pl.ANY)


def comm_call(kernel, name, cid, out_shape, in_specs, out_specs, scratch, *args):
    return pl.pallas_call(
        kernel,
        out_shape=out_shape,
        in_specs=in_specs,
        out_specs=out_specs,
        scratch_shapes=scratch,
        compiler_params=pltpu.CompilerParams(collective_id=cid, has_side_effects=True, vmem_limit_bytes=60 << 20),
        cost_estimate=pl.CostEstimate(flops=0, bytes_accessed=160_000_000, transcendentals=0),
        name=name,
    )(*args)


def sds(shape, kind):
    return jax.ShapeDtypeStruct(shape, kind)


def plain(kernel, name, grid, in_specs, out_specs, out_shape, flops, nbytes, *args, scratch=(), aliases=None):
    return pl.pallas_call(
        kernel,
        out_shape=out_shape,
        grid=grid,
        in_specs=in_specs,
        out_specs=out_specs,
        scratch_shapes=scratch,
        input_output_aliases=aliases or {},
        compiler_params=pltpu.CompilerParams(vmem_limit_bytes=52 << 20),
        cost_estimate=pl.CostEstimate(flops=flops, bytes_accessed=nbytes, transcendentals=0),
        name=name,
    )(*args)


def whole(shape):
    return pl.BlockSpec(shape, lambda *i: (0,) * len(shape), pipeline_mode=pl.Buffered(1))


def by_rows(tm, width):
    return pl.BlockSpec((tm, width), lambda i: (i, 0))


def mlp_fwd_kernel(x_ref, w_ref, gu_ref, h_ref):
    t = h_ref.shape[1]
    y = dg(x_ref[...], w_ref[...], NN)
    gate, up = y[:, :t], y[:, t:]
    s = jax.nn.sigmoid(gate)
    silu = gate * s
    h_ref[...] = (silu * up).astype(BF)
    gu_ref[:, :t] = (up * s * (1.0 + gate * (1.0 - s))).astype(BF)
    gu_ref[:, t:] = silu.astype(BF)


def mlp_fwd(x, w, t):
    rows, dim = x.shape
    ff2 = w.shape[1]
    return plain(
        mlp_fwd_kernel, "mlp_fwd", (ff2 // (2 * t),),
        [whole((rows, dim)), pl.BlockSpec((dim, 2 * t), lambda i: (0, i))],
        [pl.BlockSpec((rows, 2 * t), lambda i: (0, i)), pl.BlockSpec((rows, t), lambda i: (0, i))],
        (sds((rows, ff2), BF), sds((rows, ff2 // 2), BF)),
        2 * rows * dim * ff2, rows * dim * 2 + dim * ff2 * 2 + rows * ff2 * 3, x, w,
    )


def fwd_kernel(groups, hd, tab, q_ref, kv_ref, o_ref, low_ref, lse_ref, acc, lsum):
    s = pl.program_id(1)
    block = q_ref.shape[0]
    diag, first, last = tab[2, s], tab[3, s], tab[4, s]

    @pl.when(first == 1)
    def _():
        acc[...] = jnp.zeros_like(acc)
        lsum[...] = jnp.zeros_like(lsum)

    def work(masked):
        k, v = kv_ref[:, :hd], kv_ref[:, hd:]
        for g in range(groups):
            at = slice(g * hd, (g + 1) * hd)
            scores = dg(q_ref[:, at], k, NT)
            if masked:
                row = lax.broadcasted_iota(jnp.int32, scores.shape, 0)
                col = lax.broadcasted_iota(jnp.int32, scores.shape, 1)
                scores = jnp.where(col <= row, scores, MASKED)
            probs = jnp.exp2(scores)
            part = probs[:, :128]
            for j in range(1, block // 128):
                part = part + probs[:, j * 128 : (j + 1) * 128]
            lsum[g] += part
            acc[:, at] += dg(probs.astype(BF), v, NN)

    @pl.when(diag == 0)
    def _():
        work(False)

    @pl.when(diag == 1)
    def _():
        work(True)

    @pl.when(last == 1)
    def _():
        lane = lax.broadcasted_iota(jnp.int32, (block, 128), 1)
        lse = jnp.zeros((block, 128), F32)
        for g in range(groups):
            at = slice(g * hd, (g + 1) * hd)
            l = jnp.sum(lsum[g], axis=1, keepdims=True)
            out = acc[:, at] / l
            o_ref[:, at] = out
            low_ref[:, at] = out.astype(BF)
            lse = jnp.where(lane == g, jnp.log2(l), lse)
        lse_ref[...] = jnp.transpose(lse)[: lse_ref.shape[0]]


def attn_fwd(tab, q, kv, groups, hd, block):
    rows, width = q.shape
    gw = groups * hd
    heads = width // gw
    steps = tab.shape[1]
    mine = pl.BlockSpec((block, gw), lambda h, s, t: (t[0, s], h))
    return pl.pallas_call(
        functools.partial(fwd_kernel, groups, hd),
        out_shape=(sds((rows, width), F32), sds((rows, width), BF), sds((8 * heads, rows), F32)),
        grid_spec=pltpu.PrefetchScalarGridSpec(
            num_scalar_prefetch=1,
            grid=(heads, steps),
            in_specs=[mine, pl.BlockSpec((block, 2 * hd), lambda h, s, t: (t[1, s], h))],
            out_specs=[mine, mine, pl.BlockSpec((8, block), lambda h, s, t: (h, t[0, s]))],
            scratch_shapes=[pltpu.VMEM((block, gw), F32), pltpu.VMEM((groups, block, 128), F32)],
        ),
        compiler_params=pltpu.CompilerParams(vmem_limit_bytes=48 << 20),
        cost_estimate=pl.CostEstimate(
            flops=heads * steps * block * block * gw * 4,
            bytes_accessed=heads * steps * block * hd * 8,
            transcendentals=heads * steps * block * block * groups,
        ),
        name="attn_fwd",
    )(tab, q, kv)


def bwd_kernel(groups, hd, tab, q_ref, do_ref, kv_ref, lse_ref, delta_ref, dq_ref, dkv_ref, dq_sum, dkv_sum):
    s = pl.program_id(1)
    block = q_ref.shape[0]
    qi, diag, first, last = tab[0, s], tab[2, s], tab[3, s], tab[4, s]

    @pl.when(s == 0)
    def _():
        dq_sum[...] = jnp.zeros_like(dq_sum)

    @pl.when(first == 1)
    def _():
        dkv_sum[...] = jnp.zeros_like(dkv_sum)

    def work(masked):
        k, v = kv_ref[:, :hd], kv_ref[:, hd:]
        for g in range(groups):
            at = slice(g * hd, (g + 1) * hd)
            q, do = q_ref[:, at], do_ref[:, at]
            scores = dg(k, q, NT) - lse_ref[g : g + 1, :]
            if masked:
                row = lax.broadcasted_iota(jnp.int32, scores.shape, 0)
                col = lax.broadcasted_iota(jnp.int32, scores.shape, 1)
                scores = jnp.where(row <= col, scores, MASKED)
            probs = jnp.exp2(scores)
            dots = dg(v, do, NT)
            dkv_sum[:, hd:] += dg(probs.astype(BF), do, NN)
            back = (probs * (dots - delta_ref[g : g + 1, :])).astype(BF)
            dkv_sum[:, :hd] += dg(back, q, NN)
            dq_sum[qi, :, at] += dg(back, k, TN)

    @pl.when(diag == 0)
    def _():
        work(False)

    @pl.when(diag == 1)
    def _():
        work(True)

    @pl.when(last == 1)
    def _():
        dkv_ref[:, :hd] = (dkv_sum[:, :hd] * math.log(2.0)).astype(BF)
        dkv_ref[:, hd:] = dkv_sum[:, hd:].astype(BF)

    @pl.when(s == pl.num_programs(1) - 1)
    def _():
        for i in range(dq_sum.shape[0]):
            dq_ref[i * block : (i + 1) * block, :] = dq_sum[i] * hd**-0.5


def attn_bwd(tab, q, do, kv, lse, delta, groups, hd, block):
    rows, width = q.shape
    gw = groups * hd
    heads = width // gw
    steps = tab.shape[1]
    mine = pl.BlockSpec((block, gw), lambda h, s, t: (t[0, s], h))
    keys = pl.BlockSpec((block, 2 * hd), lambda h, s, t: (t[1, s], h))
    stat = pl.BlockSpec((8, block), lambda h, s, t: (h, t[0, s]))
    return pl.pallas_call(
        functools.partial(bwd_kernel, groups, hd),
        out_shape=(sds((rows, width), F32), sds(kv.shape, BF)),
        grid_spec=pltpu.PrefetchScalarGridSpec(
            num_scalar_prefetch=1,
            grid=(heads, steps),
            in_specs=[mine, mine, keys, stat, stat],
            out_specs=[pl.BlockSpec((rows, gw), lambda h, s, t: (0, h)), keys],
            scratch_shapes=[pltpu.VMEM((rows // block, block, gw), F32), pltpu.VMEM((block, 2 * hd), F32)],
        ),
        compiler_params=pltpu.CompilerParams(vmem_limit_bytes=48 << 20),
        cost_estimate=pl.CostEstimate(
            flops=heads * steps * block * block * gw * 10,
            bytes_accessed=heads * steps * block * hd * 16,
            transcendentals=heads * steps * block * block * groups,
        ),
        name="attn_bwd",
    )(tab, q, do, kv, lse, delta)


def place(w):
    k, core = w // 2, w % 2
    return 4 * k + core, 4 * k + 3 - core


def block_row(b):
    m = b % 4
    core = jnp.where((m == 1) | (m == 2), 1, 0)
    return 2 * (2 * (b // 4) + core) + jnp.where(m < 2, 0, 1)


def tables(w, chips):
    a, b = place(w)
    count = a + b + 2
    every = jnp.arange(8 * chips - 2, dtype=jnp.int32)
    s, idle = jnp.minimum(every, count - 1), every >= count
    in_a = s <= a
    key = jnp.where(in_a, s, s - a - 1)
    diag = jnp.where(in_a, s == a, s == count - 1)
    fwd = [jnp.where(in_a, 0, 1), block_row(key), jnp.where(idle, 2, diag), ~idle & (key == 0), ~idle & diag]
    both = s < 2 * (a + 1)
    even = s % 2 == 0
    key = jnp.where(both, s // 2, s - (a + 1))
    query = jnp.where(both & even, 0, 1)
    diag = key == jnp.where(query == 0, a, b)
    zero = (every >= count) & (w % 2 == 1)
    key = jnp.where(zero, b + 1, key)
    only = zero & (every == count)
    bwd = [query, block_row(key), jnp.where(idle, 2, diag), only | ~idle & (~both | even), only | ~idle & (~both | ~even)]
    return tuple(jnp.stack([row.astype(jnp.int32) for row in rows]) for rows in (fwd, bwd))


def per_device(
    wide, narrow,
    layer_input, w_query, w_key, w_value, w_output, w_gate, w_up, w_down,
    attn_gain, mlp_gain, query_gain, key_gain, out_grad,
):
    hd = query_gain.shape[0]
    rows, dim = layer_input.shape
    all_rows = narrow * rows
    chips = wide // 2
    block = all_rows // 2
    qw, kw = w_query.shape[1], w_key.shape[1]
    ff = w_gate.shape[1]
    groups = qw // kw
    kv_heads = kw // hd
    w = lax.axis_index("wide")
    fwd_tab, bwd_tab = tables(w, chips)
    def gather(shard):
        return lax.all_gather(shard, "wide", axis=0, tiled=True)

    def scatter(grad):
        return lax.psum_scatter(grad, "wide", scatter_dimension=0, tiled=True)

    t = math.gcd(ff, 256)

    spread_s = spread_sems(narrow)
    sum_s = [*sum_bufs(narrow, rows, dim), *sum_sems(narrow)]
    row_buf = pltpu.VMEM((rows, dim), BF)
    low_rows, full_rows, all_low = sds((rows, dim), BF), sds((rows, dim), F32), sds((all_rows, dim), BF)
    ring = functools.partial
    qg, kg = query_gain[None], key_gain[None]
    after = lax.optimization_barrier

    in_scratch = [*spread_s, *line_sems(chips)]
    table = sds((all_rows, hd), F32)
    s_rows, s_cols = w_query.shape[0], 2 * qw + 2 * kw
    normed_all, w_attn, gu_shard, d_shard, cos_table, sin_table = comm_call(
        ring(input_kernel, wide, narrow), "input_rows", 0,
        (all_low, sds((dim, s_cols), BF), sds((s_rows, 2 * ff), BF), sds((s_rows, ff), BF), table, table),
        [VM] * 9, (HB,) * 6,
        [pltpu.VMEM((s_rows, 2 * ff), BF), pltpu.VMEM((s_rows, ff), BF), *[pltpu.VMEM((all_rows, hd), F32)] * 2,
         row_buf, pltpu.VMEM((s_rows, s_cols), BF), DMA((4,)), *in_scratch],
        layer_input, attn_gain[None], w_query, w_key, w_value, w_output, w_gate, w_up, w_down,
    )
    width = qw + 2 * kw
    grad_all, kv, query_proj, key_proj, queries = comm_call(
        ring(qkv_kernel, wide, narrow, qw, kw, hd**-0.5 * math.log2(math.e)), "qkv_rows", 1,
        (all_low, sds((wide * all_rows, 2 * kw), BF), sds((all_rows, qw), F32),
         sds((all_rows, kw), F32), sds((all_rows, qw), BF)),
        [VM, HB, HB, VM, VM, VM, VM], (HB, HB, HB, HB, HB),
        [pltpu.VMEM((all_rows, qw), F32), pltpu.VMEM((all_rows, kw), F32), pltpu.VMEM((all_rows, qw), BF),
         pltpu.VMEM((all_rows, 2 * kw), BF), pltpu.VMEM((dim, width), BF),
         pltpu.VMEM((all_rows, dim), BF), DMA((2,)), DMA((3,)), *in_scratch],
        out_grad, normed_all, w_attn, cos_table, sin_table, qg, kg,
    )
    gu_shard, d_shard, kv = after((gu_shard, d_shard, kv))
    w_gu, w_d = gather(gu_shard), gather(d_shard)
    attended, attended_low, lse = attn_fwd(fwd_tab, queries, kv, groups, hd, block)
    w_o = w_attn[:, qw + 2 * kw :]
    middle, normed_mlp = comm_call(
        ring(middle_kernel, wide, narrow), "middle_rows", 2, (full_rows, all_low), [HB, VM, VM], (VM, HB),
        [row_buf, *sum_s, *spread_s], dg(attended_low, w_o, NT).astype(BF), layer_input, mlp_gain[None],
    )
    factors, hidden_low = mlp_fwd(normed_mlp, w_gu, t)
    grad_down = dg(grad_all, hidden_low, TN).astype(BF)
    w_d, _ = after((w_d, grad_down))
    middle_back, middle_low, mlp_gain_part, grad_gu = comm_call(
        ring(mlp_back_kernel, wide, narrow), "mlp_back", 6,
        (full_rows, low_rows, sds((1, dim), F32), sds((dim, 2 * ff), BF)), [HB, HB, HB, HB, HB, HB, VM, HB], (HB, VM, VM, HB),
        [pltpu.VMEM((all_rows, dim), BF), pltpu.VMEM((2, dim, t), BF), pltpu.VMEM((2, all_rows, 2 * t), BF),
         pltpu.VMEM((all_rows, 2 * ff), BF), pltpu.VMEM((dim, 2 * ff), BF), pltpu.VMEM((all_rows, dim), BF),
         pltpu.VMEM((rows, dim), F32), row_buf, pltpu.VMEM((rows, dim), F32), pltpu.VMEM((2, 256, 2 * ff), BF),
         product_bufs(narrow, rows, dim), DMA((6,)), DMA((2, 2)), DMA((2,)), DMA, *sum_s],
        grad_all, w_d, factors, w_gu, normed_mlp, middle, mlp_gain[None], out_grad,
    )
    grad_down, grad_gu = scatter(grad_down), scatter(grad_gu)
    middle_all, down_part, back, delta = comm_call(
        ring(middle_back_kernel, wide, narrow, (width, qw), groups, hd), "middle_back", 3,
        (all_low, all_low, sds((all_rows, qw), BF), sds((8 * kv_heads, all_rows), F32)),
        [VM, HB, HB, HB, HB], (HB, HB, VM, VM),
        [pltpu.VMEM((all_rows, dim), BF), pltpu.VMEM((all_rows, dim), BF), pltpu.VMEM((all_rows, ff), BF), pltpu.VMEM((dim, ff), BF), pltpu.VMEM((dim, qw), BF), pltpu.VMEM((all_rows, qw), F32),
         DMA((4,)), DMA((narrow,)), DMA((all_rows // 256,)), *spread_s],
        middle_low, hidden_low, w_d, w_attn, attended,
    )
    query_back, dkv = attn_bwd(bwd_tab, queries, back, kv, lse, delta, groups, hd, block)
    dkv, grad_down = after((dkv, grad_down))
    layer_output, kv_sum, q_low, query_gain_part, grad_qo = comm_call(
        ring(output_kernel, wide, narrow), "output_rows", 4,
        (low_rows, sds((all_rows, 2 * kw), BF), sds((all_rows, qw), BF), sds((1, hd), F32), sds((dim, 2 * qw), BF)),
        [HB, VM, HB, HB, HB, VM, VM, VM, HB, HB, HB], (HB, VM, HB, VM, HB),
        [row_buf, pltpu.VMEM((all_rows, qw), BF), pltpu.VMEM((dim, 2 * qw), BF), pltpu.VMEM((all_rows, qw), F32), pltpu.VMEM((all_rows, qw), F32), pltpu.VMEM((all_rows, dim), BF),
         pltpu.VMEM((all_rows, dim), BF), pltpu.VMEM((all_rows, qw), BF), DMA((5,)), DMA((dim // 256,)), DMA((2,)), *sum_s,
         *line_sum_bufs(chips, all_rows, 2 * kw), *line_sum_sems(chips)],
        down_part, middle, dkv, query_back, query_proj, cos_table, sin_table, qg, normed_all, middle_all, attended_low,
    )
    kv_sum, grad_gu = after((kv_sum, grad_gu))
    gains = sds((1, 2 * dim + 2 * hd), F32)
    w_rows = dim // wide
    input_grad, gain_sums, grad_qo, grad_kv = comm_call(
        ring(input_back_kernel, wide, narrow, qw, kw), "input_back", 5,
        (full_rows, gains, sds((w_rows, 2 * qw), F32), sds((w_rows, 2 * kw), F32)),
        [HB, VM, HB, VM, VM, HB, VM, VM, VM, VM, VM, VM, HB, HB],
        (HB, VM, VM, VM),
        [pltpu.VMEM((narrow, *gains.shape), F32), pltpu.VMEM((wide, *gains.shape), F32),
         pltpu.VMEM((all_rows, width), BF), pltpu.VMEM((all_rows, dim), BF), pltpu.VMEM((dim, 2 * kw), BF),
         pltpu.VMEM((dim, width), BF), pltpu.VMEM((all_rows, dim), BF),
         row_buf, pltpu.VMEM((rows, dim), F32), pltpu.VMEM((rows, dim), F32), DMA((4,)), DMA, DMA((narrow,)), DMA((narrow,)), DMA((wide,)), DMA((wide,)), *sum_s,
         *line_sum_bufs(chips, w_rows, 2 * qw)[:4], *line_sum_sems(chips),
         *line_sum_bufs(chips, w_rows, 2 * kw)[:4], *line_sum_sems(chips)],
        layer_input, attn_gain[None], middle_back, mlp_gain_part, query_gain_part, grad_qo, q_low, kv_sum, key_proj, cos_table, sin_table, kg, w_attn, normed_all,
    )
    tm = min(w_rows, 128)
    turned = lambda height: pl.BlockSpec((height, tm), lambda i: (0, i))
    grads = plain(
        finish_kernel, "finish", (w_rows // tm,),
        [by_rows(tm, 2 * ff), by_rows(tm, ff), by_rows(tm, 2 * qw), by_rows(tm, 2 * kw)],
        [by_rows(tm, ff), by_rows(tm, ff), turned(ff), by_rows(tm, qw), by_rows(tm, kw), by_rows(tm, kw), turned(qw)],
        [sds(shape, F32) for shape in (w_gate.shape, w_up.shape, w_down.shape, w_query.shape, w_key.shape, w_value.shape,
                                       w_output.shape)],
        0, 10 * dim // wide * (3 * ff + qw), grad_gu, grad_down, grad_qo, grad_kv,
    )
    grad_gate, grad_up, grad_down, grad_query, grad_key, grad_value, grad_output = grads
    g = gain_sums[0]
    return (
        layer_output, input_grad, grad_query, grad_key, grad_value, grad_output, grad_gate, grad_up, grad_down,
        g[:dim], g[dim : 2 * dim], g[2 * dim : 2 * dim + hd], g[2 * dim + hd :],
    )


def solution(mesh):
    rows = P(("wide", "narrow"), None)
    weight, turned = P("wide", "narrow"), P("narrow", "wide")
    return jax.shard_map(
        functools.partial(per_device, mesh.shape["wide"], mesh.shape["narrow"]),
        mesh=mesh,
        in_specs=(rows, weight, weight, weight, turned, weight, weight, turned, P(), P(), P(), P(), rows),
        out_specs=(rows, rows, weight, weight, weight, turned, weight, weight, turned, P(), P(), P(), P()),
        check_vma=False,
    )
```

```python
import functools
import math

import jax
import jax.numpy as jnp
from jax import lax
from jax.experimental import pallas as pl
from jax.experimental.pallas import tpu as pltpu
from jax.sharding import PartitionSpec as P

EPSILON = 1e-06
MASKED = -1e30
F32 = jnp.float32
BF = jnp.bfloat16
MESH = pl.DeviceIdType.MESH
NT = (((1,), (1,)), ((), ()))
NN = (((1,), (0,)), ((), ()))
TN = (((0,), (0,)), ((), ()))


def dg(a, b, dims):
    return lax.dot_general(a, b, dims, preferred_element_type=F32)
DMA = pltpu.SemaphoreType.DMA


class Place:
    def __init__(self, wide, narrow):
        self.W, self.N = wide, narrow
        self.C, self.half = wide // 2, narrow // 2
        self.w, self.n = lax.axis_index("wide"), lax.axis_index("narrow")
        self.k, self.c = self.w // 2, lax.rem(self.w, 2)
        late = (self.n >= self.half).astype(jnp.int32)
        self.group = lax.rem(self.c + late, 2)
        self.slot = jnp.where(self.group == 0, self.n, lax.rem(self.n + self.half, self.N))

    def owner(self, j):
        core = 1 if j >= self.half else 0
        n = jnp.where(self.c == 0, j, (j + self.half) % self.N)
        return core, n

    def owner_is_me(self, j):
        core, n = self.owner(j)
        return (self.c == core) & (self.n == n)


def enter(p, line=False, ring=False):
    barrier = pltpu.get_barrier_semaphore()

    def greet(device):
        pl.semaphore_signal(barrier, inc=1, device_id=device, device_id_type=MESH)

    for core in range(2):
        for n in range(p.N):

            @pl.when((p.c != core) | (p.n != n))
            def _():
                greet((2 * p.k + core, n))

    peers = 2 * p.N - 1
    if line or ring:
        for k in range(p.C):

            @pl.when(p.k != k)
            def _():
                greet((2 * k + p.c, p.n))
                if ring:
                    greet((2 * k + 1 - p.c, p.n))

        peers += (2 if ring else 1) * (p.C - 1)
    pl.semaphore_wait(barrier, peers)


def slot_of(p, n, group):
    return jnp.where(group == 0, n, lax.rem(n + p.half, p.N))


def neighbours(p):
    return p.n + 1 - 2 * lax.rem(p.n, 2), lax.rem(p.n + 2, 4), 3 - p.n


def to(src, dst, send, recv, wide, narrow):
    return pltpu.make_async_remote_copy(
        src_ref=src, dst_ref=dst, send_sem=send, recv_sem=recv, device_id=(wide, narrow), device_id_type=MESH
    )


def spread_sems(narrow):
    return [DMA((narrow, 2)), DMA((narrow, 2)), DMA((2,)), DMA((2,))]


def spread_start(p, src, gathered, rows, send, recv, local, onward):
    half = rows // 2
    view = lambda i: gathered.at[pl.ds(pl.multiple_of(p.slot * rows + i * half, half), half)]
    part = lambda i: src.at[pl.ds(i * half, half)]
    mine = p.group == p.c
    square = p.N == 4
    if square:
        nx, ny, _ = neighbours(p)
        targets = [(nx, (0, 1)), (ny, (1, 0))]
        order = [(t, q, i) for q in range(2) for t, halves in targets for i in (halves[q],)]
        for t, q, i in order:
            at = 0 if t is nx else 1
            to(part(i), view(i), send.at[at, i], recv.at[p.slot, i], 2 * p.k + p.group, t).start()
    else:
        for t in range(p.N):

            @pl.when(p.n != t)
            def _():
                for i in range(2):
                    to(part(i), view(i), send.at[t, i], recv.at[p.slot, i], 2 * p.k + p.group, t).start()

    @pl.when(mine)
    def _():
        for i in range(2):
            pltpu.make_async_copy(part(i), view(i), local.at[i]).start()

    @pl.when(jnp.logical_not(mine))
    def _():
        for i in range(2):
            to(part(i), view(i), local.at[i], recv.at[p.slot, i], 2 * p.k + p.group, p.n).start()


def spread_pass(p, src, gathered, rows, send, recv, local, onward):
    if p.N == 4:
        half = rows // 2
        piece = src.at[pl.ds(0, half)]
        nx, ny, _ = neighbours(p)
        for i, (n, other) in enumerate(((nx, ny), (ny, nx))):
            j = slot_of(p, n, p.c)
            here = gathered.at[pl.ds(pl.multiple_of(j * rows + i * half, half), half)]
            pltpu.make_async_copy(piece, here, recv.at[j, i]).wait()
            to(here, here, onward.at[i], recv.at[j, i], p.w, other).start()


def spread_end(p, src, gathered, rows, send, recv, local, onward, on_slot=lambda j: None):
    half = rows // 2
    piece = src.at[pl.ds(0, half)]
    mine = p.group == p.c
    at = lambda j, i: gathered.at[pl.ds(pl.multiple_of(j * rows + i * half, half), half)]

    def arrive(j, i):
        pltpu.make_async_copy(piece, at(j, i), recv.at[j, i]).wait()

    for i in range(2):
        pltpu.make_async_copy(piece, at(0, 0), local.at[i]).wait()
    here = slot_of(p, p.n, p.c)

    @pl.when(jnp.logical_not(mine))
    def _():
        arrive(here, 0)
        arrive(here, 1)

    on_slot(here)
    if p.N == 4:
        nx, ny, nd = neighbours(p)
        jx, jy, jd = (slot_of(p, n, p.c) for n in (nx, ny, nd))
        arrive(jx, 1)
        on_slot(jx)
        arrive(jy, 0)
        on_slot(jy)
        arrive(jd, 0)
        arrive(jd, 1)
        on_slot(jd)
        for i in range(2):
            pltpu.make_async_copy(piece, at(0, 0), onward.at[i]).wait()
            for t in range(2):
                pltpu.make_async_copy(piece, at(0, 0), send.at[t, i]).wait()
    else:
        for t in range(p.N):

            @pl.when(p.n != t)
            def _():
                for i in range(2):
                    pltpu.make_async_copy(piece, at(0, 0), send.at[t, i]).wait()
                    arrive(slot_of(p, t, p.c), i)
                on_slot(slot_of(p, t, p.c))


def sum_bufs(narrow, rows, dim):
    if narrow == 4:
        half = pltpu.VMEM((2, 2, rows, dim // 2), BF)
        return [half, half, pltpu.VMEM((2, rows, dim), BF)]
    return [pltpu.VMEM((narrow, rows, dim), BF)]


def sum_sems(narrow):
    if narrow == 4:
        return [DMA((2, 2)), DMA((2, 2)), DMA((2, 2)), DMA((4,)), DMA((4,))]
    return [DMA((narrow,)), DMA((narrow,)), DMA]


def pieces(p, part, rows, dim):
    half = dim // 2
    return lambda j, i: part.at[pl.ds(pl.multiple_of(j * rows, rows), rows), pl.ds(i * half, half)]


def sum_start(p, part, rows, dim, bufs, sems):
    if p.N != 4:
        (got,), (send, recv, local) = bufs, sems
        for j in range(p.N):
            core, n = p.owner(j)
            mine = p.owner_is_me(j)
            src = part.at[pl.ds(j * rows, rows)]

            @pl.when(mine)
            def _():
                pltpu.make_async_copy(src, got.at[p.n], local).start()

            @pl.when(jnp.logical_not(mine))
            def _():
                to(src, got.at[p.n], send.at[j], recv.at[p.n], 2 * p.k + core, n).start()

        return
    own, inbox, _ = bufs
    load, send, recv, _, _ = sems
    piece = pieces(p, part, rows, dim)
    nx, ny, nd = neighbours(p)
    across, here = slot_of(p, nd, p.c), slot_of(p, p.n, p.c)
    for i, n in enumerate((nx, ny)):
        to(piece(across, i), inbox.at[i, 0], send.at[i, 0], recv.at[i, 0], p.w, n).start()
    for i, n in enumerate((ny, nx)):
        pltpu.make_async_copy(piece(slot_of(p, n, p.c), i), own.at[i, 0], load.at[i, 0]).start()
    for i, n in enumerate((nx, ny)):
        to(piece(slot_of(p, n, p.c), i), inbox.at[i, 1], send.at[i, 1], recv.at[i, 1], p.w, n).start()
        pltpu.make_async_copy(piece(here, i), own.at[i, 1], load.at[i, 1]).start()


def product_bufs(narrow, rows, dim):
    shape = (4, rows, dim // 2) if narrow == 4 else (narrow * rows, dim)
    return pltpu.VMEM(shape, BF)


def sum_start_of(p, product, out, rows, dim, bufs, sems):
    half = dim // 2
    if p.N != 4:

        def one(j, carry):
            for i in range(2):
                out[pl.ds(pl.multiple_of(j * rows, rows), rows), i * half : (i + 1) * half] = product(j, i)
            return carry

        lax.fori_loop(0, p.N, one, 0)
        sum_start(p, out, rows, dim, bufs, sems)
        return
    own, inbox, _ = bufs
    _, send, recv, _, _ = sems
    nx, ny, nd = neighbours(p)
    across, jx, jy, here = (slot_of(p, n, p.c) for n in (nd, nx, ny, p.n))

    def one(t, carry):
        i = lax.rem(t, 2)
        q = lax.rem(t // 2, 2)
        beside = jnp.where(i == 0, jx, jy)
        other = jnp.where(i == 0, jy, jx)
        j = jnp.where(t < 4, jnp.where(q == 0, across, beside), jnp.where(q == 0, other, here))
        y = product(j, i)

        @pl.when(t < 4)
        def _():
            out[t] = y
            to(out.at[t], inbox.at[i, q], send.at[i, q], recv.at[i, q], p.w, jnp.where(i == 0, nx, ny)).start()

        @pl.when(t >= 4)
        def _():
            own[i, q] = y

        return carry

    lax.fori_loop(0, 8, one, 0)


def core_of(p, j):
    return (j >= p.half).astype(jnp.int32)


def sum_pass(p, part, rows, dim, bufs, sems, loaded=False):
    if p.N != 4:
        return
    own, inbox, box = bufs
    load, send, recv, send2, recv2 = sems
    piece = lambda j, i: own.at[0, 0]
    half = dim // 2
    nx, ny, _ = neighbours(p)
    cols = lambda i: pl.ds(i * half, half)

    def add(i, q):
        if not loaded:
            pltpu.make_async_copy(piece(0, 0), own.at[i, q], load.at[i, q]).wait()
        pltpu.make_async_copy(piece(0, 0), inbox.at[i, q], recv.at[i, q]).wait()

        def body(at):
            own[i, q, at, :] = (own[i, q, at, :].astype(F32) + inbox[i, q, at, :].astype(F32)).astype(BF)

        row_loop(rows, 64, body)

    for i, n in enumerate((ny, nx)):
        add(i, 0)
        j = slot_of(p, n, p.c)
        to(own.at[i, 0], box.at[1, :, cols(i)], send2.at[i], recv2.at[i], 2 * p.k + core_of(p, j), n).start()
    j = slot_of(p, p.n, p.c)
    keep = core_of(p, j) == p.c
    for i in range(2):
        add(i, 1)

        @pl.when(keep)
        def _():
            pltpu.make_async_copy(own.at[i, 1], box.at[0, :, cols(i)], send2.at[2 + i]).start()

        @pl.when(jnp.logical_not(keep))
        def _():
            to(own.at[i, 1], box.at[0, :, cols(i)], send2.at[2 + i], recv2.at[2 + i], 2 * p.k + core_of(p, j), p.n).start()


def sum_end(p, part, rows, dim, bufs, sems):
    if p.N != 4:
        (got,), (send, recv, local) = bufs, sems
        for t in range(p.N):
            mine = (p.group == p.c) & (p.n == t)

            @pl.when(mine)
            def _():
                pltpu.make_async_copy(part.at[pl.ds(0, rows)], got.at[t], local).wait()

            @pl.when(jnp.logical_not(mine))
            def _():
                pltpu.make_async_copy(part.at[pl.ds(0, rows)], got.at[t], recv.at[t]).wait()

        for j in range(p.N):

            @pl.when(jnp.logical_not(p.owner_is_me(j)))
            def _():
                pltpu.make_async_copy(part.at[pl.ds(j * rows, rows)], got.at[0], send.at[j]).wait()

        return
    own, inbox, box = bufs
    load, send, recv, send2, recv2 = sems
    piece = lambda j, i: own.at[0, 0]
    half = dim // 2
    cols = lambda i: pl.ds(i * half, half)
    for i in range(2):
        for q in range(2):
            pltpu.make_async_copy(piece(0, 0), inbox.at[i, q], send.at[i, q]).wait()
        pltpu.make_async_copy(own.at[i, 0], box.at[1, :, cols(i)], send2.at[i]).wait()
        pltpu.make_async_copy(own.at[i, 0], box.at[1, :, cols(i)], recv2.at[i]).wait()
        pltpu.make_async_copy(own.at[i, 1], box.at[0, :, cols(i)], send2.at[2 + i]).wait()

        @pl.when(p.group != p.c)
        def _():
            pltpu.make_async_copy(own.at[i, 1], box.at[0, :, cols(i)], recv2.at[2 + i]).wait()


def total(p, bufs, at):
    if p.N == 4:
        box = bufs[2]
        return box[0, at, :].astype(F32) + box[1, at, :].astype(F32)
    got = bufs[0]
    out = got[0, at, :].astype(F32)
    for t in range(1, p.N):
        out = out + got[t, at, :].astype(F32)
    return out


PARTS = 4


def line_sems(chips):
    return [DMA((2, chips, PARTS)), DMA((chips, PARTS)), DMA((chips, PARTS)), DMA((chips, PARTS)), DMA((PARTS,))]


def line_parts(p, full, rows):
    size = rows // PARTS

    def at(s, core, q=None):
        first = (2 * s + core) * rows
        if q is None:
            return full.at[pl.ds(pl.multiple_of(first, rows), rows)]
        return full.at[pl.ds(pl.multiple_of(first + q * size, size), size)]

    return at


def each_part(body):
    def one(q, carry):
        body(q)
        return carry

    lax.fori_loop(0, PARTS, one, 0)


def line_copy(p, src, dst, send, recv, k, core):
    return pltpu.make_async_remote_copy(
        src_ref=src, dst_ref=dst, send_sem=send, recv_sem=recv, device_id=(2 * k + core, p.n), device_id_type=MESH
    )


def inside(p, k):
    return (k >= 0) & (k < p.C)


BOTH, UP, DOWN = ((0, 1), (1, -1)), ((0, 1),), ((1, -1),)


def line_push(p, src, full, rows, zsend, zrecv, csend, crecv, local, q, ways=BOTH):
    size = rows // PARTS
    part = src.at[pl.ds(pl.multiple_of(q * size, size), size)]
    there = line_parts(p, full, rows)(p.k, p.c, q)
    for i, sign in ways:

        @pl.when(inside(p, p.k + sign))
        def _():
            line_copy(p, part, there, zsend.at[i, 0, q], zrecv.at[p.k, q], p.k + sign, p.c).start()

    line_copy(p, part, there, csend.at[p.k, q], crecv.at[p.k, q], p.k, 1 - p.c).start()
    pltpu.make_async_copy(part, there, local.at[q]).start()


def came(p, s, ways):
    if ways == BOTH:
        return s == s
    return s <= p.k if ways == UP else s >= p.k


def line_steps(p, src, full, rows, zsend, zrecv, csend, crecv, local, ways=BOTH):
    at = line_parts(p, full, rows)
    piece = src.at[pl.ds(0, rows // PARTS)]

    def at_distance(d):
        def onward(q):
            for i, sign in ways:
                s, t = p.k - sign * d, p.k + sign

                @pl.when(inside(p, s))
                def _():
                    here = at(s, p.c, q)
                    pltpu.make_async_copy(piece, here, zrecv.at[s, q]).wait()

                    @pl.when(inside(p, t))
                    def _():
                        line_copy(p, here, here, zsend.at[i, d, q], zrecv.at[s, q], t, p.c).start()

                    line_copy(p, here, here, csend.at[s, q], crecv.at[s, q], p.k, 1 - p.c).start()

        each_part(onward)

    def settle(q):
        here = at(p.k, p.c, q)
        pltpu.make_async_copy(piece, here, local.at[q]).wait()
        for s in range(p.C):

            @pl.when(came(p, jnp.int32(s), ways))
            def _():
                pltpu.make_async_copy(piece, here, csend.at[s, q]).wait()
                pltpu.make_async_copy(piece, at(s, 1 - p.c, q), crecv.at[s, q]).wait()

        for i, sign in ways:
            for d in range(p.C):

                @pl.when(inside(p, p.k - sign * d) & inside(p, p.k + sign))
                def _():
                    pltpu.make_async_copy(piece, here, zsend.at[i, d, q]).wait()

    return [functools.partial(at_distance, d) for d in range(1, p.C)] + [lambda: each_part(settle)]


def line_sum_bufs(chips, rows, width):
    return [pltpu.VMEM((chips, rows, width), BF)] * 3 + [pltpu.VMEM((2, rows, width), BF), pltpu.VMEM((rows, width), F32)]


def line_sum_sems(chips):
    return [
        DMA((chips, PARTS)), DMA((chips, PARTS)), DMA((chips, PARTS)), DMA((2, chips, PARTS)), DMA((chips, PARTS)),
        DMA((2, PARTS)),
    ]


OTHER = {BOTH: BOTH, UP: DOWN, DOWN: UP}


def line_sum_start(p, part, rows, bufs, sems, ways=BOTH):
    own, inbox, _, _, _ = bufs
    load, csend, crecv, _, _, _ = sems
    at = line_parts(p, part, rows)
    size = rows // PARTS

    def share(s):
        def one(q):
            here = pl.ds(pl.multiple_of(q * size, size), size)
            line_copy(p, at(s, 1 - p.c, q), inbox.at[s, here], csend.at[s, q], crecv.at[s, q], p.k, 1 - p.c).start()
            pltpu.make_async_copy(at(s, p.c, q), own.at[s, here], load.at[s, q]).start()

        each_part(one)

    for d in range(p.C - 1, 0, -1):
        for _, sign in ways:
            s = p.k + sign * d

            @pl.when(inside(p, s))
            def _():
                share(s)

    share(p.k)


def line_sum_steps(p, part, rows, bufs, sems, ways=BOTH):
    own, inbox, relay, box, acc = bufs
    load, csend, crecv, zsend, rrecv, zrecv = sems
    size = rows // PARTS
    step = math.gcd(size, 128)
    piece = line_parts(p, part, rows)(0, 0, 0)

    def rows_of(q):
        return pl.ds(pl.multiple_of(q * size, size), size)

    def add(q, body):
        def one(j, carry):
            body(pl.ds(pl.multiple_of(q * size + j * step, step), step))
            return carry

        lax.fori_loop(0, size // step, one, 0)

    def pair(t, q):
        pltpu.make_async_copy(piece, own.at[t, rows_of(q)], load.at[t, q]).wait()
        pltpu.make_async_copy(piece, inbox.at[t, rows_of(q)], crecv.at[t, q]).wait()

    def at_distance(d):
        def onward(q):
            here = rows_of(q)
            for i, sign in ways:
                t = p.k + sign * d
                behind = inside(p, p.k - sign)

                @pl.when(inside(p, t))
                def _():
                    pair(t, q)

                    @pl.when(jnp.logical_not(behind))
                    def _():
                        def two(at):
                            own[t, at, :] = (own[t, at, :].astype(F32) + inbox[t, at, :].astype(F32)).astype(BF)

                        add(q, two)

                    @pl.when(behind)
                    def _():
                        pltpu.make_async_copy(piece, relay.at[t, here], rrecv.at[t, q]).wait()

                        def three(at):
                            both = own[t, at, :].astype(F32) + inbox[t, at, :].astype(F32)
                            own[t, at, :] = (both + relay[t, at, :].astype(F32)).astype(BF)

                        add(q, three)

                    src = own.at[t, here]
                    if d >= 2:
                        line_copy(p, src, relay.at[t, here], zsend.at[i, d, q], rrecv.at[t, q], p.k + sign, p.c).start()
                    else:
                        line_copy(p, src, box.at[i, here], zsend.at[i, d, q], zrecv.at[i, q], t, p.c).start()

        each_part(onward)

    def last(q):
        here = rows_of(q)
        pair(p.k, q)

        def first(at):
            acc[at, :] = own[p.k, at, :].astype(F32) + inbox[p.k, at, :].astype(F32)

        add(q, first)
        for i, sign in ways:

            @pl.when(inside(p, p.k - sign))
            def _():
                pltpu.make_async_copy(piece, box.at[i, here], zrecv.at[i, q]).wait()

                def more(at):
                    acc[at, :] += box[i, at, :].astype(F32)

                add(q, more)

            for d in range(1, p.C):

                @pl.when(inside(p, p.k + sign * d))
                def _():
                    pltpu.make_async_copy(piece, own.at[0, here], zsend.at[i, d, q]).wait()

        for s in range(p.C):

            @pl.when(came(p, jnp.int32(s), OTHER[ways]))
            def _():
                pltpu.make_async_copy(piece, inbox.at[s, here], csend.at[s, q]).wait()


    return [functools.partial(at_distance, d) for d in range(p.C - 1, 0, -1)] + [lambda: each_part(last)]


def row_loop(rows, step, body):
    def one(i, carry):
        body(pl.ds(pl.multiple_of(i * step, step), step))
        return carry

    lax.fori_loop(0, rows // step, one, 0)


STEP = 64


def inv_rms(u):
    return lax.rsqrt(jnp.mean(u * u, axis=-1, keepdims=True) + EPSILON)


def weave(gate_ref, up_ref, both_ref):
    ff = gate_ref.shape[1]
    t = math.gcd(ff, 256)
    for i in range(0, ff, t):
        both_ref[:, 2 * i : 2 * i + t] = gate_ref[:, i : i + t]
        both_ref[:, 2 * i + t : 2 * i + 2 * t] = up_ref[:, i : i + t]


def finish_kernel(both_ref, down_ref, qo_ref, kv_ref, gate_out, up_out, down_out, q_out, k_out, v_out, o_out):
    ff = gate_out.shape[1]
    t = math.gcd(ff, 256)
    for i in range(0, ff, t):
        gate_out[:, i : i + t] = both_ref[:, 2 * i : 2 * i + t].astype(F32)
        up_out[:, i : i + t] = both_ref[:, 2 * i + t : 2 * i + 2 * t].astype(F32)
    down_out[...] = jnp.transpose(down_ref[...].astype(F32))
    qw, kw = q_out.shape[1], k_out.shape[1]
    q_out[...] = qo_ref[:, :qw]
    o_out[...] = jnp.transpose(qo_ref[:, qw:])
    k_out[...] = kv_ref[:, :kw]
    v_out[...] = kv_ref[:, kw:]


def rotation(p, cos_ref, sin_ref):
    all_rows, hd = cos_ref.shape
    block, half, step = all_rows // 2, hd // 2, 64
    lane = lax.broadcasted_iota(jnp.int32, (step, hd), 1)
    column = jnp.where(lane < half, lane, lane - half).astype(F32)
    inverse = jnp.exp(column * (-2.0 * math.log(1000000.0) / hd))
    row = lax.broadcasted_iota(jnp.int32, (step, hd), 0)

    def body(i, carry):
        at = i * step
        first = jnp.where(at < block, (4 * p.k + p.c) * block + at, (4 * p.k + 3 - p.c) * block + at - block)
        angles = (first + row).astype(F32) * inverse
        here = pl.ds(pl.multiple_of(at, step), step)
        cos_ref[here, :] = jnp.cos(angles)
        sine = jnp.sin(angles)
        sin_ref[here, :] = jnp.where(lane < half, -sine, sine)
        return carry

    lax.fori_loop(0, all_rows // step, body, 0)


def input_kernel(
    wide, narrow, x_ref, gain_ref, wq_ref, wk_ref, wv_ref, wo_ref, gate_ref, up_ref, down_ref,
    gathered, full, gu_out, d_out, cos_out, sin_out, gu_ref, d_ref, cos_ref, sin_ref, buf, shard, store, *sems
):
    p = Place(wide, narrow)
    rows = x_ref.shape[0]
    lo = 0
    for w_ref in (wq_ref, wk_ref, wv_ref):
        shard[:, lo : lo + w_ref.shape[1]] = w_ref[...]
        lo += w_ref.shape[1]
    shard[:, lo:] = jnp.transpose(wo_ref[...])
    spread, line = sems[:4], (shard, full, shard.shape[0], *sems[4:])
    enter(p, line=True)
    each_part(lambda q: line_push(p, *line, q))
    *steps, end = line_steps(p, *line)

    def body(at):
        u = x_ref[at, :].astype(F32)
        buf[at, :] = (u * inv_rms(u) * gain_ref[...]).astype(BF)

    row_loop(rows, STEP, body)
    spread_start(p, buf, gathered, rows, *spread)
    weave(gate_ref, up_ref, gu_ref)
    d_ref[...] = jnp.transpose(down_ref[...])
    steps[0]()
    rotation(p, cos_ref, sin_ref)
    pairs = ((gu_ref, gu_out), (d_ref, d_out), (cos_ref, cos_out), (sin_ref, sin_out))
    stores = [pltpu.make_async_copy(src, dst, store.at[i]) for i, (src, dst) in enumerate(pairs)]
    for copy in stores:
        copy.start()
    spread_pass(p, buf, gathered, rows, *spread)
    for step in steps[1:]:
        step()
    spread_end(p, buf, gathered, rows, *spread)
    end()
    for copy in stores:
        copy.wait()


def turn(u):
    return pltpu.roll(u, u.shape[-1] // 2, 1)


def qkv_kernel(
    wide, narrow, qw, kw, fold, g_ref, x_ref, w_ref, cos_ref, sin_ref, qg_ref, kg_ref,
    gathered, full, qproj_out, kproj_out, q_out, qproj_ref, kproj_ref, q_ref, kv_ref, w_buf, x_buf, load, store, *sems,
):
    p = Place(wide, narrow)
    rows = g_ref.shape[0]
    hd = cos_ref.shape[1]
    all_rows = x_ref.shape[0]
    size = all_rows // 4
    spread, line = sems[:4], (kv_ref, full, all_rows, *sems[4:])
    weights = pltpu.make_async_copy(w_ref.at[:, pl.ds(0, w_buf.shape[1])], w_buf, load.at[0])
    normed = pltpu.make_async_copy(x_ref, x_buf, load.at[1])
    normed.start()
    weights.start()
    enter(p, line=True)

    def project(q):
        at = pl.ds(pl.multiple_of(q * size, size), size)
        y = dg(x_buf[at, :], w_buf[...], NN)
        cos, sin = cos_ref[at, :], sin_ref[at, :]
        qproj_ref[at, :] = y[:, :qw]
        kproj_ref[at, :] = y[:, qw : qw + kw]

        def head(lo, gain):
            u = y[:, lo : lo + hd]
            v = u * inv_rms(u) * gain
            return v * cos + turn(v) * sin

        for h in range(kw // hd):
            kv_ref[at, 2 * h * hd : (2 * h + 1) * hd] = head(qw + h * hd, kg_ref[...]).astype(BF)
            kv_ref[at, (2 * h + 1) * hd : (2 * h + 2) * hd] = y[:, qw + kw + h * hd : qw + kw + (h + 1) * hd].astype(BF)
        for i in range(PARTS // 4):
            line_push(p, *line, q * (PARTS // 4) + i, ways=UP)
        for h in range(qw // hd):
            q_ref[at, h * hd : (h + 1) * hd] = (head(h * hd, qg_ref[...]) * fold).astype(BF)

    normed.wait()
    weights.wait()

    def one(q, carry):
        project(q)
        return carry

    lax.fori_loop(0, 4, one, 0)
    pairs = ((qproj_ref, qproj_out), (kproj_ref, kproj_out), (q_ref, q_out))
    stores = [pltpu.make_async_copy(src, dst, store.at[i]) for i, (src, dst) in enumerate(pairs)]
    spread_start(p, g_ref, gathered, rows, *spread)
    for copy in stores:
        copy.start()
    *steps, end = line_steps(p, *line, ways=UP)
    steps[0]()
    spread_pass(p, g_ref, gathered, rows, *spread)
    for step in steps[1:]:
        step()
    spread_end(p, g_ref, gathered, rows, *spread)
    end()
    for copy in stores:
        copy.wait()


def middle_kernel(wide, narrow, part, own_ref, gain_ref, mid_ref, gathered, buf, *refs):
    p = Place(wide, narrow)
    rows, dim = own_ref.shape
    bufs, sems, spread = split_refs(narrow, refs)
    enter(p)
    sum_start(p, part, rows, dim, bufs, sems)
    sum_pass(p, part, rows, dim, bufs, sems)
    sum_end(p, part, rows, dim, bufs, sems)

    def body(at):
        u = own_ref[at, :].astype(F32) + total(p, bufs, at)
        mid_ref[at, :] = u
        buf[at, :] = (u * inv_rms(u) * gain_ref[...]).astype(BF)

    row_loop(rows, STEP, body)
    spread_start(p, buf, gathered, rows, *spread)
    spread_pass(p, buf, gathered, rows, *spread)
    spread_end(p, buf, gathered, rows, *spread)


def split_refs(narrow, refs):
    bufs, sems = (3, 5) if narrow == 4 else (1, 3)
    return refs[:bufs], refs[bufs : bufs + sems], refs[bufs + sems :]


def norm_back(u, gain, cot):
    r = inv_rms(u)
    a = cot * gain
    du = r * a - u * (r * r * r) * jnp.mean(a * u, axis=-1, keepdims=True)
    return du, jnp.sum(cot * u * r, axis=0, keepdims=True)


def mlp_back_kernel(
    wide, narrow, g_ref, wd_ref, gu_ref, w_ref, x_ref, mid_ref, gain_ref, grad_ref, back_out, rows_ref, dgain_ref, wgrad,
    g_buf, wd_buf, gu_buf, low, w_buf, x_buf, mid_buf, grad_buf, back_ref, stage, out, load, tiles_in, store, leave, *refs
):
    p = Place(wide, narrow)
    rows, dim = mid_ref.shape
    half = dim // 2
    t = wd_buf.shape[2]
    bufs, sems, _ = split_refs(narrow, refs)

    def tile_of(i):
        slot = lax.rem(i, 2)
        return (
            pltpu.make_async_copy(wd_ref.at[:, pl.ds(pl.multiple_of(i * t, t), t)], wd_buf.at[slot], tiles_in.at[0, slot]),
            pltpu.make_async_copy(gu_ref.at[:, pl.ds(pl.multiple_of(2 * i * t, t), 2 * t)], gu_buf.at[slot], tiles_in.at[1, slot]),
        )

    loads = [pltpu.make_async_copy(g_ref, g_buf, load.at[0])]
    for i in range(2):
        at = pl.ds(i * half, half)
        loads.append(pltpu.make_async_copy(w_ref.at[at], w_buf.at[at], load.at[1 + i]))
    loads.append(pltpu.make_async_copy(x_ref, x_buf, load.at[3]))
    loads.append(pltpu.make_async_copy(mid_ref, mid_buf, load.at[4]))
    loads.append(pltpu.make_async_copy(grad_ref, grad_buf, load.at[5]))
    loads[0].start()
    for copy in tile_of(0):
        copy.start()
    enter(p)
    loads[0].wait()
    count = wd_ref.shape[1] // t

    def gates(i, carry):
        @pl.when(i + 1 < count)
        def _():
            for copy in tile_of(i + 1):
                copy.start()

        for copy in tile_of(i):
            copy.wait()

        @pl.when(i == 0)
        def _():
            for copy in loads[1:3]:
                copy.start()

        slot = lax.rem(i, 2)
        hb = dg(g_buf[...], wd_buf[slot], NN)
        at = pl.multiple_of(2 * i * t, t)
        low[:, pl.ds(at, t)] = (hb * gu_buf[slot, :, :t]).astype(BF)
        low[:, pl.ds(pl.multiple_of(at + t, t), t)] = (hb * gu_buf[slot, :, t:]).astype(BF)
        return carry

    lax.fori_loop(0, count, gates, 0)
    for copy in loads[3:]:
        copy.start()
    for copy in loads[1:3]:
        copy.wait()

    def product(j, i):
        a = low[pl.ds(pl.multiple_of(j * rows, rows), rows), :]
        return dg(a, w_buf[pl.ds(pl.multiple_of(i * half, half), half), :], NT).astype(BF)

    sum_start_of(p, product, out, rows, dim, bufs, sems)
    dgain_ref[...] = jnp.zeros_like(dgain_ref)
    loads[3].wait()
    tile = 256

    def write(i):
        return pltpu.make_async_copy(
            stage.at[lax.rem(i, 2)], wgrad.at[pl.ds(pl.multiple_of(i * tile, tile), tile)], store.at[lax.rem(i, 2)]
        )

    def grads(first, last):
        def one(i, carry):
            @pl.when(i >= 2)
            def _():
                write(i - 2).wait()

            stage[lax.rem(i, 2)] = dg(x_buf[:, pl.ds(pl.multiple_of(i * tile, tile), tile)], low[...], TN).astype(BF)
            write(i).start()
            return carry

        lax.fori_loop(first, last, one, 0)

    tiles = dim // tile
    early = 3
    grads(0, early)
    sum_pass(p, out, rows, dim, bufs, sems, loaded=narrow == 4)
    grads(early, tiles)
    sum_end(p, out, rows, dim, bufs, sems)
    for copy in loads[4:]:
        copy.wait()

    def body(at):
        du, dgain = norm_back(mid_buf[at, :], gain_ref[...], total(p, bufs, at))
        back = grad_buf[at, :].astype(F32) + du
        back_ref[at, :] = back
        pltpu.make_async_copy(back_ref.at[at], back_out.at[at], leave).start()
        rows_ref[at, :] = back.astype(BF)
        dgain_ref[...] += dgain

    row_loop(rows, STEP, body)
    pltpu.make_async_copy(back_ref, back_out, leave).wait()
    write(tiles - 2).wait()
    write(tiles - 1).wait()


def middle_back_kernel(
    wide, narrow, wo_at, groups, hd, rows_ref, hidden, w_ref, wo_ref, o_ref, all_ref, next_ref, back_ref, delta_ref,
    gathered, next_buf, h_buf, w_buf, wo_buf, o_buf, load, store, next_store, *spread
):
    p = Place(wide, narrow)
    rows = rows_ref.shape[0]
    pairs = ((hidden, h_buf), (w_ref, w_buf), (wo_ref.at[:, pl.ds(*wo_at)], wo_buf), (o_ref, o_buf))
    loads = [pltpu.make_async_copy(src, dst, load.at[i]) for i, (src, dst) in enumerate(pairs)]
    enter(p)
    spread_start(p, rows_ref, gathered, rows, *spread)
    for copy in loads:
        copy.start()
    for copy in loads[:2]:
        copy.wait()

    def write_next(i):
        at = pl.ds(pl.multiple_of(i * 256, 256), 256)
        return pltpu.make_async_copy(next_buf.at[at], next_ref.at[at], next_store.at[i])

    def write_slot(j):
        at = pl.ds(pl.multiple_of(j * rows, rows), rows)
        return pltpu.make_async_copy(gathered.at[at], all_ref.at[at], store.at[j])

    def downs(first, last):
        def one(i, carry):
            at = pl.ds(pl.multiple_of(i * 256, 256), 256)
            next_buf[at, :] = dg(h_buf[at, :], w_buf[...], NT).astype(BF)
            write_next(i).start()
            return carry

        lax.fori_loop(first, last, one, 0)

    blocks = next_buf.shape[0] // 256
    downs(0, blocks // 2)

    def on_slot(j):
        at = pl.ds(pl.multiple_of(j * rows, rows), rows)
        write_slot(j).start()
        back = dg(gathered[at, :], wo_buf[...], NN).astype(BF)
        back_ref[at, :] = back
        lane = lax.broadcasted_iota(jnp.int32, (rows, hd), 1)
        out = jnp.zeros((rows, hd), F32)
        for h in range(back.shape[1] // hd):
            mine = slice(h * hd, (h + 1) * hd)
            row = 8 * (h // groups) + h % groups
            delta = jnp.sum(back[:, mine].astype(F32) * o_buf[at, mine], axis=1, keepdims=True)
            out = jnp.where(lane == row, delta, out)
        delta_ref[:, at] = jnp.transpose(out)[: delta_ref.shape[0]]

    spread_pass(p, rows_ref, gathered, rows, *spread)
    downs(blocks // 2, blocks)
    for copy in loads[2:]:
        copy.wait()
    spread_end(p, rows_ref, gathered, rows, *spread, on_slot=on_slot)
    for i in range(blocks):
        write_next(i).wait()
    for j in range(p.N):
        write_slot(j).wait()


def share_start(me, count, here, slots, sends, recvs, device):
    slots[me] = here[...]
    for t in range(count):

        @pl.when(me != t)
        def _():
            wide_at, narrow_at = device(t)
            to(here, slots.at[me], sends.at[t], recvs.at[me], wide_at, narrow_at).start()


def share_end(me, count, here, slots, sends, recvs):
    for t in range(count):

        @pl.when(me != t)
        def _():
            pltpu.make_async_copy(here, slots.at[t], sends.at[t]).wait()
            pltpu.make_async_copy(here, slots.at[t], recvs.at[t]).wait()

    out = slots[0]
    for t in range(1, count):
        out = out + slots[t]
    here[...] = out


def head_back(cot, u, gain, cos, sin):
    cot = cot * cos - turn(cot) * sin
    return norm_back(u, gain, cot)


def output_kernel(
    wide, narrow, part, mid_ref, dkv, dq, qproj, cos_ref, sin_ref, g_ref, x_ref, m_ref, a_ref,
    out_out, kv_ref, low_out, dgain_ref, wgrad_out, out_ref, low_ref, wgrad_ref, dq_buf, u_buf, x_buf, m_buf, a_buf, mid_buf, load, store, leave, *refs
):
    p = Place(wide, narrow)
    rows, dim = mid_ref.shape
    kv_rows = kv_ref.shape[0]
    width = low_ref.shape[1]
    hd = cos_ref.shape[1]
    bufs, sems, line = split_refs(narrow, refs)
    sums = (part, rows, dim, bufs, sems)
    chain = (p, dkv, kv_rows, line[:5], line[5:])
    pairs = ((dq, dq_buf), (qproj, u_buf), (x_ref, x_buf), (m_ref, m_buf), (a_ref, a_buf), (mid_ref, mid_buf))
    loads = [pltpu.make_async_copy(src, dst, load.at[i]) for i, (src, dst) in enumerate(pairs)]
    enter(p, line=True)
    line_sum_start(*chain, ways=DOWN)
    sum_start(p, *sums)
    for copy in loads:
        copy.start()
    first, *steps, last = line_sum_steps(*chain, ways=DOWN)
    first()
    dgain_ref[...] = jnp.zeros_like(dgain_ref)
    for copy in loads[:2]:
        copy.wait()

    def through_heads(at):
        for h in range(width // hd):
            mine = slice(h * hd, (h + 1) * hd)
            du, dgain = head_back(dq_buf[at, mine], u_buf[at, mine], g_ref[...], cos_ref[at, :], sin_ref[at, :])
            low_ref[at, mine] = du.astype(BF)
            dgain_ref[...] += dgain

    row_loop(low_ref.shape[0], 128, through_heads)
    low_store = pltpu.make_async_copy(low_ref, low_out, leave.at[0])
    low_store.start()
    for copy in loads[2:]:
        copy.wait()

    def write(i):
        at = pl.ds(pl.multiple_of(i * 256, 256), 256)
        return pltpu.make_async_copy(wgrad_ref.at[at], wgrad_out.at[at], store.at[i])

    def grads(first_tile, last_tile):
        def one(i, carry):
            at = pl.ds(pl.multiple_of(i * 256, 256), 256)
            wgrad_ref[at, :width] = dg(x_buf[:, at], low_ref[...], TN).astype(BF)
            wgrad_ref[at, width:] = dg(m_buf[:, at], a_buf[...], TN).astype(BF)
            write(i).start()
            return carry

        lax.fori_loop(first_tile, last_tile, one, 0)

    tiles = dim // 256
    grads(0, tiles // 2)
    sum_pass(p, *sums)
    steps[0]()
    grads(tiles // 2, tiles)
    sum_end(p, *sums)

    def body(at):
        out_ref[at, :] = (mid_buf[at, :] + total(p, bufs, at)).astype(BF)

    row_loop(rows, STEP, body)
    out_store = pltpu.make_async_copy(out_ref, out_out, leave.at[1])
    out_store.start()
    for step in steps[1:]:
        step()
    last()
    row_loop(kv_rows, 128, lambda at: kv_ref.__setitem__((at, slice(None)), line[4][at, :].astype(BF)))
    for i in range(tiles):
        write(i).wait()
    low_store.wait()
    out_store.wait()


def input_back_kernel(
    wide, narrow, qw, kw, own_ref, gain_ref, back_ref, mlp_ref, qg_ref, wgrad, q_ref, kv_ref, proj_ref, cos_ref, sin_ref, kg_ref,
    w_ref, x_ref, out_out, gsum_ref, wsum_ref, kvsum_ref,
    gbuf, gbuf2, low, part, kvgrad, w_buf, x_buf, own_buf, back_buf, out_ref, load, leave, gsend, grecv, gsend2, grecv2, *refs,
):
    p = Place(wide, narrow)
    rows, dim = own_ref.shape
    hd = cos_ref.shape[1]
    all_rows = x_ref.shape[0]
    w_rows = wsum_ref.shape[0]
    bufs, sems, line = split_refs(narrow, refs)
    sums = (part, rows, dim, bufs, sems)
    first_line = (p, wgrad, w_rows, (*line[:4], wsum_ref), line[4:10])
    second_line = (p, kvgrad, w_rows, (*line[10:14], kvsum_ref), line[14:])
    weights = pltpu.make_async_copy(w_ref.at[:, pl.ds(0, w_buf.shape[1])], w_buf, load.at[0])
    weights.start()
    normed = pltpu.make_async_copy(x_ref, x_buf, load.at[1])
    normed.start()
    later = [pltpu.make_async_copy(own_ref, own_buf, load.at[2]), pltpu.make_async_copy(back_ref, back_buf, load.at[3])]
    for copy in later:
        copy.start()
    enter(p, ring=True)
    line_sum_start(*first_line)
    gsum_ref[...] = jnp.zeros_like(gsum_ref)
    gsum_ref[:, dim : 2 * dim] = mlp_ref[...]
    gsum_ref[:, 2 * dim : 2 * dim + hd] = qg_ref[...]
    size = min(all_rows, 256)
    first = line_sum_steps(*first_line)
    first[0]()
    weights.wait()

    def through_heads(at):
        low[at, :qw] = q_ref[at, :]
        for h in range(kw // hd):
            key = slice(2 * h * hd, (2 * h + 1) * hd)
            value = slice((2 * h + 1) * hd, (2 * h + 2) * hd)
            mine = slice(qw + h * hd, qw + (h + 1) * hd)
            du, dgain = head_back(
                kv_ref[at, key].astype(F32), proj_ref[at, h * hd : (h + 1) * hd], kg_ref[...], cos_ref[at, :], sin_ref[at, :]
            )
            low[at, mine] = du.astype(BF)
            low[at, qw + kw + h * hd : qw + kw + (h + 1) * hd] = kv_ref[at, value]
            gsum_ref[:, 2 * dim + hd :] += dgain
        part[at, :] = dg(low[at, :], w_buf[...], NT).astype(BF)

    row_loop(all_rows, size, through_heads)
    sum_start(p, *sums)
    first[1]()

    normed.wait()

    def key_grads(at):
        kvgrad[at, :] = dg(x_buf[:, at], low[:, qw:], TN).astype(BF)

    row_loop(dim, 256, key_grads)
    line_sum_start(*second_line)
    second = line_sum_steps(*second_line)
    second[0]()
    for step in first[2:-1]:
        step()
    sum_pass(p, *sums)
    for step in second[1:-1]:
        step()
    sum_end(p, *sums)
    for copy in later:
        copy.wait()

    def body(at):
        du, dgain = norm_back(own_buf[at, :].astype(F32), gain_ref[...], total(p, bufs, at))
        out_ref[at, :] = back_buf[at, :] + du
        gsum_ref[:, :dim] += dgain

    row_loop(rows, STEP, body)
    out_store = pltpu.make_async_copy(out_ref, out_out, leave)
    out_store.start()

    share_start(p.n, narrow, gsum_ref, gbuf, gsend, grecv, lambda t: (p.w, t))
    first[-1]()
    share_end(p.n, narrow, gsum_ref, gbuf, gsend, grecv)
    share_start(p.w, wide, gsum_ref, gbuf2, gsend2, grecv2, lambda t: (t, p.n))
    second[-1]()
    share_end(p.w, wide, gsum_ref, gbuf2, gsend2, grecv2)
    out_store.wait()


VM = pl.BlockSpec(memory_space=pltpu.VMEM)


HB = pl.BlockSpec(memory_space=pl.ANY)


def comm_call(kernel, name, cid, out_shape, in_specs, out_specs, scratch, *args):
    return pl.pallas_call(
        kernel,
        out_shape=out_shape,
        in_specs=in_specs,
        out_specs=out_specs,
        scratch_shapes=scratch,
        compiler_params=pltpu.CompilerParams(collective_id=cid, has_side_effects=True, vmem_limit_bytes=60 << 20),
        cost_estimate=pl.CostEstimate(flops=0, bytes_accessed=160_000_000, transcendentals=0),
        name=name,
    )(*args)


def sds(shape, kind):
    return jax.ShapeDtypeStruct(shape, kind)


def plain(kernel, name, grid, in_specs, out_specs, out_shape, flops, nbytes, *args, scratch=(), aliases=None):
    return pl.pallas_call(
        kernel,
        out_shape=out_shape,
        grid=grid,
        in_specs=in_specs,
        out_specs=out_specs,
        scratch_shapes=scratch,
        input_output_aliases=aliases or {},
        compiler_params=pltpu.CompilerParams(vmem_limit_bytes=52 << 20),
        cost_estimate=pl.CostEstimate(flops=flops, bytes_accessed=nbytes, transcendentals=0),
        name=name,
    )(*args)


def whole(shape):
    return pl.BlockSpec(shape, lambda *i: (0,) * len(shape), pipeline_mode=pl.Buffered(1))


def by_rows(tm, width):
    return pl.BlockSpec((tm, width), lambda i: (i, 0))


def mlp_fwd_kernel(x_ref, w_ref, gu_ref, h_ref):
    t = h_ref.shape[1]
    y = dg(x_ref[...], w_ref[...], NN)
    gate, up = y[:, :t], y[:, t:]
    s = jax.nn.sigmoid(gate)
    silu = gate * s
    h_ref[...] = (silu * up).astype(BF)
    gu_ref[:, :t] = (up * s * (1.0 + gate * (1.0 - s))).astype(BF)
    gu_ref[:, t:] = silu.astype(BF)


def mlp_fwd(x, w, t):
    rows, dim = x.shape
    ff2 = w.shape[1]
    return plain(
        mlp_fwd_kernel, "mlp_fwd", (ff2 // (2 * t),),
        [whole((rows, dim)), pl.BlockSpec((dim, 2 * t), lambda i: (0, i))],
        [pl.BlockSpec((rows, 2 * t), lambda i: (0, i)), pl.BlockSpec((rows, t), lambda i: (0, i))],
        (sds((rows, ff2), BF), sds((rows, ff2 // 2), BF)),
        2 * rows * dim * ff2, rows * dim * 2 + dim * ff2 * 2 + rows * ff2 * 3, x, w,
    )


def fwd_kernel(groups, hd, tab, q_ref, kv_ref, o_ref, low_ref, lse_ref, acc, lsum):
    s = pl.program_id(1)
    block = q_ref.shape[0]
    diag, first, last = tab[2, s], tab[3, s], tab[4, s]

    @pl.when(first == 1)
    def _():
        acc[...] = jnp.zeros_like(acc)
        lsum[...] = jnp.zeros_like(lsum)

    def work(masked):
        k, v = kv_ref[:, :hd], kv_ref[:, hd:]
        for g in range(groups):
            at = slice(g * hd, (g + 1) * hd)
            scores = dg(q_ref[:, at], k, NT)
            if masked:
                row = lax.broadcasted_iota(jnp.int32, scores.shape, 0)
                col = lax.broadcasted_iota(jnp.int32, scores.shape, 1)
                scores = jnp.where(col <= row, scores, MASKED)
            probs = jnp.exp2(scores)
            part = probs[:, :128]
            for j in range(1, block // 128):
                part = part + probs[:, j * 128 : (j + 1) * 128]
            lsum[g] += part
            acc[:, at] += dg(probs.astype(BF), v, NN)

    @pl.when(diag == 0)
    def _():
        work(False)

    @pl.when(diag == 1)
    def _():
        work(True)

    @pl.when(last == 1)
    def _():
        lane = lax.broadcasted_iota(jnp.int32, (block, 128), 1)
        lse = jnp.zeros((block, 128), F32)
        for g in range(groups):
            at = slice(g * hd, (g + 1) * hd)
            l = jnp.sum(lsum[g], axis=1, keepdims=True)
            out = acc[:, at] / l
            o_ref[:, at] = out
            low_ref[:, at] = out.astype(BF)
            lse = jnp.where(lane == g, jnp.log2(l), lse)
        lse_ref[...] = jnp.transpose(lse)[: lse_ref.shape[0]]


def attn_fwd(tab, q, kv, groups, hd, block):
    rows, width = q.shape
    gw = groups * hd
    heads = width // gw
    steps = tab.shape[1]
    mine = pl.BlockSpec((block, gw), lambda h, s, t: (t[0, s], h))
    return pl.pallas_call(
        functools.partial(fwd_kernel, groups, hd),
        out_shape=(sds((rows, width), F32), sds((rows, width), BF), sds((8 * heads, rows), F32)),
        grid_spec=pltpu.PrefetchScalarGridSpec(
            num_scalar_prefetch=1,
            grid=(heads, steps),
            in_specs=[mine, pl.BlockSpec((block, 2 * hd), lambda h, s, t: (t[1, s], h))],
            out_specs=[mine, mine, pl.BlockSpec((8, block), lambda h, s, t: (h, t[0, s]))],
            scratch_shapes=[pltpu.VMEM((block, gw), F32), pltpu.VMEM((groups, block, 128), F32)],
        ),
        compiler_params=pltpu.CompilerParams(vmem_limit_bytes=48 << 20),
        cost_estimate=pl.CostEstimate(
            flops=heads * steps * block * block * gw * 4,
            bytes_accessed=heads * steps * block * hd * 8,
            transcendentals=heads * steps * block * block * groups,
        ),
        name="attn_fwd",
    )(tab, q, kv)


def bwd_kernel(groups, hd, tab, q_ref, do_ref, kv_ref, lse_ref, delta_ref, dq_ref, dkv_ref, dq_sum, dkv_sum):
    s = pl.program_id(1)
    block = q_ref.shape[0]
    qi, diag, first, last = tab[0, s], tab[2, s], tab[3, s], tab[4, s]

    @pl.when(s == 0)
    def _():
        dq_sum[...] = jnp.zeros_like(dq_sum)

    @pl.when(first == 1)
    def _():
        dkv_sum[...] = jnp.zeros_like(dkv_sum)

    def work(masked):
        k, v = kv_ref[:, :hd], kv_ref[:, hd:]
        for g in range(groups):
            at = slice(g * hd, (g + 1) * hd)
            q, do = q_ref[:, at], do_ref[:, at]
            scores = dg(k, q, NT) - lse_ref[g : g + 1, :]
            if masked:
                row = lax.broadcasted_iota(jnp.int32, scores.shape, 0)
                col = lax.broadcasted_iota(jnp.int32, scores.shape, 1)
                scores = jnp.where(row <= col, scores, MASKED)
            probs = jnp.exp2(scores)
            dots = dg(v, do, NT)
            dkv_sum[:, hd:] += dg(probs.astype(BF), do, NN)
            back = (probs * (dots - delta_ref[g : g + 1, :])).astype(BF)
            dkv_sum[:, :hd] += dg(back, q, NN)
            dq_sum[qi, :, at] += dg(back, k, TN)

    @pl.when(diag == 0)
    def _():
        work(False)

    @pl.when(diag == 1)
    def _():
        work(True)

    @pl.when(last == 1)
    def _():
        dkv_ref[:, :hd] = (dkv_sum[:, :hd] * math.log(2.0)).astype(BF)
        dkv_ref[:, hd:] = dkv_sum[:, hd:].astype(BF)

    @pl.when(s == pl.num_programs(1) - 1)
    def _():
        for i in range(dq_sum.shape[0]):
            dq_ref[i * block : (i + 1) * block, :] = dq_sum[i] * hd**-0.5


def attn_bwd(tab, q, do, kv, lse, delta, groups, hd, block):
    rows, width = q.shape
    gw = groups * hd
    heads = width // gw
    steps = tab.shape[1]
    mine = pl.BlockSpec((block, gw), lambda h, s, t: (t[0, s], h))
    keys = pl.BlockSpec((block, 2 * hd), lambda h, s, t: (t[1, s], h))
    stat = pl.BlockSpec((8, block), lambda h, s, t: (h, t[0, s]))
    return pl.pallas_call(
        functools.partial(bwd_kernel, groups, hd),
        out_shape=(sds((rows, width), F32), sds(kv.shape, BF)),
        grid_spec=pltpu.PrefetchScalarGridSpec(
            num_scalar_prefetch=1,
            grid=(heads, steps),
            in_specs=[mine, mine, keys, stat, stat],
            out_specs=[pl.BlockSpec((rows, gw), lambda h, s, t: (0, h)), keys],
            scratch_shapes=[pltpu.VMEM((rows // block, block, gw), F32), pltpu.VMEM((block, 2 * hd), F32)],
        ),
        compiler_params=pltpu.CompilerParams(vmem_limit_bytes=48 << 20),
        cost_estimate=pl.CostEstimate(
            flops=heads * steps * block * block * gw * 10,
            bytes_accessed=heads * steps * block * hd * 16,
            transcendentals=heads * steps * block * block * groups,
        ),
        name="attn_bwd",
    )(tab, q, do, kv, lse, delta)


def place(w):
    k, core = w // 2, w % 2
    return 4 * k + core, 4 * k + 3 - core


def block_row(b):
    m = b % 4
    core = jnp.where((m == 1) | (m == 2), 1, 0)
    return 2 * (2 * (b // 4) + core) + jnp.where(m < 2, 0, 1)


def tables(w, chips):
    a, b = place(w)
    count = a + b + 2
    every = jnp.arange(8 * chips - 2, dtype=jnp.int32)
    s, idle = jnp.minimum(every, count - 1), every >= count
    in_a = s <= a
    key = jnp.where(in_a, s, s - a - 1)
    diag = jnp.where(in_a, s == a, s == count - 1)
    fwd = [jnp.where(in_a, 0, 1), block_row(key), jnp.where(idle, 2, diag), ~idle & (key == 0), ~idle & diag]
    both = s < 2 * (a + 1)
    even = s % 2 == 0
    key = jnp.where(both, s // 2, s - (a + 1))
    query = jnp.where(both & even, 0, 1)
    diag = key == jnp.where(query == 0, a, b)
    zero = (every >= count) & (w % 2 == 1)
    key = jnp.where(zero, b + 1, key)
    only = zero & (every == count)
    bwd = [query, block_row(key), jnp.where(idle, 2, diag), only | ~idle & (~both | even), only | ~idle & (~both | ~even)]
    return tuple(jnp.stack([row.astype(jnp.int32) for row in rows]) for rows in (fwd, bwd))


def per_device(
    wide, narrow,
    layer_input, w_query, w_key, w_value, w_output, w_gate, w_up, w_down,
    attn_gain, mlp_gain, query_gain, key_gain, out_grad,
):
    hd = query_gain.shape[0]
    rows, dim = layer_input.shape
    all_rows = narrow * rows
    chips = wide // 2
    block = all_rows // 2
    qw, kw = w_query.shape[1], w_key.shape[1]
    ff = w_gate.shape[1]
    groups = qw // kw
    kv_heads = kw // hd
    w = lax.axis_index("wide")
    fwd_tab, bwd_tab = tables(w, chips)
    def gather(shard):
        return lax.all_gather(shard, "wide", axis=0, tiled=True)

    def scatter(grad):
        return lax.psum_scatter(grad, "wide", scatter_dimension=0, tiled=True)

    t = math.gcd(ff, 256)

    spread_s = spread_sems(narrow)
    sum_s = [*sum_bufs(narrow, rows, dim), *sum_sems(narrow)]
    row_buf = pltpu.VMEM((rows, dim), BF)
    low_rows, full_rows, all_low = sds((rows, dim), BF), sds((rows, dim), F32), sds((all_rows, dim), BF)
    ring = functools.partial
    qg, kg = query_gain[None], key_gain[None]
    after = lax.optimization_barrier

    in_scratch = [*spread_s, *line_sems(chips)]
    table = sds((all_rows, hd), F32)
    s_rows, s_cols = w_query.shape[0], 2 * qw + 2 * kw
    normed_all, w_attn, gu_shard, d_shard, cos_table, sin_table = comm_call(
        ring(input_kernel, wide, narrow), "input_rows", 0,
        (all_low, sds((dim, s_cols), BF), sds((s_rows, 2 * ff), BF), sds((s_rows, ff), BF), table, table),
        [VM] * 9, (HB,) * 6,
        [pltpu.VMEM((s_rows, 2 * ff), BF), pltpu.VMEM((s_rows, ff), BF), *[pltpu.VMEM((all_rows, hd), F32)] * 2,
         row_buf, pltpu.VMEM((s_rows, s_cols), BF), DMA((4,)), *in_scratch],
        layer_input, attn_gain[None], w_query, w_key, w_value, w_output, w_gate, w_up, w_down,
    )
    width = qw + 2 * kw
    grad_all, kv, query_proj, key_proj, queries = comm_call(
        ring(qkv_kernel, wide, narrow, qw, kw, hd**-0.5 * math.log2(math.e)), "qkv_rows", 1,
        (all_low, sds((wide * all_rows, 2 * kw), BF), sds((all_rows, qw), F32),
         sds((all_rows, kw), F32), sds((all_rows, qw), BF)),
        [VM, HB, HB, VM, VM, VM, VM], (HB, HB, HB, HB, HB),
        [pltpu.VMEM((all_rows, qw), F32), pltpu.VMEM((all_rows, kw), F32), pltpu.VMEM((all_rows, qw), BF),
         pltpu.VMEM((all_rows, 2 * kw), BF), pltpu.VMEM((dim, width), BF),
         pltpu.VMEM((all_rows, dim), BF), DMA((2,)), DMA((3,)), *in_scratch],
        out_grad, normed_all, w_attn, cos_table, sin_table, qg, kg,
    )
    gu_shard, d_shard, kv = after((gu_shard, d_shard, kv))
    w_gu, w_d = gather(gu_shard), gather(d_shard)
    attended, attended_low, lse = attn_fwd(fwd_tab, queries, kv, groups, hd, block)
    w_o = w_attn[:, qw + 2 * kw :]
    middle, normed_mlp = comm_call(
        ring(middle_kernel, wide, narrow), "middle_rows", 2, (full_rows, all_low), [HB, VM, VM], (VM, HB),
        [row_buf, *sum_s, *spread_s], dg(attended_low, w_o, NT).astype(BF), layer_input, mlp_gain[None],
    )
    factors, hidden_low = mlp_fwd(normed_mlp, w_gu, t)
    grad_down = dg(grad_all, hidden_low, TN).astype(BF)
    w_d, _ = after((w_d, grad_down))
    middle_back, middle_low, mlp_gain_part, grad_gu = comm_call(
        ring(mlp_back_kernel, wide, narrow), "mlp_back", 6,
        (full_rows, low_rows, sds((1, dim), F32), sds((dim, 2 * ff), BF)), [HB, HB, HB, HB, HB, HB, VM, HB], (HB, VM, VM, HB),
        [pltpu.VMEM((all_rows, dim), BF), pltpu.VMEM((2, dim, t), BF), pltpu.VMEM((2, all_rows, 2 * t), BF),
         pltpu.VMEM((all_rows, 2 * ff), BF), pltpu.VMEM((dim, 2 * ff), BF), pltpu.VMEM((all_rows, dim), BF),
         pltpu.VMEM((rows, dim), F32), row_buf, pltpu.VMEM((rows, dim), F32), pltpu.VMEM((2, 256, 2 * ff), BF),
         product_bufs(narrow, rows, dim), DMA((6,)), DMA((2, 2)), DMA((2,)), DMA, *sum_s],
        grad_all, w_d, factors, w_gu, normed_mlp, middle, mlp_gain[None], out_grad,
    )
    grad_down, grad_gu = scatter(grad_down), scatter(grad_gu)
    middle_all, down_part, back, delta = comm_call(
        ring(middle_back_kernel, wide, narrow, (width, qw), groups, hd), "middle_back", 3,
        (all_low, all_low, sds((all_rows, qw), BF), sds((8 * kv_heads, all_rows), F32)),
        [VM, HB, HB, HB, HB], (HB, HB, VM, VM),
        [pltpu.VMEM((all_rows, dim), BF), pltpu.VMEM((all_rows, dim), BF), pltpu.VMEM((all_rows, ff), BF), pltpu.VMEM((dim, ff), BF), pltpu.VMEM((dim, qw), BF), pltpu.VMEM((all_rows, qw), F32),
         DMA((4,)), DMA((narrow,)), DMA((all_rows // 256,)), *spread_s],
        middle_low, hidden_low, w_d, w_attn, attended,
    )
    query_back, dkv = attn_bwd(bwd_tab, queries, back, kv, lse, delta, groups, hd, block)
    dkv, grad_down = after((dkv, grad_down))
    layer_output, kv_sum, q_low, query_gain_part, grad_qo = comm_call(
        ring(output_kernel, wide, narrow), "output_rows", 4,
        (low_rows, sds((all_rows, 2 * kw), BF), sds((all_rows, qw), BF), sds((1, hd), F32), sds((dim, 2 * qw), BF)),
        [HB, HB, HB, HB, HB, VM, VM, VM, HB, HB, HB], (HB, VM, HB, VM, HB),
        [row_buf, pltpu.VMEM((all_rows, qw), BF), pltpu.VMEM((dim, 2 * qw), BF), pltpu.VMEM((all_rows, qw), F32), pltpu.VMEM((all_rows, qw), F32), pltpu.VMEM((all_rows, dim), BF),
         pltpu.VMEM((all_rows, dim), BF), pltpu.VMEM((all_rows, qw), BF), pltpu.VMEM((rows, dim), F32), DMA((6,)), DMA((dim // 256,)),
         DMA((2,)), *sum_s,
         *line_sum_bufs(chips, all_rows, 2 * kw), *line_sum_sems(chips)],
        down_part, middle, dkv, query_back, query_proj, cos_table, sin_table, qg, normed_all, middle_all, attended_low,
    )
    kv_sum, grad_gu = after((kv_sum, grad_gu))
    gains = sds((1, 2 * dim + 2 * hd), F32)
    w_rows = dim // wide
    input_grad, gain_sums, grad_qo, grad_kv = comm_call(
        ring(input_back_kernel, wide, narrow, qw, kw), "input_back", 5,
        (full_rows, gains, sds((w_rows, 2 * qw), F32), sds((w_rows, 2 * kw), F32)),
        [HB, VM, HB, VM, VM, HB, VM, VM, VM, VM, VM, VM, HB, HB],
        (HB, VM, VM, VM),
        [pltpu.VMEM((narrow, *gains.shape), F32), pltpu.VMEM((wide, *gains.shape), F32),
         pltpu.VMEM((all_rows, width), BF), pltpu.VMEM((all_rows, dim), BF), pltpu.VMEM((dim, 2 * kw), BF),
         pltpu.VMEM((dim, width), BF), pltpu.VMEM((all_rows, dim), BF),
         row_buf, pltpu.VMEM((rows, dim), F32), pltpu.VMEM((rows, dim), F32), DMA((4,)), DMA, DMA((narrow,)), DMA((narrow,)), DMA((wide,)), DMA((wide,)), *sum_s,
         *line_sum_bufs(chips, w_rows, 2 * qw)[:4], *line_sum_sems(chips),
         *line_sum_bufs(chips, w_rows, 2 * kw)[:4], *line_sum_sems(chips)],
        layer_input, attn_gain[None], middle_back, mlp_gain_part, query_gain_part, grad_qo, q_low, kv_sum, key_proj, cos_table, sin_table, kg, w_attn, normed_all,
    )
    tm = min(w_rows, 128)
    turned = lambda height: pl.BlockSpec((height, tm), lambda i: (0, i))
    grads = plain(
        finish_kernel, "finish", (w_rows // tm,),
        [by_rows(tm, 2 * ff), by_rows(tm, ff), by_rows(tm, 2 * qw), by_rows(tm, 2 * kw)],
        [by_rows(tm, ff), by_rows(tm, ff), turned(ff), by_rows(tm, qw), by_rows(tm, kw), by_rows(tm, kw), turned(qw)],
        [sds(shape, F32) for shape in (w_gate.shape, w_up.shape, w_down.shape, w_query.shape, w_key.shape, w_value.shape,
                                       w_output.shape)],
        0, 10 * dim // wide * (3 * ff + qw), grad_gu, grad_down, grad_qo, grad_kv,
    )
    grad_gate, grad_up, grad_down, grad_query, grad_key, grad_value, grad_output = grads
    g = gain_sums[0]
    return (
        layer_output, input_grad, grad_query, grad_key, grad_value, grad_output, grad_gate, grad_up, grad_down,
        g[:dim], g[dim : 2 * dim], g[2 * dim : 2 * dim + hd], g[2 * dim + hd :],
    )


def solution(mesh):
    rows = P(("wide", "narrow"), None)
    weight, turned = P("wide", "narrow"), P("narrow", "wide")
    return jax.shard_map(
        functools.partial(per_device, mesh.shape["wide"], mesh.shape["narrow"]),
        mesh=mesh,
        in_specs=(rows, weight, weight, weight, turned, weight, weight, turned, P(), P(), P(), P(), rows),
        out_specs=(rows, rows, weight, weight, weight, turned, weight, weight, turned, P(), P(), P(), P()),
        check_vma=False,
    )
```
